32 devices in a mesh: dp: 8 (over z, core), seq: 4 (over y, x).
Axes of the slice: x: 2, y: 2, z: 4, core: 2. Of those that a mesh axis runs over, the one named last changes fastest.
Arguments:
- hidden_in: bfloat16 [2, 8, 2048, 1024], P(None, 'dp', 'seq'), may hold values from -6 to 6
- encoder_states: bfloat16 [2, 8, 512, 1024], P(None, 'dp', 'seq'), may hold values from -6 to 6
- segments: int32 [2, 8, 2048], P(None, 'dp', 'seq'), may hold values from 0 to 14, never falling along the last dimension, each value on 1 to 1280 neighbouring positions
- enc_segments: int32 [2, 8, 512], P(None, 'dp', 'seq'), may hold values from 0 to 14, never falling along the last dimension, each value on 1 to 256 neighbouring positions
- grad_out: bfloat16 [2, 8, 2048, 1024], P(None, 'dp', 'seq'), may hold values from -6 to 6
- norm_self: bfloat16 [1024], P(('dp', 'seq')), may hold values from 0.5 to 1.5
- q_self: bfloat16 [1024, 1024], P(('dp', 'seq')), may hold values from -0.046875 to 0.046875
- k_self: bfloat16 [1024, 1024], P(('dp', 'seq')), may hold values from -0.1875 to 0.1875
- v_self: bfloat16 [1024, 1024], P(('dp', 'seq')), may hold values from -0.1875 to 0.1875
- o_self: bfloat16 [1024, 1024], P(('dp', 'seq')), may hold values from -0.75 to 0.75
- rel_bias: bfloat16 [512], P(('dp', 'seq')), may hold values from -4 to 4
- norm_cross: bfloat16 [1024], P(('dp', 'seq')), may hold values from 0.5 to 1.5
- q_cross: bfloat16 [1024, 1024], P(('dp', 'seq')), may hold values from -0.046875 to 0.046875
- k_cross: bfloat16 [1024, 1024], P(('dp', 'seq')), may hold values from -0.1875 to 0.1875
- v_cross: bfloat16 [1024, 1024], P(('dp', 'seq')), may hold values from -0.1875 to 0.1875
- o_cross: bfloat16 [1024, 1024], P(('dp', 'seq')), may hold values from -0.75 to 0.75
- norm_ff: bfloat16 [1024], P(('dp', 'seq')), may hold values from 0.5 to 1.5
- wi_gate: bfloat16 [1024, 2816], P(('dp', 'seq')), may hold values from -0.1875 to 0.1875
- wi_up: bfloat16 [1024, 2816], P(('dp', 'seq')), may hold values from -0.1875 to 0.1875
- wo_ff: bfloat16 [2816, 1024], P(('dp', 'seq')), may hold values from -0.109375 to 0.109375
Outputs:
- block_out: bfloat16 [2, 8, 2048, 1024], P(None, 'dp', 'seq')
- grad_hidden_in: float32 [2, 8, 2048, 1024], P(None, 'dp', 'seq')
- grad_encoder: float32 [2, 8, 512, 1024], P(None, 'dp', 'seq')
- grad_norm_self: float32 [1024], P(('dp', 'seq'))
- grad_q_self: float32 [1024, 1024], P(('dp', 'seq'))
- grad_k_self: float32 [1024, 1024], P(('dp', 'seq'))
- grad_v_self: float32 [1024, 1024], P(('dp', 'seq'))
- grad_o_self: float32 [1024, 1024], P(('dp', 'seq'))
- grad_rel_bias: float32 [512], P(('dp', 'seq'))
- grad_norm_cross: float32 [1024], P(('dp', 'seq'))
- grad_q_cross: float32 [1024, 1024], P(('dp', 'seq'))
- grad_k_cross: float32 [1024, 1024], P(('dp', 'seq'))
- grad_v_cross: float32 [1024, 1024], P(('dp', 'seq'))
- grad_o_cross: float32 [1024, 1024], P(('dp', 'seq'))
- grad_norm_ff: float32 [1024], P(('dp', 'seq'))
- grad_wi_gate: float32 [1024, 2816], P(('dp', 'seq'))
- grad_wi_up: float32 [1024, 2816], P(('dp', 'seq'))
- grad_wo_ff: float32 [2816, 1024], P(('dp', 'seq'))
The draws below stay inside these ranges and needn't reach their ends.
Inputs may be any that keep to these rules, and one draw needn't show every extreme that they name: `segments`: within each sequence the document numbers never fall; every number from 0 to 14 appears, one document has exactly 1280 tokens. `enc_segments`: within each sequence the numbers never fall and every document of the sequence has at least one encoder state; one has exactly 256.
All inputs are finite; a program needn't handle non-finite values.
Results may differ from the reference program's by a relative error of at most 0.023.
The reference program's roundings to bfloat16 on the way count: a program that leaves them out, or rounds other values in their place, can miss the bound.
Values may be sent and summed in bfloat16 or wider, within the bound.
A program may use at most 512 MiB of HBM per device.

```python
import math
import jax
import jax.numpy as jnp
import numpy as np
from jax import lax

D = 1024
HEADS = 16
HEAD_DIM = 64
FF = 2816
BUCKETS = 32
MAX_DIST = 128
MICRO = 2
SEQ_LEN = 2048
ENC_LEN = 512
BATCH = 8


def level_of(key, dims, cuts, smallest, largest):
    level, own = 1.0, jax.random.fold_in(key, 6)
    for position, parts in cuts:
        draws = jnp.exp(jax.random.uniform(jax.random.fold_in(own, position), (parts,), jnp.float32, smallest / len(cuts), largest / len(cuts)))
        level = level * jnp.repeat(draws, dims[position] // parts).reshape([-1 if axis == position else 1 for axis in range(len(dims))])
    return level


def length_profile(number_of, total, bound, lean):
    weights = [(1 << 20) // math.isqrt(grade ** lean) + 1 for grade in range(2, number_of + 1)]
    rest, holding = total - bound - (number_of - 1), [1] * (number_of - 1)
    while rest > 0:
        candidates = [i for i in range(number_of - 1) if holding[i] < bound]
        pool, remaining = sum([weights[i] for i in candidates]), rest
        for i in candidates:
            more = min(bound - holding[i], max(1, remaining * weights[i] // pool), rest)
            holding[i] = holding[i] + more
            rest = rest - more
    return np.array([bound] + holding)


def ragged_sizes(own_key, count, total, reach, skew):
    if count == 2:
        one = jax.random.randint(own_key, (), max(1, total - reach), min(reach, total - 1) + 1)
        return jnp.stack([one, total - one])
    lengths = jnp.asarray(length_profile(count, total, reach, skew), jnp.int32)
    twos = (count - 1) // 2
    source_of, receiver = lengths[1:1 + 2 * twos:2], lengths[2:2 + 2 * twos:2]
    room = jnp.minimum(source_of - 1, reach - receiver)
    moved = jax.random.randint(jax.random.fold_in(own_key, 1), (twos,), 0, 1 << 20) % (room + 1)
    lengths = lengths.at[1:1 + 2 * twos:2].set(source_of - moved).at[2:2 + 2 * twos:2].set(receiver + moved)
    return lengths[jax.random.permutation(jax.random.fold_in(own_key, 2), count)]


def scatter_about(rng, extent, width, limit, split=(), held_as=jnp.bfloat16):
    values = width * jax.random.normal(rng, extent, jnp.float32)
    if split:
        values = values * level_of(rng, extent, split, -0.22, 0.18)
    return jnp.clip(values, -limit, limit).astype(held_as)


def setup_inputs(seed: int = 0) -> dict:
    arg_keys = jax.random.split(jax.random.key(seed), 21)
    return {
        "hidden_in": scatter_about(arg_keys[0], (MICRO, BATCH, SEQ_LEN, D), 1.0, 6.0, ((1, 8), (2, 4))),
        "encoder_states": scatter_about(arg_keys[1], (MICRO, BATCH, ENC_LEN, D), 1.0, 6.0, ((1, 8), (2, 4))),
        "segments": jax.vmap(lambda own: jnp.searchsorted(jnp.cumsum(ragged_sizes(own, SEQ_LEN // 160 + 3, SEQ_LEN, SEQ_LEN * 5 // 8, 2)), jnp.arange(SEQ_LEN), side="right"))(jax.random.split(arg_keys[2], MICRO * BATCH)).reshape((MICRO, BATCH, SEQ_LEN)).astype(jnp.int32),
        "enc_segments": jax.vmap(lambda own: jnp.searchsorted(jnp.cumsum(ragged_sizes(own, SEQ_LEN // 160 + 3, ENC_LEN, ENC_LEN // 2, 2)), jnp.arange(ENC_LEN), side="right"))(jax.random.split(arg_keys[3], MICRO * BATCH)).reshape((MICRO, BATCH, ENC_LEN)).astype(jnp.int32),
        "grad_out": scatter_about(arg_keys[4], (MICRO, BATCH, SEQ_LEN, D), 1.0, 6.0, ((1, 8), (2, 4))),
        "norm_self": jnp.clip(1.0 + 0.1 * jax.random.normal(arg_keys[5], (D,), jnp.float32), 0.5, 1.5).astype(jnp.bfloat16),
        "q_self": scatter_about(arg_keys[6], (D, D), (16 * D) ** -0.5, 0.046875, ((0, 32),)),
        "k_self": scatter_about(arg_keys[7], (D, D), D ** -0.5, 0.1875, ((0, 32),)),
        "v_self": scatter_about(arg_keys[8], (D, D), D ** -0.5, 0.1875, ((0, 32),)),
        "o_self": scatter_about(arg_keys[9], (D, D), (D // 16) ** -0.5, 0.75, ((0, 32),)),
        "rel_bias": scatter_about(arg_keys[10], (BUCKETS * HEADS,), 1.0, 4.0, ((0, 32),)),
        "norm_cross": jnp.clip(1.0 + 0.1 * jax.random.normal(arg_keys[11], (D,), jnp.float32), 0.5, 1.5).astype(jnp.bfloat16),
        "q_cross": scatter_about(arg_keys[12], (D, D), (16 * D) ** -0.5, 0.046875, ((0, 32),)),
        "k_cross": scatter_about(arg_keys[13], (D, D), D ** -0.5, 0.1875, ((0, 32),)),
        "v_cross": scatter_about(arg_keys[14], (D, D), D ** -0.5, 0.1875, ((0, 32),)),
        "o_cross": scatter_about(arg_keys[15], (D, D), (D // 16) ** -0.5, 0.75, ((0, 32),)),
        "norm_ff": jnp.clip(1.0 + 0.1 * jax.random.normal(arg_keys[16], (D,), jnp.float32), 0.5, 1.5).astype(jnp.bfloat16),
        "wi_gate": scatter_about(arg_keys[17], (D, FF), D ** -0.5, 0.1875, ((0, 32),)),
        "wi_up": scatter_about(arg_keys[18], (D, FF), D ** -0.5, 0.1875, ((0, 32),)),
        "wo_ff": scatter_about(arg_keys[19], (FF, D), FF ** -0.5, 0.109375, ((0, 32),)),
    }


@jax.custom_vjp
def low(v):
    return lax.optimization_barrier(v.astype(jnp.bfloat16)).astype(jnp.float32)

@jax.custom_vjp
def low_back(v):
    return v

def low_keep(v):
    return (low(v), None)

def low_pass(kept, grad):
    return (grad,)

def back_keep(v):
    return (v, None)

def back_low(kept, grad):
    return (low(grad),)
low.defvjp(low_keep, low_pass)
low_back.defvjp(back_keep, back_low)
HIGH = lax.Precision.HIGHEST
NEG = -1e+30
EPS = 1e-06

def matmul(left, right):
    return jnp.dot(left, right, precision=HIGH, preferred_element_type=jnp.float32)

def norm_rows(value, gain):
    return value * lax.rsqrt(lax.optimization_barrier(jnp.mean(value * value, axis=-1, keepdims=True)) + EPS) * gain

def bucket_edges():
    half = BUCKETS // 2
    return [math.ceil(half * (MAX_DIST / half) ** (step / half)) for step in range(1, half)]

def buckets_of(distance):
    half = BUCKETS // 2
    far = half + sum(((distance >= edge).astype(jnp.int32) for edge in bucket_edges()))
    return jnp.where(distance < half, distance, far).astype(jnp.int32)

def attention_rows(q_rows, keys, values, bias_rows, allowed):
    scores = jnp.einsum('qhd,khd->hqk', q_rows, keys, precision=HIGH) + bias_rows
    scores = low_back(scores)
    scores = jnp.where(allowed[None], scores, NEG)
    probs = low(jax.nn.softmax(scores, axis=-1))
    return jnp.einsum('hqk,khd->qhd', probs, values, precision=HIGH)

def self_attention(queries, keys, values, seg, table):
    length = queries.shape[0]
    block = min(512, length)
    q_blocks = queries.reshape(length // block, block, HEADS, HEAD_DIM)
    key_heads = keys.reshape(length, HEADS, HEAD_DIM)
    value_heads = values.reshape(length, HEADS, HEAD_DIM)
    columns = jnp.arange(length, dtype=jnp.int32)

    def one_block(items):
        q_rows, start = items
        positions = start + jnp.arange(block, dtype=jnp.int32)
        distance = jnp.maximum(positions[:, None] - columns[None, :], 0)
        bias_rows = jnp.transpose(table[buckets_of(distance)], (2, 0, 1))
        seg_rows = lax.dynamic_slice_in_dim(seg, start, block)
        allowed = (seg_rows[:, None] == seg[None, :]) & (columns[None, :] <= positions[:, None])
        return attention_rows(q_rows, key_heads, value_heads, bias_rows, allowed)
    starts = (jnp.arange(length // block, dtype=jnp.int32) * block).astype(jnp.int32)
    result = lax.map(jax.checkpoint(one_block), (q_blocks, starts))
    return result.reshape(length, HEADS * HEAD_DIM)

def cross_attention(queries, keys, values, seg, enc_seg):
    length = queries.shape[0]
    block = min(512, length)
    q_blocks = queries.reshape(length // block, block, HEADS, HEAD_DIM)
    key_heads = keys.reshape(keys.shape[0], HEADS, HEAD_DIM)
    value_heads = values.reshape(values.shape[0], HEADS, HEAD_DIM)

    def one_block(items):
        q_rows, start = items
        seg_rows = lax.dynamic_slice_in_dim(seg, start, block)
        allowed = seg_rows[:, None] == enc_seg[None, :]
        return attention_rows(q_rows, key_heads, value_heads, 0.0, allowed)
    starts = (jnp.arange(length // block, dtype=jnp.int32) * block).astype(jnp.int32)
    result = lax.map(jax.checkpoint(one_block), (q_blocks, starts))
    return result.reshape(length, HEADS * HEAD_DIM)

def layer(inputs, encoder, seg, enc_seg, params):
    gain_self, wq, wk, wv, wo, table_flat, gain_cross, cq, ck, cv, co, gain_ff, w_gate, w_up, w_down = params
    table = table_flat.reshape(BUCKETS, HEADS)
    normed_self = low(norm_rows(inputs, gain_self))
    query = low_back(low(matmul(normed_self, wq)))
    key = low_back(low(matmul(normed_self, wk)))
    value = low_back(low(matmul(normed_self, wv)))
    mixed = low_back(low(self_attention(query, key, value, seg, table)))
    after_self = inputs + low_back(matmul(mixed, wo))
    normed_cross = low(norm_rows(after_self, gain_cross))
    cross_query = low_back(low(matmul(normed_cross, cq)))
    cross_key = low_back(low(matmul(encoder, ck)))
    cross_value = low_back(low(matmul(encoder, cv)))
    cross_mixed = low_back(low(cross_attention(cross_query, cross_key, cross_value, seg, enc_seg)))
    after_cross = after_self + low_back(matmul(cross_mixed, co))
    normed_ff = low(norm_rows(after_cross, gain_ff))
    gate = low_back(matmul(normed_ff, w_gate))
    up_values = low_back(matmul(normed_ff, w_up))
    hidden = low(jax.nn.gelu(gate, approximate=True) * up_values)
    return after_cross + low_back(matmul(hidden, w_down))

def reference(hidden_in, encoder_states, segments, enc_segments, grad_out, norm_self, q_self, k_self, v_self, o_self, rel_bias, norm_cross, q_cross, k_cross, v_cross, o_cross, norm_ff, wi_gate, wi_up, wo_ff):
    weights = tuple((piece.astype(jnp.float32) for piece in (norm_self, q_self, k_self, v_self, o_self, rel_bias, norm_cross, q_cross, k_cross, v_cross, o_cross, norm_ff, wi_gate, wi_up, wo_ff)))
    count = hidden_in.shape[0] * hidden_in.shape[1]
    inputs = hidden_in.reshape(count, SEQ_LEN, D).astype(jnp.float32)
    encoder_outputs = encoder_states.reshape(count, ENC_LEN, D).astype(jnp.float32)
    seg_all = segments.reshape(count, SEQ_LEN)
    enc_seg_all = enc_segments.reshape(count, ENC_LEN)
    cotangents = grad_out.reshape(count, SEQ_LEN, D).astype(jnp.float32)

    def step(totals, items):
        x_seq, enc_seq, seg, enc_seg, cotangent = items

        def forward(x_in, enc_in, *params):
            return layer(x_in, enc_in, seg, enc_seg, params)
        result, pull = jax.vjp(forward, x_seq, enc_seq, *weights)
        grads = pull(cotangent)
        totals = tuple((total + grad for total, grad in zip(totals, grads[2:])))
        return (totals, (result, grads[0], grads[1]))
    zeros = tuple((jnp.zeros(piece.shape, jnp.float32) for piece in weights))
    totals, (results, grad_inputs, grad_encoders) = lax.scan(step, zeros, (inputs, encoder_outputs, seg_all, enc_seg_all, cotangents))
    block_out = results.reshape(hidden_in.shape).astype(jnp.bfloat16)
    grad_hidden_in = grad_inputs.reshape(hidden_in.shape)
    grad_encoder = grad_encoders.reshape(encoder_states.shape)
    return (block_out, grad_hidden_in, grad_encoder, totals[0], totals[1], totals[2], totals[3], totals[4], totals[5], totals[6], totals[7], totals[8], totals[9], totals[10], totals[11], totals[12], totals[13], totals[14])
```

```python
import functools
import math

import jax
import jax.numpy as jnp
from jax import lax
from jax.experimental import pallas as pl
from jax.experimental.pallas import tpu as pltpu
from jax.sharding import PartitionSpec as P

HEADS = 16
HEAD_DIM = 64
BUCKETS = 32
MAX_DIST = 128


EPS = 1e-06
NEG = -1e30


def norm_rows(value, gain):
    return value * lax.rsqrt(jnp.mean(value * value, axis=-1, keepdims=True) + EPS) * gain


def bucket_edges():
    half = BUCKETS // 2
    return [math.ceil(half * (MAX_DIST / half) ** (step / half)) for step in range(1, half)]


def buckets_of(distance):
    half = BUCKETS // 2
    far = half + sum(((distance >= edge).astype(jnp.int32) for edge in bucket_edges()))
    return jnp.where(distance < half, distance, far)


def by_heads(values):
    return values.reshape(values.shape[0], values.shape[1], HEADS, HEAD_DIM)


def join_heads(values):
    return values.reshape(values.shape[0], values.shape[1], HEADS * HEAD_DIM)


def project(rows, weight_matrix):
    return jnp.dot(rows, weight_matrix, preferred_element_type=jnp.float32)


def project_back(grads, weight_matrix):
    return jnp.einsum("stn,kn->stk", grads, weight_matrix, preferred_element_type=jnp.float32)


def weight_grad(rows, grads):
    return jnp.einsum("stk,stn->kn", rows, grads, preferred_element_type=jnp.float32)


def gelu_mix(gate, up_values):
    return jax.nn.gelu(gate, approximate=True) * up_values


def scores_of(q_rows, keys, bias, allowed):
    scores = jnp.einsum("sqhd,skhd->shqk", q_rows, keys, preferred_element_type=jnp.float32) + bias
    return jnp.where(allowed[:, None], scores, NEG)


def attend(q_rows, keys, values, bias, allowed):
    scores = scores_of(q_rows, keys, bias, allowed)
    largest = jnp.max(scores, axis=-1, keepdims=True)
    raised = jnp.exp(scores - largest)
    total = jnp.sum(raised, axis=-1, keepdims=True)
    probs = raised / total
    mixed = jnp.einsum(
        "shqk,skhd->sqhd", probs.astype(jnp.bfloat16), values, preferred_element_type=jnp.float32
    )
    return (join_heads(mixed).astype(jnp.bfloat16), largest + jnp.log(total))


def attend_back(q_rows, keys, values, bias, allowed, log_total, grad_mixed):
    scores = scores_of(q_rows, keys, bias, allowed)
    probs = jnp.exp(scores - log_total)
    grad_probs = jnp.einsum(
        "sqhd,skhd->shqk", grad_mixed, values, preferred_element_type=jnp.float32
    )
    inner = jnp.sum(probs * grad_probs, axis=-1, keepdims=True)
    grad_scores = (probs * (grad_probs - inner)).astype(jnp.bfloat16)
    grad_query = jnp.einsum(
        "shqk,skhd->sqhd", grad_scores, keys, preferred_element_type=jnp.float32
    )
    grad_keys = jnp.einsum(
        "shqk,sqhd->skhd", grad_scores, q_rows, preferred_element_type=jnp.float32
    )
    grad_values = jnp.einsum(
        "shqk,sqhd->skhd",
        probs.astype(jnp.bfloat16),
        grad_mixed,
        preferred_element_type=jnp.float32,
    )
    return (join_heads(grad_query), join_heads(grad_keys), join_heads(grad_values), grad_scores)


def general_body(
    hidden_in,
    encoder_states,
    segments,
    enc_segments,
    grad_out,
    norm_self,
    q_self,
    k_self,
    v_self,
    o_self,
    rel_bias,
    norm_cross,
    q_cross,
    k_cross,
    v_cross,
    o_cross,
    norm_ff,
    wi_gate,
    wi_up,
    wo_ff,
):
    shards = (
        norm_self,
        q_self,
        k_self,
        v_self,
        o_self,
        rel_bias,
        norm_cross,
        q_cross,
        k_cross,
        v_cross,
        o_cross,
        norm_ff,
        wi_gate,
        wi_up,
        wo_ff,
    )
    micro_count = hidden_in.shape[0]
    rows_dev = hidden_in.shape[2]
    seg_whole, enc_seg_whole = (
        lax.all_gather(segments, "seq", axis=2, tiled=True),
        lax.all_gather(enc_segments, "seq", axis=2, tiled=True),
    )
    length = seg_whole.shape[2]
    positions = lax.axis_index("seq") * rows_dev + jnp.arange(rows_dev, dtype=jnp.int32)
    columns = jnp.arange(length, dtype=jnp.int32)
    distance = jnp.maximum(positions[:, None] - columns[None, :], 0)
    bucket_indicator = (
        buckets_of(distance)[None] == jnp.arange(BUCKETS, dtype=jnp.int32)[:, None, None]
    ).astype(jnp.bfloat16)
    causal = columns[None, :] <= positions[:, None]
    grad_shards = tuple((jnp.zeros(piece.shape, jnp.float32) for piece in shards))
    outputs, grad_inputs, grad_encoders = ([], [], [])
    for micro in range(micro_count):
        params = (
            lax.all_gather(shards[0], ("dp", "seq"), axis=0, tiled=True),
            lax.all_gather(shards[1], ("dp", "seq"), axis=0, tiled=True),
            lax.all_gather(shards[2], ("dp", "seq"), axis=0, tiled=True),
            lax.all_gather(shards[3], ("dp", "seq"), axis=0, tiled=True),
            lax.all_gather(shards[4], ("dp", "seq"), axis=0, tiled=True),
            lax.all_gather(shards[5], ("dp", "seq"), axis=0, tiled=True),
            lax.all_gather(shards[6], ("dp", "seq"), axis=0, tiled=True),
            lax.all_gather(shards[7], ("dp", "seq"), axis=0, tiled=True),
            lax.all_gather(shards[8], ("dp", "seq"), axis=0, tiled=True),
            lax.all_gather(shards[9], ("dp", "seq"), axis=0, tiled=True),
            lax.all_gather(shards[10], ("dp", "seq"), axis=0, tiled=True),
            lax.all_gather(shards[11], ("dp", "seq"), axis=0, tiled=True),
            lax.all_gather(shards[12], ("dp", "seq"), axis=0, tiled=True),
            lax.all_gather(shards[13], ("dp", "seq"), axis=0, tiled=True),
            lax.all_gather(shards[14], ("dp", "seq"), axis=0, tiled=True),
        )
        (
            gain_self,
            wq,
            wk,
            wv,
            wo,
            table_flat,
            gain_cross,
            cq,
            ck,
            cv,
            co,
            gain_ff,
            w_gate,
            w_up,
            w_down,
        ) = params
        bias = jnp.einsum(
            "pia,pw->wia",
            bucket_indicator,
            table_flat.reshape(BUCKETS, HEADS),
            preferred_element_type=jnp.float32,
        )
        inputs = hidden_in[micro].astype(jnp.float32)
        encoder = encoder_states[micro]
        seg_own = segments[micro]
        self_allowed = (seg_own[:, :, None] == seg_whole[micro][:, None, :]) & causal[None]
        cross_allowed = seg_own[:, :, None] == enc_seg_whole[micro][:, None, :]
        self_norm_scale = gain_self.astype(jnp.float32)
        cross_gain = gain_cross.astype(jnp.float32)
        ff_gain = gain_ff.astype(jnp.float32)
        normed_self = norm_rows(inputs, self_norm_scale).astype(jnp.bfloat16)
        query = project(normed_self, wq).astype(jnp.bfloat16)
        key_own = project(normed_self, wk).astype(jnp.bfloat16)
        value_own = project(normed_self, wv).astype(jnp.bfloat16)
        cross_key_own = project(encoder, ck).astype(jnp.bfloat16)
        cross_value_own = project(encoder, cv).astype(jnp.bfloat16)
        keys, values, cross_keys, cross_values = (
            lax.all_gather(key_own, "seq", axis=1, tiled=True),
            lax.all_gather(value_own, "seq", axis=1, tiled=True),
            lax.all_gather(cross_key_own, "seq", axis=1, tiled=True),
            lax.all_gather(cross_value_own, "seq", axis=1, tiled=True),
        )
        mixed, self_log_normalizer = attend(
            by_heads(query), by_heads(keys), by_heads(values), bias, self_allowed
        )
        after_self = inputs + project(mixed, wo)
        normed_cross = norm_rows(after_self, cross_gain).astype(jnp.bfloat16)
        cross_query = project(normed_cross, cq).astype(jnp.bfloat16)
        cross_mixed, cross_log = attend(
            by_heads(cross_query), by_heads(cross_keys), by_heads(cross_values), 0.0, cross_allowed
        )
        after_cross = after_self + project(cross_mixed, co)
        normed_ff = norm_rows(after_cross, ff_gain).astype(jnp.bfloat16)
        gate = project(normed_ff, w_gate)
        up_values = project(normed_ff, w_up)
        hidden = gelu_mix(gate, up_values).astype(jnp.bfloat16)
        result = after_cross + project(hidden, w_down)
        outputs.append(result.astype(jnp.bfloat16))
        params = (
            lax.all_gather(shards[0], ("dp", "seq"), axis=0, tiled=True),
            lax.all_gather(shards[1], ("dp", "seq"), axis=0, tiled=True),
            lax.all_gather(shards[2], ("dp", "seq"), axis=0, tiled=True),
            lax.all_gather(shards[3], ("dp", "seq"), axis=0, tiled=True),
            lax.all_gather(shards[4], ("dp", "seq"), axis=0, tiled=True),
            lax.all_gather(shards[5], ("dp", "seq"), axis=0, tiled=True),
            lax.all_gather(shards[6], ("dp", "seq"), axis=0, tiled=True),
            lax.all_gather(shards[7], ("dp", "seq"), axis=0, tiled=True),
            lax.all_gather(shards[8], ("dp", "seq"), axis=0, tiled=True),
            lax.all_gather(shards[9], ("dp", "seq"), axis=0, tiled=True),
            lax.all_gather(shards[10], ("dp", "seq"), axis=0, tiled=True),
            lax.all_gather(shards[11], ("dp", "seq"), axis=0, tiled=True),
            lax.all_gather(shards[12], ("dp", "seq"), axis=0, tiled=True),
            lax.all_gather(shards[13], ("dp", "seq"), axis=0, tiled=True),
            lax.all_gather(shards[14], ("dp", "seq"), axis=0, tiled=True),
        )
        (
            gain_self,
            wq,
            wk,
            wv,
            wo,
            table_flat,
            gain_cross,
            cq,
            ck,
            cv,
            co,
            gain_ff,
            w_gate,
            w_up,
            w_down,
        ) = params
        grad_result = grad_out[micro].astype(jnp.float32)
        out_low = grad_out[micro]
        grad_w_down = weight_grad(hidden, out_low)
        grad_hidden = project_back(out_low, w_down)
        mix_value, mix_pull = jax.vjp(gelu_mix, gate, up_values)
        grad_gate, grad_up = mix_pull(grad_hidden)
        grad_gate = grad_gate.astype(jnp.bfloat16)
        grad_up = grad_up.astype(jnp.bfloat16)
        gate_weight_gradient = weight_grad(normed_ff, grad_gate)
        grad_w_up = weight_grad(normed_ff, grad_up)
        grad_normed_ff = project_back(grad_gate, w_gate) + project_back(grad_up, w_up)
        norm_value, norm_pull = jax.vjp(norm_rows, after_cross, ff_gain)
        ff_part, grad_gain_ff = norm_pull(grad_normed_ff)
        grad_after_cross = grad_result + ff_part
        cross_out_low = grad_after_cross.astype(jnp.bfloat16)
        grad_co = weight_grad(cross_mixed, cross_out_low)
        grad_cross_mixed = project_back(cross_out_low, co).astype(jnp.bfloat16)
        grad_cross_query, cross_key_terms, cross_value_terms, cross_scores = attend_back(
            by_heads(cross_query),
            by_heads(cross_keys),
            by_heads(cross_values),
            0.0,
            cross_allowed,
            cross_log,
            by_heads(grad_cross_mixed),
        )
        grad_cross_key, grad_cross_value = (
            lax.psum_scatter(
                cross_key_terms.astype(jnp.bfloat16), "seq", scatter_dimension=1, tiled=True
            ).astype(jnp.float32),
            lax.psum_scatter(
                cross_value_terms.astype(jnp.bfloat16), "seq", scatter_dimension=1, tiled=True
            ).astype(jnp.float32),
        )
        grad_cross_key = grad_cross_key.astype(jnp.bfloat16)
        grad_cross_value = grad_cross_value.astype(jnp.bfloat16)
        cross_key_gradient = weight_grad(encoder, grad_cross_key)
        grad_cv = weight_grad(encoder, grad_cross_value)
        grad_encoders.append(project_back(grad_cross_key, ck) + project_back(grad_cross_value, cv))
        grad_cross_query = grad_cross_query.astype(jnp.bfloat16)
        grad_cq = weight_grad(normed_cross, grad_cross_query)
        grad_normed_cross = project_back(grad_cross_query, cq)
        norm_value, norm_pull = jax.vjp(norm_rows, after_self, cross_gain)
        cross_part, grad_gain_cross = norm_pull(grad_normed_cross)
        grad_after_self = grad_after_cross + cross_part
        self_out_low = grad_after_self.astype(jnp.bfloat16)
        grad_wo = weight_grad(mixed, self_out_low)
        grad_mixed = project_back(self_out_low, wo).astype(jnp.bfloat16)
        grad_query, key_terms, value_terms, self_attention_logits = attend_back(
            by_heads(query),
            by_heads(keys),
            by_heads(values),
            bias,
            self_allowed,
            self_log_normalizer,
            by_heads(grad_mixed),
        )
        grad_table = jnp.einsum(
            "dcma,uma->uc",
            self_attention_logits,
            bucket_indicator,
            preferred_element_type=jnp.float32,
        ).reshape(-1)
        grad_key, grad_value = (
            lax.psum_scatter(
                key_terms.astype(jnp.bfloat16), "seq", scatter_dimension=1, tiled=True
            ).astype(jnp.float32),
            lax.psum_scatter(
                value_terms.astype(jnp.bfloat16), "seq", scatter_dimension=1, tiled=True
            ).astype(jnp.float32),
        )
        grad_key = grad_key.astype(jnp.bfloat16)
        grad_value = grad_value.astype(jnp.bfloat16)
        grad_query = grad_query.astype(jnp.bfloat16)
        grad_wq = weight_grad(normed_self, grad_query)
        grad_wk = weight_grad(normed_self, grad_key)
        grad_wv = weight_grad(normed_self, grad_value)
        grad_normed_self = (
            project_back(grad_query, wq) + project_back(grad_key, wk) + project_back(grad_value, wv)
        )
        norm_value, norm_pull = jax.vjp(norm_rows, inputs, self_norm_scale)
        self_part, grad_gain_self = norm_pull(grad_normed_self)
        grad_inputs.append(grad_after_self + self_part)
        local = (
            grad_gain_self,
            grad_wq,
            grad_wk,
            grad_wv,
            grad_wo,
            grad_table,
            grad_gain_cross,
            grad_cq,
            cross_key_gradient,
            grad_cv,
            grad_co,
            grad_gain_ff,
            gate_weight_gradient,
            grad_w_up,
            grad_w_down,
        )
        summed = (
            lax.psum_scatter(local[0], ("dp", "seq"), scatter_dimension=0, tiled=True),
            lax.psum_scatter(local[1], ("dp", "seq"), scatter_dimension=0, tiled=True),
            lax.psum_scatter(local[2], ("dp", "seq"), scatter_dimension=0, tiled=True),
            lax.psum_scatter(local[3], ("dp", "seq"), scatter_dimension=0, tiled=True),
            lax.psum_scatter(local[4], ("dp", "seq"), scatter_dimension=0, tiled=True),
            lax.psum_scatter(local[5], ("dp", "seq"), scatter_dimension=0, tiled=True),
            lax.psum_scatter(local[6], ("dp", "seq"), scatter_dimension=0, tiled=True),
            lax.psum_scatter(local[7], ("dp", "seq"), scatter_dimension=0, tiled=True),
            lax.psum_scatter(local[8], ("dp", "seq"), scatter_dimension=0, tiled=True),
            lax.psum_scatter(local[9], ("dp", "seq"), scatter_dimension=0, tiled=True),
            lax.psum_scatter(local[10], ("dp", "seq"), scatter_dimension=0, tiled=True),
            lax.psum_scatter(local[11], ("dp", "seq"), scatter_dimension=0, tiled=True),
            lax.psum_scatter(local[12], ("dp", "seq"), scatter_dimension=0, tiled=True),
            lax.psum_scatter(local[13], ("dp", "seq"), scatter_dimension=0, tiled=True),
            lax.psum_scatter(local[14], ("dp", "seq"), scatter_dimension=0, tiled=True),
        )
        grad_shards = tuple((before + after for before, after in zip(grad_shards, summed)))
    return (jnp.stack(outputs), jnp.stack(grad_inputs), jnp.stack(grad_encoders)) + tuple(
        grad_shards
    )


TILE = 256
GROUP = 4
LANES = 128
F32 = jnp.float32
BF16 = jnp.bfloat16


def contract(left, right, left_dim, right_dim):
    return lax.dot_general(
        left, right, (((left_dim,), (right_dim,)), ((), ())), preferred_element_type=F32
    )


def head_mask(head):
    lane = lax.broadcasted_iota(jnp.int32, (1, LANES), 1)
    keep = (lane < HEAD_DIM) if head % 2 == 0 else (lane >= HEAD_DIM)
    return keep.astype(F32).astype(BF16)


def bias_table(line):
    first = jnp.concatenate(
        [line if j == 0 else pltpu.roll(line, j, 1) for j in range(8)], axis=0
    )
    return [first if r == 0 else pltpu.roll(first, 8 * r, 1) for r in range(TILE // 8)]


def line_of(table):
    total = None
    for r in range(TILE // 8):
        part = table[8 * r : 8 * r + 8, :]
        part = part if r == 0 else pltpu.roll(part, TILE - 8 * r, 1)
        total = part if total is None else total + part
    line = total[0:1, :]
    for j in range(1, 8):
        line = line + pltpu.roll(total[j : j + 1, :], TILE - j, 1)
    return line


def allowed_keys(segq, segk_ref, row, diagonal):
    segk = segk_ref[pl.ds(row, TILE), :]
    segk = jnp.concatenate([segk] * (TILE // LANES), axis=1)
    same = segk == segq
    if diagonal:
        k_pos = lax.broadcasted_iota(jnp.int32, (TILE, TILE), 0)
        q_pos = lax.broadcasted_iota(jnp.int32, (TILE, TILE), 1)
        same = same & (k_pos <= q_pos)
    return same


def pair_lanes(head):
    return slice((head // 2) * LANES, (head // 2 + 1) * LANES)


def load_keys(refs, own_rows, par_rows, kb, vb):
    ko, vo, kp, vp = refs
    kb[0:own_rows, :] = ko[...]
    vb[0:own_rows, :] = vo[...]
    kb[own_rows : own_rows + par_rows, :] = kp[...]
    vb[own_rows : own_rows + par_rows, :] = vp[...]


def fill_tables(line_ref, tab, adj):
    for h in range(GROUP):
        line = line_ref[h]
        for r, rows in enumerate(bias_table(line)):
            tab[h, 8 * r : 8 * r + 8, :] = rows
        table = tab[h]
        k_pos = lax.broadcasted_iota(jnp.int32, (TILE, TILE), 0)
        q_pos = lax.broadcasted_iota(jnp.int32, (TILE, TILE), 1)
        adj[h] = jnp.where(k_pos > q_pos, table, line[:, TILE - 1 : TILE])


def visit_tiles(causal, kinds_ref, tile, tiles):
    if not causal:
        for t in range(tiles):
            tile(t * TILE, 0)
        return
    i = pl.program_id(1)
    tile(pl.multiple_of(i * TILE, TILE), 3)

    def step(p, carry):
        kind = kinds_ref[i * tiles + p]
        row = pl.multiple_of(p * TILE, TILE)

        @pl.when(kind == 1)
        def _():
            tile(row, 1)

        @pl.when(kind == 2)
        def _():
            tile(row, 2)

        return carry

    lax.fori_loop(0, tiles, step, 0)


def with_bias(scores, kind, h, line_ref, tab, adj):
    if kind == 3:
        return scores + tab[h]
    if kind == 2:
        return scores + adj[h]
    if kind == 1:
        return scores + line_ref[h][:, TILE - 1 : TILE]
    return scores


def attend_kernel(causal, own_rows, par_rows, kinds_ref, q_ref, ko, vo, kp, vp, segq_ref, segk_ref,
                  line_ref, o_ref, lse_ref, kb, vb, qm, tab, adj, m_s, l_s, acc):
    @pl.when(pl.program_id(1) == 0)
    def _():
        load_keys((ko, vo, kp, vp), own_rows, par_rows, kb, vb)
        if causal:
            fill_tables(line_ref, tab, adj)

    for h in range(GROUP):
        qm[h] = q_ref[:, pair_lanes(h)] * head_mask(h)
    m_s[...] = jnp.full(m_s.shape, NEG, F32)
    l_s[...] = jnp.zeros(l_s.shape, F32)
    acc[...] = jnp.zeros(acc.shape, F32)
    segq = segq_ref[0:1, :]

    def tile(row, kind):
        allowed = allowed_keys(segq, segk_ref, row, kind == 3)
        for h in range(GROUP):
            scores = contract(kb[pl.ds(row, TILE), pair_lanes(h)], qm[h], 1, 1)
            scores = jnp.where(allowed, with_bias(scores, kind, h, line_ref, tab, adj), NEG)
            before = m_s[h : h + 1, :]
            largest = jnp.maximum(before, jnp.max(scores, axis=0, keepdims=True))
            raised = jnp.exp(scores - largest)
            scale = jnp.exp(before - largest)
            m_s[h : h + 1, :] = largest
            l_s[h : h + 1, :] = l_s[h : h + 1, :] * scale + jnp.sum(raised, axis=0, keepdims=True)
            mixed = contract(vb[pl.ds(row, TILE), pair_lanes(h)], raised.astype(BF16), 0, 0)
            half = (h % 2) * HEAD_DIM
            rows = slice(h * HEAD_DIM, (h + 1) * HEAD_DIM)
            acc[rows, :] = acc[rows, :] * scale + mixed[half : half + HEAD_DIM, :]

    visit_tiles(causal, kinds_ref, tile, (own_rows + par_rows) // TILE)
    for h in range(GROUP):
        rows = slice(h * HEAD_DIM, (h + 1) * HEAD_DIM)
        acc[rows, :] = acc[rows, :] / l_s[h : h + 1, :]
        lse_ref[0, h : h + 1, :] = m_s[h : h + 1, :] + jnp.log(l_s[h : h + 1, :])
    o_ref[...] = acc[...].T.astype(BF16)


def attend_back_kernel(causal, own_rows, par_rows, kinds_ref, q_ref, ko, vo, kp, vp, segq_ref, segk_ref,
                       line_ref, do_ref, o_ref, lse_ref, dq_ref, own_ref, par_ref, gline_ref, gfar_ref,
                       kb, vb, qm, dm, tab, adj, d_s, dq_acc, dk_acc, dv_acc, gt, gfar):
    i = pl.program_id(1)

    @pl.when(i == 0)
    def _():
        load_keys((ko, vo, kp, vp), own_rows, par_rows, kb, vb)
        dk_acc[...] = jnp.zeros(dk_acc.shape, F32)
        dv_acc[...] = jnp.zeros(dv_acc.shape, F32)
        gt[...] = jnp.zeros(gt.shape, F32)
        gfar[...] = jnp.zeros(gfar.shape, F32)
        if causal:
            fill_tables(line_ref, tab, adj)

    for h in range(GROUP):
        lanes = pair_lanes(h)
        pair, rows = h // 2, slice((h % 2) * TILE, (h % 2 + 1) * TILE)
        qm[pair, rows, :] = q_ref[:, lanes] * head_mask(h)
        dm[pair, rows, :] = do_ref[:, lanes] * head_mask(h)
        product = do_ref[:, lanes].astype(F32) * o_ref[:, lanes].astype(F32)
        ones = jnp.broadcast_to(head_mask(h).astype(F32), (8, LANES))
        inner = lax.dot_general(
            ones, product, (((1,), (1,)), ((), ())),
            precision=lax.Precision.HIGHEST, preferred_element_type=F32,
        )
        d_s[h : h + 1, :] = inner[0:1, :]
    dq_acc[...] = jnp.zeros(dq_acc.shape, F32)
    segq = segq_ref[0:1, :]

    def tile(row, kind):
        allowed = allowed_keys(segq, segk_ref, row, kind == 3)
        for pair in range(GROUP // 2):
            lanes = slice(pair * LANES, (pair + 1) * LANES)
            keys = kb[pl.ds(row, TILE), lanes]
            values = vb[pl.ds(row, TILE), lanes]
            probs_pair, grads_pair = [], []
            for h in (2 * pair, 2 * pair + 1):
                half = slice((h % 2) * TILE, (h % 2 + 1) * TILE)
                scores = contract(keys, qm[pair, half, :], 1, 1)
                scores = jnp.where(allowed, with_bias(scores, kind, h, line_ref, tab, adj), NEG)
                probs = jnp.exp(scores - lse_ref[0, h : h + 1, :])
                grad_probs = contract(values, dm[pair, half, :], 1, 1)
                grads = probs * (grad_probs - d_s[h : h + 1, :])
                low = grads.astype(BF16)
                probs_pair.append(probs.astype(BF16))
                grads_pair.append(low)
                if causal:
                    rounded = low.astype(F32)
                    if kind == 3:
                        gt[h] += rounded
                    elif kind == 2:
                        k_pos = lax.broadcasted_iota(jnp.int32, (TILE, TILE), 0)
                        q_pos = lax.broadcasted_iota(jnp.int32, (TILE, TILE), 1)
                        near = jnp.where(k_pos > q_pos, rounded, 0.0)
                        gt[h] += near
                        gfar[h] += jnp.sum((rounded - near).reshape(TILE // 8, 8, TILE), axis=0)
                    else:
                        gfar[h] += jnp.sum(rounded.reshape(TILE // 8, 8, TILE), axis=0)
                back = contract(keys, low, 0, 0)
                rows = slice(h * HEAD_DIM, (h + 1) * HEAD_DIM)
                start = (h % 2) * HEAD_DIM
                dq_acc[rows, :] += back[start : start + HEAD_DIM, :]
            dv_acc[pl.ds(row, TILE), lanes] += contract(
                jnp.concatenate(probs_pair, axis=1), dm[pair], 1, 0
            )
            dk_acc[pl.ds(row, TILE), lanes] += contract(
                jnp.concatenate(grads_pair, axis=1), qm[pair], 1, 0
            )

    visit_tiles(causal, kinds_ref, tile, (own_rows + par_rows) // TILE)
    dq_ref[...] = dq_acc[...].T.astype(BF16)

    @pl.when(i == pl.num_programs(1) - 1)
    def _():
        own_ref[0] = dk_acc[0:own_rows, :].astype(BF16)
        own_ref[1] = dv_acc[0:own_rows, :].astype(BF16)
        par_ref[0] = dk_acc[own_rows : own_rows + par_rows, :].astype(BF16)
        par_ref[1] = dv_acc[own_rows : own_rows + par_rows, :].astype(BF16)
        for h in range(GROUP):
            if causal:
                gline_ref[h] = line_of(gt[h])
                gfar_ref[h] = jnp.sum(gfar[h], axis=0, keepdims=True)
            else:
                gline_ref[h] = jnp.zeros((1, TILE), F32)
                gfar_ref[h] = jnp.zeros((1, TILE), F32)


VMEM_LIMIT = 60 * 1024 * 1024


def attention_specs(tokens, width, own_rows, par_rows):
    groups = HEADS // GROUP
    lanes = GROUP * HEAD_DIM
    keys = own_rows + par_rows
    return [
        pl.BlockSpec((TILE, lanes), lambda g, i, kinds: (i, g)),
        pl.BlockSpec((own_rows, lanes), lambda g, i, kinds: (0, g)),
        pl.BlockSpec((own_rows, lanes), lambda g, i, kinds: (0, groups + g)),
        pl.BlockSpec((par_rows, lanes), lambda g, i, kinds: (0, g)),
        pl.BlockSpec((par_rows, lanes), lambda g, i, kinds: (0, groups + g)),
        pl.BlockSpec((8, TILE), lambda g, i, kinds: (0, i)),
        pl.BlockSpec((keys, LANES), lambda g, i, kinds: (0, 0)),
        pl.BlockSpec((GROUP, 1, TILE), lambda g, i, kinds: (g, 0, 0)),
    ]


def attend_fast(kinds, query, kv_own, kv_par, segq, segk, line, causal):
    tokens, width = query.shape
    own_rows, par_rows = kv_own.shape[0], kv_par.shape[0]
    keys = own_rows + par_rows
    groups, lanes = HEADS // GROUP, GROUP * HEAD_DIM
    table = (GROUP, TILE, TILE) if causal else (1, 8, LANES)
    return pl.pallas_call(
        functools.partial(attend_kernel, causal, own_rows, par_rows),
        grid_spec=pltpu.PrefetchScalarGridSpec(
            num_scalar_prefetch=1,
            grid=(groups, tokens // TILE),
            in_specs=attention_specs(tokens, width, own_rows, par_rows),
            out_specs=[
                pl.BlockSpec((TILE, lanes), lambda g, i, kinds: (i, g)),
                pl.BlockSpec((1, GROUP, TILE), lambda g, i, kinds: (g, 0, i)),
            ],
            scratch_shapes=[
                pltpu.VMEM((keys, lanes), BF16),
                pltpu.VMEM((keys, lanes), BF16),
                pltpu.VMEM((GROUP, TILE, LANES), BF16),
                pltpu.VMEM(table, F32),
                pltpu.VMEM(table, F32),
                pltpu.VMEM((8, TILE), F32),
                pltpu.VMEM((8, TILE), F32),
                pltpu.VMEM((lanes, TILE), F32),
            ],
        ),
        out_shape=[
            jax.ShapeDtypeStruct((tokens, width), BF16),
            jax.ShapeDtypeStruct((groups, GROUP, tokens), F32),
        ],
        compiler_params=pltpu.CompilerParams(vmem_limit_bytes=VMEM_LIMIT),
        cost_estimate=pl.CostEstimate(
            flops=tokens * keys * width * 4, bytes_accessed=4 * (tokens + keys) * width,
            transcendentals=tokens * keys * HEADS // 2,
        ),
        name="attend_self" if causal else "attend_cross",
    )(kinds, query, kv_own, kv_own, kv_par, kv_par, segq, segk, line)


def attend_back_fast(kinds, query, kv_own, kv_par, segq, segk, line, grad_mixed, mixed, lse, causal):
    tokens, width = query.shape
    own_rows, par_rows = kv_own.shape[0], kv_par.shape[0]
    keys = own_rows + par_rows
    groups, lanes = HEADS // GROUP, GROUP * HEAD_DIM
    table = (GROUP, TILE, TILE) if causal else (1, 8, LANES)
    block = pl.BlockSpec((TILE, lanes), lambda g, i, kinds: (i, g))
    line_spec = pl.BlockSpec((GROUP, 1, TILE), lambda g, i, kinds: (g, 0, 0))
    return pl.pallas_call(
        functools.partial(attend_back_kernel, causal, own_rows, par_rows),
        grid_spec=pltpu.PrefetchScalarGridSpec(
            num_scalar_prefetch=1,
            grid=(groups, tokens // TILE),
            in_specs=attention_specs(tokens, width, own_rows, par_rows)
            + [block, block, pl.BlockSpec((1, GROUP, TILE), lambda g, i, kinds: (g, 0, i))],
            out_specs=[
                block,
                pl.BlockSpec((2, own_rows, lanes), lambda g, i, kinds: (0, 0, g)),
                pl.BlockSpec((2, par_rows, lanes), lambda g, i, kinds: (0, 0, g)),
                line_spec,
                line_spec,
            ],
            scratch_shapes=[
                pltpu.VMEM((keys, lanes), BF16),
                pltpu.VMEM((keys, lanes), BF16),
                pltpu.VMEM((GROUP // 2, 2 * TILE, LANES), BF16),
                pltpu.VMEM((GROUP // 2, 2 * TILE, LANES), BF16),
                pltpu.VMEM(table, F32),
                pltpu.VMEM(table, F32),
                pltpu.VMEM((8, TILE), F32),
                pltpu.VMEM((lanes, TILE), F32),
                pltpu.VMEM((keys, lanes), F32),
                pltpu.VMEM((keys, lanes), F32),
                pltpu.VMEM(table, F32),
                pltpu.VMEM((GROUP, 8, TILE), F32),
            ],
        ),
        out_shape=[
            jax.ShapeDtypeStruct((tokens, width), BF16),
            jax.ShapeDtypeStruct((2, own_rows, width), BF16),
            jax.ShapeDtypeStruct((2, par_rows, width), BF16),
            jax.ShapeDtypeStruct((HEADS, 1, TILE), F32),
            jax.ShapeDtypeStruct((HEADS, 1, TILE), F32),
        ],
        compiler_params=pltpu.CompilerParams(vmem_limit_bytes=VMEM_LIMIT),
        cost_estimate=pl.CostEstimate(
            flops=tokens * keys * width * 10, bytes_accessed=10 * (tokens + keys) * width,
            transcendentals=tokens * keys * HEADS // 2,
        ),
        name="attend_self_back" if causal else "attend_cross_back",
    )(kinds, query, kv_own, kv_own, kv_par, kv_par, segq, segk, line, grad_mixed, mixed, lse)


AXES = ("dp", "seq")


def exchange(value, dp_bit, seq_bit):
    pairs = [
        (dp * 4 + seq, (dp ^ dp_bit) * 4 + (seq ^ seq_bit)) for dp in range(8) for seq in range(4)
    ]
    return lax.ppermute(value, AXES, pairs)


CORE, Z_LOW, Z_HIGH, X, Y = (1, 0), (2, 0), (4, 0), (0, 1), (0, 2)


def move_pairs(a, b):
    pairs = []
    for z in range(4):
        for core in range(2):
            for s in range(4):
                micro, half_core = (s >> 1) ^ a, (s & 1) ^ b
                pairs.append(((2 * z + core) * 4 + s, (2 * z + half_core) * 4 + 2 * core + micro))
    return pairs


ROUNDS = ((0, 0), (0, 1), (1, 0), (1, 1))


def in_order(flag, first, second):
    return jnp.stack([jnp.where(flag == 0, first, second), jnp.where(flag == 0, second, first)])


def take(value, index, axis):
    return lax.dynamic_index_in_dim(value, index, axis, keepdims=False)


def assemble_kernel(rows, widths, *refs):
    pieces, (outs, scratch) = refs[:16], (refs[16 : 16 + len(widths)], refs[16 + len(widths) :])
    sems_in, sems_out = scratch[-2:]
    buffers = scratch[0]
    half = buffers.shape[-1]
    loads = []
    for p in range(16):
        load = pltpu.make_async_copy(pieces[p], buffers.at[p], sems_in.at[p])
        load.start()
        loads.append(load)
    dp, seq = lax.axis_index("dp"), lax.axis_index("seq")
    core, x, y = lax.rem(dp, 2), lax.rem(seq, 2), seq // 2
    stores = []
    for p in range(16):
        loads[p].wait()
        rel_core, column, rel_y, rel_x = p // 8, (p // 4) % 2, (p // 2) % 2, p % 2
        to_core = lax.rem(core + rel_core, 2)
        to_y, to_x = lax.rem(y + rel_y, 2), lax.rem(x + rel_x, 2)
        starts = [sum(widths[:w]) for w in range(len(widths))]
        for w, start in enumerate(starts):
            low, high = max(start, column * half), min(start + widths[w], (column + 1) * half)
            if low >= high:
                continue
            store = pltpu.make_async_copy(
                buffers.at[p, :, :, pl.ds(low - column * half, high - low)],
                outs[w].at[:, to_core, to_y, to_x, :, pl.ds(low - start, high - low)],
                sems_out.at[p, w],
            )
            store.start()
            stores.append(store)
    for store in stores:
        store.wait()


def assemble(pieces, widths):
    rows, half = pieces[0].shape[1:]
    outs = pl.pallas_call(
        functools.partial(assemble_kernel, rows, widths),
        in_specs=[pl.BlockSpec(memory_space=pl.ANY)] * 16,
        out_specs=[pl.BlockSpec(memory_space=pl.ANY)] * len(widths),
        out_shape=[jax.ShapeDtypeStruct((4, 2, 2, 2, rows, width), BF16) for width in widths],
        scratch_shapes=[
            pltpu.VMEM((16, 4, rows, half), BF16),
            pltpu.SemaphoreType.DMA((16,)),
            pltpu.SemaphoreType.DMA((16, len(widths))),
        ],
        compiler_params=pltpu.CompilerParams(vmem_limit_bytes=VMEM_LIMIT),
        cost_estimate=pl.CostEstimate(
            flops=0, transcendentals=0, bytes_accessed=4 * 64 * rows * half
        ),
        name="assemble",
    )(*pieces)
    return [out.reshape(32 * rows, out.shape[-1]) for out in outs]


def gather_weights(shard, widths, place):
    core, z_low, z_high = place[0], place[1], place[2]
    low = in_order(z_low, shard, exchange(shard, *Z_LOW))
    both = in_order(z_high, low, exchange(low, *Z_HIGH)).reshape(4, *shard.shape)
    half = shard.shape[1] // 2
    left, right = both[..., :half], both[..., half:]
    left_x, right_y = exchange(left, *X), exchange(right, *Y)
    left_y, left_xy = exchange(left, *Y), exchange(left_x, *Y)
    right_x, right_xy = exchange(right, *X), exchange(right_y, *X)
    own = [left, left_x, left_y, left_xy, right, right_x, right_y, right_xy]
    return assemble(own + [exchange(piece, *CORE) for piece in own], widths)


def add_low(first, second):
    return (first.astype(F32) + second.astype(F32)).astype(BF16)


def scatter_grads(grads, place):
    core, z_low, z_high, y, x = place
    rows, width = grads.shape[0] // 32, grads.shape[1]
    half = width // 2
    whole = grads.reshape(4, 2, 2, 2, rows, width)
    got = exchange(take(whole, 1 - core, 1), *CORE)
    kept = add_low(take(whole, core, 1), got)
    left, right = kept[..., :half], kept[..., half:]
    left_got = exchange(take(left, 1 - x, 2), *X)
    right_got = exchange(take(right, 1 - y, 1), *Y)
    left = add_low(take(left, x, 2), left_got)
    right = add_low(take(right, y, 1), right_got)
    left_got = exchange(take(left, 1 - y, 1), *Y)
    right_got = exchange(take(right, 1 - x, 1), *X)
    left = add_low(take(left, y, 1), left_got)
    right = add_low(take(right, x, 1), right_got)
    both = jnp.concatenate([left, right], axis=-1).reshape(2, 2, rows, width)
    got = exchange(take(both, 1 - z_high, 0), *Z_HIGH)
    both = add_low(take(both, z_high, 0), got)
    got = exchange(take(both, 1 - z_low, 0), *Z_LOW)
    return take(both, z_low, 0).astype(F32) + got.astype(F32)


def gather_small(shard, place):
    core, z_low, z_high, y, x = place
    value = in_order(x, shard, exchange(shard, *X))
    value = in_order(y, value, exchange(value, *Y))
    value = in_order(core, value, exchange(value, *CORE))
    value = in_order(z_low, value, exchange(value, *Z_LOW))
    value = in_order(z_high, value, exchange(value, *Z_HIGH))
    return value.reshape(32, *shard.shape)


def scatter_small(value, place):
    core, z_low, z_high, y, x = place
    value = value.reshape(2, 2, 2, 2, 2, *value.shape[1:])
    for flag, link in ((z_high, Z_HIGH), (z_low, Z_LOW), (core, CORE), (y, Y), (x, X)):
        value = take(value, flag, 0) + exchange(take(value, 1 - flag, 0), *link)
    return value


def norm_scale(value):
    return lax.rsqrt(jnp.mean(value * value, axis=-1, keepdims=True) + EPS)


def normed(value, gain):
    return (value * norm_scale(value) * gain).astype(BF16)


def norm_back(value, gain, grad):
    scale = norm_scale(value)
    scaled = grad * gain
    inner = jnp.mean(scaled * value, axis=-1, keepdims=True)
    return (
        scale * scaled - (scale * scale * scale) * value * inner,
        jnp.sum(grad * value * scale, axis=0),
    )


def dot(rows, weight):
    return jnp.dot(rows, weight, preferred_element_type=F32)


def dot_back(grads, weight):
    return contract(grads, weight, 1, 1)


def dot_weight(rows, grads):
    return contract(rows, grads, 0, 0).astype(BF16)


def fast_body(
    hidden_in,
    encoder_states,
    segments,
    enc_segments,
    grad_out,
    norm_self,
    q_self,
    k_self,
    v_self,
    o_self,
    rel_bias,
    norm_cross,
    q_cross,
    k_cross,
    v_cross,
    o_cross,
    norm_ff,
    wi_gate,
    wi_up,
    wo_ff,
):
    dp, seq = lax.axis_index("dp"), lax.axis_index("seq")
    core, z_low, z_high, y, x = dp % 2, (dp // 2) % 2, dp // 4, seq // 2, seq % 2
    place = (core, z_low, z_high, y, x)
    rows_dev, width = hidden_in.shape[2], hidden_in.shape[3]
    enc_dev = encoder_states.shape[2]
    part, enc_part = rows_dev // 2, enc_dev // 2
    owned_micro = seq % 2

    def send_tokens(pieces_of):
        return [
            lax.ppermute(pieces_of((seq // 2) ^ a, b), AXES, move_pairs(a, b)) for a, b in ROUNDS
        ]

    def settle(received):
        slots = []
        for s in range(4):
            index = 2 * ((s >> 1) ^ owned_micro) + ((s & 1) ^ core)
            slots.append(lax.select_n(index, *received))
        return jnp.stack(slots)

    def return_tokens(value):
        received = []
        for a, b in ROUNDS:
            index = 2 * (owned_micro ^ a) + (core ^ b)
            back = [(target, source) for source, target in move_pairs(a, b)]
            received.append(lax.ppermute(take(value, index, 0), AXES, back))
        flag = seq // 2
        micro = []
        for m in range(2):
            micro.append(
                jnp.concatenate(
                    [jnp.where((flag ^ m) == 0, received[b], received[2 + b]) for b in range(2)],
                    axis=0,
                )
            )
        return jnp.stack(micro)[:, None]

    codes = jnp.concatenate([segments[:, 0], enc_segments[:, 0]], axis=1).astype(BF16)
    codes = jnp.pad(codes, ((0, 0), (0, width - codes.shape[1])))

    def bundle(micro, b):
        return jnp.concatenate(
            [
                take(hidden_in[:, 0, b * part : (b + 1) * part], micro, 0),
                take(encoder_states[:, 0, b * enc_part : (b + 1) * enc_part], micro, 0),
                jnp.broadcast_to(take(codes, micro, 0)[None], (16, width)),
            ],
            axis=0,
        )

    bundles = send_tokens(bundle)

    small = jnp.concatenate([norm_self, norm_cross, norm_ff, rel_bias])
    small_rows = norm_self.shape[0]
    small = gather_small(jnp.pad(small, (0, LANES - small.shape[0])).reshape(1, LANES), place)
    small = small.reshape(32, LANES).astype(F32)
    gain_self, gain_cross, gain_ff = (
        small[:, j * small_rows : (j + 1) * small_rows].reshape(-1) for j in range(3)
    )
    table = small[:, 3 * small_rows : 3 * small_rows + rel_bias.shape[0]].reshape(BUCKETS, HEADS)

    wq, wkv = gather_weights(
        jnp.concatenate([q_self, k_self, v_self], axis=1), (width, 2 * width), place
    )
    wo, cq, co, ckv = gather_weights(
        jnp.concatenate([o_self, q_cross, o_cross, k_cross, v_cross], axis=1),
        (width, width, width, 2 * width),
        place,
    )
    ff = wi_gate.shape[1]
    w_gate, w_up = gather_weights(jnp.concatenate([wi_gate, wi_up], axis=1), (ff, ff), place)
    (w_down,) = gather_weights(wo_ff, (width,), place)

    inputs_low = settle([piece[:part] for piece in bundles]).reshape(4 * part, width)
    encoder = settle([piece[part : part + enc_part] for piece in bundles]).reshape(4 * enc_part, width)
    codes = settle([piece[part + enc_part : part + enc_part + 1] for piece in bundles])[:, 0]
    codes = codes.astype(jnp.int32)
    seg_parts = codes[:, :rows_dev].reshape(4, 2, part)
    enc_parts = codes[:, rows_dev : rows_dev + enc_dev].reshape(4, 2, enc_part)

    def of_core(parts, which):
        return jnp.stack([take(parts[s], which ^ (s & 1), 0) for s in range(4)])

    seg_own, seg_par = of_core(seg_parts, core), of_core(seg_parts, 1 - core)
    enc_own, enc_par = of_core(enc_parts, core), of_core(enc_parts, 1 - core)
    seg_keys = jnp.concatenate([seg_own, seg_par])
    quarter = jnp.arange(4, dtype=jnp.int32)
    at_own = 2 * quarter + (core ^ (quarter % 2))
    at_par = 2 * quarter + ((1 - core) ^ (quarter % 2))
    at_keys = jnp.concatenate([at_own, at_par])
    needed = (at_keys[None, :] < at_own[:, None]) & (seg_keys[None, :, -1] >= seg_own[:, :1])
    kinds = jnp.where(needed, jnp.where(at_keys[None, :] == at_own[:, None] - 1, 2, 1), 0)
    kinds = kinds.astype(jnp.int32).reshape(-1)
    segq = jnp.broadcast_to(seg_own.reshape(1, -1), (8, 4 * part))
    segk = jnp.broadcast_to(seg_keys.reshape(-1, 1), (8 * part, LANES))
    enc_segk = jnp.broadcast_to(
        jnp.concatenate([enc_own, enc_par]).reshape(-1, 1), (8 * enc_part, LANES)
    )
    near = (
        buckets_of(jnp.arange(TILE, dtype=jnp.int32))[:, None] == jnp.arange(BUCKETS)[None, :]
    ).astype(F32)
    line = jnp.dot(near, table, precision=lax.Precision.HIGHEST).T.reshape(HEADS, 1, TILE)

    inputs = inputs_low.astype(F32)
    normed_self = normed(inputs, gain_self)
    kv_own = dot(normed_self, wkv).astype(BF16)
    kv_par = exchange(kv_own, *CORE)
    query = dot(normed_self, wq).astype(BF16)
    cross_kv_own = dot(encoder, ckv).astype(BF16)
    cross_kv_par = exchange(cross_kv_own, *CORE)
    mixed, self_lse = attend_fast(kinds, query, kv_own, kv_par, segq, segk, line, True)
    after_self = inputs + dot(mixed, wo)
    normed_cross = normed(after_self, gain_cross)
    cross_query = dot(normed_cross, cq).astype(BF16)
    cross_mixed, cross_lse = attend_fast(
        kinds, cross_query, cross_kv_own, cross_kv_par, segq, enc_segk, line, False
    )
    after_cross = after_self + dot(cross_mixed, co)
    normed_ff = normed(after_cross, gain_ff)
    gate, up_values = dot(normed_ff, w_gate), dot(normed_ff, w_up)
    hidden = gelu_mix(gate, up_values).astype(BF16)
    result = (after_cross + dot(hidden, w_down)).astype(BF16)
    block_out = return_tokens(result.reshape(4, part, width))

    out_low = settle(
        send_tokens(lambda micro, b: take(grad_out[:, 0, b * part : (b + 1) * part], micro, 0))
    ).reshape(4 * part, width)
    grad_result = out_low.astype(F32)
    grad_w_down = scatter_grads(dot_weight(hidden, out_low), place)
    grad_hidden = dot_back(out_low, w_down)
    mix_value, mix_pull = jax.vjp(gelu_mix, gate, up_values)
    grad_gate, grad_up = (piece.astype(BF16) for piece in mix_pull(grad_hidden))
    grad_w_in = scatter_grads(
        jnp.concatenate([dot_weight(normed_ff, grad_gate), dot_weight(normed_ff, grad_up)], axis=1),
        place,
    )
    grad_normed_ff = dot_back(grad_gate, w_gate) + dot_back(grad_up, w_up)
    ff_part, grad_gain_ff = norm_back(after_cross, gain_ff, grad_normed_ff)
    grad_after_cross = grad_result + ff_part
    cross_out_low = grad_after_cross.astype(BF16)
    grad_co = dot_weight(cross_mixed, cross_out_low)
    grad_cross_mixed = dot_back(cross_out_low, co).astype(BF16)
    grad_cross_query, cross_own, cross_par, unused, unused = attend_back_fast(
        kinds, cross_query, cross_kv_own, cross_kv_par, segq, enc_segk, line,
        grad_cross_mixed, cross_mixed, cross_lse, False,
    )
    cross_got = add_low(cross_own, exchange(cross_par, *CORE))
    grad_cross_kv = jnp.concatenate([cross_got[0], cross_got[1]], axis=1)
    grad_ckv = dot_weight(encoder, grad_cross_kv)
    grad_encoder = dot_back(grad_cross_kv, ckv).astype(BF16)
    grad_encoder = return_tokens(grad_encoder.reshape(4, enc_part, width)).astype(F32)
    grad_cq = dot_weight(normed_cross, grad_cross_query)
    grad_normed_cross = dot_back(grad_cross_query, cq)
    cross_part, grad_gain_cross = norm_back(after_self, gain_cross, grad_normed_cross)
    grad_after_self = grad_after_cross + cross_part
    self_out_low = grad_after_self.astype(BF16)
    grad_wo = dot_weight(mixed, self_out_low)
    grad_middle = scatter_grads(jnp.concatenate([grad_wo, grad_cq, grad_co, grad_ckv], axis=1), place)
    grad_mixed = dot_back(self_out_low, wo).astype(BF16)
    grad_query, self_own, self_par, grad_line, grad_far = attend_back_fast(
        kinds, query, kv_own, kv_par, segq, segk, line, grad_mixed, mixed, self_lse, True
    )
    self_got = add_low(self_own, exchange(self_par, *CORE))
    grad_kv = jnp.concatenate([self_got[0], self_got[1]], axis=1)
    grad_qkv = scatter_grads(
        jnp.concatenate([dot_weight(normed_self, grad_query), dot_weight(normed_self, grad_kv)], axis=1),
        place,
    )
    grad_normed_self = dot_back(grad_query, wq) + dot_back(grad_kv, wkv)
    self_part, grad_gain_self = norm_back(inputs, gain_self, grad_normed_self)
    grad_hidden_in = return_tokens((grad_after_self + self_part).astype(BF16).reshape(4, part, width))

    grad_table = jnp.dot(near.T, grad_line.reshape(HEADS, TILE).T, precision=lax.Precision.HIGHEST)
    grad_table = grad_table.at[BUCKETS - 1].add(jnp.sum(grad_far.reshape(HEADS, TILE), axis=1))
    small_grads = [piece.reshape(32, -1) for piece in (grad_gain_self, grad_gain_cross, grad_gain_ff)]
    small_grads = jnp.concatenate(small_grads + [grad_table.reshape(32, -1)], axis=1)
    small_grads = jnp.pad(small_grads, ((0, 0), (0, LANES - small_grads.shape[1])))
    small_grads = scatter_small(small_grads.reshape(32, 1, LANES), place).reshape(-1)
    return (
        block_out,
        grad_hidden_in.astype(F32),
        grad_encoder,
        small_grads[:small_rows],
        grad_qkv[:, :width],
        grad_qkv[:, width : 2 * width],
        grad_qkv[:, 2 * width :],
        grad_middle[:, :width],
        small_grads[3 * small_rows : 3 * small_rows + rel_bias.shape[0]],
        small_grads[small_rows : 2 * small_rows],
        grad_middle[:, width : 2 * width],
        grad_middle[:, 3 * width : 4 * width],
        grad_middle[:, 4 * width :],
        grad_middle[:, 2 * width : 3 * width],
        small_grads[2 * small_rows : 3 * small_rows],
        grad_w_in[:, :ff],
        grad_w_in[:, ff:],
        grad_w_down,
    )


def fits_fast(mesh):
    return mesh.shape["dp"] == 8 and mesh.shape["seq"] == 4


def solution(mesh):
    return jax.shard_map(
        fast_body if fits_fast(mesh) else general_body,
        mesh=mesh,
        in_specs=(
            P(None, "dp", "seq", None),
            P(None, "dp", "seq", None),
            P(None, "dp", "seq"),
            P(None, "dp", "seq"),
            P(None, "dp", "seq", None),
            P(("dp", "seq")),
            P(("dp", "seq"), None),
            P(("dp", "seq"), None),
            P(("dp", "seq"), None),
            P(("dp", "seq"), None),
            P(("dp", "seq")),
            P(("dp", "seq")),
            P(("dp", "seq"), None),
            P(("dp", "seq"), None),
            P(("dp", "seq"), None),
            P(("dp", "seq"), None),
            P(("dp", "seq")),
            P(("dp", "seq"), None),
            P(("dp", "seq"), None),
            P(("dp", "seq"), None),
        ),
        out_specs=(
            P(None, "dp", "seq", None),
            P(None, "dp", "seq", None),
            P(None, "dp", "seq", None),
            P(("dp", "seq")),
            P(("dp", "seq"), None),
            P(("dp", "seq"), None),
            P(("dp", "seq"), None),
            P(("dp", "seq"), None),
            P(("dp", "seq")),
            P(("dp", "seq")),
            P(("dp", "seq"), None),
            P(("dp", "seq"), None),
            P(("dp", "seq"), None),
            P(("dp", "seq"), None),
            P(("dp", "seq")),
            P(("dp", "seq"), None),
            P(("dp", "seq"), None),
            P(("dp", "seq"), None),
        ),
        check_vma=False,
    )
```

```python
import functools
import math

import jax
import jax.numpy as jnp
from jax import lax
from jax.experimental import pallas as pl
from jax.experimental.pallas import tpu as pltpu
from jax.sharding import PartitionSpec as P

HEADS = 16
HEAD_DIM = 64
BUCKETS = 32
MAX_DIST = 128


EPS = 1e-06
NEG = -1e30


def norm_rows(value, gain):
    return value * lax.rsqrt(jnp.mean(value * value, axis=-1, keepdims=True) + EPS) * gain


def bucket_edges():
    half = BUCKETS // 2
    return [math.ceil(half * (MAX_DIST / half) ** (step / half)) for step in range(1, half)]


def buckets_of(distance):
    half = BUCKETS // 2
    far = half + sum(((distance >= edge).astype(jnp.int32) for edge in bucket_edges()))
    return jnp.where(distance < half, distance, far)


def by_heads(values):
    return values.reshape(values.shape[0], values.shape[1], HEADS, HEAD_DIM)


def join_heads(values):
    return values.reshape(values.shape[0], values.shape[1], HEADS * HEAD_DIM)


def project(rows, weight_matrix):
    return jnp.dot(rows, weight_matrix, preferred_element_type=jnp.float32)


def project_back(grads, weight_matrix):
    return jnp.einsum("stn,kn->stk", grads, weight_matrix, preferred_element_type=jnp.float32)


def weight_grad(rows, grads):
    return jnp.einsum("stk,stn->kn", rows, grads, preferred_element_type=jnp.float32)


def gelu_mix(gate, up_values):
    return jax.nn.gelu(gate, approximate=True) * up_values


def scores_of(q_rows, keys, bias, allowed):
    scores = jnp.einsum("sqhd,skhd->shqk", q_rows, keys, preferred_element_type=jnp.float32) + bias
    return jnp.where(allowed[:, None], scores, NEG)


def attend(q_rows, keys, values, bias, allowed):
    scores = scores_of(q_rows, keys, bias, allowed)
    largest = jnp.max(scores, axis=-1, keepdims=True)
    raised = jnp.exp(scores - largest)
    total = jnp.sum(raised, axis=-1, keepdims=True)
    probs = raised / total
    mixed = jnp.einsum(
        "shqk,skhd->sqhd", probs.astype(jnp.bfloat16), values, preferred_element_type=jnp.float32
    )
    return (join_heads(mixed).astype(jnp.bfloat16), largest + jnp.log(total))


def attend_back(q_rows, keys, values, bias, allowed, log_total, grad_mixed):
    scores = scores_of(q_rows, keys, bias, allowed)
    probs = jnp.exp(scores - log_total)
    grad_probs = jnp.einsum(
        "sqhd,skhd->shqk", grad_mixed, values, preferred_element_type=jnp.float32
    )
    inner = jnp.sum(probs * grad_probs, axis=-1, keepdims=True)
    grad_scores = (probs * (grad_probs - inner)).astype(jnp.bfloat16)
    grad_query = jnp.einsum(
        "shqk,skhd->sqhd", grad_scores, keys, preferred_element_type=jnp.float32
    )
    grad_keys = jnp.einsum(
        "shqk,sqhd->skhd", grad_scores, q_rows, preferred_element_type=jnp.float32
    )
    grad_values = jnp.einsum(
        "shqk,sqhd->skhd",
        probs.astype(jnp.bfloat16),
        grad_mixed,
        preferred_element_type=jnp.float32,
    )
    return (join_heads(grad_query), join_heads(grad_keys), join_heads(grad_values), grad_scores)


def general_body(
    hidden_in,
    encoder_states,
    segments,
    enc_segments,
    grad_out,
    norm_self,
    q_self,
    k_self,
    v_self,
    o_self,
    rel_bias,
    norm_cross,
    q_cross,
    k_cross,
    v_cross,
    o_cross,
    norm_ff,
    wi_gate,
    wi_up,
    wo_ff,
):
    shards = (
        norm_self,
        q_self,
        k_self,
        v_self,
        o_self,
        rel_bias,
        norm_cross,
        q_cross,
        k_cross,
        v_cross,
        o_cross,
        norm_ff,
        wi_gate,
        wi_up,
        wo_ff,
    )
    micro_count = hidden_in.shape[0]
    rows_dev = hidden_in.shape[2]
    seg_whole, enc_seg_whole = (
        lax.all_gather(segments, "seq", axis=2, tiled=True),
        lax.all_gather(enc_segments, "seq", axis=2, tiled=True),
    )
    length = seg_whole.shape[2]
    positions = lax.axis_index("seq") * rows_dev + jnp.arange(rows_dev, dtype=jnp.int32)
    columns = jnp.arange(length, dtype=jnp.int32)
    distance = jnp.maximum(positions[:, None] - columns[None, :], 0)
    bucket_indicator = (
        buckets_of(distance)[None] == jnp.arange(BUCKETS, dtype=jnp.int32)[:, None, None]
    ).astype(jnp.bfloat16)
    causal = columns[None, :] <= positions[:, None]
    grad_shards = tuple((jnp.zeros(piece.shape, jnp.float32) for piece in shards))
    outputs, grad_inputs, grad_encoders = ([], [], [])
    for micro in range(micro_count):
        params = (
            lax.all_gather(shards[0], ("dp", "seq"), axis=0, tiled=True),
            lax.all_gather(shards[1], ("dp", "seq"), axis=0, tiled=True),
            lax.all_gather(shards[2], ("dp", "seq"), axis=0, tiled=True),
            lax.all_gather(shards[3], ("dp", "seq"), axis=0, tiled=True),
            lax.all_gather(shards[4], ("dp", "seq"), axis=0, tiled=True),
            lax.all_gather(shards[5], ("dp", "seq"), axis=0, tiled=True),
            lax.all_gather(shards[6], ("dp", "seq"), axis=0, tiled=True),
            lax.all_gather(shards[7], ("dp", "seq"), axis=0, tiled=True),
            lax.all_gather(shards[8], ("dp", "seq"), axis=0, tiled=True),
            lax.all_gather(shards[9], ("dp", "seq"), axis=0, tiled=True),
            lax.all_gather(shards[10], ("dp", "seq"), axis=0, tiled=True),
            lax.all_gather(shards[11], ("dp", "seq"), axis=0, tiled=True),
            lax.all_gather(shards[12], ("dp", "seq"), axis=0, tiled=True),
            lax.all_gather(shards[13], ("dp", "seq"), axis=0, tiled=True),
            lax.all_gather(shards[14], ("dp", "seq"), axis=0, tiled=True),
        )
        (
            gain_self,
            wq,
            wk,
            wv,
            wo,
            table_flat,
            gain_cross,
            cq,
            ck,
            cv,
            co,
            gain_ff,
            w_gate,
            w_up,
            w_down,
        ) = params
        bias = jnp.einsum(
            "pia,pw->wia",
            bucket_indicator,
            table_flat.reshape(BUCKETS, HEADS),
            preferred_element_type=jnp.float32,
        )
        inputs = hidden_in[micro].astype(jnp.float32)
        encoder = encoder_states[micro]
        seg_own = segments[micro]
        self_allowed = (seg_own[:, :, None] == seg_whole[micro][:, None, :]) & causal[None]
        cross_allowed = seg_own[:, :, None] == enc_seg_whole[micro][:, None, :]
        self_norm_scale = gain_self.astype(jnp.float32)
        cross_gain = gain_cross.astype(jnp.float32)
        ff_gain = gain_ff.astype(jnp.float32)
        normed_self = norm_rows(inputs, self_norm_scale).astype(jnp.bfloat16)
        query = project(normed_self, wq).astype(jnp.bfloat16)
        key_own = project(normed_self, wk).astype(jnp.bfloat16)
        value_own = project(normed_self, wv).astype(jnp.bfloat16)
        cross_key_own = project(encoder, ck).astype(jnp.bfloat16)
        cross_value_own = project(encoder, cv).astype(jnp.bfloat16)
        keys, values, cross_keys, cross_values = (
            lax.all_gather(key_own, "seq", axis=1, tiled=True),
            lax.all_gather(value_own, "seq", axis=1, tiled=True),
            lax.all_gather(cross_key_own, "seq", axis=1, tiled=True),
            lax.all_gather(cross_value_own, "seq", axis=1, tiled=True),
        )
        mixed, self_log_normalizer = attend(
            by_heads(query), by_heads(keys), by_heads(values), bias, self_allowed
        )
        after_self = inputs + project(mixed, wo)
        normed_cross = norm_rows(after_self, cross_gain).astype(jnp.bfloat16)
        cross_query = project(normed_cross, cq).astype(jnp.bfloat16)
        cross_mixed, cross_log = attend(
            by_heads(cross_query), by_heads(cross_keys), by_heads(cross_values), 0.0, cross_allowed
        )
        after_cross = after_self + project(cross_mixed, co)
        normed_ff = norm_rows(after_cross, ff_gain).astype(jnp.bfloat16)
        gate = project(normed_ff, w_gate)
        up_values = project(normed_ff, w_up)
        hidden = gelu_mix(gate, up_values).astype(jnp.bfloat16)
        result = after_cross + project(hidden, w_down)
        outputs.append(result.astype(jnp.bfloat16))
        params = (
            lax.all_gather(shards[0], ("dp", "seq"), axis=0, tiled=True),
            lax.all_gather(shards[1], ("dp", "seq"), axis=0, tiled=True),
            lax.all_gather(shards[2], ("dp", "seq"), axis=0, tiled=True),
            lax.all_gather(shards[3], ("dp", "seq"), axis=0, tiled=True),
            lax.all_gather(shards[4], ("dp", "seq"), axis=0, tiled=True),
            lax.all_gather(shards[5], ("dp", "seq"), axis=0, tiled=True),
            lax.all_gather(shards[6], ("dp", "seq"), axis=0, tiled=True),
            lax.all_gather(shards[7], ("dp", "seq"), axis=0, tiled=True),
            lax.all_gather(shards[8], ("dp", "seq"), axis=0, tiled=True),
            lax.all_gather(shards[9], ("dp", "seq"), axis=0, tiled=True),
            lax.all_gather(shards[10], ("dp", "seq"), axis=0, tiled=True),
            lax.all_gather(shards[11], ("dp", "seq"), axis=0, tiled=True),
            lax.all_gather(shards[12], ("dp", "seq"), axis=0, tiled=True),
            lax.all_gather(shards[13], ("dp", "seq"), axis=0, tiled=True),
            lax.all_gather(shards[14], ("dp", "seq"), axis=0, tiled=True),
        )
        (
            gain_self,
            wq,
            wk,
            wv,
            wo,
            table_flat,
            gain_cross,
            cq,
            ck,
            cv,
            co,
            gain_ff,
            w_gate,
            w_up,
            w_down,
        ) = params
        grad_result = grad_out[micro].astype(jnp.float32)
        out_low = grad_out[micro]
        grad_w_down = weight_grad(hidden, out_low)
        grad_hidden = project_back(out_low, w_down)
        mix_value, mix_pull = jax.vjp(gelu_mix, gate, up_values)
        grad_gate, grad_up = mix_pull(grad_hidden)
        grad_gate = grad_gate.astype(jnp.bfloat16)
        grad_up = grad_up.astype(jnp.bfloat16)
        gate_weight_gradient = weight_grad(normed_ff, grad_gate)
        grad_w_up = weight_grad(normed_ff, grad_up)
        grad_normed_ff = project_back(grad_gate, w_gate) + project_back(grad_up, w_up)
        norm_value, norm_pull = jax.vjp(norm_rows, after_cross, ff_gain)
        ff_part, grad_gain_ff = norm_pull(grad_normed_ff)
        grad_after_cross = grad_result + ff_part
        cross_out_low = grad_after_cross.astype(jnp.bfloat16)
        grad_co = weight_grad(cross_mixed, cross_out_low)
        grad_cross_mixed = project_back(cross_out_low, co).astype(jnp.bfloat16)
        grad_cross_query, cross_key_terms, cross_value_terms, cross_scores = attend_back(
            by_heads(cross_query),
            by_heads(cross_keys),
            by_heads(cross_values),
            0.0,
            cross_allowed,
            cross_log,
            by_heads(grad_cross_mixed),
        )
        grad_cross_key, grad_cross_value = (
            lax.psum_scatter(
                cross_key_terms.astype(jnp.bfloat16), "seq", scatter_dimension=1, tiled=True
            ).astype(jnp.float32),
            lax.psum_scatter(
                cross_value_terms.astype(jnp.bfloat16), "seq", scatter_dimension=1, tiled=True
            ).astype(jnp.float32),
        )
        grad_cross_key = grad_cross_key.astype(jnp.bfloat16)
        grad_cross_value = grad_cross_value.astype(jnp.bfloat16)
        cross_key_gradient = weight_grad(encoder, grad_cross_key)
        grad_cv = weight_grad(encoder, grad_cross_value)
        grad_encoders.append(project_back(grad_cross_key, ck) + project_back(grad_cross_value, cv))
        grad_cross_query = grad_cross_query.astype(jnp.bfloat16)
        grad_cq = weight_grad(normed_cross, grad_cross_query)
        grad_normed_cross = project_back(grad_cross_query, cq)
        norm_value, norm_pull = jax.vjp(norm_rows, after_self, cross_gain)
        cross_part, grad_gain_cross = norm_pull(grad_normed_cross)
        grad_after_self = grad_after_cross + cross_part
        self_out_low = grad_after_self.astype(jnp.bfloat16)
        grad_wo = weight_grad(mixed, self_out_low)
        grad_mixed = project_back(self_out_low, wo).astype(jnp.bfloat16)
        grad_query, key_terms, value_terms, self_attention_logits = attend_back(
            by_heads(query),
            by_heads(keys),
            by_heads(values),
            bias,
            self_allowed,
            self_log_normalizer,
            by_heads(grad_mixed),
        )
        grad_table = jnp.einsum(
            "dcma,uma->uc",
            self_attention_logits,
            bucket_indicator,
            preferred_element_type=jnp.float32,
        ).reshape(-1)
        grad_key, grad_value = (
            lax.psum_scatter(
                key_terms.astype(jnp.bfloat16), "seq", scatter_dimension=1, tiled=True
            ).astype(jnp.float32),
            lax.psum_scatter(
                value_terms.astype(jnp.bfloat16), "seq", scatter_dimension=1, tiled=True
            ).astype(jnp.float32),
        )
        grad_key = grad_key.astype(jnp.bfloat16)
        grad_value = grad_value.astype(jnp.bfloat16)
        grad_query = grad_query.astype(jnp.bfloat16)
        grad_wq = weight_grad(normed_self, grad_query)
        grad_wk = weight_grad(normed_self, grad_key)
        grad_wv = weight_grad(normed_self, grad_value)
        grad_normed_self = (
            project_back(grad_query, wq) + project_back(grad_key, wk) + project_back(grad_value, wv)
        )
        norm_value, norm_pull = jax.vjp(norm_rows, inputs, self_norm_scale)
        self_part, grad_gain_self = norm_pull(grad_normed_self)
        grad_inputs.append(grad_after_self + self_part)
        local = (
            grad_gain_self,
            grad_wq,
            grad_wk,
            grad_wv,
            grad_wo,
            grad_table,
            grad_gain_cross,
            grad_cq,
            cross_key_gradient,
            grad_cv,
            grad_co,
            grad_gain_ff,
            gate_weight_gradient,
            grad_w_up,
            grad_w_down,
        )
        summed = (
            lax.psum_scatter(local[0], ("dp", "seq"), scatter_dimension=0, tiled=True),
            lax.psum_scatter(local[1], ("dp", "seq"), scatter_dimension=0, tiled=True),
            lax.psum_scatter(local[2], ("dp", "seq"), scatter_dimension=0, tiled=True),
            lax.psum_scatter(local[3], ("dp", "seq"), scatter_dimension=0, tiled=True),
            lax.psum_scatter(local[4], ("dp", "seq"), scatter_dimension=0, tiled=True),
            lax.psum_scatter(local[5], ("dp", "seq"), scatter_dimension=0, tiled=True),
            lax.psum_scatter(local[6], ("dp", "seq"), scatter_dimension=0, tiled=True),
            lax.psum_scatter(local[7], ("dp", "seq"), scatter_dimension=0, tiled=True),
            lax.psum_scatter(local[8], ("dp", "seq"), scatter_dimension=0, tiled=True),
            lax.psum_scatter(local[9], ("dp", "seq"), scatter_dimension=0, tiled=True),
            lax.psum_scatter(local[10], ("dp", "seq"), scatter_dimension=0, tiled=True),
            lax.psum_scatter(local[11], ("dp", "seq"), scatter_dimension=0, tiled=True),
            lax.psum_scatter(local[12], ("dp", "seq"), scatter_dimension=0, tiled=True),
            lax.psum_scatter(local[13], ("dp", "seq"), scatter_dimension=0, tiled=True),
            lax.psum_scatter(local[14], ("dp", "seq"), scatter_dimension=0, tiled=True),
        )
        grad_shards = tuple((before + after for before, after in zip(grad_shards, summed)))
    return (jnp.stack(outputs), jnp.stack(grad_inputs), jnp.stack(grad_encoders)) + tuple(
        grad_shards
    )


TILE = 256
GROUP = 4
LANES = 128
F32 = jnp.float32
BF16 = jnp.bfloat16


def contract(left, right, left_dim, right_dim):
    return lax.dot_general(
        left, right, (((left_dim,), (right_dim,)), ((), ())), preferred_element_type=F32
    )


def head_mask(head):
    lane = lax.broadcasted_iota(jnp.int32, (1, LANES), 1)
    keep = (lane < HEAD_DIM) if head % 2 == 0 else (lane >= HEAD_DIM)
    return keep.astype(F32).astype(BF16)


def bias_table(line):
    first = jnp.concatenate(
        [line if j == 0 else pltpu.roll(line, j, 1) for j in range(8)], axis=0
    )
    return [first if r == 0 else pltpu.roll(first, 8 * r, 1) for r in range(TILE // 8)]


def line_of(table):
    total = None
    for r in range(TILE // 8):
        part = table[8 * r : 8 * r + 8, :]
        part = part if r == 0 else pltpu.roll(part, TILE - 8 * r, 1)
        total = part if total is None else total + part
    line = total[0:1, :]
    for j in range(1, 8):
        line = line + pltpu.roll(total[j : j + 1, :], TILE - j, 1)
    return line


def allowed_keys(segq, segk_ref, row, diagonal):
    segk = segk_ref[pl.ds(row, TILE), :]
    segk = jnp.concatenate([segk] * (TILE // LANES), axis=1)
    same = segk == segq
    if diagonal:
        k_pos = lax.broadcasted_iota(jnp.int32, (TILE, TILE), 0)
        q_pos = lax.broadcasted_iota(jnp.int32, (TILE, TILE), 1)
        same = same & (k_pos <= q_pos)
    return same


def pair_lanes(head):
    return slice((head // 2) * LANES, (head // 2 + 1) * LANES)


def load_keys(refs, own_rows, par_rows, kb, vb):
    ko, vo, kp, vp = refs
    kb[0:own_rows, :] = ko[...]
    vb[0:own_rows, :] = vo[...]
    kb[own_rows : own_rows + par_rows, :] = kp[...]
    vb[own_rows : own_rows + par_rows, :] = vp[...]


def fill_tables(line_ref, tab, adj):
    for h in range(GROUP):
        line = line_ref[h]
        for r, rows in enumerate(bias_table(line)):
            tab[h, 8 * r : 8 * r + 8, :] = rows
        table = tab[h]
        k_pos = lax.broadcasted_iota(jnp.int32, (TILE, TILE), 0)
        q_pos = lax.broadcasted_iota(jnp.int32, (TILE, TILE), 1)
        adj[h] = jnp.where(k_pos > q_pos, table, line[:, TILE - 1 : TILE])


def visit_tiles(causal, kinds_ref, tile, tiles):
    if not causal:
        for t in range(tiles):
            tile(t * TILE, 0)
        return
    i = pl.program_id(1)
    tile(pl.multiple_of(i * TILE, TILE), 3)

    def step(p, carry):
        kind = kinds_ref[i * tiles + p]
        row = pl.multiple_of(p * TILE, TILE)

        @pl.when(kind == 1)
        def _():
            tile(row, 1)

        @pl.when(kind == 2)
        def _():
            tile(row, 2)

        return carry

    lax.fori_loop(0, tiles, step, 0)


def with_bias(scores, kind, h, line_ref, tab, adj):
    if kind == 3:
        return scores + tab[h]
    if kind == 2:
        return scores + adj[h]
    if kind == 1:
        return scores + line_ref[h][:, TILE - 1 : TILE]
    return scores


def attend_kernel(causal, own_rows, par_rows, kinds_ref, q_ref, ko, vo, kp, vp, segq_ref, segk_ref,
                  line_ref, o_ref, lse_ref, kb, vb, qm, tab, adj, m_s, l_s, acc):
    @pl.when(pl.program_id(1) == 0)
    def _():
        load_keys((ko, vo, kp, vp), own_rows, par_rows, kb, vb)
        if causal:
            fill_tables(line_ref, tab, adj)

    for h in range(GROUP):
        qm[h] = q_ref[:, pair_lanes(h)] * head_mask(h)
    m_s[...] = jnp.full(m_s.shape, NEG, F32)
    l_s[...] = jnp.zeros(l_s.shape, F32)
    acc[...] = jnp.zeros(acc.shape, F32)
    segq = segq_ref[0:1, :]

    def tile(row, kind):
        allowed = allowed_keys(segq, segk_ref, row, kind == 3)
        for h in range(GROUP):
            scores = contract(kb[pl.ds(row, TILE), pair_lanes(h)], qm[h], 1, 1)
            scores = jnp.where(allowed, with_bias(scores, kind, h, line_ref, tab, adj), NEG)
            before = m_s[h : h + 1, :]
            largest = jnp.maximum(before, jnp.max(scores, axis=0, keepdims=True))
            raised = jnp.exp(scores - largest)
            scale = jnp.exp(before - largest)
            m_s[h : h + 1, :] = largest
            l_s[h : h + 1, :] = l_s[h : h + 1, :] * scale + jnp.sum(raised, axis=0, keepdims=True)
            mixed = contract(vb[pl.ds(row, TILE), pair_lanes(h)], raised.astype(BF16), 0, 0)
            half = (h % 2) * HEAD_DIM
            rows = slice(h * HEAD_DIM, (h + 1) * HEAD_DIM)
            acc[rows, :] = acc[rows, :] * scale + mixed[half : half + HEAD_DIM, :]

    visit_tiles(causal, kinds_ref, tile, (own_rows + par_rows) // TILE)
    for h in range(GROUP):
        rows = slice(h * HEAD_DIM, (h + 1) * HEAD_DIM)
        acc[rows, :] = acc[rows, :] / l_s[h : h + 1, :]
        lse_ref[0, h : h + 1, :] = m_s[h : h + 1, :] + jnp.log(l_s[h : h + 1, :])
    o_ref[...] = acc[...].T.astype(BF16)


def attend_back_kernel(causal, own_rows, par_rows, kinds_ref, q_ref, ko, vo, kp, vp, segq_ref, segk_ref,
                       line_ref, do_ref, o_ref, lse_ref, dq_ref, own_ref, par_ref, gline_ref, gfar_ref,
                       kb, vb, qm, dm, tab, adj, d_s, dq_acc, dk_acc, dv_acc, gt, gfar):
    i = pl.program_id(1)

    @pl.when(i == 0)
    def _():
        load_keys((ko, vo, kp, vp), own_rows, par_rows, kb, vb)
        dk_acc[...] = jnp.zeros(dk_acc.shape, F32)
        dv_acc[...] = jnp.zeros(dv_acc.shape, F32)
        gt[...] = jnp.zeros(gt.shape, F32)
        gfar[...] = jnp.zeros(gfar.shape, F32)
        if causal:
            fill_tables(line_ref, tab, adj)

    for h in range(GROUP):
        lanes = pair_lanes(h)
        pair, rows = h // 2, slice((h % 2) * TILE, (h % 2 + 1) * TILE)
        qm[pair, rows, :] = q_ref[:, lanes] * head_mask(h)
        dm[pair, rows, :] = do_ref[:, lanes] * head_mask(h)
        product = do_ref[:, lanes].astype(F32) * o_ref[:, lanes].astype(F32)
        ones = jnp.broadcast_to(head_mask(h).astype(F32), (8, LANES))
        inner = lax.dot_general(
            ones, product, (((1,), (1,)), ((), ())),
            precision=lax.Precision.HIGHEST, preferred_element_type=F32,
        )
        d_s[h : h + 1, :] = inner[0:1, :]
    dq_acc[...] = jnp.zeros(dq_acc.shape, F32)
    segq = segq_ref[0:1, :]

    def tile(row, kind):
        allowed = allowed_keys(segq, segk_ref, row, kind == 3)
        for pair in range(GROUP // 2):
            lanes = slice(pair * LANES, (pair + 1) * LANES)
            keys = kb[pl.ds(row, TILE), lanes]
            values = vb[pl.ds(row, TILE), lanes]
            probs_pair, grads_pair = [], []
            for h in (2 * pair, 2 * pair + 1):
                half = slice((h % 2) * TILE, (h % 2 + 1) * TILE)
                scores = contract(keys, qm[pair, half, :], 1, 1)
                scores = jnp.where(allowed, with_bias(scores, kind, h, line_ref, tab, adj), NEG)
                probs = jnp.exp(scores - lse_ref[0, h : h + 1, :])
                grad_probs = contract(values, dm[pair, half, :], 1, 1)
                grads = probs * (grad_probs - d_s[h : h + 1, :])
                low = grads.astype(BF16)
                probs_pair.append(probs.astype(BF16))
                grads_pair.append(low)
                if causal:
                    rounded = low.astype(F32)
                    if kind == 3:
                        gt[h] += rounded
                    elif kind == 2:
                        k_pos = lax.broadcasted_iota(jnp.int32, (TILE, TILE), 0)
                        q_pos = lax.broadcasted_iota(jnp.int32, (TILE, TILE), 1)
                        near = jnp.where(k_pos > q_pos, rounded, 0.0)
                        gt[h] += near
                        gfar[h] += jnp.sum((rounded - near).reshape(TILE // 8, 8, TILE), axis=0)
                    else:
                        gfar[h] += jnp.sum(rounded.reshape(TILE // 8, 8, TILE), axis=0)
                back = contract(keys, low, 0, 0)
                rows = slice(h * HEAD_DIM, (h + 1) * HEAD_DIM)
                start = (h % 2) * HEAD_DIM
                dq_acc[rows, :] += back[start : start + HEAD_DIM, :]
            dv_acc[pl.ds(row, TILE), lanes] += contract(
                jnp.concatenate(probs_pair, axis=1), dm[pair], 1, 0
            )
            dk_acc[pl.ds(row, TILE), lanes] += contract(
                jnp.concatenate(grads_pair, axis=1), qm[pair], 1, 0
            )

    visit_tiles(causal, kinds_ref, tile, (own_rows + par_rows) // TILE)
    dq_ref[...] = dq_acc[...].T.astype(BF16)

    @pl.when(i == pl.num_programs(1) - 1)
    def _():
        own_ref[0] = dk_acc[0:own_rows, :].astype(BF16)
        own_ref[1] = dv_acc[0:own_rows, :].astype(BF16)
        par_ref[0] = dk_acc[own_rows : own_rows + par_rows, :].astype(BF16)
        par_ref[1] = dv_acc[own_rows : own_rows + par_rows, :].astype(BF16)
        for h in range(GROUP):
            if causal:
                gline_ref[h] = line_of(gt[h])
                gfar_ref[h] = jnp.sum(gfar[h], axis=0, keepdims=True)
            else:
                gline_ref[h] = jnp.zeros((1, TILE), F32)
                gfar_ref[h] = jnp.zeros((1, TILE), F32)


VMEM_LIMIT = 60 * 1024 * 1024


def attention_specs(tokens, width, own_rows, par_rows):
    groups = HEADS // GROUP
    lanes = GROUP * HEAD_DIM
    keys = own_rows + par_rows
    return [
        pl.BlockSpec((TILE, lanes), lambda g, i, kinds: (i, g)),
        pl.BlockSpec((own_rows, lanes), lambda g, i, kinds: (0, g)),
        pl.BlockSpec((own_rows, lanes), lambda g, i, kinds: (0, groups + g)),
        pl.BlockSpec((par_rows, lanes), lambda g, i, kinds: (0, g)),
        pl.BlockSpec((par_rows, lanes), lambda g, i, kinds: (0, groups + g)),
        pl.BlockSpec((8, TILE), lambda g, i, kinds: (0, i)),
        pl.BlockSpec((keys, LANES), lambda g, i, kinds: (0, 0)),
        pl.BlockSpec((GROUP, 1, TILE), lambda g, i, kinds: (g, 0, 0)),
    ]


def attend_fast(kinds, query, kv_own, kv_par, segq, segk, line, causal):
    tokens, width = query.shape
    own_rows, par_rows = kv_own.shape[0], kv_par.shape[0]
    keys = own_rows + par_rows
    groups, lanes = HEADS // GROUP, GROUP * HEAD_DIM
    table = (GROUP, TILE, TILE) if causal else (1, 8, LANES)
    return pl.pallas_call(
        functools.partial(attend_kernel, causal, own_rows, par_rows),
        grid_spec=pltpu.PrefetchScalarGridSpec(
            num_scalar_prefetch=1,
            grid=(groups, tokens // TILE),
            in_specs=attention_specs(tokens, width, own_rows, par_rows),
            out_specs=[
                pl.BlockSpec((TILE, lanes), lambda g, i, kinds: (i, g)),
                pl.BlockSpec((1, GROUP, TILE), lambda g, i, kinds: (g, 0, i)),
            ],
            scratch_shapes=[
                pltpu.VMEM((keys, lanes), BF16),
                pltpu.VMEM((keys, lanes), BF16),
                pltpu.VMEM((GROUP, TILE, LANES), BF16),
                pltpu.VMEM(table, F32),
                pltpu.VMEM(table, F32),
                pltpu.VMEM((8, TILE), F32),
                pltpu.VMEM((8, TILE), F32),
                pltpu.VMEM((lanes, TILE), F32),
            ],
        ),
        out_shape=[
            jax.ShapeDtypeStruct((tokens, width), BF16),
            jax.ShapeDtypeStruct((groups, GROUP, tokens), F32),
        ],
        compiler_params=pltpu.CompilerParams(vmem_limit_bytes=VMEM_LIMIT),
        cost_estimate=pl.CostEstimate(
            flops=tokens * keys * width * 4, bytes_accessed=4 * (tokens + keys) * width,
            transcendentals=tokens * keys * HEADS // 2,
        ),
        name="attend_self" if causal else "attend_cross",
    )(kinds, query, kv_own, kv_own, kv_par, kv_par, segq, segk, line)


def attend_back_fast(kinds, query, kv_own, kv_par, segq, segk, line, grad_mixed, mixed, lse, causal):
    tokens, width = query.shape
    own_rows, par_rows = kv_own.shape[0], kv_par.shape[0]
    keys = own_rows + par_rows
    groups, lanes = HEADS // GROUP, GROUP * HEAD_DIM
    table = (GROUP, TILE, TILE) if causal else (1, 8, LANES)
    block = pl.BlockSpec((TILE, lanes), lambda g, i, kinds: (i, g))
    line_spec = pl.BlockSpec((GROUP, 1, TILE), lambda g, i, kinds: (g, 0, 0))
    return pl.pallas_call(
        functools.partial(attend_back_kernel, causal, own_rows, par_rows),
        grid_spec=pltpu.PrefetchScalarGridSpec(
            num_scalar_prefetch=1,
            grid=(groups, tokens // TILE),
            in_specs=attention_specs(tokens, width, own_rows, par_rows)
            + [block, block, pl.BlockSpec((1, GROUP, TILE), lambda g, i, kinds: (g, 0, i))],
            out_specs=[
                block,
                pl.BlockSpec((2, own_rows, lanes), lambda g, i, kinds: (0, 0, g)),
                pl.BlockSpec((2, par_rows, lanes), lambda g, i, kinds: (0, 0, g)),
                line_spec,
                line_spec,
            ],
            scratch_shapes=[
                pltpu.VMEM((keys, lanes), BF16),
                pltpu.VMEM((keys, lanes), BF16),
                pltpu.VMEM((GROUP // 2, 2 * TILE, LANES), BF16),
                pltpu.VMEM((GROUP // 2, 2 * TILE, LANES), BF16),
                pltpu.VMEM(table, F32),
                pltpu.VMEM(table, F32),
                pltpu.VMEM((8, TILE), F32),
                pltpu.VMEM((lanes, TILE), F32),
                pltpu.VMEM((keys, lanes), F32),
                pltpu.VMEM((keys, lanes), F32),
                pltpu.VMEM(table, F32),
                pltpu.VMEM((GROUP, 8, TILE), F32),
            ],
        ),
        out_shape=[
            jax.ShapeDtypeStruct((tokens, width), BF16),
            jax.ShapeDtypeStruct((2, own_rows, width), BF16),
            jax.ShapeDtypeStruct((2, par_rows, width), BF16),
            jax.ShapeDtypeStruct((HEADS, 1, TILE), F32),
            jax.ShapeDtypeStruct((HEADS, 1, TILE), F32),
        ],
        compiler_params=pltpu.CompilerParams(vmem_limit_bytes=VMEM_LIMIT),
        cost_estimate=pl.CostEstimate(
            flops=tokens * keys * width * 10, bytes_accessed=10 * (tokens + keys) * width,
            transcendentals=tokens * keys * HEADS // 2,
        ),
        name="attend_self_back" if causal else "attend_cross_back",
    )(kinds, query, kv_own, kv_own, kv_par, kv_par, segq, segk, line, grad_mixed, mixed, lse)


AXES = ("dp", "seq")


def exchange(value, dp_bit, seq_bit):
    pairs = [
        (dp * 4 + seq, (dp ^ dp_bit) * 4 + (seq ^ seq_bit)) for dp in range(8) for seq in range(4)
    ]
    return lax.ppermute(value, AXES, pairs)


CORE, Z_LOW, Z_HIGH, X, Y = (1, 0), (2, 0), (4, 0), (0, 1), (0, 2)


def move_pairs(a, b):
    pairs = []
    for z in range(4):
        for core in range(2):
            for s in range(4):
                micro, half_core = (s >> 1) ^ a, (s & 1) ^ b
                pairs.append(((2 * z + core) * 4 + s, (2 * z + half_core) * 4 + 2 * core + micro))
    return pairs


ROUNDS = ((0, 0), (0, 1), (1, 0), (1, 1))


def take(value, index, axis):
    return lax.dynamic_index_in_dim(value, index, axis, keepdims=False)


def gather_kernel(count, *refs):
    shards, wholes = refs[:count], refs[count : 2 * count]
    local_sem, send_sem, recv_sem = refs[2 * count :]
    dp, seq = lax.axis_index("dp"), lax.axis_index("seq")
    z, core, y, x = dp // 2, dp % 2, seq // 2, seq % 2
    at_z = [{"dp": ((z + k) % 4) * 2 + core, "seq": seq} for k in (1, 2, 3)]
    at_x = {"dp": dp, "seq": seq + 1 - 2 * x}
    at_y = {"dp": dp, "seq": seq + 2 - 4 * y}
    at_core = {"dp": dp + 1 - 2 * core, "seq": seq}
    partners = at_z + [at_x, at_y, at_core]
    barrier = pltpu.get_barrier_semaphore()
    for partner in partners:
        pl.semaphore_signal(barrier, inc=1, device_id=partner, device_id_type=pl.DeviceIdType.MESH)
    pl.semaphore_wait(barrier, len(partners))

    def send(w, slot, source, target, device):
        copy = pltpu.make_async_remote_copy(
            src_ref=source,
            dst_ref=target,
            send_sem=send_sem.at[w, slot],
            recv_sem=recv_sem.at[w, slot],
            device_id=device,
            device_id_type=pl.DeviceIdType.MESH,
        )
        copy.start()
        return copy

    locals_, rounds = [], [[], [], [], []]
    for w in range(count):
        own = wholes[w].at[z, core, y, x]
        copy = pltpu.make_async_copy(shards[w], own, local_sem.at[w])
        copy.start()
        locals_.append(copy)
        rounds[0].append([send(w, k, shards[w], own, at_z[k]) for k in range(3)])
    for t in range(count + 2):
        if t < count:
            w, half = t, wholes[t].shape[-1] // 2
            left, right = pl.ds(0, half), pl.ds(half, half)
            locals_[w].wait()
            for copy in rounds[0][w]:
                copy.wait_recv()
            one = wholes[w].at[:, core, y, x, :, left]
            two = wholes[w].at[:, core, y, x, :, right]
            rounds[1].append([send(w, 3, one, one, at_x), send(w, 4, two, two, at_y)])
        if 0 <= t - 1 < count:
            w, half = t - 1, wholes[t - 1].shape[-1] // 2
            left, right = pl.ds(0, half), pl.ds(half, half)
            for copy in rounds[1][w]:
                copy.wait_recv()
            one = wholes[w].at[:, core, y, :, :, left]
            two = wholes[w].at[:, core, :, x, :, right]
            rounds[2].append([send(w, 5, one, one, at_y), send(w, 6, two, two, at_x)])
        if 0 <= t - 2 < count:
            w = t - 2
            for copy in rounds[2][w]:
                copy.wait_recv()
            both = wholes[w].at[:, core]
            rounds[3].append([send(w, 7, both, both, at_core)])
    for w in range(count):
        for copy in rounds[3][w]:
            copy.wait_recv()
        for stage in rounds:
            for copy in stage[w]:
                copy.wait_send()


def gather_weights(shards):
    count = len(shards)
    sent = sum(shard.size for shard in shards) * 2
    wholes = pl.pallas_call(
        functools.partial(gather_kernel, count),
        in_specs=[pl.BlockSpec(memory_space=pltpu.VMEM)] * count,
        out_specs=[pl.BlockSpec(memory_space=pl.ANY)] * count,
        out_shape=[jax.ShapeDtypeStruct((4, 2, 2, 2, *shard.shape), BF16) for shard in shards],
        scratch_shapes=[
            pltpu.SemaphoreType.DMA((count,)),
            pltpu.SemaphoreType.DMA((count, 8)),
            pltpu.SemaphoreType.DMA((count, 8)),
        ],
        compiler_params=pltpu.CompilerParams(
            vmem_limit_bytes=VMEM_LIMIT, collective_id=0, has_side_effects=True
        ),
        cost_estimate=pl.CostEstimate(flops=0, transcendentals=0, bytes_accessed=500 * sent),
        name="gather_weights",
    )(*shards)
    return [whole.reshape(-1, whole.shape[-1]) for whole in wholes]


def add_low(first, second):
    return (first.astype(F32) + second.astype(F32)).astype(BF16)


def scatter_kernel(shapes, *refs):
    count = len(shapes)
    grads, sums = refs[:count], refs[count : 2 * count]
    scratch = refs[2 * count :]
    kept, got_one, got_two, got_z = (scratch[j * count : (j + 1) * count] for j in range(4))
    own, totals = scratch[4 * count : 5 * count], scratch[5 * count : 6 * count]
    load_sem, store_sem, send_sem, recv_sem = scratch[6 * count :]
    dp, seq = lax.axis_index("dp"), lax.axis_index("seq")
    z, core, y, x = dp // 2, dp % 2, seq // 2, seq % 2
    at_z = [{"dp": ((z + k) % 4) * 2 + core, "seq": seq} for k in (1, 2, 3)]
    at_x = {"dp": dp, "seq": seq + 1 - 2 * x}
    at_y = {"dp": dp, "seq": seq + 2 - 4 * y}
    at_core = {"dp": dp + 1 - 2 * core, "seq": seq}
    partners = at_z + [at_x, at_y, at_core]
    barrier = pltpu.get_barrier_semaphore()
    for partner in partners:
        pl.semaphore_signal(barrier, inc=1, device_id=partner, device_id_type=pl.DeviceIdType.MESH)
    pl.semaphore_wait(barrier, len(partners))

    def send(w, slot, source, target, device):
        copy = pltpu.make_async_remote_copy(
            src_ref=source,
            dst_ref=target,
            send_sem=send_sem.at[w, slot],
            recv_sem=recv_sem.at[w, slot],
            device_id=device,
            device_id_type=pl.DeviceIdType.MESH,
        )
        copy.start()
        return copy

    def halves(w):
        half = shapes[w][1] // 2
        return pl.ds(0, half), pl.ds(half, half)

    def add(first, second, dtype):
        return (first.astype(F32) + second.astype(F32)).astype(dtype)

    stages, loads, stores = [[] for _ in range(4)], [], []
    for w in range(count):
        stages[0].append([send(w, 0, grads[w].at[:, 1 - core], kept[w], at_core)])
        load = pltpu.make_async_copy(grads[w].at[:, core], own[w], load_sem.at[w])
        load.start()
        loads.append(load)
    for t in range(count + 3):
        if t < count:
            w, dtype = t, kept[t].dtype
            left, right = halves(w)
            loads[w].wait()
            stages[0][w][0].wait_recv()

            def core_step(b, carry, w=w, dtype=dtype):
                zz, yy, xx = b // 4, (b // 2) % 2, b % 2
                kept[w][zz, yy, xx] = add(kept[w][zz, yy, xx], own[w][zz, yy, xx], dtype)
                return carry

            lax.fori_loop(0, 16, core_step, 0)
            half = shapes[w][1] // 2
            stages[1].append([
                send(w, 1, kept[w].at[:, :, 1 - x, :, left], got_one[w].at[0], at_x),
                send(w, 2, kept[w].at[:, 1 - y, :, :, right], got_one[w].at[1], at_y),
            ])
        if 0 <= t - 1 < count:
            w, dtype = t - 1, kept[t - 1].dtype
            left, right = halves(w)
            half = shapes[w][1] // 2
            for copy in stages[1][w]:
                copy.wait_recv()

            def one_step(b, carry, w=w, dtype=dtype, half=half):
                zz, other = b // 2, b % 2
                kept[w][zz, other, x, :, 0:half] = add(
                    kept[w][zz, other, x, :, 0:half], got_one[w][0, zz, other], dtype
                )
                kept[w][zz, y, other, :, half : 2 * half] = add(
                    kept[w][zz, y, other, :, half : 2 * half], got_one[w][1, zz, other], dtype
                )
                return carry

            lax.fori_loop(0, 8, one_step, 0)
            stages[2].append([
                send(w, 3, kept[w].at[:, 1 - y, x, :, left], got_two[w].at[0], at_y),
                send(w, 4, kept[w].at[:, y, 1 - x, :, right], got_two[w].at[1], at_x),
            ])
        if 0 <= t - 2 < count:
            w, dtype = t - 2, kept[t - 2].dtype
            half = shapes[w][1] // 2
            for copy in stages[2][w]:
                copy.wait_recv()

            def two_step(zz, carry, w=w, dtype=dtype, half=half):
                kept[w][zz, y, x, :, 0:half] = add(
                    kept[w][zz, y, x, :, 0:half], got_two[w][0, zz], dtype
                )
                kept[w][zz, y, x, :, half : 2 * half] = add(
                    kept[w][zz, y, x, :, half : 2 * half], got_two[w][1, zz], dtype
                )
                return carry

            lax.fori_loop(0, 4, two_step, 0)
            stages[3].append([
                send(w, 5 + k, kept[w].at[(z + k + 1) % 4, y, x], got_z[w].at[k], at_z[k])
                for k in range(3)
            ])
        if 0 <= t - 3 < count:
            w = t - 3
            for copy in stages[3][w]:
                copy.wait_recv()
            total = kept[w][z, y, x].astype(F32)
            for k in range(3):
                total = total + got_z[w][k].astype(F32)
            totals[w][...] = total
            store = pltpu.make_async_copy(totals[w], sums[w], store_sem.at[w])
            store.start()
            stores.append(store)
    for w in range(count):
        stores[w].wait()
        for stage in stages:
            for copy in stage[w]:
                copy.wait_send()


def scatter_grads(grads):
    count = len(grads)
    shapes = [(grad.shape[0] // 32, grad.shape[1]) for grad in grads]
    types = [grad.dtype for grad in grads]

    def buffers(*lead, halved=False):
        return [
            pltpu.VMEM((*lead, rows, width // 2 if halved else width), kind)
            for (rows, width), kind in zip(shapes, types)
        ]

    return pl.pallas_call(
        functools.partial(scatter_kernel, shapes),
        in_specs=[pl.BlockSpec(memory_space=pl.ANY)] * count,
        out_specs=[pl.BlockSpec(memory_space=pl.ANY)] * count,
        out_shape=[jax.ShapeDtypeStruct(shape, F32) for shape in shapes],
        scratch_shapes=buffers(4, 2, 2)
        + buffers(2, 4, 2, halved=True)
        + buffers(2, 4, halved=True)
        + buffers(3)
        + buffers(4, 2, 2)
        + [pltpu.VMEM(shape, F32) for shape in shapes]
        + [
            pltpu.SemaphoreType.DMA((count,)),
            pltpu.SemaphoreType.DMA((count,)),
            pltpu.SemaphoreType.DMA((count, 8)),
            pltpu.SemaphoreType.DMA((count, 8)),
        ],
        compiler_params=pltpu.CompilerParams(
            vmem_limit_bytes=67043328, collective_id=1, has_side_effects=True
        ),
        cost_estimate=pl.CostEstimate(
            flops=0, transcendentals=0, bytes_accessed=16 * sum(grad.size for grad in grads)
        ),
        name="scatter_grads",
    )(*[
        grad.reshape(4, 2, 2, 2, rows, width) for grad, (rows, width) in zip(grads, shapes)
    ])


def norm_scale(value):
    return lax.rsqrt(jnp.mean(value * value, axis=-1, keepdims=True) + EPS)


def normed(value, gain):
    return (value * norm_scale(value) * gain).astype(BF16)


def norm_back(value, gain, grad):
    scale = norm_scale(value)
    scaled = grad * gain
    inner = jnp.mean(scaled * value, axis=-1, keepdims=True)
    return (
        scale * scaled - (scale * scale * scale) * value * inner,
        jnp.sum(grad * value * scale, axis=0),
    )


def dot(rows, weight):
    return jnp.dot(rows, weight, preferred_element_type=F32)


def dot_back(grads, weight):
    return contract(grads, weight, 1, 1)


def dot_weight(rows, grads):
    return contract(rows, grads, 0, 0).astype(BF16)


def fast_body(
    hidden_in,
    encoder_states,
    segments,
    enc_segments,
    grad_out,
    norm_self,
    q_self,
    k_self,
    v_self,
    o_self,
    rel_bias,
    norm_cross,
    q_cross,
    k_cross,
    v_cross,
    o_cross,
    norm_ff,
    wi_gate,
    wi_up,
    wo_ff,
):
    dp, seq = lax.axis_index("dp"), lax.axis_index("seq")
    core, z_low, z_high, y, x = dp % 2, (dp // 2) % 2, dp // 4, seq // 2, seq % 2
    place = (core, z_low, z_high, y, x)
    rows_dev, width = hidden_in.shape[2], hidden_in.shape[3]
    enc_dev = encoder_states.shape[2]
    part, enc_part = rows_dev // 2, enc_dev // 2
    owned_micro = seq % 2

    def send_tokens(pieces_of):
        return [
            lax.ppermute(pieces_of((seq // 2) ^ a, b), AXES, move_pairs(a, b)) for a, b in ROUNDS
        ]

    def settle(received):
        slots = []
        for s in range(4):
            index = 2 * ((s >> 1) ^ owned_micro) + ((s & 1) ^ core)
            slots.append(lax.select_n(index, *received))
        return jnp.stack(slots)

    def return_tokens(value):
        received = []
        for a, b in ROUNDS:
            index = 2 * (owned_micro ^ a) + (core ^ b)
            back = [(target, source) for source, target in move_pairs(a, b)]
            received.append(lax.ppermute(take(value, index, 0), AXES, back))
        flag = seq // 2
        micro = []
        for m in range(2):
            micro.append(
                jnp.concatenate(
                    [jnp.where((flag ^ m) == 0, received[b], received[2 + b]) for b in range(2)],
                    axis=0,
                )
            )
        return jnp.stack(micro)[:, None]

    codes = jnp.concatenate([segments[:, 0], enc_segments[:, 0]], axis=1).astype(BF16)
    codes = jnp.pad(codes, ((0, 0), (0, width - codes.shape[1])))

    def bundle(micro, b):
        return jnp.concatenate(
            [
                take(hidden_in[:, 0, b * part : (b + 1) * part], micro, 0),
                take(encoder_states[:, 0, b * enc_part : (b + 1) * enc_part], micro, 0),
                jnp.broadcast_to(take(codes, micro, 0)[None], (16, width)),
            ],
            axis=0,
        )

    bundles = send_tokens(bundle)

    small = jnp.concatenate([norm_self, norm_cross, norm_ff, rel_bias])
    small_rows = norm_self.shape[0]
    small = jnp.broadcast_to(jnp.pad(small, (0, 2 * LANES - small.shape[0])), (8, 2 * LANES))
    small, wk, wv, wq, ck, cv, wo, cq, co, w_gate, w_up, w_down = gather_weights(
        [small, k_self, v_self, q_self, k_cross, v_cross, o_self, q_cross, o_cross, wi_gate, wi_up, wo_ff]
    )
    small = small.reshape(32, 8, 2 * LANES)[:, 0].astype(F32)
    gain_self, gain_cross, gain_ff = (
        small[:, j * small_rows : (j + 1) * small_rows].reshape(-1) for j in range(3)
    )
    table = small[:, 3 * small_rows : 3 * small_rows + rel_bias.shape[0]].reshape(BUCKETS, HEADS)
    ff = wi_gate.shape[1]

    inputs_low = settle([piece[:part] for piece in bundles]).reshape(4 * part, width)
    encoder = settle([piece[part : part + enc_part] for piece in bundles]).reshape(4 * enc_part, width)
    codes = settle([piece[part + enc_part : part + enc_part + 1] for piece in bundles])[:, 0]
    codes = codes.astype(jnp.int32)
    seg_parts = codes[:, :rows_dev].reshape(4, 2, part)
    enc_parts = codes[:, rows_dev : rows_dev + enc_dev].reshape(4, 2, enc_part)

    def of_core(parts, which):
        return jnp.stack([take(parts[s], which ^ (s & 1), 0) for s in range(4)])

    seg_own, seg_par = of_core(seg_parts, core), of_core(seg_parts, 1 - core)
    enc_own, enc_par = of_core(enc_parts, core), of_core(enc_parts, 1 - core)
    seg_keys = jnp.concatenate([seg_own, seg_par])
    quarter = jnp.arange(4, dtype=jnp.int32)
    at_own = 2 * quarter + (core ^ (quarter % 2))
    at_par = 2 * quarter + ((1 - core) ^ (quarter % 2))
    at_keys = jnp.concatenate([at_own, at_par])
    needed = (at_keys[None, :] < at_own[:, None]) & (seg_keys[None, :, -1] >= seg_own[:, :1])
    kinds = jnp.where(needed, jnp.where(at_keys[None, :] == at_own[:, None] - 1, 2, 1), 0)
    kinds = kinds.astype(jnp.int32).reshape(-1)
    segq = jnp.broadcast_to(seg_own.reshape(1, -1), (8, 4 * part))
    segk = jnp.broadcast_to(seg_keys.reshape(-1, 1), (8 * part, LANES))
    enc_segk = jnp.broadcast_to(
        jnp.concatenate([enc_own, enc_par]).reshape(-1, 1), (8 * enc_part, LANES)
    )
    near = (
        buckets_of(jnp.arange(TILE, dtype=jnp.int32))[:, None] == jnp.arange(BUCKETS)[None, :]
    ).astype(F32)
    line = jnp.dot(near, table, precision=lax.Precision.HIGHEST).T.reshape(HEADS, 1, TILE)

    inputs = inputs_low.astype(F32)
    normed_self = normed(inputs, gain_self)
    kv_own = jnp.concatenate(
        [dot(normed_self, wk).astype(BF16), dot(normed_self, wv).astype(BF16)], axis=1
    )
    kv_par = exchange(kv_own, *CORE)
    query = dot(normed_self, wq).astype(BF16)
    cross_kv_own = jnp.concatenate(
        [dot(encoder, ck).astype(BF16), dot(encoder, cv).astype(BF16)], axis=1
    )
    cross_kv_par = exchange(cross_kv_own, *CORE)
    mixed, self_lse = attend_fast(kinds, query, kv_own, kv_par, segq, segk, line, True)
    after_self = inputs + dot(mixed, wo)
    normed_cross = normed(after_self, gain_cross)
    cross_query = dot(normed_cross, cq).astype(BF16)
    cross_mixed, cross_lse = attend_fast(
        kinds, cross_query, cross_kv_own, cross_kv_par, segq, enc_segk, line, False
    )
    after_cross = after_self + dot(cross_mixed, co)
    normed_ff = normed(after_cross, gain_ff)
    gate, up_values = dot(normed_ff, w_gate), dot(normed_ff, w_up)
    hidden = gelu_mix(gate, up_values).astype(BF16)
    result = (after_cross + dot(hidden, w_down)).astype(BF16)
    block_out = return_tokens(result.reshape(4, part, width))

    out_low = settle(
        send_tokens(lambda micro, b: take(grad_out[:, 0, b * part : (b + 1) * part], micro, 0))
    ).reshape(4 * part, width)
    grad_result = out_low.astype(F32)
    grad_w_down = dot_weight(hidden, out_low)
    grad_hidden = dot_back(out_low, w_down)
    mix_value, mix_pull = jax.vjp(gelu_mix, gate, up_values)
    grad_gate, grad_up = (piece.astype(BF16) for piece in mix_pull(grad_hidden))
    grad_w_gate, grad_w_up = dot_weight(normed_ff, grad_gate), dot_weight(normed_ff, grad_up)
    grad_normed_ff = dot_back(grad_gate, w_gate) + dot_back(grad_up, w_up)
    ff_part, grad_gain_ff = norm_back(after_cross, gain_ff, grad_normed_ff)
    grad_after_cross = grad_result + ff_part
    cross_out_low = grad_after_cross.astype(BF16)
    grad_co = dot_weight(cross_mixed, cross_out_low)
    grad_cross_mixed = dot_back(cross_out_low, co).astype(BF16)
    grad_cross_query, cross_own, cross_par, unused, unused = attend_back_fast(
        kinds, cross_query, cross_kv_own, cross_kv_par, segq, enc_segk, line,
        grad_cross_mixed, cross_mixed, cross_lse, False,
    )
    cross_got = add_low(cross_own, exchange(cross_par, *CORE))
    grad_ck, grad_cv = dot_weight(encoder, cross_got[0]), dot_weight(encoder, cross_got[1])
    grad_encoder = (dot_back(cross_got[0], ck) + dot_back(cross_got[1], cv)).astype(BF16)
    grad_encoder = return_tokens(grad_encoder.reshape(4, enc_part, width)).astype(F32)
    grad_cq = dot_weight(normed_cross, grad_cross_query)
    grad_normed_cross = dot_back(grad_cross_query, cq)
    cross_part, grad_gain_cross = norm_back(after_self, gain_cross, grad_normed_cross)
    grad_after_self = grad_after_cross + cross_part
    self_out_low = grad_after_self.astype(BF16)
    grad_wo = dot_weight(mixed, self_out_low)
    grad_mixed = dot_back(self_out_low, wo).astype(BF16)
    grad_query, self_own, self_par, grad_line, grad_far = attend_back_fast(
        kinds, query, kv_own, kv_par, segq, segk, line, grad_mixed, mixed, self_lse, True
    )
    self_got = add_low(self_own, exchange(self_par, *CORE))
    grad_wq = dot_weight(normed_self, grad_query)
    grad_wk, grad_wv = dot_weight(normed_self, self_got[0]), dot_weight(normed_self, self_got[1])
    grad_normed_self = (
        dot_back(grad_query, wq) + dot_back(self_got[0], wk) + dot_back(self_got[1], wv)
    )
    self_part, grad_gain_self = norm_back(inputs, gain_self, grad_normed_self)
    grad_hidden_in = return_tokens((grad_after_self + self_part).astype(BF16).reshape(4, part, width))

    grad_table = jnp.dot(near.T, grad_line.reshape(HEADS, TILE).T, precision=lax.Precision.HIGHEST)
    grad_table = grad_table.at[BUCKETS - 1].add(jnp.sum(grad_far.reshape(HEADS, TILE), axis=1))
    small_grads = [piece.reshape(32, -1) for piece in (grad_gain_self, grad_gain_cross, grad_gain_ff)]
    small_grads = jnp.concatenate(small_grads + [grad_table.reshape(32, -1)], axis=1)
    small_grads = jnp.pad(small_grads, ((0, 0), (0, 2 * LANES - small_grads.shape[1])))
    small_grads = jnp.broadcast_to(small_grads[:, None], (32, 8, 2 * LANES)).reshape(256, 2 * LANES)
    order = [
        grad_wk, grad_wv, grad_w_gate, grad_w_up, grad_w_down, grad_ck, grad_cv, grad_cq, grad_co,
        grad_wo, grad_wq, small_grads,
    ]
    (
        grad_wk, grad_wv, grad_w_gate, grad_w_up, grad_w_down, grad_ck, grad_cv, grad_cq, grad_co,
        grad_wo, grad_wq, small_grads,
    ) = scatter_grads(order)
    small_grads = small_grads[0]
    return (
        block_out,
        grad_hidden_in.astype(F32),
        grad_encoder,
        small_grads[:small_rows],
        grad_wq,
        grad_wk,
        grad_wv,
        grad_wo,
        small_grads[3 * small_rows : 3 * small_rows + rel_bias.shape[0]],
        small_grads[small_rows : 2 * small_rows],
        grad_cq,
        grad_ck,
        grad_cv,
        grad_co,
        small_grads[2 * small_rows : 3 * small_rows],
        grad_w_gate,
        grad_w_up,
        grad_w_down,
    )


def fits_fast(mesh):
    return mesh.shape["dp"] == 8 and mesh.shape["seq"] == 4


def solution(mesh):
    return jax.shard_map(
        fast_body if fits_fast(mesh) else general_body,
        mesh=mesh,
        in_specs=(
            P(None, "dp", "seq", None),
            P(None, "dp", "seq", None),
            P(None, "dp", "seq"),
            P(None, "dp", "seq"),
            P(None, "dp", "seq", None),
            P(("dp", "seq")),
            P(("dp", "seq"), None),
            P(("dp", "seq"), None),
            P(("dp", "seq"), None),
            P(("dp", "seq"), None),
            P(("dp", "seq")),
            P(("dp", "seq")),
            P(("dp", "seq"), None),
            P(("dp", "seq"), None),
            P(("dp", "seq"), None),
            P(("dp", "seq"), None),
            P(("dp", "seq")),
            P(("dp", "seq"), None),
            P(("dp", "seq"), None),
            P(("dp", "seq"), None),
        ),
        out_specs=(
            P(None, "dp", "seq", None),
            P(None, "dp", "seq", None),
            P(None, "dp", "seq", None),
            P(("dp", "seq")),
            P(("dp", "seq"), None),
            P(("dp", "seq"), None),
            P(("dp", "seq"), None),
            P(("dp", "seq"), None),
            P(("dp", "seq")),
            P(("dp", "seq")),
            P(("dp", "seq"), None),
            P(("dp", "seq"), None),
            P(("dp", "seq"), None),
            P(("dp", "seq"), None),
            P(("dp", "seq")),
            P(("dp", "seq"), None),
            P(("dp", "seq"), None),
            P(("dp", "seq"), None),
        ),
        check_vma=False,
    )
```

```python
import functools
import math

import jax
import jax.numpy as jnp
from jax import lax
from jax.experimental import pallas as pl
from jax.experimental.pallas import tpu as pltpu
from jax.sharding import PartitionSpec as P

HEADS = 16
HEAD_DIM = 64
BUCKETS = 32
MAX_DIST = 128


EPS = 1e-06
NEG = -1e30


def norm_rows(value, gain):
    return value * lax.rsqrt(jnp.mean(value * value, axis=-1, keepdims=True) + EPS) * gain


def bucket_edges():
    half = BUCKETS // 2
    return [math.ceil(half * (MAX_DIST / half) ** (step / half)) for step in range(1, half)]


def buckets_of(distance):
    half = BUCKETS // 2
    far = half + sum(((distance >= edge).astype(jnp.int32) for edge in bucket_edges()))
    return jnp.where(distance < half, distance, far)


def by_heads(values):
    return values.reshape(values.shape[0], values.shape[1], HEADS, HEAD_DIM)


def join_heads(values):
    return values.reshape(values.shape[0], values.shape[1], HEADS * HEAD_DIM)


def project(rows, weight_matrix):
    return jnp.dot(rows, weight_matrix, preferred_element_type=jnp.float32)


def project_back(grads, weight_matrix):
    return jnp.einsum("stn,kn->stk", grads, weight_matrix, preferred_element_type=jnp.float32)


def weight_grad(rows, grads):
    return jnp.einsum("stk,stn->kn", rows, grads, preferred_element_type=jnp.float32)


def gelu_mix(gate, up_values):
    return jax.nn.gelu(gate, approximate=True) * up_values


def scores_of(q_rows, keys, bias, allowed):
    scores = jnp.einsum("sqhd,skhd->shqk", q_rows, keys, preferred_element_type=jnp.float32) + bias
    return jnp.where(allowed[:, None], scores, NEG)


def attend(q_rows, keys, values, bias, allowed):
    scores = scores_of(q_rows, keys, bias, allowed)
    largest = jnp.max(scores, axis=-1, keepdims=True)
    raised = jnp.exp(scores - largest)
    total = jnp.sum(raised, axis=-1, keepdims=True)
    probs = raised / total
    mixed = jnp.einsum(
        "shqk,skhd->sqhd", probs.astype(jnp.bfloat16), values, preferred_element_type=jnp.float32
    )
    return (join_heads(mixed).astype(jnp.bfloat16), largest + jnp.log(total))


def attend_back(q_rows, keys, values, bias, allowed, log_total, grad_mixed):
    scores = scores_of(q_rows, keys, bias, allowed)
    probs = jnp.exp(scores - log_total)
    grad_probs = jnp.einsum(
        "sqhd,skhd->shqk", grad_mixed, values, preferred_element_type=jnp.float32
    )
    inner = jnp.sum(probs * grad_probs, axis=-1, keepdims=True)
    grad_scores = (probs * (grad_probs - inner)).astype(jnp.bfloat16)
    grad_query = jnp.einsum(
        "shqk,skhd->sqhd", grad_scores, keys, preferred_element_type=jnp.float32
    )
    grad_keys = jnp.einsum(
        "shqk,sqhd->skhd", grad_scores, q_rows, preferred_element_type=jnp.float32
    )
    grad_values = jnp.einsum(
        "shqk,sqhd->skhd",
        probs.astype(jnp.bfloat16),
        grad_mixed,
        preferred_element_type=jnp.float32,
    )
    return (join_heads(grad_query), join_heads(grad_keys), join_heads(grad_values), grad_scores)


def general_body(
    hidden_in,
    encoder_states,
    segments,
    enc_segments,
    grad_out,
    norm_self,
    q_self,
    k_self,
    v_self,
    o_self,
    rel_bias,
    norm_cross,
    q_cross,
    k_cross,
    v_cross,
    o_cross,
    norm_ff,
    wi_gate,
    wi_up,
    wo_ff,
):
    shards = (
        norm_self,
        q_self,
        k_self,
        v_self,
        o_self,
        rel_bias,
        norm_cross,
        q_cross,
        k_cross,
        v_cross,
        o_cross,
        norm_ff,
        wi_gate,
        wi_up,
        wo_ff,
    )
    micro_count = hidden_in.shape[0]
    rows_dev = hidden_in.shape[2]
    seg_whole, enc_seg_whole = (
        lax.all_gather(segments, "seq", axis=2, tiled=True),
        lax.all_gather(enc_segments, "seq", axis=2, tiled=True),
    )
    length = seg_whole.shape[2]
    positions = lax.axis_index("seq") * rows_dev + jnp.arange(rows_dev, dtype=jnp.int32)
    columns = jnp.arange(length, dtype=jnp.int32)
    distance = jnp.maximum(positions[:, None] - columns[None, :], 0)
    bucket_indicator = (
        buckets_of(distance)[None] == jnp.arange(BUCKETS, dtype=jnp.int32)[:, None, None]
    ).astype(jnp.bfloat16)
    causal = columns[None, :] <= positions[:, None]
    grad_shards = tuple((jnp.zeros(piece.shape, jnp.float32) for piece in shards))
    outputs, grad_inputs, grad_encoders = ([], [], [])
    for micro in range(micro_count):
        params = (
            lax.all_gather(shards[0], ("dp", "seq"), axis=0, tiled=True),
            lax.all_gather(shards[1], ("dp", "seq"), axis=0, tiled=True),
            lax.all_gather(shards[2], ("dp", "seq"), axis=0, tiled=True),
            lax.all_gather(shards[3], ("dp", "seq"), axis=0, tiled=True),
            lax.all_gather(shards[4], ("dp", "seq"), axis=0, tiled=True),
            lax.all_gather(shards[5], ("dp", "seq"), axis=0, tiled=True),
            lax.all_gather(shards[6], ("dp", "seq"), axis=0, tiled=True),
            lax.all_gather(shards[7], ("dp", "seq"), axis=0, tiled=True),
            lax.all_gather(shards[8], ("dp", "seq"), axis=0, tiled=True),
            lax.all_gather(shards[9], ("dp", "seq"), axis=0, tiled=True),
            lax.all_gather(shards[10], ("dp", "seq"), axis=0, tiled=True),
            lax.all_gather(shards[11], ("dp", "seq"), axis=0, tiled=True),
            lax.all_gather(shards[12], ("dp", "seq"), axis=0, tiled=True),
            lax.all_gather(shards[13], ("dp", "seq"), axis=0, tiled=True),
            lax.all_gather(shards[14], ("dp", "seq"), axis=0, tiled=True),
        )
        (
            gain_self,
            wq,
            wk,
            wv,
            wo,
            table_flat,
            gain_cross,
            cq,
            ck,
            cv,
            co,
            gain_ff,
            w_gate,
            w_up,
            w_down,
        ) = params
        bias = jnp.einsum(
            "pia,pw->wia",
            bucket_indicator,
            table_flat.reshape(BUCKETS, HEADS),
            preferred_element_type=jnp.float32,
        )
        inputs = hidden_in[micro].astype(jnp.float32)
        encoder = encoder_states[micro]
        seg_own = segments[micro]
        self_allowed = (seg_own[:, :, None] == seg_whole[micro][:, None, :]) & causal[None]
        cross_allowed = seg_own[:, :, None] == enc_seg_whole[micro][:, None, :]
        self_norm_scale = gain_self.astype(jnp.float32)
        cross_gain = gain_cross.astype(jnp.float32)
        ff_gain = gain_ff.astype(jnp.float32)
        normed_self = norm_rows(inputs, self_norm_scale).astype(jnp.bfloat16)
        query = project(normed_self, wq).astype(jnp.bfloat16)
        key_own = project(normed_self, wk).astype(jnp.bfloat16)
        value_own = project(normed_self, wv).astype(jnp.bfloat16)
        cross_key_own = project(encoder, ck).astype(jnp.bfloat16)
        cross_value_own = project(encoder, cv).astype(jnp.bfloat16)
        keys, values, cross_keys, cross_values = (
            lax.all_gather(key_own, "seq", axis=1, tiled=True),
            lax.all_gather(value_own, "seq", axis=1, tiled=True),
            lax.all_gather(cross_key_own, "seq", axis=1, tiled=True),
            lax.all_gather(cross_value_own, "seq", axis=1, tiled=True),
        )
        mixed, self_log_normalizer = attend(
            by_heads(query), by_heads(keys), by_heads(values), bias, self_allowed
        )
        after_self = inputs + project(mixed, wo)
        normed_cross = norm_rows(after_self, cross_gain).astype(jnp.bfloat16)
        cross_query = project(normed_cross, cq).astype(jnp.bfloat16)
        cross_mixed, cross_log = attend(
            by_heads(cross_query), by_heads(cross_keys), by_heads(cross_values), 0.0, cross_allowed
        )
        after_cross = after_self + project(cross_mixed, co)
        normed_ff = norm_rows(after_cross, ff_gain).astype(jnp.bfloat16)
        gate = project(normed_ff, w_gate)
        up_values = project(normed_ff, w_up)
        hidden = gelu_mix(gate, up_values).astype(jnp.bfloat16)
        result = after_cross + project(hidden, w_down)
        outputs.append(result.astype(jnp.bfloat16))
        params = (
            lax.all_gather(shards[0], ("dp", "seq"), axis=0, tiled=True),
            lax.all_gather(shards[1], ("dp", "seq"), axis=0, tiled=True),
            lax.all_gather(shards[2], ("dp", "seq"), axis=0, tiled=True),
            lax.all_gather(shards[3], ("dp", "seq"), axis=0, tiled=True),
            lax.all_gather(shards[4], ("dp", "seq"), axis=0, tiled=True),
            lax.all_gather(shards[5], ("dp", "seq"), axis=0, tiled=True),
            lax.all_gather(shards[6], ("dp", "seq"), axis=0, tiled=True),
            lax.all_gather(shards[7], ("dp", "seq"), axis=0, tiled=True),
            lax.all_gather(shards[8], ("dp", "seq"), axis=0, tiled=True),
            lax.all_gather(shards[9], ("dp", "seq"), axis=0, tiled=True),
            lax.all_gather(shards[10], ("dp", "seq"), axis=0, tiled=True),
            lax.all_gather(shards[11], ("dp", "seq"), axis=0, tiled=True),
            lax.all_gather(shards[12], ("dp", "seq"), axis=0, tiled=True),
            lax.all_gather(shards[13], ("dp", "seq"), axis=0, tiled=True),
            lax.all_gather(shards[14], ("dp", "seq"), axis=0, tiled=True),
        )
        (
            gain_self,
            wq,
            wk,
            wv,
            wo,
            table_flat,
            gain_cross,
            cq,
            ck,
            cv,
            co,
            gain_ff,
            w_gate,
            w_up,
            w_down,
        ) = params
        grad_result = grad_out[micro].astype(jnp.float32)
        out_low = grad_out[micro]
        grad_w_down = weight_grad(hidden, out_low)
        grad_hidden = project_back(out_low, w_down)
        mix_value, mix_pull = jax.vjp(gelu_mix, gate, up_values)
        grad_gate, grad_up = mix_pull(grad_hidden)
        grad_gate = grad_gate.astype(jnp.bfloat16)
        grad_up = grad_up.astype(jnp.bfloat16)
        gate_weight_gradient = weight_grad(normed_ff, grad_gate)
        grad_w_up = weight_grad(normed_ff, grad_up)
        grad_normed_ff = project_back(grad_gate, w_gate) + project_back(grad_up, w_up)
        norm_value, norm_pull = jax.vjp(norm_rows, after_cross, ff_gain)
        ff_part, grad_gain_ff = norm_pull(grad_normed_ff)
        grad_after_cross = grad_result + ff_part
        cross_out_low = grad_after_cross.astype(jnp.bfloat16)
        grad_co = weight_grad(cross_mixed, cross_out_low)
        grad_cross_mixed = project_back(cross_out_low, co).astype(jnp.bfloat16)
        grad_cross_query, cross_key_terms, cross_value_terms, cross_scores = attend_back(
            by_heads(cross_query),
            by_heads(cross_keys),
            by_heads(cross_values),
            0.0,
            cross_allowed,
            cross_log,
            by_heads(grad_cross_mixed),
        )
        grad_cross_key, grad_cross_value = (
            lax.psum_scatter(
                cross_key_terms.astype(jnp.bfloat16), "seq", scatter_dimension=1, tiled=True
            ).astype(jnp.float32),
            lax.psum_scatter(
                cross_value_terms.astype(jnp.bfloat16), "seq", scatter_dimension=1, tiled=True
            ).astype(jnp.float32),
        )
        grad_cross_key = grad_cross_key.astype(jnp.bfloat16)
        grad_cross_value = grad_cross_value.astype(jnp.bfloat16)
        cross_key_gradient = weight_grad(encoder, grad_cross_key)
        grad_cv = weight_grad(encoder, grad_cross_value)
        grad_encoders.append(project_back(grad_cross_key, ck) + project_back(grad_cross_value, cv))
        grad_cross_query = grad_cross_query.astype(jnp.bfloat16)
        grad_cq = weight_grad(normed_cross, grad_cross_query)
        grad_normed_cross = project_back(grad_cross_query, cq)
        norm_value, norm_pull = jax.vjp(norm_rows, after_self, cross_gain)
        cross_part, grad_gain_cross = norm_pull(grad_normed_cross)
        grad_after_self = grad_after_cross + cross_part
        self_out_low = grad_after_self.astype(jnp.bfloat16)
        grad_wo = weight_grad(mixed, self_out_low)
        grad_mixed = project_back(self_out_low, wo).astype(jnp.bfloat16)
        grad_query, key_terms, value_terms, self_attention_logits = attend_back(
            by_heads(query),
            by_heads(keys),
            by_heads(values),
            bias,
            self_allowed,
            self_log_normalizer,
            by_heads(grad_mixed),
        )
        grad_table = jnp.einsum(
            "dcma,uma->uc",
            self_attention_logits,
            bucket_indicator,
            preferred_element_type=jnp.float32,
        ).reshape(-1)
        grad_key, grad_value = (
            lax.psum_scatter(
                key_terms.astype(jnp.bfloat16), "seq", scatter_dimension=1, tiled=True
            ).astype(jnp.float32),
            lax.psum_scatter(
                value_terms.astype(jnp.bfloat16), "seq", scatter_dimension=1, tiled=True
            ).astype(jnp.float32),
        )
        grad_key = grad_key.astype(jnp.bfloat16)
        grad_value = grad_value.astype(jnp.bfloat16)
        grad_query = grad_query.astype(jnp.bfloat16)
        grad_wq = weight_grad(normed_self, grad_query)
        grad_wk = weight_grad(normed_self, grad_key)
        grad_wv = weight_grad(normed_self, grad_value)
        grad_normed_self = (
            project_back(grad_query, wq) + project_back(grad_key, wk) + project_back(grad_value, wv)
        )
        norm_value, norm_pull = jax.vjp(norm_rows, inputs, self_norm_scale)
        self_part, grad_gain_self = norm_pull(grad_normed_self)
        grad_inputs.append(grad_after_self + self_part)
        local = (
            grad_gain_self,
            grad_wq,
            grad_wk,
            grad_wv,
            grad_wo,
            grad_table,
            grad_gain_cross,
            grad_cq,
            cross_key_gradient,
            grad_cv,
            grad_co,
            grad_gain_ff,
            gate_weight_gradient,
            grad_w_up,
            grad_w_down,
        )
        summed = (
            lax.psum_scatter(local[0], ("dp", "seq"), scatter_dimension=0, tiled=True),
            lax.psum_scatter(local[1], ("dp", "seq"), scatter_dimension=0, tiled=True),
            lax.psum_scatter(local[2], ("dp", "seq"), scatter_dimension=0, tiled=True),
            lax.psum_scatter(local[3], ("dp", "seq"), scatter_dimension=0, tiled=True),
            lax.psum_scatter(local[4], ("dp", "seq"), scatter_dimension=0, tiled=True),
            lax.psum_scatter(local[5], ("dp", "seq"), scatter_dimension=0, tiled=True),
            lax.psum_scatter(local[6], ("dp", "seq"), scatter_dimension=0, tiled=True),
            lax.psum_scatter(local[7], ("dp", "seq"), scatter_dimension=0, tiled=True),
            lax.psum_scatter(local[8], ("dp", "seq"), scatter_dimension=0, tiled=True),
            lax.psum_scatter(local[9], ("dp", "seq"), scatter_dimension=0, tiled=True),
            lax.psum_scatter(local[10], ("dp", "seq"), scatter_dimension=0, tiled=True),
            lax.psum_scatter(local[11], ("dp", "seq"), scatter_dimension=0, tiled=True),
            lax.psum_scatter(local[12], ("dp", "seq"), scatter_dimension=0, tiled=True),
            lax.psum_scatter(local[13], ("dp", "seq"), scatter_dimension=0, tiled=True),
            lax.psum_scatter(local[14], ("dp", "seq"), scatter_dimension=0, tiled=True),
        )
        grad_shards = tuple((before + after for before, after in zip(grad_shards, summed)))
    return (jnp.stack(outputs), jnp.stack(grad_inputs), jnp.stack(grad_encoders)) + tuple(
        grad_shards
    )


TILE = 256
GROUP = 8
LANES = 128
AHEAD = 2
F32 = jnp.float32
BF16 = jnp.bfloat16


def contract(left, right, left_dim, right_dim):
    return lax.dot_general(
        left, right, (((left_dim,), (right_dim,)), ((), ())), preferred_element_type=F32
    )


def head_mask(head):
    lane = lax.broadcasted_iota(jnp.int32, (1, LANES), 1)
    keep = (lane < HEAD_DIM) if head % 2 == 0 else (lane >= HEAD_DIM)
    return keep.astype(F32).astype(BF16)


def bias_table(line):
    first = jnp.concatenate(
        [line if j == 0 else pltpu.roll(line, j, 1) for j in range(8)], axis=0
    )
    return [first if r == 0 else pltpu.roll(first, 8 * r, 1) for r in range(TILE // 8)]


def line_of(table):
    total = None
    for r in range(TILE // 8):
        part = table[8 * r : 8 * r + 8, :]
        part = part if r == 0 else pltpu.roll(part, TILE - 8 * r, 1)
        total = part if total is None else total + part
    line = total[0:1, :]
    for j in range(1, 8):
        line = line + pltpu.roll(total[j : j + 1, :], TILE - j, 1)
    return line


def positions():
    return (
        lax.broadcasted_iota(jnp.int32, (TILE, TILE), 0),
        lax.broadcasted_iota(jnp.int32, (TILE, TILE), 1),
    )


def pair_lanes(head):
    return slice((head // 2) * LANES, (head // 2 + 1) * LANES)


def head_rows(head):
    return slice(head * HEAD_DIM, (head + 1) * HEAD_DIM)


def place_tiles(causal, meta_ref, own, par):
    moves = []
    count = own.shape[0] // TILE
    for ref, base in ((own, 0), (par, count)):
        for s in range(count):
            target = meta_ref[base + s] + 1 if causal else base + s
            moves.append((ref, s, target))
    return moves


def rows_at(tile):
    return pl.ds(pl.multiple_of(tile * TILE, TILE), TILE)


def fill_tables(line_ref, tab, adj):
    for h in range(GROUP):
        line = line_ref[h]
        far = line[:, TILE - 1 : TILE]
        for r, rows in enumerate(bias_table(line - far)):
            adj[h, 8 * r : 8 * r + 8, :] = rows
        k_pos, q_pos = positions()
        table = adj[h]
        tab[h] = jnp.where(k_pos <= q_pos, table, NEG)
        adj[h] = jnp.where(k_pos > q_pos, table, 0.0)


BIAS_LANE, EMPTY_LANE = 16, 17


def lane_of():
    return lax.broadcasted_iota(jnp.int32, (1, LANES), 1) % HEAD_DIM


def by_parity(lanes):
    even = (jnp.arange(LANES) < HEAD_DIM)[None, :]
    zero = jnp.zeros_like(lanes)
    return jnp.stack([jnp.where(even, zero, lanes), jnp.where(even, lanes, zero)])


def key_lanes(codes):
    lane = jnp.arange(LANES, dtype=jnp.int32)[None, :] % HEAD_DIM
    documents = (codes[:, None] == lane) & (lane < BIAS_LANE)
    ones = (lane >= BIAS_LANE) & (lane < EMPTY_LANE)
    return by_parity((documents | ones | ((lane == EMPTY_LANE) & (codes[:, None] < 0))).astype(BF16))


def query_lanes(codes):
    lane = jnp.arange(LANES, dtype=jnp.int32)[None, :] % HEAD_DIM
    other = ((codes[:, None] != lane) & (lane < BIAS_LANE)) | (lane == EMPTY_LANE)
    return by_parity(jnp.where(other, NEG, 0.0).astype(BF16))


def with_lanes(head, rows, lanes):
    return rows * head_mask(head) + lanes


def far_lane(head, line_ref):
    lane = lax.broadcasted_iota(jnp.int32, (1, LANES), 1)
    at = BIAS_LANE + (HEAD_DIM if head % 2 == 0 else 0)
    return jnp.where(lane == at, line_ref[head][:, TILE - 1 : TILE], 0.0).astype(BF16)


def query_with_lanes(causal, h, q_ref, qext_ref, line_ref):
    rows = with_lanes(h, q_ref[:, pair_lanes(h)], qext_ref[h % 2])
    return rows + far_lane(h, line_ref) if causal else rows


def visit_pairs(causal, meta_ref, region):
    if not causal:
        region(0, False)
        return
    i = pl.program_id(1)
    own = meta_ref[i]
    region(own, True)
    lax.fori_loop(0, meta_ref[8 + i], lambda j, c: (region(own - 2 * (j + 1), False), c)[1], 0)


def biased(scores, causal, near, j, h, tab, adj):
    if causal and near:
        return scores + (tab[h] if j else adj[h])
    return scores


def attend_kernel(causal, meta_ref, q_ref, ko, vo, kp, vp, qext_ref, kext_ref, line_ref,
                  o_ref, lse_ref, kb, vt, qx, tab, adj, m_s, l_s, acc):
    @pl.when(pl.program_id(1) == 0)
    def _():
        for ref, s, target in place_tiles(causal, meta_ref, ko, kp):
            for h in range(GROUP):
                kb[h, rows_at(target), :] = with_lanes(
                    h, ref[s * TILE : (s + 1) * TILE, pair_lanes(h)], kext_ref[h % 2, rows_at(target), :]
                )
        for ref, s, target in place_tiles(causal, meta_ref, vo, vp):
            vt[target] = ref[s * TILE : (s + 1) * TILE, :].T
        if causal:
            for h in range(GROUP):
                kb[h, 0:TILE, :] = kext_ref[h % 2, 0:TILE, :]
            vt[0] = jnp.zeros(vt.shape[1:], BF16)
            fill_tables(line_ref, tab, adj)

    for h in range(GROUP):
        qx[h] = query_with_lanes(causal, h, q_ref, qext_ref, line_ref)
    m_s[...] = jnp.full(m_s.shape, NEG, F32)
    l_s[...] = jnp.zeros(l_s.shape, F32)
    acc[...] = jnp.zeros(acc.shape, F32)

    def region(tile, near):
        def scores_of_head(h):
            return [contract(kb[h, rows_at(tile + j), :], qx[h], 1, 1) for j in range(2)]

        ready = [scores_of_head(h) for h in range(AHEAD)]
        for h in range(GROUP):
            if h + AHEAD < GROUP:
                ready.append(scores_of_head(h + AHEAD))
            scores = [biased(ready[h][j], causal, near, j, h, tab, adj) for j in range(2)]
            before = m_s[h : h + 1, :]
            largest = jnp.maximum(
                before, jnp.max(jnp.maximum(scores[0], scores[1]), axis=0, keepdims=True)
            )
            raised = [jnp.exp(piece - largest) for piece in scores]
            scale = jnp.exp(before - largest)
            m_s[h : h + 1, :] = largest
            l_s[h : h + 1, :] = l_s[h : h + 1, :] * scale + jnp.sum(
                raised[0] + raised[1], axis=0, keepdims=True
            )
            rows = head_rows(h)
            mixed = contract(vt[tile, rows, :], raised[0].astype(BF16), 1, 0) + contract(
                vt[tile + 1, rows, :], raised[1].astype(BF16), 1, 0
            )
            acc[rows, :] = acc[rows, :] * scale + mixed

    visit_pairs(causal, meta_ref, region)
    for h in range(GROUP):
        rows = head_rows(h)
        acc[rows, :] = acc[rows, :] / l_s[h : h + 1, :]
        lse_ref[0, h : h + 1, :] = m_s[h : h + 1, :] + jnp.log(l_s[h : h + 1, :])
    o_ref[...] = acc[...].T.astype(BF16)


def attend_back_kernel(causal, meta_ref, q_ref, ko, vo, kp, vp, qext_ref, kext_ref, line_ref,
                       do_ref, o_ref, lse_ref, dq_ref, own_ref, par_ref, gline_ref, gall_ref,
                       kb, vb, kt, qm, dm, qx, d_s, tab, adj, dq_acc, dk_acc, dv_acc, gt, gall):
    i = pl.program_id(1)

    @pl.when(i == 0)
    def _():
        for ref, s, target in place_tiles(causal, meta_ref, ko, kp):
            for h in range(GROUP):
                kb[h, rows_at(target), :] = with_lanes(
                    h, ref[s * TILE : (s + 1) * TILE, pair_lanes(h)], kext_ref[h % 2, rows_at(target), :]
                )
        for ref, s, target in place_tiles(causal, meta_ref, vo, vp):
            vb[rows_at(target), :] = ref[s * TILE : (s + 1) * TILE, :]
        for ref, s, target in place_tiles(causal, meta_ref, ko, kp):
            turned = ref[s * TILE : (s + 1) * TILE, :].T
            for h in range(GROUP):
                kt[target, h, 0:HEAD_DIM, :] = turned[head_rows(h), :]
        dk_acc[...] = jnp.zeros(dk_acc.shape, F32)
        dv_acc[...] = jnp.zeros(dv_acc.shape, F32)
        if causal:
            for h in range(GROUP):
                kb[h, 0:TILE, :] = kext_ref[h % 2, 0:TILE, :]
            vb[0:TILE, :] = jnp.zeros((TILE, vb.shape[1]), BF16)
            kt[0] = jnp.zeros(kt.shape[1:], BF16)
            for t in range(kt.shape[0]):
                for h in range(GROUP):
                    kt[t, h, HEAD_DIM:, :] = jnp.ones((kt.shape[2] - HEAD_DIM, TILE), BF16)
            gt[...] = jnp.zeros(gt.shape, F32)
            gall[...] = jnp.zeros(gall.shape, F32)
            fill_tables(line_ref, tab, adj)

    for h in range(GROUP):
        lanes = pair_lanes(h)
        pair, rows = h // 2, slice((h % 2) * TILE, (h % 2 + 1) * TILE)
        qm[pair, rows, :] = q_ref[:, lanes] * head_mask(h)
        dm[pair, rows, :] = do_ref[:, lanes] * head_mask(h)
        qx[h] = query_with_lanes(causal, h, q_ref, qext_ref, line_ref)
    both = jnp.concatenate([head_mask(0)] * 8 + [head_mask(1)] * 8, axis=0)
    for pair in range(GROUP // 2):
        lanes = pair_lanes(2 * pair)
        product = do_ref[:, lanes].astype(F32) * o_ref[:, lanes].astype(F32)
        high = product.astype(BF16)
        low = (product - high.astype(F32)).astype(BF16)
        inner = contract(both, high, 1, 1) + contract(both, low, 1, 1)
        d_s[2 * pair : 2 * pair + 1, :] = inner[0:1, :]
        d_s[2 * pair + 1 : 2 * pair + 2, :] = inner[8:9, :]
    dq_acc[...] = jnp.zeros(dq_acc.shape, F32)

    def region(tile, near):
        def products_of_head(h):
            half = slice((h % 2) * TILE, (h % 2 + 1) * TILE)
            return [
                (
                    contract(kb[h, rows_at(tile + j), :], qx[h], 1, 1),
                    contract(vb[rows_at(tile + j), pair_lanes(h)], dm[h // 2, half, :], 1, 1),
                )
                for j in range(2)
            ]

        ready = [products_of_head(h) for h in range(AHEAD)]
        probs_low, grads_low = {}, {}
        for h in range(GROUP):
            if h + AHEAD < GROUP:
                ready.append(products_of_head(h + AHEAD))
            back = None
            for j in range(2):
                scores, grad_probs = ready[h][j]
                probs = jnp.exp(biased(scores, causal, near, j, h, tab, adj) - lse_ref[0, h : h + 1, :])
                grads = probs * (grad_probs - d_s[h : h + 1, :])
                low = grads.astype(BF16)
                probs_low[h, j], grads_low[h, j] = probs.astype(BF16), low
                if causal and near:
                    rounded = low.astype(F32)
                    if j == 0:
                        k_pos, q_pos = positions()
                        rounded = jnp.where(k_pos > q_pos, rounded, 0.0)
                    gt[h] += rounded
                part = contract(kt[tile + j, h], low, 1, 0)
                back = part if back is None else back + part
            dq_acc[head_rows(h), :] += back[0:HEAD_DIM, :]
            if causal:
                gall[h : h + 1, :] += back[HEAD_DIM : HEAD_DIM + 1, :]
            if h % 2 == 1:
                pair = h // 2
                lanes = pair_lanes(h)
                for j in range(2):
                    dv_acc[rows_at(tile + j), lanes] += contract(
                        jnp.concatenate([probs_low[h - 1, j], probs_low[h, j]], axis=1), dm[pair], 1, 0
                    )
                    dk_acc[rows_at(tile + j), lanes] += contract(
                        jnp.concatenate([grads_low[h - 1, j], grads_low[h, j]], axis=1), qm[pair], 1, 0
                    )

    visit_pairs(causal, meta_ref, region)
    dq_ref[...] = dq_acc[...].T.astype(BF16)

    @pl.when(i == pl.num_programs(1) - 1)
    def _():
        for j, total in enumerate((dk_acc, dv_acc)):
            for ref, s, target in place_tiles(causal, meta_ref, own_ref.at[j], par_ref.at[j]):
                ref[s * TILE : (s + 1) * TILE, :] = total[rows_at(target), :].astype(BF16)
        for h in range(GROUP):
            if causal:
                gline_ref[h] = line_of(gt[h])
                gall_ref[h] = gall[h : h + 1, :]
            else:
                gline_ref[h] = jnp.zeros((1, TILE), F32)
                gall_ref[h] = jnp.zeros((1, TILE), F32)


VMEM_LIMIT = 60 * 1024 * 1024


def attention_specs(own_rows, par_rows, keys):
    groups = HEADS // GROUP
    lanes = GROUP * HEAD_DIM
    return [
        pl.BlockSpec((TILE, lanes), lambda g, i, meta: (i, g)),
        pl.BlockSpec((own_rows, lanes), lambda g, i, meta: (0, g)),
        pl.BlockSpec((own_rows, lanes), lambda g, i, meta: (0, groups + g)),
        pl.BlockSpec((par_rows, lanes), lambda g, i, meta: (0, g)),
        pl.BlockSpec((par_rows, lanes), lambda g, i, meta: (0, groups + g)),
        pl.BlockSpec((2, TILE, LANES), lambda g, i, meta: (0, i, 0)),
        pl.BlockSpec((2, keys, LANES), lambda g, i, meta: (0, 0, 0)),
        pl.BlockSpec((GROUP, 1, TILE), lambda g, i, meta: (g, 0, 0)),
    ]


def attend_fast(meta, query, kv_own, kv_par, qext, kext, line, causal):
    tokens, width = query.shape
    own_rows, par_rows, keys = kv_own.shape[0], kv_par.shape[0], kext.shape[1]
    groups, lanes = HEADS // GROUP, GROUP * HEAD_DIM
    table = (GROUP, TILE, TILE) if causal else (1, 8, LANES)
    return pl.pallas_call(
        functools.partial(attend_kernel, causal),
        grid_spec=pltpu.PrefetchScalarGridSpec(
            num_scalar_prefetch=1,
            grid=(groups, tokens // TILE),
            in_specs=attention_specs(own_rows, par_rows, keys),
            out_specs=[
                pl.BlockSpec((TILE, lanes), lambda g, i, meta: (i, g)),
                pl.BlockSpec((1, GROUP, TILE), lambda g, i, meta: (g, 0, i)),
            ],
            scratch_shapes=[
                pltpu.VMEM((GROUP, keys, LANES), BF16),
                pltpu.VMEM((keys // TILE, lanes, TILE), BF16),
                pltpu.VMEM((GROUP, TILE, LANES), BF16),
                pltpu.VMEM(table, F32),
                pltpu.VMEM(table, F32),
                pltpu.VMEM((8, TILE), F32),
                pltpu.VMEM((8, TILE), F32),
                pltpu.VMEM((lanes, TILE), F32),
            ],
        ),
        out_shape=[
            jax.ShapeDtypeStruct((tokens, width), BF16),
            jax.ShapeDtypeStruct((groups, GROUP, tokens), F32),
        ],
        compiler_params=pltpu.CompilerParams(vmem_limit_bytes=VMEM_LIMIT),
        cost_estimate=pl.CostEstimate(
            flops=tokens * keys * width * 4, bytes_accessed=4 * (tokens + keys) * width,
            transcendentals=tokens * keys * HEADS // 2,
        ),
        name="attend_self" if causal else "attend_cross",
    )(meta, query, kv_own, kv_own, kv_par, kv_par, qext, kext, line)


def attend_back_fast(meta, query, kv_own, kv_par, qext, kext, line, grad_mixed, mixed, lse, causal):
    tokens, width = query.shape
    own_rows, par_rows, keys = kv_own.shape[0], kv_par.shape[0], kext.shape[1]
    groups, lanes = HEADS // GROUP, GROUP * HEAD_DIM
    table = (GROUP, TILE, TILE) if causal else (1, 8, LANES)
    block = pl.BlockSpec((TILE, lanes), lambda g, i, meta: (i, g))
    line_spec = pl.BlockSpec((GROUP, 1, TILE), lambda g, i, meta: (g, 0, 0))
    return pl.pallas_call(
        functools.partial(attend_back_kernel, causal),
        grid_spec=pltpu.PrefetchScalarGridSpec(
            num_scalar_prefetch=1,
            grid=(groups, tokens // TILE),
            in_specs=attention_specs(own_rows, par_rows, keys)
            + [block, block, pl.BlockSpec((1, GROUP, TILE), lambda g, i, meta: (g, 0, i))],
            out_specs=[
                block,
                pl.BlockSpec((2, own_rows, lanes), lambda g, i, meta: (0, 0, g)),
                pl.BlockSpec((2, par_rows, lanes), lambda g, i, meta: (0, 0, g)),
                line_spec,
                line_spec,
            ],
            scratch_shapes=[
                pltpu.VMEM((GROUP, keys, LANES), BF16),
                pltpu.VMEM((keys, lanes), BF16),
                pltpu.VMEM((keys // TILE, GROUP, HEAD_DIM + (16 if causal else 0), TILE), BF16),
                pltpu.VMEM((GROUP // 2, 2 * TILE, LANES), BF16),
                pltpu.VMEM((GROUP // 2, 2 * TILE, LANES), BF16),
                pltpu.VMEM((GROUP, TILE, LANES), BF16),
                pltpu.VMEM((8, TILE), F32),
                pltpu.VMEM(table, F32),
                pltpu.VMEM(table, F32),
                pltpu.VMEM((lanes, TILE), F32),
                pltpu.VMEM((keys, lanes), F32),
                pltpu.VMEM((keys, lanes), F32),
                pltpu.VMEM(table, F32),
                pltpu.VMEM((8, TILE), F32),
            ],
        ),
        out_shape=[
            jax.ShapeDtypeStruct((tokens, width), BF16),
            jax.ShapeDtypeStruct((2, own_rows, width), BF16),
            jax.ShapeDtypeStruct((2, par_rows, width), BF16),
            jax.ShapeDtypeStruct((HEADS, 1, TILE), F32),
            jax.ShapeDtypeStruct((HEADS, 1, TILE), F32),
        ],
        compiler_params=pltpu.CompilerParams(vmem_limit_bytes=VMEM_LIMIT),
        cost_estimate=pl.CostEstimate(
            flops=tokens * keys * width * 10, bytes_accessed=10 * (tokens + keys) * width,
            transcendentals=tokens * keys * HEADS // 2,
        ),
        name="attend_self_back" if causal else "attend_cross_back",
    )(meta, query, kv_own, kv_own, kv_par, kv_par, qext, kext, line, grad_mixed, mixed, lse)


AXES = ("dp", "seq")


def exchange(value, dp_bit, seq_bit):
    pairs = [
        (dp * 4 + seq, (dp ^ dp_bit) * 4 + (seq ^ seq_bit)) for dp in range(8) for seq in range(4)
    ]
    return lax.ppermute(value, AXES, pairs)


CORE, Z_LOW, Z_HIGH, X, Y = (1, 0), (2, 0), (4, 0), (0, 1), (0, 2)


def move_pairs(a, b):
    pairs = []
    for z in range(4):
        for core in range(2):
            for s in range(4):
                micro, half_core = (s >> 1) ^ a, (s & 1) ^ b
                pairs.append(((2 * z + core) * 4 + s, (2 * z + half_core) * 4 + 2 * core + micro))
    return pairs


ROUNDS = ((0, 0), (0, 1), (1, 0), (1, 1))


def take(value, index, axis):
    return lax.dynamic_index_in_dim(value, index, axis, keepdims=False)


MESH = pl.DeviceIdType.MESH


class Links:
    def __init__(self):
        dp, seq = lax.axis_index("dp"), lax.axis_index("seq")
        self.seq = seq
        self.z, self.core, self.y, self.x = dp // 2, dp % 2, seq // 2, seq % 2
        self.at_z = [{"dp": ((self.z + k) % 4) * 2 + self.core, "seq": seq} for k in (1, 2, 3)]
        self.at_x = {"dp": dp, "seq": seq + 1 - 2 * self.x}
        self.at_y = {"dp": dp, "seq": seq + 2 - 4 * self.y}
        self.at_core = {"dp": dp + 1 - 2 * self.core, "seq": seq}

    def at_plane(self, core, seq):
        return {"dp": 2 * self.z + core, "seq": seq}

    def greet(self):
        partners = list(self.at_z)
        for flip in (0, 1):
            for k in range(4):
                if flip or k:
                    core = 1 - self.core if flip else self.core
                    partners.append(self.at_plane(core, (self.seq + k) % 4))
        barrier = pltpu.get_barrier_semaphore()
        for partner in partners:
            pl.semaphore_signal(barrier, inc=1, device_id=partner, device_id_type=MESH)
        pl.semaphore_wait(barrier, len(partners))


def remote(source, target, send_sem, recv_sem, device):
    return pltpu.make_async_remote_copy(
        src_ref=source,
        dst_ref=target,
        send_sem=send_sem,
        recv_sem=recv_sem,
        device_id=device,
        device_id_type=MESH,
    )


def move_tokens(links, sources, targets, parts, local_sem, send_sem, recv_sem):
    waits = []
    for r, (a, b) in enumerate(ROUNDS):
        micro = 1 - links.y if a else links.y
        core = 1 - links.x if b else links.x
        chip = 2 * links.core + micro
        stays = (core == links.core) & (chip == links.seq)
        for n, (source, target, part) in enumerate(zip(sources, targets, parts)):
            if part is None:
                piece = source.at[micro]
            else:
                piece = source.at[micro, 0, pl.ds(b * part, part)]
            slot = target.at[links.seq]
            here = pltpu.make_async_copy(piece, slot, local_sem.at[r, n])
            away = remote(piece, slot, send_sem.at[r, n], recv_sem.at[r, n], links.at_plane(core, chip))

            @pl.when(stays)
            def _(here=here):
                here.start()

            @pl.when(jnp.logical_not(stays))
            def _(away=away):
                away.start()

            waits.append((stays, here, away))

    def finish():
        for stays, here, away in waits:
            @pl.when(stays)
            def _(here=here):
                here.wait()

            @pl.when(jnp.logical_not(stays))
            def _(away=away):
                away.wait()

    return finish


def gather_kernel(count, parts, *refs):
    tokens = len(parts)
    shards, moved = refs[:count], refs[count : count + tokens]
    refs = refs[count + tokens :]
    wholes, settled = refs[:count], refs[count : count + tokens]
    local_sem, send_sem, recv_sem, move_local, move_send, move_recv = refs[count + tokens :]
    links = Links()
    z, core, y, x = links.z, links.core, links.y, links.x
    links.greet()
    finish = move_tokens(links, moved, settled, parts, move_local, move_send, move_recv)

    def send(w, slot, source, target, device):
        copy = remote(source, target, send_sem.at[w, slot], recv_sem.at[w, slot], device)
        copy.start()
        return copy

    locals_, rounds = [], [[], [], [], []]
    for w in range(count):
        own = wholes[w].at[z, core, y, x]
        copy = pltpu.make_async_copy(shards[w], own, local_sem.at[w])
        copy.start()
        locals_.append(copy)
        rounds[0].append([send(w, k, shards[w], own, links.at_z[k]) for k in range(3)])
    for t in range(count + 2):
        if t < count:
            w, half = t, wholes[t].shape[-1] // 2
            left, right = pl.ds(0, half), pl.ds(half, half)
            locals_[w].wait()
            for copy in rounds[0][w]:
                copy.wait_recv()
            one = wholes[w].at[:, core, y, x, :, left]
            two = wholes[w].at[:, core, y, x, :, right]
            rounds[1].append([send(w, 3, one, one, links.at_x), send(w, 4, two, two, links.at_y)])
        if 0 <= t - 1 < count:
            w, half = t - 1, wholes[t - 1].shape[-1] // 2
            left, right = pl.ds(0, half), pl.ds(half, half)
            for copy in rounds[1][w]:
                copy.wait_recv()
            one = wholes[w].at[:, core, y, :, :, left]
            two = wholes[w].at[:, core, :, x, :, right]
            rounds[2].append([send(w, 5, one, one, links.at_y), send(w, 6, two, two, links.at_x)])
        if 0 <= t - 2 < count:
            w = t - 2
            for copy in rounds[2][w]:
                copy.wait_recv()
            both = wholes[w].at[:, core]
            rounds[3].append([send(w, 7, both, both, links.at_core)])
    for w in range(count):
        for copy in rounds[3][w]:
            copy.wait_recv()
        for stage in rounds:
            for copy in stage[w]:
                copy.wait_send()
    finish()


def gather_weights(shards, moved):
    count = len(shards)
    sent = sum(shard.size for shard in shards) * 2
    parts = [None if value.ndim == 3 else value.shape[2] // 2 for value in moved]
    settled = [
        jax.ShapeDtypeStruct((4, value.shape[1] if part is None else part, value.shape[-1]), BF16)
        for value, part in zip(moved, parts)
    ]
    outs = pl.pallas_call(
        functools.partial(gather_kernel, count, parts),
        in_specs=[pl.BlockSpec(memory_space=pltpu.VMEM)] * count
        + [pl.BlockSpec(memory_space=pl.ANY)] * len(moved),
        out_specs=[pl.BlockSpec(memory_space=pl.ANY)] * (count + len(moved)),
        out_shape=[jax.ShapeDtypeStruct((4, 2, 2, 2, *shard.shape), BF16) for shard in shards] + settled,
        scratch_shapes=[
            pltpu.SemaphoreType.DMA((count,)),
            pltpu.SemaphoreType.DMA((count, 8)),
            pltpu.SemaphoreType.DMA((count, 8)),
            pltpu.SemaphoreType.DMA((4, len(moved))),
            pltpu.SemaphoreType.DMA((4, len(moved))),
            pltpu.SemaphoreType.DMA((4, len(moved))),
        ],
        compiler_params=pltpu.CompilerParams(
            vmem_limit_bytes=VMEM_LIMIT, collective_id=0, has_side_effects=True
        ),
        cost_estimate=pl.CostEstimate(flops=0, transcendentals=0, bytes_accessed=500 * sent),
        name="gather_weights",
    )(*shards, *moved)
    return [whole.reshape(-1, whole.shape[-1]) for whole in outs[:count]], outs[count:]


def add_low(first, second):
    return (first.astype(F32) + second.astype(F32)).astype(BF16)


def return_tokens_kernel(links, source, target, part, local_sem, send_sem, recv_sem):
    waits = []
    mine = 2 * (links.seq % 2) + links.core
    for s in range(4):
        half = (links.core + s) % 2
        slot = target.at[links.seq % 2, pl.ds(pl.multiple_of(half * part, part), part)]
        stays = (links.y == links.core) & (links.seq == s)
        here = pltpu.make_async_copy(source.at[s], slot, local_sem)
        away = remote(source.at[s], slot, send_sem.at[s], recv_sem.at[mine], links.at_plane(links.y, s))

        @pl.when(stays)
        def _(here=here):
            here.start()

        @pl.when(jnp.logical_not(stays))
        def _(away=away):
            away.start()

        waits.append((stays, here, away))

    def finish():
        for stays, here, away in waits:
            @pl.when(stays)
            def _(here=here):
                here.wait()

            @pl.when(jnp.logical_not(stays))
            def _(away=away):
                away.wait_send()

        for j in range(4):
            arrived = remote(
                source.at[0], target.at[0, pl.ds(0, part)], send_sem.at[0], recv_sem.at[j],
                links.at_core,
            )

            @pl.when(jnp.logical_not((links.y == links.core) & (mine == j)))
            def _(arrived=arrived):
                arrived.wait_recv()

    return finish


def scatter_kernel(shapes, part, *refs):
    count = len(shapes)
    grads, tokens, sums, returned = refs[:count], refs[count], refs[count + 1 : 2 * count + 1], refs[2 * count + 1]
    scratch = refs[2 * count + 2 :]
    kept, got_one, got_two, got_z = (scratch[j * count : (j + 1) * count] for j in range(4))
    own, totals = scratch[4 * count : 5 * count], scratch[5 * count : 6 * count]
    load_sem, store_sem, send_sem, recv_sem, back_local, back_send, back_recv = scratch[6 * count :]
    links = Links()
    z, core, y, x = links.z, links.core, links.y, links.x
    at_z, at_x, at_y, at_core = links.at_z, links.at_x, links.at_y, links.at_core
    links.greet()
    finish = return_tokens_kernel(links, tokens, returned, part, back_local, back_send, back_recv)

    def send(w, slot, source, target, device):
        copy = remote(source, target, send_sem.at[w, slot], recv_sem.at[w, slot], device)
        copy.start()
        return copy

    def halves(w):
        half = shapes[w][1] // 2
        return pl.ds(0, half), pl.ds(half, half)

    def add(first, second, dtype):
        return (first.astype(F32) + second.astype(F32)).astype(dtype)

    stages, loads, stores = [[] for _ in range(4)], [], []
    for w in range(count):
        stages[0].append([send(w, 0, grads[w].at[:, 1 - core], kept[w], at_core)])
        load = pltpu.make_async_copy(grads[w].at[:, core], own[w], load_sem.at[w])
        load.start()
        loads.append(load)
    for t in range(count + 3):
        if t < count:
            w, dtype = t, kept[t].dtype
            left, right = halves(w)
            loads[w].wait()
            stages[0][w][0].wait_recv()

            def core_step(b, carry, w=w, dtype=dtype):
                zz, yy, xx = b // 4, (b // 2) % 2, b % 2
                kept[w][zz, yy, xx] = add(kept[w][zz, yy, xx], own[w][zz, yy, xx], dtype)
                return carry

            lax.fori_loop(0, 16, core_step, 0)
            half = shapes[w][1] // 2
            stages[1].append([
                send(w, 1, kept[w].at[:, :, 1 - x, :, left], got_one[w].at[0], at_x),
                send(w, 2, kept[w].at[:, 1 - y, :, :, right], got_one[w].at[1], at_y),
            ])
        if 0 <= t - 1 < count:
            w, dtype = t - 1, kept[t - 1].dtype
            left, right = halves(w)
            half = shapes[w][1] // 2
            for copy in stages[1][w]:
                copy.wait_recv()

            def one_step(b, carry, w=w, dtype=dtype, half=half):
                zz, other = b // 2, b % 2
                kept[w][zz, other, x, :, 0:half] = add(
                    kept[w][zz, other, x, :, 0:half], got_one[w][0, zz, other], dtype
                )
                kept[w][zz, y, other, :, half : 2 * half] = add(
                    kept[w][zz, y, other, :, half : 2 * half], got_one[w][1, zz, other], dtype
                )
                return carry

            lax.fori_loop(0, 8, one_step, 0)
            stages[2].append([
                send(w, 3, kept[w].at[:, 1 - y, x, :, left], got_two[w].at[0], at_y),
                send(w, 4, kept[w].at[:, y, 1 - x, :, right], got_two[w].at[1], at_x),
            ])
        if 0 <= t - 2 < count:
            w, dtype = t - 2, kept[t - 2].dtype
            half = shapes[w][1] // 2
            for copy in stages[2][w]:
                copy.wait_recv()

            def two_step(zz, carry, w=w, dtype=dtype, half=half):
                kept[w][zz, y, x, :, 0:half] = add(
                    kept[w][zz, y, x, :, 0:half], got_two[w][0, zz], dtype
                )
                kept[w][zz, y, x, :, half : 2 * half] = add(
                    kept[w][zz, y, x, :, half : 2 * half], got_two[w][1, zz], dtype
                )
                return carry

            lax.fori_loop(0, 4, two_step, 0)
            stages[3].append([
                send(w, 5 + k, kept[w].at[(z + k + 1) % 4, y, x], got_z[w].at[k], at_z[k])
                for k in range(3)
            ])
        if 0 <= t - 3 < count:
            w = t - 3
            for copy in stages[3][w]:
                copy.wait_recv()
            total = kept[w][z, y, x].astype(F32)
            for k in range(3):
                total = total + got_z[w][k].astype(F32)
            totals[w][...] = total
            store = pltpu.make_async_copy(totals[w], sums[w], store_sem.at[w])
            store.start()
            stores.append(store)
    for w in range(count):
        stores[w].wait()
        for stage in stages:
            for copy in stage[w]:
                copy.wait_send()
    finish()


def scatter_grads(grads, tokens):
    part = tokens.shape[1]
    count = len(grads)
    shapes = [(grad.shape[0] // 32, grad.shape[1]) for grad in grads]
    types = [grad.dtype for grad in grads]

    def buffers(*lead, halved=False):
        return [
            pltpu.VMEM((*lead, rows, width // 2 if halved else width), kind)
            for (rows, width), kind in zip(shapes, types)
        ]

    return pl.pallas_call(
        functools.partial(scatter_kernel, shapes, part),
        in_specs=[pl.BlockSpec(memory_space=pl.ANY)] * (count + 1),
        out_specs=[pl.BlockSpec(memory_space=pl.ANY)] * (count + 1),
        out_shape=[jax.ShapeDtypeStruct(shape, F32) for shape in shapes]
        + [jax.ShapeDtypeStruct((2, 2 * part, tokens.shape[2]), BF16)],
        scratch_shapes=buffers(4, 2, 2)
        + buffers(2, 4, 2, halved=True)
        + buffers(2, 4, halved=True)
        + buffers(3)
        + buffers(4, 2, 2)
        + [pltpu.VMEM(shape, F32) for shape in shapes]
        + [
            pltpu.SemaphoreType.DMA((count,)),
            pltpu.SemaphoreType.DMA((count,)),
            pltpu.SemaphoreType.DMA((count, 8)),
            pltpu.SemaphoreType.DMA((count, 8)),
            pltpu.SemaphoreType.DMA,
            pltpu.SemaphoreType.DMA((4,)),
            pltpu.SemaphoreType.DMA((4,)),
        ],
        compiler_params=pltpu.CompilerParams(
            vmem_limit_bytes=67043328, collective_id=1, has_side_effects=True
        ),
        cost_estimate=pl.CostEstimate(
            flops=0, transcendentals=0, bytes_accessed=16 * sum(grad.size for grad in grads)
        ),
        name="scatter_grads",
    )(*[
        grad.reshape(4, 2, 2, 2, rows, width) for grad, (rows, width) in zip(grads, shapes)
    ], tokens)


def norm_scale(value):
    return lax.rsqrt(jnp.mean(value * value, axis=-1, keepdims=True) + EPS)


def normed(value, gain):
    return (value * norm_scale(value) * gain).astype(BF16)


def norm_back(value, gain, grad):
    scale = norm_scale(value)
    scaled = grad * gain
    inner = jnp.mean(scaled * value, axis=-1, keepdims=True)
    return (
        scale * scaled - (scale * scale * scale) * value * inner,
        jnp.sum(grad * value * scale, axis=0),
    )


def dot(rows, weight):
    return jnp.dot(rows, weight, preferred_element_type=F32)


def dot_back(grads, weight):
    return contract(grads, weight, 1, 1)


def dot_weight(rows, grads):
    return contract(rows, grads, 0, 0).astype(BF16)


def fast_body(
    hidden_in,
    encoder_states,
    segments,
    enc_segments,
    grad_out,
    norm_self,
    q_self,
    k_self,
    v_self,
    o_self,
    rel_bias,
    norm_cross,
    q_cross,
    k_cross,
    v_cross,
    o_cross,
    norm_ff,
    wi_gate,
    wi_up,
    wo_ff,
):
    dp, seq = lax.axis_index("dp"), lax.axis_index("seq")
    core, z_low, z_high, y, x = dp % 2, (dp // 2) % 2, dp // 4, seq // 2, seq % 2
    place = (core, z_low, z_high, y, x)
    rows_dev, width = hidden_in.shape[2], hidden_in.shape[3]
    enc_dev = encoder_states.shape[2]
    part, enc_part = rows_dev // 2, enc_dev // 2
    owned_micro = seq % 2

    def send_tokens(pieces_of):
        return [
            lax.ppermute(pieces_of((seq // 2) ^ a, b), AXES, move_pairs(a, b)) for a, b in ROUNDS
        ]

    def settle(received):
        slots = []
        for s in range(4):
            index = 2 * ((s >> 1) ^ owned_micro) + ((s & 1) ^ core)
            slots.append(lax.select_n(index, *received))
        return jnp.stack(slots)

    def return_tokens(value):
        received = []
        for a, b in ROUNDS:
            index = 2 * (owned_micro ^ a) + (core ^ b)
            back = [(target, source) for source, target in move_pairs(a, b)]
            received.append(lax.ppermute(take(value, index, 0), AXES, back))
        flag = seq // 2
        micro = []
        for m in range(2):
            micro.append(
                jnp.concatenate(
                    [jnp.where((flag ^ m) == 0, received[b], received[2 + b]) for b in range(2)],
                    axis=0,
                )
            )
        return jnp.stack(micro)[:, None]

    codes = jnp.concatenate([segments[:, 0], enc_segments[:, 0]], axis=1).astype(BF16)
    codes = jnp.pad(codes, ((0, 0), (0, width - codes.shape[1])))
    codes = jnp.broadcast_to(codes[:, None], (2, 8, width))

    small = jnp.concatenate([norm_self, norm_cross, norm_ff, rel_bias])
    small_rows = norm_self.shape[0]
    small = jnp.broadcast_to(jnp.pad(small, (0, 2 * LANES - small.shape[0])), (8, 2 * LANES))
    wholes, (inputs_low, encoder, codes) = gather_weights(
        [small, k_self, v_self, q_self, k_cross, v_cross, o_self, q_cross, o_cross, wi_gate, wi_up, wo_ff],
        [hidden_in, encoder_states, codes],
    )
    small, wk, wv, wq, ck, cv, wo, cq, co, w_gate, w_up, w_down = wholes
    small = small.reshape(32, 8, 2 * LANES)[:, 0].astype(F32)
    gain_self, gain_cross, gain_ff = (
        small[:, j * small_rows : (j + 1) * small_rows].reshape(-1) for j in range(3)
    )
    table = small[:, 3 * small_rows : 3 * small_rows + rel_bias.shape[0]].reshape(BUCKETS, HEADS)
    ff = wi_gate.shape[1]

    inputs_low = inputs_low.reshape(4 * part, width)
    encoder = encoder.reshape(4 * enc_part, width)
    codes = codes[:, 0].astype(jnp.int32)
    seg_parts = codes[:, :rows_dev].reshape(4, 2, part)
    enc_parts = codes[:, rows_dev : rows_dev + enc_dev].reshape(4, 2, enc_part)

    def of_core(parts, which):
        return jnp.stack([take(parts[s], which ^ (s & 1), 0) for s in range(4)])

    seg_own = of_core(seg_parts, core)
    enc_own, enc_par = of_core(enc_parts, core), of_core(enc_parts, 1 - core)
    quarter = jnp.arange(4, dtype=jnp.int32)
    at_own = 2 * quarter + (core ^ (quarter % 2))
    at_par = 2 * quarter + ((1 - core) ^ (quarter % 2))
    tile_last = seg_parts.reshape(8, part)[:, -1]
    first_tile = jnp.sum((tile_last[None, :] < seg_own[:, :1]).astype(jnp.int32), axis=1)
    pairs = jnp.maximum(at_own - first_tile, 0) // 2
    meta = jnp.concatenate([at_own, at_par, pairs]).astype(jnp.int32)
    seg_keys = jnp.concatenate([jnp.full((part,), -1, jnp.int32), seg_parts.reshape(-1)])
    query_codes, key_codes = query_lanes(seg_own.reshape(-1)), key_lanes(seg_keys)
    cross_codes = key_lanes(jnp.concatenate([enc_own, enc_par]).reshape(-1))
    near = (
        buckets_of(jnp.arange(TILE, dtype=jnp.int32))[:, None] == jnp.arange(BUCKETS)[None, :]
    ).astype(F32)
    line = jnp.dot(near, table, precision=lax.Precision.HIGHEST).T.reshape(HEADS, 1, TILE)

    inputs = inputs_low.astype(F32)
    normed_self = normed(inputs, gain_self)
    kv_own = jnp.concatenate(
        [dot(normed_self, wk).astype(BF16), dot(normed_self, wv).astype(BF16)], axis=1
    )
    kv_par = exchange(kv_own, *CORE)
    query = dot(normed_self, wq).astype(BF16)
    cross_kv_own = jnp.concatenate(
        [dot(encoder, ck).astype(BF16), dot(encoder, cv).astype(BF16)], axis=1
    )
    cross_kv_par = exchange(cross_kv_own, *CORE)
    kv_par, cross_kv_par, late_grad = lax.optimization_barrier((kv_par, cross_kv_par, grad_out))
    out_parts = send_tokens(lambda micro, b: take(late_grad[:, 0, b * part : (b + 1) * part], micro, 0))
    mixed, self_lse = attend_fast(meta, query, kv_own, kv_par, query_codes, key_codes, line, True)
    after_self = inputs + dot(mixed, wo)
    normed_cross = normed(after_self, gain_cross)
    cross_query = dot(normed_cross, cq).astype(BF16)
    cross_mixed, cross_lse = attend_fast(
        meta, cross_query, cross_kv_own, cross_kv_par, query_codes, cross_codes, line, False
    )
    after_cross = after_self + dot(cross_mixed, co)
    normed_ff = normed(after_cross, gain_ff)
    gate, up_values = dot(normed_ff, w_gate), dot(normed_ff, w_up)
    hidden = gelu_mix(gate, up_values).astype(BF16)
    result = (after_cross + dot(hidden, w_down)).astype(BF16)
    block_out = return_tokens(result.reshape(4, part, width))

    out_low = settle(out_parts).reshape(4 * part, width)
    grad_result = out_low.astype(F32)
    grad_w_down = dot_weight(hidden, out_low)
    grad_hidden = dot_back(out_low, w_down)
    mix_value, mix_pull = jax.vjp(gelu_mix, gate, up_values)
    grad_gate, grad_up = (piece.astype(BF16) for piece in mix_pull(grad_hidden))
    grad_w_gate, grad_w_up = dot_weight(normed_ff, grad_gate), dot_weight(normed_ff, grad_up)
    grad_normed_ff = dot_back(grad_gate, w_gate) + dot_back(grad_up, w_up)
    ff_part, grad_gain_ff = norm_back(after_cross, gain_ff, grad_normed_ff)
    grad_after_cross = grad_result + ff_part
    cross_out_low = grad_after_cross.astype(BF16)
    grad_co = dot_weight(cross_mixed, cross_out_low)
    grad_cross_mixed = dot_back(cross_out_low, co).astype(BF16)
    grad_cross_query, cross_own, cross_par, unused, unused = attend_back_fast(
        meta, cross_query, cross_kv_own, cross_kv_par, query_codes, cross_codes, line,
        grad_cross_mixed, cross_mixed, cross_lse, False,
    )
    grad_cross_query, block_out = lax.optimization_barrier((grad_cross_query, block_out))
    cross_got = add_low(cross_own, exchange(cross_par, *CORE))
    grad_ck, grad_cv = dot_weight(encoder, cross_got[0]), dot_weight(encoder, cross_got[1])
    grad_encoder = (dot_back(cross_got[0], ck) + dot_back(cross_got[1], cv)).astype(BF16)
    grad_encoder = return_tokens(grad_encoder.reshape(4, enc_part, width)).astype(F32)
    grad_cq = dot_weight(normed_cross, grad_cross_query)
    grad_normed_cross = dot_back(grad_cross_query, cq)
    cross_part, grad_gain_cross = norm_back(after_self, gain_cross, grad_normed_cross)
    grad_after_self = grad_after_cross + cross_part
    self_out_low = grad_after_self.astype(BF16)
    grad_wo = dot_weight(mixed, self_out_low)
    grad_mixed = dot_back(self_out_low, wo).astype(BF16)
    grad_query, self_own, self_par, grad_line, grad_all = attend_back_fast(
        meta, query, kv_own, kv_par, query_codes, key_codes, line, grad_mixed, mixed, self_lse, True
    )
    grad_query, grad_encoder = lax.optimization_barrier((grad_query, grad_encoder))
    self_got = add_low(self_own, exchange(self_par, *CORE))
    grad_wq = dot_weight(normed_self, grad_query)
    grad_wk, grad_wv = dot_weight(normed_self, self_got[0]), dot_weight(normed_self, self_got[1])
    grad_normed_self = (
        dot_back(grad_query, wq) + dot_back(self_got[0], wk) + dot_back(self_got[1], wv)
    )
    self_part, grad_gain_self = norm_back(inputs, gain_self, grad_normed_self)
    grad_hidden_in = (grad_after_self + self_part).astype(BF16).reshape(4, part, width)

    grad_table = jnp.dot(near.T, grad_line.reshape(HEADS, TILE).T, precision=lax.Precision.HIGHEST)
    grad_far = jnp.sum((grad_all - grad_line).reshape(HEADS, TILE), axis=1)
    grad_table = grad_table.at[BUCKETS - 1].add(grad_far)
    small_grads = [piece.reshape(32, -1) for piece in (grad_gain_self, grad_gain_cross, grad_gain_ff)]
    small_grads = jnp.concatenate(small_grads + [grad_table.reshape(32, -1)], axis=1)
    small_grads = jnp.pad(small_grads, ((0, 0), (0, 2 * LANES - small_grads.shape[1])))
    small_grads = jnp.broadcast_to(small_grads[:, None], (32, 8, 2 * LANES)).reshape(256, 2 * LANES)
    order = [
        grad_wk, grad_wv, grad_w_gate, grad_w_up, grad_w_down, grad_ck, grad_cv, grad_cq, grad_co,
        grad_wo, grad_wq, small_grads,
    ]
    (
        grad_wk, grad_wv, grad_w_gate, grad_w_up, grad_w_down, grad_ck, grad_cv, grad_cq, grad_co,
        grad_wo, grad_wq, small_grads, grad_hidden_in,
    ) = scatter_grads(order, grad_hidden_in)
    small_grads = small_grads[0]
    return (
        block_out,
        grad_hidden_in.astype(F32)[:, None],
        grad_encoder,
        small_grads[:small_rows],
        grad_wq,
        grad_wk,
        grad_wv,
        grad_wo,
        small_grads[3 * small_rows : 3 * small_rows + rel_bias.shape[0]],
        small_grads[small_rows : 2 * small_rows],
        grad_cq,
        grad_ck,
        grad_cv,
        grad_co,
        small_grads[2 * small_rows : 3 * small_rows],
        grad_w_gate,
        grad_w_up,
        grad_w_down,
    )


def fits_fast(mesh):
    return mesh.shape["dp"] == 8 and mesh.shape["seq"] == 4


def solution(mesh):
    return jax.shard_map(
        fast_body if fits_fast(mesh) else general_body,
        mesh=mesh,
        in_specs=(
            P(None, "dp", "seq", None),
            P(None, "dp", "seq", None),
            P(None, "dp", "seq"),
            P(None, "dp", "seq"),
            P(None, "dp", "seq", None),
            P(("dp", "seq")),
            P(("dp", "seq"), None),
            P(("dp", "seq"), None),
            P(("dp", "seq"), None),
            P(("dp", "seq"), None),
            P(("dp", "seq")),
            P(("dp", "seq")),
            P(("dp", "seq"), None),
            P(("dp", "seq"), None),
            P(("dp", "seq"), None),
            P(("dp", "seq"), None),
            P(("dp", "seq")),
            P(("dp", "seq"), None),
            P(("dp", "seq"), None),
            P(("dp", "seq"), None),
        ),
        out_specs=(
            P(None, "dp", "seq", None),
            P(None, "dp", "seq", None),
            P(None, "dp", "seq", None),
            P(("dp", "seq")),
            P(("dp", "seq"), None),
            P(("dp", "seq"), None),
            P(("dp", "seq"), None),
            P(("dp", "seq"), None),
            P(("dp", "seq")),
            P(("dp", "seq")),
            P(("dp", "seq"), None),
            P(("dp", "seq"), None),
            P(("dp", "seq"), None),
            P(("dp", "seq"), None),
            P(("dp", "seq")),
            P(("dp", "seq"), None),
            P(("dp", "seq"), None),
            P(("dp", "seq"), None),
        ),
        check_vma=False,
    )
```

```python
import functools
import math

import jax
import jax.numpy as jnp
from jax import lax
from jax.experimental import pallas as pl
from jax.experimental.pallas import tpu as pltpu
from jax.sharding import PartitionSpec as P

HEADS = 16
HEAD_DIM = 64
BUCKETS = 32
MAX_DIST = 128


EPS = 1e-06
NEG = -1e30


def norm_rows(value, gain):
    return value * lax.rsqrt(jnp.mean(value * value, axis=-1, keepdims=True) + EPS) * gain


def bucket_edges():
    half = BUCKETS // 2
    return [math.ceil(half * (MAX_DIST / half) ** (step / half)) for step in range(1, half)]


def buckets_of(distance):
    half = BUCKETS // 2
    far = half + sum(((distance >= edge).astype(jnp.int32) for edge in bucket_edges()))
    return jnp.where(distance < half, distance, far)


def by_heads(values):
    return values.reshape(values.shape[0], values.shape[1], HEADS, HEAD_DIM)


def join_heads(values):
    return values.reshape(values.shape[0], values.shape[1], HEADS * HEAD_DIM)


def project(rows, weight_matrix):
    return jnp.dot(rows, weight_matrix, preferred_element_type=jnp.float32)


def project_back(grads, weight_matrix):
    return jnp.einsum("stn,kn->stk", grads, weight_matrix, preferred_element_type=jnp.float32)


def weight_grad(rows, grads):
    return jnp.einsum("stk,stn->kn", rows, grads, preferred_element_type=jnp.float32)


def gelu_mix(gate, up_values):
    return jax.nn.gelu(gate, approximate=True) * up_values


def scores_of(q_rows, keys, bias, allowed):
    scores = jnp.einsum("sqhd,skhd->shqk", q_rows, keys, preferred_element_type=jnp.float32) + bias
    return jnp.where(allowed[:, None], scores, NEG)


def attend(q_rows, keys, values, bias, allowed):
    scores = scores_of(q_rows, keys, bias, allowed)
    largest = jnp.max(scores, axis=-1, keepdims=True)
    raised = jnp.exp(scores - largest)
    total = jnp.sum(raised, axis=-1, keepdims=True)
    probs = raised / total
    mixed = jnp.einsum(
        "shqk,skhd->sqhd", probs.astype(jnp.bfloat16), values, preferred_element_type=jnp.float32
    )
    return (join_heads(mixed).astype(jnp.bfloat16), largest + jnp.log(total))


def attend_back(q_rows, keys, values, bias, allowed, log_total, grad_mixed):
    scores = scores_of(q_rows, keys, bias, allowed)
    probs = jnp.exp(scores - log_total)
    grad_probs = jnp.einsum(
        "sqhd,skhd->shqk", grad_mixed, values, preferred_element_type=jnp.float32
    )
    inner = jnp.sum(probs * grad_probs, axis=-1, keepdims=True)
    grad_scores = (probs * (grad_probs - inner)).astype(jnp.bfloat16)
    grad_query = jnp.einsum(
        "shqk,skhd->sqhd", grad_scores, keys, preferred_element_type=jnp.float32
    )
    grad_keys = jnp.einsum(
        "shqk,sqhd->skhd", grad_scores, q_rows, preferred_element_type=jnp.float32
    )
    grad_values = jnp.einsum(
        "shqk,sqhd->skhd",
        probs.astype(jnp.bfloat16),
        grad_mixed,
        preferred_element_type=jnp.float32,
    )
    return (join_heads(grad_query), join_heads(grad_keys), join_heads(grad_values), grad_scores)


def general_body(
    hidden_in,
    encoder_states,
    segments,
    enc_segments,
    grad_out,
    norm_self,
    q_self,
    k_self,
    v_self,
    o_self,
    rel_bias,
    norm_cross,
    q_cross,
    k_cross,
    v_cross,
    o_cross,
    norm_ff,
    wi_gate,
    wi_up,
    wo_ff,
):
    shards = (
        norm_self,
        q_self,
        k_self,
        v_self,
        o_self,
        rel_bias,
        norm_cross,
        q_cross,
        k_cross,
        v_cross,
        o_cross,
        norm_ff,
        wi_gate,
        wi_up,
        wo_ff,
    )
    micro_count = hidden_in.shape[0]
    rows_dev = hidden_in.shape[2]
    seg_whole, enc_seg_whole = (
        lax.all_gather(segments, "seq", axis=2, tiled=True),
        lax.all_gather(enc_segments, "seq", axis=2, tiled=True),
    )
    length = seg_whole.shape[2]
    positions = lax.axis_index("seq") * rows_dev + jnp.arange(rows_dev, dtype=jnp.int32)
    columns = jnp.arange(length, dtype=jnp.int32)
    distance = jnp.maximum(positions[:, None] - columns[None, :], 0)
    bucket_indicator = (
        buckets_of(distance)[None] == jnp.arange(BUCKETS, dtype=jnp.int32)[:, None, None]
    ).astype(jnp.bfloat16)
    causal = columns[None, :] <= positions[:, None]
    grad_shards = tuple((jnp.zeros(piece.shape, jnp.float32) for piece in shards))
    outputs, grad_inputs, grad_encoders = ([], [], [])
    for micro in range(micro_count):
        params = (
            lax.all_gather(shards[0], ("dp", "seq"), axis=0, tiled=True),
            lax.all_gather(shards[1], ("dp", "seq"), axis=0, tiled=True),
            lax.all_gather(shards[2], ("dp", "seq"), axis=0, tiled=True),
            lax.all_gather(shards[3], ("dp", "seq"), axis=0, tiled=True),
            lax.all_gather(shards[4], ("dp", "seq"), axis=0, tiled=True),
            lax.all_gather(shards[5], ("dp", "seq"), axis=0, tiled=True),
            lax.all_gather(shards[6], ("dp", "seq"), axis=0, tiled=True),
            lax.all_gather(shards[7], ("dp", "seq"), axis=0, tiled=True),
            lax.all_gather(shards[8], ("dp", "seq"), axis=0, tiled=True),
            lax.all_gather(shards[9], ("dp", "seq"), axis=0, tiled=True),
            lax.all_gather(shards[10], ("dp", "seq"), axis=0, tiled=True),
            lax.all_gather(shards[11], ("dp", "seq"), axis=0, tiled=True),
            lax.all_gather(shards[12], ("dp", "seq"), axis=0, tiled=True),
            lax.all_gather(shards[13], ("dp", "seq"), axis=0, tiled=True),
            lax.all_gather(shards[14], ("dp", "seq"), axis=0, tiled=True),
        )
        (
            gain_self,
            wq,
            wk,
            wv,
            wo,
            table_flat,
            gain_cross,
            cq,
            ck,
            cv,
            co,
            gain_ff,
            w_gate,
            w_up,
            w_down,
        ) = params
        bias = jnp.einsum(
            "pia,pw->wia",
            bucket_indicator,
            table_flat.reshape(BUCKETS, HEADS),
            preferred_element_type=jnp.float32,
        )
        inputs = hidden_in[micro].astype(jnp.float32)
        encoder = encoder_states[micro]
        seg_own = segments[micro]
        self_allowed = (seg_own[:, :, None] == seg_whole[micro][:, None, :]) & causal[None]
        cross_allowed = seg_own[:, :, None] == enc_seg_whole[micro][:, None, :]
        self_norm_scale = gain_self.astype(jnp.float32)
        cross_gain = gain_cross.astype(jnp.float32)
        ff_gain = gain_ff.astype(jnp.float32)
        normed_self = norm_rows(inputs, self_norm_scale).astype(jnp.bfloat16)
        query = project(normed_self, wq).astype(jnp.bfloat16)
        key_own = project(normed_self, wk).astype(jnp.bfloat16)
        value_own = project(normed_self, wv).astype(jnp.bfloat16)
        cross_key_own = project(encoder, ck).astype(jnp.bfloat16)
        cross_value_own = project(encoder, cv).astype(jnp.bfloat16)
        keys, values, cross_keys, cross_values = (
            lax.all_gather(key_own, "seq", axis=1, tiled=True),
            lax.all_gather(value_own, "seq", axis=1, tiled=True),
            lax.all_gather(cross_key_own, "seq", axis=1, tiled=True),
            lax.all_gather(cross_value_own, "seq", axis=1, tiled=True),
        )
        mixed, self_log_normalizer = attend(
            by_heads(query), by_heads(keys), by_heads(values), bias, self_allowed
        )
        after_self = inputs + project(mixed, wo)
        normed_cross = norm_rows(after_self, cross_gain).astype(jnp.bfloat16)
        cross_query = project(normed_cross, cq).astype(jnp.bfloat16)
        cross_mixed, cross_log = attend(
            by_heads(cross_query), by_heads(cross_keys), by_heads(cross_values), 0.0, cross_allowed
        )
        after_cross = after_self + project(cross_mixed, co)
        normed_ff = norm_rows(after_cross, ff_gain).astype(jnp.bfloat16)
        gate = project(normed_ff, w_gate)
        up_values = project(normed_ff, w_up)
        hidden = gelu_mix(gate, up_values).astype(jnp.bfloat16)
        result = after_cross + project(hidden, w_down)
        outputs.append(result.astype(jnp.bfloat16))
        params = (
            lax.all_gather(shards[0], ("dp", "seq"), axis=0, tiled=True),
            lax.all_gather(shards[1], ("dp", "seq"), axis=0, tiled=True),
            lax.all_gather(shards[2], ("dp", "seq"), axis=0, tiled=True),
            lax.all_gather(shards[3], ("dp", "seq"), axis=0, tiled=True),
            lax.all_gather(shards[4], ("dp", "seq"), axis=0, tiled=True),
            lax.all_gather(shards[5], ("dp", "seq"), axis=0, tiled=True),
            lax.all_gather(shards[6], ("dp", "seq"), axis=0, tiled=True),
            lax.all_gather(shards[7], ("dp", "seq"), axis=0, tiled=True),
            lax.all_gather(shards[8], ("dp", "seq"), axis=0, tiled=True),
            lax.all_gather(shards[9], ("dp", "seq"), axis=0, tiled=True),
            lax.all_gather(shards[10], ("dp", "seq"), axis=0, tiled=True),
            lax.all_gather(shards[11], ("dp", "seq"), axis=0, tiled=True),
            lax.all_gather(shards[12], ("dp", "seq"), axis=0, tiled=True),
            lax.all_gather(shards[13], ("dp", "seq"), axis=0, tiled=True),
            lax.all_gather(shards[14], ("dp", "seq"), axis=0, tiled=True),
        )
        (
            gain_self,
            wq,
            wk,
            wv,
            wo,
            table_flat,
            gain_cross,
            cq,
            ck,
            cv,
            co,
            gain_ff,
            w_gate,
            w_up,
            w_down,
        ) = params
        grad_result = grad_out[micro].astype(jnp.float32)
        out_low = grad_out[micro]
        grad_w_down = weight_grad(hidden, out_low)
        grad_hidden = project_back(out_low, w_down)
        mix_value, mix_pull = jax.vjp(gelu_mix, gate, up_values)
        grad_gate, grad_up = mix_pull(grad_hidden)
        grad_gate = grad_gate.astype(jnp.bfloat16)
        grad_up = grad_up.astype(jnp.bfloat16)
        gate_weight_gradient = weight_grad(normed_ff, grad_gate)
        grad_w_up = weight_grad(normed_ff, grad_up)
        grad_normed_ff = project_back(grad_gate, w_gate) + project_back(grad_up, w_up)
        norm_value, norm_pull = jax.vjp(norm_rows, after_cross, ff_gain)
        ff_part, grad_gain_ff = norm_pull(grad_normed_ff)
        grad_after_cross = grad_result + ff_part
        cross_out_low = grad_after_cross.astype(jnp.bfloat16)
        grad_co = weight_grad(cross_mixed, cross_out_low)
        grad_cross_mixed = project_back(cross_out_low, co).astype(jnp.bfloat16)
        grad_cross_query, cross_key_terms, cross_value_terms, cross_scores = attend_back(
            by_heads(cross_query),
            by_heads(cross_keys),
            by_heads(cross_values),
            0.0,
            cross_allowed,
            cross_log,
            by_heads(grad_cross_mixed),
        )
        grad_cross_key, grad_cross_value = (
            lax.psum_scatter(
                cross_key_terms.astype(jnp.bfloat16), "seq", scatter_dimension=1, tiled=True
            ).astype(jnp.float32),
            lax.psum_scatter(
                cross_value_terms.astype(jnp.bfloat16), "seq", scatter_dimension=1, tiled=True
            ).astype(jnp.float32),
        )
        grad_cross_key = grad_cross_key.astype(jnp.bfloat16)
        grad_cross_value = grad_cross_value.astype(jnp.bfloat16)
        cross_key_gradient = weight_grad(encoder, grad_cross_key)
        grad_cv = weight_grad(encoder, grad_cross_value)
        grad_encoders.append(project_back(grad_cross_key, ck) + project_back(grad_cross_value, cv))
        grad_cross_query = grad_cross_query.astype(jnp.bfloat16)
        grad_cq = weight_grad(normed_cross, grad_cross_query)
        grad_normed_cross = project_back(grad_cross_query, cq)
        norm_value, norm_pull = jax.vjp(norm_rows, after_self, cross_gain)
        cross_part, grad_gain_cross = norm_pull(grad_normed_cross)
        grad_after_self = grad_after_cross + cross_part
        self_out_low = grad_after_self.astype(jnp.bfloat16)
        grad_wo = weight_grad(mixed, self_out_low)
        grad_mixed = project_back(self_out_low, wo).astype(jnp.bfloat16)
        grad_query, key_terms, value_terms, self_attention_logits = attend_back(
            by_heads(query),
            by_heads(keys),
            by_heads(values),
            bias,
            self_allowed,
            self_log_normalizer,
            by_heads(grad_mixed),
        )
        grad_table = jnp.einsum(
            "dcma,uma->uc",
            self_attention_logits,
            bucket_indicator,
            preferred_element_type=jnp.float32,
        ).reshape(-1)
        grad_key, grad_value = (
            lax.psum_scatter(
                key_terms.astype(jnp.bfloat16), "seq", scatter_dimension=1, tiled=True
            ).astype(jnp.float32),
            lax.psum_scatter(
                value_terms.astype(jnp.bfloat16), "seq", scatter_dimension=1, tiled=True
            ).astype(jnp.float32),
        )
        grad_key = grad_key.astype(jnp.bfloat16)
        grad_value = grad_value.astype(jnp.bfloat16)
        grad_query = grad_query.astype(jnp.bfloat16)
        grad_wq = weight_grad(normed_self, grad_query)
        grad_wk = weight_grad(normed_self, grad_key)
        grad_wv = weight_grad(normed_self, grad_value)
        grad_normed_self = (
            project_back(grad_query, wq) + project_back(grad_key, wk) + project_back(grad_value, wv)
        )
        norm_value, norm_pull = jax.vjp(norm_rows, inputs, self_norm_scale)
        self_part, grad_gain_self = norm_pull(grad_normed_self)
        grad_inputs.append(grad_after_self + self_part)
        local = (
            grad_gain_self,
            grad_wq,
            grad_wk,
            grad_wv,
            grad_wo,
            grad_table,
            grad_gain_cross,
            grad_cq,
            cross_key_gradient,
            grad_cv,
            grad_co,
            grad_gain_ff,
            gate_weight_gradient,
            grad_w_up,
            grad_w_down,
        )
        summed = (
            lax.psum_scatter(local[0], ("dp", "seq"), scatter_dimension=0, tiled=True),
            lax.psum_scatter(local[1], ("dp", "seq"), scatter_dimension=0, tiled=True),
            lax.psum_scatter(local[2], ("dp", "seq"), scatter_dimension=0, tiled=True),
            lax.psum_scatter(local[3], ("dp", "seq"), scatter_dimension=0, tiled=True),
            lax.psum_scatter(local[4], ("dp", "seq"), scatter_dimension=0, tiled=True),
            lax.psum_scatter(local[5], ("dp", "seq"), scatter_dimension=0, tiled=True),
            lax.psum_scatter(local[6], ("dp", "seq"), scatter_dimension=0, tiled=True),
            lax.psum_scatter(local[7], ("dp", "seq"), scatter_dimension=0, tiled=True),
            lax.psum_scatter(local[8], ("dp", "seq"), scatter_dimension=0, tiled=True),
            lax.psum_scatter(local[9], ("dp", "seq"), scatter_dimension=0, tiled=True),
            lax.psum_scatter(local[10], ("dp", "seq"), scatter_dimension=0, tiled=True),
            lax.psum_scatter(local[11], ("dp", "seq"), scatter_dimension=0, tiled=True),
            lax.psum_scatter(local[12], ("dp", "seq"), scatter_dimension=0, tiled=True),
            lax.psum_scatter(local[13], ("dp", "seq"), scatter_dimension=0, tiled=True),
            lax.psum_scatter(local[14], ("dp", "seq"), scatter_dimension=0, tiled=True),
        )
        grad_shards = tuple((before + after for before, after in zip(grad_shards, summed)))
    return (jnp.stack(outputs), jnp.stack(grad_inputs), jnp.stack(grad_encoders)) + tuple(
        grad_shards
    )


TILE = 256
GROUP = 8
LANES = 128
AHEAD = 2
F32 = jnp.float32
BF16 = jnp.bfloat16


def contract(left, right, left_dim, right_dim):
    return lax.dot_general(
        left, right, (((left_dim,), (right_dim,)), ((), ())), preferred_element_type=F32
    )


def head_mask(head):
    lane = lax.broadcasted_iota(jnp.int32, (1, LANES), 1)
    keep = (lane < HEAD_DIM) if head % 2 == 0 else (lane >= HEAD_DIM)
    return keep.astype(F32).astype(BF16)


def bias_table(line):
    first = jnp.concatenate(
        [line if j == 0 else pltpu.roll(line, j, 1) for j in range(8)], axis=0
    )
    return [first if r == 0 else pltpu.roll(first, 8 * r, 1) for r in range(TILE // 8)]


def line_of(table):
    total = None
    for r in range(TILE // 8):
        part = table[8 * r : 8 * r + 8, :]
        part = part if r == 0 else pltpu.roll(part, TILE - 8 * r, 1)
        total = part if total is None else total + part
    line = total[0:1, :]
    for j in range(1, 8):
        line = line + pltpu.roll(total[j : j + 1, :], TILE - j, 1)
    return line


def positions():
    return (
        lax.broadcasted_iota(jnp.int32, (TILE, TILE), 0),
        lax.broadcasted_iota(jnp.int32, (TILE, TILE), 1),
    )


def pair_lanes(head):
    return slice((head // 2) * LANES, (head // 2 + 1) * LANES)


def head_rows(head):
    return slice(head * HEAD_DIM, (head + 1) * HEAD_DIM)


def tile_places():
    core = lax.axis_index("dp") % 2
    own = [2 * s + (core + s) % 2 for s in range(4)]
    par = [2 * s + (1 - core + s) % 2 for s in range(4)]
    return own + par + [tile // 2 for tile in own]


def place_tiles(causal, meta_ref, own, par):
    moves = []
    count = own.shape[0] // TILE
    places = tile_places() if causal and meta_ref is None else meta_ref
    for ref, base in ((own, 0), (par, count)):
        for s in range(count):
            target = places[base + s] + 1 if causal else base + s
            moves.append((ref, s, target))
    return moves


def rows_at(tile):
    return pl.ds(pl.multiple_of(tile * TILE, TILE), TILE)


def fill_tables(line_ref, tab, adj):
    for h in range(GROUP):
        line = line_ref[h]
        far = line[:, TILE - 1 : TILE]
        for r, rows in enumerate(bias_table(line - far)):
            adj[h, 8 * r : 8 * r + 8, :] = rows
        k_pos, q_pos = positions()
        table = adj[h]
        tab[h] = jnp.where(k_pos <= q_pos, table, NEG)
        adj[h] = jnp.where(k_pos > q_pos, table, 0.0)


BIAS_LANE, EMPTY_LANE = 16, 17


def lane_of():
    return lax.broadcasted_iota(jnp.int32, (1, LANES), 1) % HEAD_DIM


def by_parity(lanes):
    even = (jnp.arange(LANES) < HEAD_DIM)[None, :]
    zero = jnp.zeros_like(lanes)
    return jnp.stack([jnp.where(even, zero, lanes), jnp.where(even, lanes, zero)])


def key_lanes(codes):
    lane = jnp.arange(LANES, dtype=jnp.int32)[None, :] % HEAD_DIM
    documents = (codes[:, None] == lane) & (lane < BIAS_LANE)
    ones = (lane >= BIAS_LANE) & (lane < EMPTY_LANE)
    return by_parity((documents | ones | ((lane == EMPTY_LANE) & (codes[:, None] < 0))).astype(BF16))


def query_lanes(codes):
    lane = jnp.arange(LANES, dtype=jnp.int32)[None, :] % HEAD_DIM
    other = ((codes[:, None] != lane) & (lane < BIAS_LANE)) | (lane == EMPTY_LANE)
    return by_parity(jnp.where(other, NEG, 0.0).astype(BF16))


def with_lanes(head, rows, lanes):
    return rows * head_mask(head) + lanes


def far_lane(head, line_ref):
    lane = lax.broadcasted_iota(jnp.int32, (1, LANES), 1)
    at = BIAS_LANE + (HEAD_DIM if head % 2 == 0 else 0)
    return jnp.where(lane == at, line_ref[head][:, TILE - 1 : TILE], 0.0).astype(BF16)


def query_with_lanes(causal, h, q_ref, qext_ref, line_ref):
    rows = with_lanes(h, q_ref[:, pair_lanes(h)], qext_ref[h % 2])
    return rows + far_lane(h, line_ref) if causal else rows


def visit_pairs(causal, meta_ref, region):
    if not causal:
        region(0, False)
        return
    i = pl.program_id(1)
    if meta_ref is None:
        own = 2 * i + (lax.axis_index("dp") + i) % 2
        pairs = own // 2
    else:
        own, pairs = meta_ref[i], meta_ref[8 + i]
    region(own, True)
    lax.fori_loop(0, pairs, lambda j, c: (region(own - 2 * (j + 1), False), c)[1], 0)


def biased(scores, causal, near, j, h, tab, adj):
    if causal and near:
        return scores + (tab[h] if j else adj[h])
    return scores


def attend_kernel(causal, meta_ref, q_ref, ko, vo, kp, vp, qext_ref, kext_ref, line_ref,
                  o_ref, lse_ref, kb, vt, qx, tab, adj, m_s, l_s, acc):
    @pl.when(pl.program_id(1) == 0)
    def _():
        for ref, s, target in place_tiles(causal, meta_ref, ko, kp):
            for h in range(GROUP):
                kb[h, rows_at(target), :] = with_lanes(
                    h, ref[s * TILE : (s + 1) * TILE, pair_lanes(h)], kext_ref[h % 2, rows_at(target), :]
                )
        for ref, s, target in place_tiles(causal, meta_ref, vo, vp):
            vt[target] = ref[s * TILE : (s + 1) * TILE, :].T
        if causal:
            for h in range(GROUP):
                kb[h, 0:TILE, :] = kext_ref[h % 2, 0:TILE, :]
            vt[0] = jnp.zeros(vt.shape[1:], BF16)
            fill_tables(line_ref, tab, adj)

    for h in range(GROUP):
        qx[h] = query_with_lanes(causal, h, q_ref, qext_ref, line_ref)
    m_s[...] = jnp.full(m_s.shape, NEG, F32)
    l_s[...] = jnp.zeros(l_s.shape, F32)
    acc[...] = jnp.zeros(acc.shape, F32)

    def region(tile, near):
        def scores_of_head(h):
            return [contract(kb[h, rows_at(tile + j), :], qx[h], 1, 1) for j in range(2)]

        ready = [scores_of_head(h) for h in range(AHEAD)]
        for h in range(GROUP):
            if h + AHEAD < GROUP:
                ready.append(scores_of_head(h + AHEAD))
            scores = [biased(ready[h][j], causal, near, j, h, tab, adj) for j in range(2)]
            before = m_s[h : h + 1, :]
            largest = jnp.maximum(
                before, jnp.max(jnp.maximum(scores[0], scores[1]), axis=0, keepdims=True)
            )
            raised = [jnp.exp(piece - largest) for piece in scores]
            scale = jnp.exp(before - largest)
            m_s[h : h + 1, :] = largest
            l_s[h : h + 1, :] = l_s[h : h + 1, :] * scale + jnp.sum(
                raised[0] + raised[1], axis=0, keepdims=True
            )
            rows = head_rows(h)
            mixed = contract(vt[tile, rows, :], raised[0].astype(BF16), 1, 0) + contract(
                vt[tile + 1, rows, :], raised[1].astype(BF16), 1, 0
            )
            acc[rows, :] = acc[rows, :] * scale + mixed

    visit_pairs(causal, meta_ref, region)
    for h in range(GROUP):
        rows = head_rows(h)
        acc[rows, :] = acc[rows, :] / l_s[h : h + 1, :]
        lse_ref[0, h : h + 1, :] = m_s[h : h + 1, :] + jnp.log(l_s[h : h + 1, :])
    o_ref[...] = acc[...].T.astype(BF16)


def attend_back_kernel(causal, meta_ref, q_ref, ko, vo, kp, vp, qext_ref, kext_ref, line_ref,
                       do_ref, o_ref, lse_ref, dq_ref, own_ref, par_ref, gline_ref, gall_ref,
                       kb, vb, kt, qm, dm, qx, d_s, tab, adj, dq_acc, dk_acc, dv_acc, gt, gall):
    i = pl.program_id(1)

    @pl.when(i == 0)
    def _():
        for ref, s, target in place_tiles(causal, meta_ref, ko, kp):
            for h in range(GROUP):
                kb[h, rows_at(target), :] = with_lanes(
                    h, ref[s * TILE : (s + 1) * TILE, pair_lanes(h)], kext_ref[h % 2, rows_at(target), :]
                )
        for ref, s, target in place_tiles(causal, meta_ref, vo, vp):
            vb[rows_at(target), :] = ref[s * TILE : (s + 1) * TILE, :]
        for ref, s, target in place_tiles(causal, meta_ref, ko, kp):
            turned = ref[s * TILE : (s + 1) * TILE, :].T
            for h in range(GROUP):
                kt[target, h, 0:HEAD_DIM, :] = turned[head_rows(h), :]
        dk_acc[...] = jnp.zeros(dk_acc.shape, F32)
        dv_acc[...] = jnp.zeros(dv_acc.shape, F32)
        if causal:
            for h in range(GROUP):
                kb[h, 0:TILE, :] = kext_ref[h % 2, 0:TILE, :]
            vb[0:TILE, :] = jnp.zeros((TILE, vb.shape[1]), BF16)
            kt[0] = jnp.zeros(kt.shape[1:], BF16)
            for t in range(kt.shape[0]):
                for h in range(GROUP):
                    kt[t, h, HEAD_DIM:, :] = jnp.ones((kt.shape[2] - HEAD_DIM, TILE), BF16)
            gt[...] = jnp.zeros(gt.shape, F32)
            gall[...] = jnp.zeros(gall.shape, F32)
            fill_tables(line_ref, tab, adj)

    for h in range(GROUP):
        lanes = pair_lanes(h)
        pair, rows = h // 2, slice((h % 2) * TILE, (h % 2 + 1) * TILE)
        qm[pair, rows, :] = q_ref[:, lanes] * head_mask(h)
        dm[pair, rows, :] = do_ref[:, lanes] * head_mask(h)
        qx[h] = query_with_lanes(causal, h, q_ref, qext_ref, line_ref)
    both = jnp.concatenate([head_mask(0)] * 8 + [head_mask(1)] * 8, axis=0)
    for pair in range(GROUP // 2):
        lanes = pair_lanes(2 * pair)
        product = do_ref[:, lanes].astype(F32) * o_ref[:, lanes].astype(F32)
        high = product.astype(BF16)
        low = (product - high.astype(F32)).astype(BF16)
        inner = contract(both, high, 1, 1) + contract(both, low, 1, 1)
        d_s[2 * pair : 2 * pair + 1, :] = inner[0:1, :]
        d_s[2 * pair + 1 : 2 * pair + 2, :] = inner[8:9, :]
    dq_acc[...] = jnp.zeros(dq_acc.shape, F32)

    def region(tile, near):
        def products_of_head(h):
            half = slice((h % 2) * TILE, (h % 2 + 1) * TILE)
            return [
                (
                    contract(kb[h, rows_at(tile + j), :], qx[h], 1, 1),
                    contract(vb[rows_at(tile + j), pair_lanes(h)], dm[h // 2, half, :], 1, 1),
                )
                for j in range(2)
            ]

        ready = [products_of_head(h) for h in range(AHEAD)]
        probs_low, grads_low = {}, {}
        for h in range(GROUP):
            if h + AHEAD < GROUP:
                ready.append(products_of_head(h + AHEAD))
            back = None
            for j in range(2):
                scores, grad_probs = ready[h][j]
                probs = jnp.exp(biased(scores, causal, near, j, h, tab, adj) - lse_ref[0, h : h + 1, :])
                grads = probs * (grad_probs - d_s[h : h + 1, :])
                low = grads.astype(BF16)
                probs_low[h, j], grads_low[h, j] = probs.astype(BF16), low
                if causal and near:
                    rounded = low.astype(F32)
                    if j == 0:
                        k_pos, q_pos = positions()
                        rounded = jnp.where(k_pos > q_pos, rounded, 0.0)
                    gt[h] += rounded
                part = contract(kt[tile + j, h], low, 1, 0)
                back = part if back is None else back + part
            dq_acc[head_rows(h), :] += back[0:HEAD_DIM, :]
            if causal:
                gall[h : h + 1, :] += back[HEAD_DIM : HEAD_DIM + 1, :]
            if h % 2 == 1:
                pair = h // 2
                lanes = pair_lanes(h)
                for j in range(2):
                    dv_acc[rows_at(tile + j), lanes] += contract(
                        jnp.concatenate([probs_low[h - 1, j], probs_low[h, j]], axis=1), dm[pair], 1, 0
                    )
                    dk_acc[rows_at(tile + j), lanes] += contract(
                        jnp.concatenate([grads_low[h - 1, j], grads_low[h, j]], axis=1), qm[pair], 1, 0
                    )

    visit_pairs(causal, meta_ref, region)
    dq_ref[...] = dq_acc[...].T.astype(BF16)

    @pl.when(i == pl.num_programs(1) - 1)
    def _():
        for j, total in enumerate((dk_acc, dv_acc)):
            for ref, s, target in place_tiles(causal, meta_ref, own_ref.at[j], par_ref.at[j]):
                ref[s * TILE : (s + 1) * TILE, :] = total[rows_at(target), :].astype(BF16)
        for h in range(GROUP):
            if causal:
                gline_ref[h] = line_of(gt[h])
                gall_ref[h] = gall[h : h + 1, :]
            else:
                gline_ref[h] = jnp.zeros((1, TILE), F32)
                gall_ref[h] = jnp.zeros((1, TILE), F32)


VMEM_LIMIT = 60 * 1024 * 1024


def attention_specs(own_rows, par_rows, keys):
    groups = HEADS // GROUP
    lanes = GROUP * HEAD_DIM
    return [
        pl.BlockSpec((TILE, lanes), lambda g, i, meta: (i, g)),
        pl.BlockSpec((own_rows, lanes), lambda g, i, meta: (0, g)),
        pl.BlockSpec((own_rows, lanes), lambda g, i, meta: (0, groups + g)),
        pl.BlockSpec((par_rows, lanes), lambda g, i, meta: (0, g)),
        pl.BlockSpec((par_rows, lanes), lambda g, i, meta: (0, groups + g)),
        pl.BlockSpec((2, TILE, LANES), lambda g, i, meta: (0, i, 0)),
        pl.BlockSpec((2, keys, LANES), lambda g, i, meta: (0, 0, 0)),
        pl.BlockSpec((GROUP, 1, TILE), lambda g, i, meta: (g, 0, 0)),
    ]


def without_meta(spec):
    return pl.BlockSpec(spec.block_shape, lambda g, i: spec.index_map(g, i, None))


def attention_scratch(keys, lanes, table):
    return [
        pltpu.VMEM((GROUP, keys, LANES), BF16),
        pltpu.VMEM((keys // TILE, lanes, TILE), BF16),
        pltpu.VMEM((GROUP, TILE, LANES), BF16),
        pltpu.VMEM(table, F32),
        pltpu.VMEM(table, F32),
        pltpu.VMEM((8, TILE), F32),
        pltpu.VMEM((8, TILE), F32),
        pltpu.VMEM((lanes, TILE), F32),
    ]


def attend_fast(meta, query, kv_own, kv_par, qext, kext, line, causal):
    tokens, width = query.shape
    own_rows, par_rows, keys = kv_own.shape[0], kv_par.shape[0], kext.shape[1]
    groups, lanes = HEADS // GROUP, GROUP * HEAD_DIM
    table = (GROUP, TILE, TILE) if causal else (1, 8, LANES)
    return pl.pallas_call(
        functools.partial(attend_kernel, causal),
        grid_spec=pltpu.PrefetchScalarGridSpec(
            num_scalar_prefetch=1,
            grid=(groups, tokens // TILE),
            in_specs=attention_specs(own_rows, par_rows, keys),
            out_specs=[
                pl.BlockSpec((TILE, lanes), lambda g, i, meta: (i, g)),
                pl.BlockSpec((1, GROUP, TILE), lambda g, i, meta: (g, 0, i)),
            ],
            scratch_shapes=attention_scratch(keys, lanes, table),
        ),
        out_shape=[
            jax.ShapeDtypeStruct((tokens, width), BF16),
            jax.ShapeDtypeStruct((groups, GROUP, tokens), F32),
        ],
        compiler_params=pltpu.CompilerParams(vmem_limit_bytes=VMEM_LIMIT),
        cost_estimate=pl.CostEstimate(
            flops=tokens * keys * width * 4, bytes_accessed=4 * (tokens + keys) * width,
            transcendentals=tokens * keys * HEADS // 2,
        ),
        name="attend_self" if causal else "attend_cross",
    )(meta, query, kv_own, kv_own, kv_par, kv_par, qext, kext, line)


def attend_back_fast(meta, query, kv_own, kv_par, qext, kext, line, grad_mixed, mixed, lse, causal):
    tokens, width = query.shape
    own_rows, par_rows, keys = kv_own.shape[0], kv_par.shape[0], kext.shape[1]
    groups, lanes = HEADS // GROUP, GROUP * HEAD_DIM
    table = (GROUP, TILE, TILE) if causal else (1, 8, LANES)
    block = pl.BlockSpec((TILE, lanes), lambda g, i, meta: (i, g))
    line_spec = pl.BlockSpec((GROUP, 1, TILE), lambda g, i, meta: (g, 0, 0))
    return pl.pallas_call(
        functools.partial(attend_back_kernel, causal),
        grid_spec=pltpu.PrefetchScalarGridSpec(
            num_scalar_prefetch=1,
            grid=(groups, tokens // TILE),
            in_specs=attention_specs(own_rows, par_rows, keys)
            + [block, block, pl.BlockSpec((1, GROUP, TILE), lambda g, i, meta: (g, 0, i))],
            out_specs=[
                block,
                pl.BlockSpec((2, own_rows, lanes), lambda g, i, meta: (0, 0, g)),
                pl.BlockSpec((2, par_rows, lanes), lambda g, i, meta: (0, 0, g)),
                line_spec,
                line_spec,
            ],
            scratch_shapes=[
                pltpu.VMEM((GROUP, keys, LANES), BF16),
                pltpu.VMEM((keys, lanes), BF16),
                pltpu.VMEM((keys // TILE, GROUP, HEAD_DIM + (16 if causal else 0), TILE), BF16),
                pltpu.VMEM((GROUP // 2, 2 * TILE, LANES), BF16),
                pltpu.VMEM((GROUP // 2, 2 * TILE, LANES), BF16),
                pltpu.VMEM((GROUP, TILE, LANES), BF16),
                pltpu.VMEM((8, TILE), F32),
                pltpu.VMEM(table, F32),
                pltpu.VMEM(table, F32),
                pltpu.VMEM((lanes, TILE), F32),
                pltpu.VMEM((keys, lanes), F32),
                pltpu.VMEM((keys, lanes), F32),
                pltpu.VMEM(table, F32),
                pltpu.VMEM((8, TILE), F32),
            ],
        ),
        out_shape=[
            jax.ShapeDtypeStruct((tokens, width), BF16),
            jax.ShapeDtypeStruct((2, own_rows, width), BF16),
            jax.ShapeDtypeStruct((2, par_rows, width), BF16),
            jax.ShapeDtypeStruct((HEADS, 1, TILE), F32),
            jax.ShapeDtypeStruct((HEADS, 1, TILE), F32),
        ],
        compiler_params=pltpu.CompilerParams(vmem_limit_bytes=VMEM_LIMIT),
        cost_estimate=pl.CostEstimate(
            flops=tokens * keys * width * 10, bytes_accessed=10 * (tokens + keys) * width,
            transcendentals=tokens * keys * HEADS // 2,
        ),
        name="attend_self_back" if causal else "attend_cross_back",
    )(meta, query, kv_own, kv_own, kv_par, kv_par, qext, kext, line, grad_mixed, mixed, lse)


AXES = ("dp", "seq")


def exchange(value, dp_bit, seq_bit):
    pairs = [
        (dp * 4 + seq, (dp ^ dp_bit) * 4 + (seq ^ seq_bit)) for dp in range(8) for seq in range(4)
    ]
    return lax.ppermute(value, AXES, pairs)


CORE, Z_LOW, Z_HIGH, X, Y = (1, 0), (2, 0), (4, 0), (0, 1), (0, 2)


def move_pairs(a, b):
    pairs = []
    for z in range(4):
        for core in range(2):
            for s in range(4):
                micro, half_core = (s >> 1) ^ a, (s & 1) ^ b
                pairs.append(((2 * z + core) * 4 + s, (2 * z + half_core) * 4 + 2 * core + micro))
    return pairs


ROUNDS = ((0, 0), (0, 1), (1, 0), (1, 1))


def take(value, index, axis):
    return lax.dynamic_index_in_dim(value, index, axis, keepdims=False)


MESH = pl.DeviceIdType.MESH


class Links:
    def __init__(self):
        dp, seq = lax.axis_index("dp"), lax.axis_index("seq")
        self.seq = seq
        self.z, self.core, self.y, self.x = dp // 2, dp % 2, seq // 2, seq % 2
        self.at_z = [{"dp": ((self.z + k) % 4) * 2 + self.core, "seq": seq} for k in (1, 2, 3)]
        self.at_x = {"dp": dp, "seq": seq + 1 - 2 * self.x}
        self.at_y = {"dp": dp, "seq": seq + 2 - 4 * self.y}
        self.at_core = {"dp": dp + 1 - 2 * self.core, "seq": seq}

    def at_plane(self, core, seq):
        return {"dp": 2 * self.z + core, "seq": seq}

    def greet(self):
        partners = list(self.at_z)
        for flip in (0, 1):
            for k in range(4):
                if flip or k:
                    core = 1 - self.core if flip else self.core
                    partners.append(self.at_plane(core, (self.seq + k) % 4))
        barrier = pltpu.get_barrier_semaphore()
        for partner in partners:
            pl.semaphore_signal(barrier, inc=1, device_id=partner, device_id_type=MESH)
        pl.semaphore_wait(barrier, len(partners))


def remote(source, target, send_sem, recv_sem, device):
    return pltpu.make_async_remote_copy(
        src_ref=source,
        dst_ref=target,
        send_sem=send_sem,
        recv_sem=recv_sem,
        device_id=device,
        device_id_type=MESH,
    )


def move_tokens(links, sources, targets, parts, local_sem, send_sem, recv_sem):
    waits = []
    for r, (a, b) in enumerate(ROUNDS):
        micro = 1 - links.y if a else links.y
        core = 1 - links.x if b else links.x
        chip = 2 * links.core + micro
        stays = (core == links.core) & (chip == links.seq)
        for n, (source, target, part) in enumerate(zip(sources, targets, parts)):
            if part is None:
                piece = source.at[micro]
            else:
                piece = source.at[micro, 0, pl.ds(b * part, part)]
            slot = target.at[links.seq]
            here = pltpu.make_async_copy(piece, slot, local_sem.at[r, n])
            away = remote(piece, slot, send_sem.at[r, n], recv_sem.at[r, n], links.at_plane(core, chip))

            @pl.when(stays)
            def _(here=here):
                here.start()

            @pl.when(jnp.logical_not(stays))
            def _(away=away):
                away.start()

            waits.append((stays, here, away))

    def finish():
        for stays, here, away in waits:
            @pl.when(stays)
            def _(here=here):
                here.wait()

            @pl.when(jnp.logical_not(stays))
            def _(away=away):
                away.wait()

    return finish


class Gather:
    def __init__(self, links, shards, wholes, local_sem, send_sem, recv_sem):
        self.links, self.shards, self.wholes = links, shards, wholes
        self.local_sem, self.send_sem, self.recv_sem = local_sem, send_sem, recv_sem

    def copy(self, w, slot, source, target, device):
        return remote(source, target, self.send_sem.at[w, slot], self.recv_sem.at[w, slot], device)

    def copies(self, stage, w):
        links, whole = self.links, self.wholes[w]
        z, core, y, x = links.z, links.core, links.y, links.x
        half = whole.shape[-1] // 2
        left, right = pl.ds(0, half), pl.ds(half, half)
        if stage == 0:
            own = whole.at[z, core, y, x]
            return [self.copy(w, k, self.shards[w], own, links.at_z[k]) for k in range(3)]
        if stage == 1:
            one, two = whole.at[:, core, y, x, :, left], whole.at[:, core, y, x, :, right]
            return [self.copy(w, 3, one, one, links.at_x), self.copy(w, 4, two, two, links.at_y)]
        if stage == 2:
            one, two = whole.at[:, core, y, :, :, left], whole.at[:, core, :, x, :, right]
            return [self.copy(w, 5, one, one, links.at_y), self.copy(w, 6, two, two, links.at_x)]
        both = whole.at[:, core]
        return [self.copy(w, 7, both, both, links.at_core)]

    def local(self, w):
        links = self.links
        own = self.wholes[w].at[links.z, links.core, links.y, links.x]
        return pltpu.make_async_copy(self.shards[w], own, self.local_sem.at[w])

    def begin(self):
        for w in range(len(self.shards)):
            self.local(w).start()
            for copy in self.copies(0, w):
                copy.start()

    def advance(self, stage, w):
        if stage == 1:
            self.local(w).wait()
        for copy in self.copies(stage - 1, w):
            copy.wait_recv()
        for copy in self.copies(stage, w):
            copy.start()

    def steps(self):
        count = len(self.shards)
        order = []
        for t in range(count + 2):
            order += [(stage, t - stage + 1) for stage in (1, 2, 3) if 0 <= t - stage + 1 < count]
        return order

    def end(self):
        for w in range(len(self.shards)):
            for copy in self.copies(3, w):
                copy.wait_recv()
            for stage in range(4):
                for copy in self.copies(stage, w):
                    copy.wait_send()


def gather_kernel(count, parts, *refs):
    tokens = len(parts)
    shards, moved = refs[:count], refs[count : count + tokens]
    refs = refs[count + tokens :]
    wholes, settled = refs[:count], refs[count : count + tokens]
    local_sem, send_sem, recv_sem, move_local, move_send, move_recv = refs[count + tokens :]
    links = Links()
    links.greet()
    gather = Gather(links, shards, wholes, local_sem, send_sem, recv_sem)
    gather.begin()
    finish = move_tokens(links, moved, settled, parts, move_local, move_send, move_recv)
    for stage, w in gather.steps():
        gather.advance(stage, w)
    gather.end()
    finish()


def attend_gather_kernel(count, q_ref, ko, vo, kp, vp, qext_ref, kext_ref, line_ref, *refs):
    sources, (o_ref, lse_ref), refs = refs[:count], refs[count : count + 2], refs[count + 2 :]
    wholes, scratch = refs[:count], refs[count : count + 8]
    shards = refs[count + 8 : 2 * count + 8]
    load_sem, local_sem, send_sem, recv_sem = refs[2 * count + 8 :]
    links = Links()
    gather = Gather(links, shards, wholes, local_sem, send_sem, recv_sem)
    step = pl.program_id(0) * pl.num_programs(1) + pl.program_id(1)
    total = (HEADS * HEAD_DIM // q_ref.shape[1]) * 4
    steps = gather.steps()

    @pl.when(step == 0)
    def _():
        links.greet()
        loads = [pltpu.make_async_copy(sources[w], shards[w], load_sem.at[w]) for w in range(count)]
        for load in loads:
            load.start()
        for load in loads:
            load.wait()
        gather.begin()

    attend_kernel(True, None, q_ref, ko, vo, kp, vp, qext_ref, kext_ref, line_ref, o_ref, lse_ref, *scratch)
    served = 0
    for n in range(total):
        upto = len(steps) if n == total - 1 else GATHER_PACE[n] if n < len(GATHER_PACE) else served
        if upto > served:
            @pl.when(step == n)
            def _(first=served, last=upto, n=n):
                for stage, w in steps[first:last]:
                    gather.advance(stage, w)
                if n == total - 1:
                    gather.end()

            served = upto


GATHER_PACE = (1, 4, 7, 9, 11, 13, 15)


def attend_gather(query, kv_own, kv_par, qext, kext, line, shards):
    tokens, width = query.shape
    own_rows, par_rows, keys = kv_own.shape[0], kv_par.shape[0], kext.shape[1]
    groups, lanes, count = HEADS // GROUP, GROUP * HEAD_DIM, len(shards)
    table = (GROUP, TILE, TILE)
    whole = pl.BlockSpec(memory_space=pl.ANY)
    outs = pl.pallas_call(
        functools.partial(attend_gather_kernel, count),
        grid=(groups, tokens // TILE),
        in_specs=[without_meta(spec) for spec in attention_specs(own_rows, par_rows, keys)] + [whole] * count,
        out_specs=[
            pl.BlockSpec((TILE, lanes), lambda g, i: (i, g)),
            pl.BlockSpec((1, GROUP, TILE), lambda g, i: (g, 0, i)),
        ]
        + [whole] * count,
        scratch_shapes=attention_scratch(keys, lanes, table)
        + [pltpu.VMEM(shard.shape, BF16) for shard in shards]
        + [
            pltpu.SemaphoreType.DMA((count,)),
            pltpu.SemaphoreType.DMA((count,)),
            pltpu.SemaphoreType.DMA((count, 8)),
            pltpu.SemaphoreType.DMA((count, 8)),
        ],
        out_shape=[
            jax.ShapeDtypeStruct((tokens, width), BF16),
            jax.ShapeDtypeStruct((groups, GROUP, tokens), F32),
        ]
        + [jax.ShapeDtypeStruct((4, 2, 2, 2, *shard.shape), BF16) for shard in shards],
        compiler_params=pltpu.CompilerParams(
            vmem_limit_bytes=VMEM_LIMIT, collective_id=2, has_side_effects=True
        ),
        cost_estimate=pl.CostEstimate(
            flops=tokens * keys * width * 4, bytes_accessed=4 * (tokens + keys) * width,
            transcendentals=tokens * keys * HEADS // 2,
        ),
        name="attend_gather",
    )(query, kv_own, kv_own, kv_par, kv_par, qext, kext, line, *shards)
    return outs[0], outs[1], [whole.reshape(-1, whole.shape[-1]) for whole in outs[2:]]


def gather_weights(shards, moved):
    count = len(shards)
    sent = sum(shard.size for shard in shards) * 2
    parts = [None if value.ndim == 3 else value.shape[2] // 2 for value in moved]
    settled = [
        jax.ShapeDtypeStruct((4, value.shape[1] if part is None else part, value.shape[-1]), BF16)
        for value, part in zip(moved, parts)
    ]
    outs = pl.pallas_call(
        functools.partial(gather_kernel, count, parts),
        in_specs=[pl.BlockSpec(memory_space=pltpu.VMEM)] * count
        + [pl.BlockSpec(memory_space=pl.ANY)] * len(moved),
        out_specs=[pl.BlockSpec(memory_space=pl.ANY)] * (count + len(moved)),
        out_shape=[jax.ShapeDtypeStruct((4, 2, 2, 2, *shard.shape), BF16) for shard in shards] + settled,
        scratch_shapes=[
            pltpu.SemaphoreType.DMA((count,)),
            pltpu.SemaphoreType.DMA((count, 8)),
            pltpu.SemaphoreType.DMA((count, 8)),
            pltpu.SemaphoreType.DMA((4, len(moved))),
            pltpu.SemaphoreType.DMA((4, len(moved))),
            pltpu.SemaphoreType.DMA((4, len(moved))),
        ],
        compiler_params=pltpu.CompilerParams(
            vmem_limit_bytes=VMEM_LIMIT, collective_id=0, has_side_effects=True
        ),
        cost_estimate=pl.CostEstimate(flops=0, transcendentals=0, bytes_accessed=500 * sent),
        name="gather_weights",
    )(*shards, *moved)
    return [whole.reshape(-1, whole.shape[-1]) for whole in outs[:count]], outs[count:]


def add_low(first, second):
    return (first.astype(F32) + second.astype(F32)).astype(BF16)


def return_tokens_kernel(links, source, target, part, local_sem, send_sem, recv_sem):
    waits = []
    mine = 2 * (links.seq % 2) + links.core
    for s in range(4):
        half = (links.core + s) % 2
        slot = target.at[links.seq % 2, pl.ds(pl.multiple_of(half * part, part), part)]
        stays = (links.y == links.core) & (links.seq == s)
        here = pltpu.make_async_copy(source.at[s], slot, local_sem)
        away = remote(source.at[s], slot, send_sem.at[s], recv_sem.at[mine], links.at_plane(links.y, s))

        @pl.when(stays)
        def _(here=here):
            here.start()

        @pl.when(jnp.logical_not(stays))
        def _(away=away):
            away.start()

        waits.append((stays, here, away))

    def finish():
        for stays, here, away in waits:
            @pl.when(stays)
            def _(here=here):
                here.wait()

            @pl.when(jnp.logical_not(stays))
            def _(away=away):
                away.wait_send()

        for j in range(4):
            arrived = remote(
                source.at[0], target.at[0, pl.ds(0, part)], send_sem.at[0], recv_sem.at[j],
                links.at_core,
            )

            @pl.when(jnp.logical_not((links.y == links.core) & (mine == j)))
            def _(arrived=arrived):
                arrived.wait_recv()

    return finish


def scatter_kernel(shapes, part, *refs):
    count = len(shapes)
    grads, tokens, sums, returned = refs[:count], refs[count], refs[count + 1 : 2 * count + 1], refs[2 * count + 1]
    scratch = refs[2 * count + 2 :]
    kept, got_one, got_two, got_z = (scratch[j * count : (j + 1) * count] for j in range(4))
    own, totals = scratch[4 * count : 5 * count], scratch[5 * count : 6 * count]
    load_sem, store_sem, send_sem, recv_sem, back_local, back_send, back_recv = scratch[6 * count :]
    links = Links()
    z, core, y, x = links.z, links.core, links.y, links.x
    at_z, at_x, at_y, at_core = links.at_z, links.at_x, links.at_y, links.at_core
    links.greet()
    finish = return_tokens_kernel(links, tokens, returned, part, back_local, back_send, back_recv)

    def send(w, slot, source, target, device):
        copy = remote(source, target, send_sem.at[w, slot], recv_sem.at[w, slot], device)
        copy.start()
        return copy

    def halves(w):
        half = shapes[w][1] // 2
        return pl.ds(0, half), pl.ds(half, half)

    def add(first, second, dtype):
        return (first.astype(F32) + second.astype(F32)).astype(dtype)

    stages, loads, stores = [[] for _ in range(4)], [], []
    for w in range(count):
        stages[0].append([send(w, 0, grads[w].at[:, 1 - core], kept[w], at_core)])
        load = pltpu.make_async_copy(grads[w].at[:, core], own[w], load_sem.at[w])
        load.start()
        loads.append(load)
    for t in range(count + 3):
        if t < count:
            w, dtype = t, kept[t].dtype
            left, right = halves(w)
            loads[w].wait()
            stages[0][w][0].wait_recv()

            def core_step(b, carry, w=w, dtype=dtype):
                zz, yy, xx = b // 4, (b // 2) % 2, b % 2
                kept[w][zz, yy, xx] = add(kept[w][zz, yy, xx], own[w][zz, yy, xx], dtype)
                return carry

            lax.fori_loop(0, 16, core_step, 0)
            half = shapes[w][1] // 2
            stages[1].append([
                send(w, 1, kept[w].at[:, :, 1 - x, :, left], got_one[w].at[0], at_x),
                send(w, 2, kept[w].at[:, 1 - y, :, :, right], got_one[w].at[1], at_y),
            ])
        if 0 <= t - 1 < count:
            w, dtype = t - 1, kept[t - 1].dtype
            left, right = halves(w)
            half = shapes[w][1] // 2
            for copy in stages[1][w]:
                copy.wait_recv()

            def one_step(b, carry, w=w, dtype=dtype, half=half):
                zz, other = b // 2, b % 2
                kept[w][zz, other, x, :, 0:half] = add(
                    kept[w][zz, other, x, :, 0:half], got_one[w][0, zz, other], dtype
                )
                kept[w][zz, y, other, :, half : 2 * half] = add(
                    kept[w][zz, y, other, :, half : 2 * half], got_one[w][1, zz, other], dtype
                )
                return carry

            lax.fori_loop(0, 8, one_step, 0)
            stages[2].append([
                send(w, 3, kept[w].at[:, 1 - y, x, :, left], got_two[w].at[0], at_y),
                send(w, 4, kept[w].at[:, y, 1 - x, :, right], got_two[w].at[1], at_x),
            ])
        if 0 <= t - 2 < count:
            w, dtype = t - 2, kept[t - 2].dtype
            half = shapes[w][1] // 2
            for copy in stages[2][w]:
                copy.wait_recv()

            def two_step(zz, carry, w=w, dtype=dtype, half=half):
                kept[w][zz, y, x, :, 0:half] = add(
                    kept[w][zz, y, x, :, 0:half], got_two[w][0, zz], dtype
                )
                kept[w][zz, y, x, :, half : 2 * half] = add(
                    kept[w][zz, y, x, :, half : 2 * half], got_two[w][1, zz], dtype
                )
                return carry

            lax.fori_loop(0, 4, two_step, 0)
            stages[3].append([
                send(w, 5 + k, kept[w].at[(z + k + 1) % 4, y, x], got_z[w].at[k], at_z[k])
                for k in range(3)
            ])
        if 0 <= t - 3 < count:
            w = t - 3
            for copy in stages[3][w]:
                copy.wait_recv()
            total = kept[w][z, y, x].astype(F32)
            for k in range(3):
                total = total + got_z[w][k].astype(F32)
            totals[w][...] = total
            store = pltpu.make_async_copy(totals[w], sums[w], store_sem.at[w])
            store.start()
            stores.append(store)
    for w in range(count):
        stores[w].wait()
        for stage in stages:
            for copy in stage[w]:
                copy.wait_send()
    finish()


def scatter_grads(grads, tokens):
    part = tokens.shape[1]
    count = len(grads)
    shapes = [(grad.shape[0] // 32, grad.shape[1]) for grad in grads]
    types = [grad.dtype for grad in grads]

    def buffers(*lead, halved=False):
        return [
            pltpu.VMEM((*lead, rows, width // 2 if halved else width), kind)
            for (rows, width), kind in zip(shapes, types)
        ]

    return pl.pallas_call(
        functools.partial(scatter_kernel, shapes, part),
        in_specs=[pl.BlockSpec(memory_space=pl.ANY)] * (count + 1),
        out_specs=[pl.BlockSpec(memory_space=pl.ANY)] * (count + 1),
        out_shape=[jax.ShapeDtypeStruct(shape, F32) for shape in shapes]
        + [jax.ShapeDtypeStruct((2, 2 * part, tokens.shape[2]), BF16)],
        scratch_shapes=buffers(4, 2, 2)
        + buffers(2, 4, 2, halved=True)
        + buffers(2, 4, halved=True)
        + buffers(3)
        + buffers(4, 2, 2)
        + [pltpu.VMEM(shape, F32) for shape in shapes]
        + [
            pltpu.SemaphoreType.DMA((count,)),
            pltpu.SemaphoreType.DMA((count,)),
            pltpu.SemaphoreType.DMA((count, 8)),
            pltpu.SemaphoreType.DMA((count, 8)),
            pltpu.SemaphoreType.DMA,
            pltpu.SemaphoreType.DMA((4,)),
            pltpu.SemaphoreType.DMA((4,)),
        ],
        compiler_params=pltpu.CompilerParams(
            vmem_limit_bytes=67043328, collective_id=1, has_side_effects=True
        ),
        cost_estimate=pl.CostEstimate(
            flops=0, transcendentals=0, bytes_accessed=16 * sum(grad.size for grad in grads)
        ),
        name="scatter_grads",
    )(*[
        grad.reshape(4, 2, 2, 2, rows, width) for grad, (rows, width) in zip(grads, shapes)
    ], tokens)


def norm_scale(value):
    return lax.rsqrt(jnp.mean(value * value, axis=-1, keepdims=True) + EPS)


def normed(value, gain):
    return (value * norm_scale(value) * gain).astype(BF16)


def norm_back(value, gain, grad):
    scale = norm_scale(value)
    scaled = grad * gain
    inner = jnp.mean(scaled * value, axis=-1, keepdims=True)
    return (
        scale * scaled - (scale * scale * scale) * value * inner,
        jnp.sum(grad * value * scale, axis=0),
    )


def dot(rows, weight):
    return jnp.dot(rows, weight, preferred_element_type=F32)


def dot_back(grads, weight):
    return contract(grads, weight, 1, 1)


def dot_weight(rows, grads):
    return contract(rows, grads, 0, 0).astype(BF16)


def fast_body(
    hidden_in,
    encoder_states,
    segments,
    enc_segments,
    grad_out,
    norm_self,
    q_self,
    k_self,
    v_self,
    o_self,
    rel_bias,
    norm_cross,
    q_cross,
    k_cross,
    v_cross,
    o_cross,
    norm_ff,
    wi_gate,
    wi_up,
    wo_ff,
):
    dp, seq = lax.axis_index("dp"), lax.axis_index("seq")
    core, z_low, z_high, y, x = dp % 2, (dp // 2) % 2, dp // 4, seq // 2, seq % 2
    place = (core, z_low, z_high, y, x)
    rows_dev, width = hidden_in.shape[2], hidden_in.shape[3]
    enc_dev = encoder_states.shape[2]
    part, enc_part = rows_dev // 2, enc_dev // 2
    owned_micro = seq % 2

    def send_tokens(pieces_of):
        return [
            lax.ppermute(pieces_of((seq // 2) ^ a, b), AXES, move_pairs(a, b)) for a, b in ROUNDS
        ]

    def settle(received):
        slots = []
        for s in range(4):
            index = 2 * ((s >> 1) ^ owned_micro) + ((s & 1) ^ core)
            slots.append(lax.select_n(index, *received))
        return jnp.stack(slots)

    def return_tokens(value):
        received = []
        for a, b in ROUNDS:
            index = 2 * (owned_micro ^ a) + (core ^ b)
            back = [(target, source) for source, target in move_pairs(a, b)]
            received.append(lax.ppermute(take(value, index, 0), AXES, back))
        flag = seq // 2
        micro = []
        for m in range(2):
            micro.append(
                jnp.concatenate(
                    [jnp.where((flag ^ m) == 0, received[b], received[2 + b]) for b in range(2)],
                    axis=0,
                )
            )
        return jnp.stack(micro)[:, None]

    codes = jnp.concatenate([segments[:, 0], enc_segments[:, 0]], axis=1).astype(BF16)
    codes = jnp.pad(codes, ((0, 0), (0, width - codes.shape[1])))
    codes = jnp.broadcast_to(codes[:, None], (2, 8, width))

    small = jnp.concatenate([norm_self, norm_cross, norm_ff, rel_bias])
    small_rows = norm_self.shape[0]
    small = jnp.broadcast_to(jnp.pad(small, (0, 2 * LANES - small.shape[0])), (8, 2 * LANES))
    wholes, (inputs_low, encoder, codes) = gather_weights(
        [small, k_self, v_self, q_self], [hidden_in, encoder_states, codes]
    )
    small, wk, wv, wq = wholes
    small = small.reshape(32, 8, 2 * LANES)[:, 0].astype(F32)
    gain_self, gain_cross, gain_ff = (
        small[:, j * small_rows : (j + 1) * small_rows].reshape(-1) for j in range(3)
    )
    table = small[:, 3 * small_rows : 3 * small_rows + rel_bias.shape[0]].reshape(BUCKETS, HEADS)
    ff = wi_gate.shape[1]

    inputs_low = inputs_low.reshape(4 * part, width)
    encoder = encoder.reshape(4 * enc_part, width)
    codes = codes[:, 0].astype(jnp.int32)
    seg_parts = codes[:, :rows_dev].reshape(4, 2, part)
    enc_parts = codes[:, rows_dev : rows_dev + enc_dev].reshape(4, 2, enc_part)

    def of_core(parts, which):
        return jnp.stack([take(parts[s], which ^ (s & 1), 0) for s in range(4)])

    seg_own = of_core(seg_parts, core)
    enc_own, enc_par = of_core(enc_parts, core), of_core(enc_parts, 1 - core)
    quarter = jnp.arange(4, dtype=jnp.int32)
    at_own = 2 * quarter + (core ^ (quarter % 2))
    at_par = 2 * quarter + ((1 - core) ^ (quarter % 2))
    tile_last = seg_parts.reshape(8, part)[:, -1]
    first_tile = jnp.sum((tile_last[None, :] < seg_own[:, :1]).astype(jnp.int32), axis=1)
    pairs = jnp.maximum(at_own - first_tile, 0) // 2
    meta = jnp.concatenate([at_own, at_par, pairs]).astype(jnp.int32)
    seg_keys = jnp.concatenate([jnp.full((part,), -1, jnp.int32), seg_parts.reshape(-1)])
    query_codes, key_codes = query_lanes(seg_own.reshape(-1)), key_lanes(seg_keys)
    cross_codes = key_lanes(jnp.concatenate([enc_own, enc_par]).reshape(-1))
    near = (
        buckets_of(jnp.arange(TILE, dtype=jnp.int32))[:, None] == jnp.arange(BUCKETS)[None, :]
    ).astype(F32)
    line = jnp.dot(near, table, precision=lax.Precision.HIGHEST).T.reshape(HEADS, 1, TILE)

    inputs = inputs_low.astype(F32)
    normed_self = normed(inputs, gain_self)
    kv_own = jnp.concatenate(
        [dot(normed_self, wk).astype(BF16), dot(normed_self, wv).astype(BF16)], axis=1
    )
    kv_par = exchange(kv_own, *CORE)
    query = dot(normed_self, wq).astype(BF16)
    mixed, self_lse, wholes = attend_gather(
        query, kv_own, kv_par, query_codes, key_codes, line,
        [k_cross, v_cross, o_self, q_cross, o_cross, wi_gate, wi_up, wo_ff],
    )
    ck, cv, wo, cq, co, w_gate, w_up, w_down = wholes
    cross_kv_own = jnp.concatenate(
        [dot(encoder, ck).astype(BF16), dot(encoder, cv).astype(BF16)], axis=1
    )
    cross_kv_par = exchange(cross_kv_own, *CORE)
    cross_kv_par, late_grad = lax.optimization_barrier((cross_kv_par, grad_out))
    out_parts = send_tokens(lambda micro, b: take(late_grad[:, 0, b * part : (b + 1) * part], micro, 0))
    after_self = inputs + dot(mixed, wo)
    normed_cross = normed(after_self, gain_cross)
    cross_query = dot(normed_cross, cq).astype(BF16)
    cross_mixed, cross_lse = attend_fast(
        meta, cross_query, cross_kv_own, cross_kv_par, query_codes, cross_codes, line, False
    )
    after_cross = after_self + dot(cross_mixed, co)
    normed_ff = normed(after_cross, gain_ff)
    gate, up_values = dot(normed_ff, w_gate), dot(normed_ff, w_up)
    hidden = gelu_mix(gate, up_values).astype(BF16)
    result = (after_cross + dot(hidden, w_down)).astype(BF16)
    block_out = return_tokens(result.reshape(4, part, width))

    out_low = settle(out_parts).reshape(4 * part, width)
    grad_result = out_low.astype(F32)
    grad_w_down = dot_weight(hidden, out_low)
    grad_hidden = dot_back(out_low, w_down)
    mix_value, mix_pull = jax.vjp(gelu_mix, gate, up_values)
    grad_gate, grad_up = (piece.astype(BF16) for piece in mix_pull(grad_hidden))
    grad_w_gate, grad_w_up = dot_weight(normed_ff, grad_gate), dot_weight(normed_ff, grad_up)
    grad_normed_ff = dot_back(grad_gate, w_gate) + dot_back(grad_up, w_up)
    ff_part, grad_gain_ff = norm_back(after_cross, gain_ff, grad_normed_ff)
    grad_after_cross = grad_result + ff_part
    cross_out_low = grad_after_cross.astype(BF16)
    grad_co = dot_weight(cross_mixed, cross_out_low)
    grad_cross_mixed = dot_back(cross_out_low, co).astype(BF16)
    grad_cross_query, cross_own, cross_par, unused, unused = attend_back_fast(
        meta, cross_query, cross_kv_own, cross_kv_par, query_codes, cross_codes, line,
        grad_cross_mixed, cross_mixed, cross_lse, False,
    )
    grad_cross_query, block_out = lax.optimization_barrier((grad_cross_query, block_out))
    cross_got = add_low(cross_own, exchange(cross_par, *CORE))
    grad_ck, grad_cv = dot_weight(encoder, cross_got[0]), dot_weight(encoder, cross_got[1])
    grad_encoder = (dot_back(cross_got[0], ck) + dot_back(cross_got[1], cv)).astype(BF16)
    grad_encoder = return_tokens(grad_encoder.reshape(4, enc_part, width)).astype(F32)
    grad_cq = dot_weight(normed_cross, grad_cross_query)
    grad_normed_cross = dot_back(grad_cross_query, cq)
    cross_part, grad_gain_cross = norm_back(after_self, gain_cross, grad_normed_cross)
    grad_after_self = grad_after_cross + cross_part
    self_out_low = grad_after_self.astype(BF16)
    grad_wo = dot_weight(mixed, self_out_low)
    grad_mixed = dot_back(self_out_low, wo).astype(BF16)
    grad_query, self_own, self_par, grad_line, grad_all = attend_back_fast(
        meta, query, kv_own, kv_par, query_codes, key_codes, line, grad_mixed, mixed, self_lse, True
    )
    grad_query, grad_encoder = lax.optimization_barrier((grad_query, grad_encoder))
    self_got = add_low(self_own, exchange(self_par, *CORE))
    grad_wq = dot_weight(normed_self, grad_query)
    grad_wk, grad_wv = dot_weight(normed_self, self_got[0]), dot_weight(normed_self, self_got[1])
    grad_normed_self = (
        dot_back(grad_query, wq) + dot_back(self_got[0], wk) + dot_back(self_got[1], wv)
    )
    self_part, grad_gain_self = norm_back(inputs, gain_self, grad_normed_self)
    grad_hidden_in = (grad_after_self + self_part).astype(BF16).reshape(4, part, width)

    grad_table = jnp.dot(near.T, grad_line.reshape(HEADS, TILE).T, precision=lax.Precision.HIGHEST)
    grad_far = jnp.sum((grad_all - grad_line).reshape(HEADS, TILE), axis=1)
    grad_table = grad_table.at[BUCKETS - 1].add(grad_far)
    small_grads = [piece.reshape(32, -1) for piece in (grad_gain_self, grad_gain_cross, grad_gain_ff)]
    small_grads = jnp.concatenate(small_grads + [grad_table.reshape(32, -1)], axis=1)
    small_grads = jnp.pad(small_grads, ((0, 0), (0, 2 * LANES - small_grads.shape[1])))
    small_grads = jnp.broadcast_to(small_grads[:, None], (32, 8, 2 * LANES)).reshape(256, 2 * LANES)
    order = [
        grad_wk, grad_wv, grad_w_gate, grad_w_up, grad_w_down, grad_ck, grad_cv, grad_cq, grad_co,
        grad_wo, grad_wq, small_grads,
    ]
    (
        grad_wk, grad_wv, grad_w_gate, grad_w_up, grad_w_down, grad_ck, grad_cv, grad_cq, grad_co,
        grad_wo, grad_wq, small_grads, grad_hidden_in,
    ) = scatter_grads(order, grad_hidden_in)
    small_grads = small_grads[0]
    return (
        block_out,
        grad_hidden_in.astype(F32)[:, None],
        grad_encoder,
        small_grads[:small_rows],
        grad_wq,
        grad_wk,
        grad_wv,
        grad_wo,
        small_grads[3 * small_rows : 3 * small_rows + rel_bias.shape[0]],
        small_grads[small_rows : 2 * small_rows],
        grad_cq,
        grad_ck,
        grad_cv,
        grad_co,
        small_grads[2 * small_rows : 3 * small_rows],
        grad_w_gate,
        grad_w_up,
        grad_w_down,
    )


def fits_fast(mesh):
    return mesh.shape["dp"] == 8 and mesh.shape["seq"] == 4


def solution(mesh):
    return jax.shard_map(
        fast_body if fits_fast(mesh) else general_body,
        mesh=mesh,
        in_specs=(
            P(None, "dp", "seq", None),
            P(None, "dp", "seq", None),
            P(None, "dp", "seq"),
            P(None, "dp", "seq"),
            P(None, "dp", "seq", None),
            P(("dp", "seq")),
            P(("dp", "seq"), None),
            P(("dp", "seq"), None),
            P(("dp", "seq"), None),
            P(("dp", "seq"), None),
            P(("dp", "seq")),
            P(("dp", "seq")),
            P(("dp", "seq"), None),
            P(("dp", "seq"), None),
            P(("dp", "seq"), None),
            P(("dp", "seq"), None),
            P(("dp", "seq")),
            P(("dp", "seq"), None),
            P(("dp", "seq"), None),
            P(("dp", "seq"), None),
        ),
        out_specs=(
            P(None, "dp", "seq", None),
            P(None, "dp", "seq", None),
            P(None, "dp", "seq", None),
            P(("dp", "seq")),
            P(("dp", "seq"), None),
            P(("dp", "seq"), None),
            P(("dp", "seq"), None),
            P(("dp", "seq"), None),
            P(("dp", "seq")),
            P(("dp", "seq")),
            P(("dp", "seq"), None),
            P(("dp", "seq"), None),
            P(("dp", "seq"), None),
            P(("dp", "seq"), None),
            P(("dp", "seq")),
            P(("dp", "seq"), None),
            P(("dp", "seq"), None),
            P(("dp", "seq"), None),
        ),
        check_vma=False,
    )
```

```python
import functools
import math

import jax
import jax.numpy as jnp
from jax import lax
from jax.experimental import pallas as pl
from jax.experimental.pallas import tpu as pltpu
from jax.sharding import PartitionSpec as P

HEADS = 16
HEAD_DIM = 64
BUCKETS = 32
MAX_DIST = 128


EPS = 1e-06
NEG = -1e30


def norm_rows(value, gain):
    return value * lax.rsqrt(jnp.mean(value * value, axis=-1, keepdims=True) + EPS) * gain


def bucket_edges():
    half = BUCKETS // 2
    return [math.ceil(half * (MAX_DIST / half) ** (step / half)) for step in range(1, half)]


def buckets_of(distance):
    half = BUCKETS // 2
    far = half + sum(((distance >= edge).astype(jnp.int32) for edge in bucket_edges()))
    return jnp.where(distance < half, distance, far)


def by_heads(values):
    return values.reshape(values.shape[0], values.shape[1], HEADS, HEAD_DIM)


def join_heads(values):
    return values.reshape(values.shape[0], values.shape[1], HEADS * HEAD_DIM)


def project(rows, weight_matrix):
    return jnp.dot(rows, weight_matrix, preferred_element_type=jnp.float32)


def project_back(grads, weight_matrix):
    return jnp.einsum("stn,kn->stk", grads, weight_matrix, preferred_element_type=jnp.float32)


def weight_grad(rows, grads):
    return jnp.einsum("stk,stn->kn", rows, grads, preferred_element_type=jnp.float32)


def gelu_mix(gate, up_values):
    return jax.nn.gelu(gate, approximate=True) * up_values


def scores_of(q_rows, keys, bias, allowed):
    scores = jnp.einsum("sqhd,skhd->shqk", q_rows, keys, preferred_element_type=jnp.float32) + bias
    return jnp.where(allowed[:, None], scores, NEG)


def attend(q_rows, keys, values, bias, allowed):
    scores = scores_of(q_rows, keys, bias, allowed)
    largest = jnp.max(scores, axis=-1, keepdims=True)
    raised = jnp.exp(scores - largest)
    total = jnp.sum(raised, axis=-1, keepdims=True)
    probs = raised / total
    mixed = jnp.einsum(
        "shqk,skhd->sqhd", probs.astype(jnp.bfloat16), values, preferred_element_type=jnp.float32
    )
    return (join_heads(mixed).astype(jnp.bfloat16), largest + jnp.log(total))


def attend_back(q_rows, keys, values, bias, allowed, log_total, grad_mixed):
    scores = scores_of(q_rows, keys, bias, allowed)
    probs = jnp.exp(scores - log_total)
    grad_probs = jnp.einsum(
        "sqhd,skhd->shqk", grad_mixed, values, preferred_element_type=jnp.float32
    )
    inner = jnp.sum(probs * grad_probs, axis=-1, keepdims=True)
    grad_scores = (probs * (grad_probs - inner)).astype(jnp.bfloat16)
    grad_query = jnp.einsum(
        "shqk,skhd->sqhd", grad_scores, keys, preferred_element_type=jnp.float32
    )
    grad_keys = jnp.einsum(
        "shqk,sqhd->skhd", grad_scores, q_rows, preferred_element_type=jnp.float32
    )
    grad_values = jnp.einsum(
        "shqk,sqhd->skhd",
        probs.astype(jnp.bfloat16),
        grad_mixed,
        preferred_element_type=jnp.float32,
    )
    return (join_heads(grad_query), join_heads(grad_keys), join_heads(grad_values), grad_scores)


def general_body(
    hidden_in,
    encoder_states,
    segments,
    enc_segments,
    grad_out,
    norm_self,
    q_self,
    k_self,
    v_self,
    o_self,
    rel_bias,
    norm_cross,
    q_cross,
    k_cross,
    v_cross,
    o_cross,
    norm_ff,
    wi_gate,
    wi_up,
    wo_ff,
):
    shards = (
        norm_self,
        q_self,
        k_self,
        v_self,
        o_self,
        rel_bias,
        norm_cross,
        q_cross,
        k_cross,
        v_cross,
        o_cross,
        norm_ff,
        wi_gate,
        wi_up,
        wo_ff,
    )
    micro_count = hidden_in.shape[0]
    rows_dev = hidden_in.shape[2]
    seg_whole, enc_seg_whole = (
        lax.all_gather(segments, "seq", axis=2, tiled=True),
        lax.all_gather(enc_segments, "seq", axis=2, tiled=True),
    )
    length = seg_whole.shape[2]
    positions = lax.axis_index("seq") * rows_dev + jnp.arange(rows_dev, dtype=jnp.int32)
    columns = jnp.arange(length, dtype=jnp.int32)
    distance = jnp.maximum(positions[:, None] - columns[None, :], 0)
    bucket_indicator = (
        buckets_of(distance)[None] == jnp.arange(BUCKETS, dtype=jnp.int32)[:, None, None]
    ).astype(jnp.bfloat16)
    causal = columns[None, :] <= positions[:, None]
    grad_shards = tuple((jnp.zeros(piece.shape, jnp.float32) for piece in shards))
    outputs, grad_inputs, grad_encoders = ([], [], [])
    for micro in range(micro_count):
        params = (
            lax.all_gather(shards[0], ("dp", "seq"), axis=0, tiled=True),
            lax.all_gather(shards[1], ("dp", "seq"), axis=0, tiled=True),
            lax.all_gather(shards[2], ("dp", "seq"), axis=0, tiled=True),
            lax.all_gather(shards[3], ("dp", "seq"), axis=0, tiled=True),
            lax.all_gather(shards[4], ("dp", "seq"), axis=0, tiled=True),
            lax.all_gather(shards[5], ("dp", "seq"), axis=0, tiled=True),
            lax.all_gather(shards[6], ("dp", "seq"), axis=0, tiled=True),
            lax.all_gather(shards[7], ("dp", "seq"), axis=0, tiled=True),
            lax.all_gather(shards[8], ("dp", "seq"), axis=0, tiled=True),
            lax.all_gather(shards[9], ("dp", "seq"), axis=0, tiled=True),
            lax.all_gather(shards[10], ("dp", "seq"), axis=0, tiled=True),
            lax.all_gather(shards[11], ("dp", "seq"), axis=0, tiled=True),
            lax.all_gather(shards[12], ("dp", "seq"), axis=0, tiled=True),
            lax.all_gather(shards[13], ("dp", "seq"), axis=0, tiled=True),
            lax.all_gather(shards[14], ("dp", "seq"), axis=0, tiled=True),
        )
        (
            gain_self,
            wq,
            wk,
            wv,
            wo,
            table_flat,
            gain_cross,
            cq,
            ck,
            cv,
            co,
            gain_ff,
            w_gate,
            w_up,
            w_down,
        ) = params
        bias = jnp.einsum(
            "pia,pw->wia",
            bucket_indicator,
            table_flat.reshape(BUCKETS, HEADS),
            preferred_element_type=jnp.float32,
        )
        inputs = hidden_in[micro].astype(jnp.float32)
        encoder = encoder_states[micro]
        seg_own = segments[micro]
        self_allowed = (seg_own[:, :, None] == seg_whole[micro][:, None, :]) & causal[None]
        cross_allowed = seg_own[:, :, None] == enc_seg_whole[micro][:, None, :]
        self_norm_scale = gain_self.astype(jnp.float32)
        cross_gain = gain_cross.astype(jnp.float32)
        ff_gain = gain_ff.astype(jnp.float32)
        normed_self = norm_rows(inputs, self_norm_scale).astype(jnp.bfloat16)
        query = project(normed_self, wq).astype(jnp.bfloat16)
        key_own = project(normed_self, wk).astype(jnp.bfloat16)
        value_own = project(normed_self, wv).astype(jnp.bfloat16)
        cross_key_own = project(encoder, ck).astype(jnp.bfloat16)
        cross_value_own = project(encoder, cv).astype(jnp.bfloat16)
        keys, values, cross_keys, cross_values = (
            lax.all_gather(key_own, "seq", axis=1, tiled=True),
            lax.all_gather(value_own, "seq", axis=1, tiled=True),
            lax.all_gather(cross_key_own, "seq", axis=1, tiled=True),
            lax.all_gather(cross_value_own, "seq", axis=1, tiled=True),
        )
        mixed, self_log_normalizer = attend(
            by_heads(query), by_heads(keys), by_heads(values), bias, self_allowed
        )
        after_self = inputs + project(mixed, wo)
        normed_cross = norm_rows(after_self, cross_gain).astype(jnp.bfloat16)
        cross_query = project(normed_cross, cq).astype(jnp.bfloat16)
        cross_mixed, cross_log = attend(
            by_heads(cross_query), by_heads(cross_keys), by_heads(cross_values), 0.0, cross_allowed
        )
        after_cross = after_self + project(cross_mixed, co)
        normed_ff = norm_rows(after_cross, ff_gain).astype(jnp.bfloat16)
        gate = project(normed_ff, w_gate)
        up_values = project(normed_ff, w_up)
        hidden = gelu_mix(gate, up_values).astype(jnp.bfloat16)
        result = after_cross + project(hidden, w_down)
        outputs.append(result.astype(jnp.bfloat16))
        params = (
            lax.all_gather(shards[0], ("dp", "seq"), axis=0, tiled=True),
            lax.all_gather(shards[1], ("dp", "seq"), axis=0, tiled=True),
            lax.all_gather(shards[2], ("dp", "seq"), axis=0, tiled=True),
            lax.all_gather(shards[3], ("dp", "seq"), axis=0, tiled=True),
            lax.all_gather(shards[4], ("dp", "seq"), axis=0, tiled=True),
            lax.all_gather(shards[5], ("dp", "seq"), axis=0, tiled=True),
            lax.all_gather(shards[6], ("dp", "seq"), axis=0, tiled=True),
            lax.all_gather(shards[7], ("dp", "seq"), axis=0, tiled=True),
            lax.all_gather(shards[8], ("dp", "seq"), axis=0, tiled=True),
            lax.all_gather(shards[9], ("dp", "seq"), axis=0, tiled=True),
            lax.all_gather(shards[10], ("dp", "seq"), axis=0, tiled=True),
            lax.all_gather(shards[11], ("dp", "seq"), axis=0, tiled=True),
            lax.all_gather(shards[12], ("dp", "seq"), axis=0, tiled=True),
            lax.all_gather(shards[13], ("dp", "seq"), axis=0, tiled=True),
            lax.all_gather(shards[14], ("dp", "seq"), axis=0, tiled=True),
        )
        (
            gain_self,
            wq,
            wk,
            wv,
            wo,
            table_flat,
            gain_cross,
            cq,
            ck,
            cv,
            co,
            gain_ff,
            w_gate,
            w_up,
            w_down,
        ) = params
        grad_result = grad_out[micro].astype(jnp.float32)
        out_low = grad_out[micro]
        grad_w_down = weight_grad(hidden, out_low)
        grad_hidden = project_back(out_low, w_down)
        mix_value, mix_pull = jax.vjp(gelu_mix, gate, up_values)
        grad_gate, grad_up = mix_pull(grad_hidden)
        grad_gate = grad_gate.astype(jnp.bfloat16)
        grad_up = grad_up.astype(jnp.bfloat16)
        gate_weight_gradient = weight_grad(normed_ff, grad_gate)
        grad_w_up = weight_grad(normed_ff, grad_up)
        grad_normed_ff = project_back(grad_gate, w_gate) + project_back(grad_up, w_up)
        norm_value, norm_pull = jax.vjp(norm_rows, after_cross, ff_gain)
        ff_part, grad_gain_ff = norm_pull(grad_normed_ff)
        grad_after_cross = grad_result + ff_part
        cross_out_low = grad_after_cross.astype(jnp.bfloat16)
        grad_co = weight_grad(cross_mixed, cross_out_low)
        grad_cross_mixed = project_back(cross_out_low, co).astype(jnp.bfloat16)
        grad_cross_query, cross_key_terms, cross_value_terms, cross_scores = attend_back(
            by_heads(cross_query),
            by_heads(cross_keys),
            by_heads(cross_values),
            0.0,
            cross_allowed,
            cross_log,
            by_heads(grad_cross_mixed),
        )
        grad_cross_key, grad_cross_value = (
            lax.psum_scatter(
                cross_key_terms.astype(jnp.bfloat16), "seq", scatter_dimension=1, tiled=True
            ).astype(jnp.float32),
            lax.psum_scatter(
                cross_value_terms.astype(jnp.bfloat16), "seq", scatter_dimension=1, tiled=True
            ).astype(jnp.float32),
        )
        grad_cross_key = grad_cross_key.astype(jnp.bfloat16)
        grad_cross_value = grad_cross_value.astype(jnp.bfloat16)
        cross_key_gradient = weight_grad(encoder, grad_cross_key)
        grad_cv = weight_grad(encoder, grad_cross_value)
        grad_encoders.append(project_back(grad_cross_key, ck) + project_back(grad_cross_value, cv))
        grad_cross_query = grad_cross_query.astype(jnp.bfloat16)
        grad_cq = weight_grad(normed_cross, grad_cross_query)
        grad_normed_cross = project_back(grad_cross_query, cq)
        norm_value, norm_pull = jax.vjp(norm_rows, after_self, cross_gain)
        cross_part, grad_gain_cross = norm_pull(grad_normed_cross)
        grad_after_self = grad_after_cross + cross_part
        self_out_low = grad_after_self.astype(jnp.bfloat16)
        grad_wo = weight_grad(mixed, self_out_low)
        grad_mixed = project_back(self_out_low, wo).astype(jnp.bfloat16)
        grad_query, key_terms, value_terms, self_attention_logits = attend_back(
            by_heads(query),
            by_heads(keys),
            by_heads(values),
            bias,
            self_allowed,
            self_log_normalizer,
            by_heads(grad_mixed),
        )
        grad_table = jnp.einsum(
            "dcma,uma->uc",
            self_attention_logits,
            bucket_indicator,
            preferred_element_type=jnp.float32,
        ).reshape(-1)
        grad_key, grad_value = (
            lax.psum_scatter(
                key_terms.astype(jnp.bfloat16), "seq", scatter_dimension=1, tiled=True
            ).astype(jnp.float32),
            lax.psum_scatter(
                value_terms.astype(jnp.bfloat16), "seq", scatter_dimension=1, tiled=True
            ).astype(jnp.float32),
        )
        grad_key = grad_key.astype(jnp.bfloat16)
        grad_value = grad_value.astype(jnp.bfloat16)
        grad_query = grad_query.astype(jnp.bfloat16)
        grad_wq = weight_grad(normed_self, grad_query)
        grad_wk = weight_grad(normed_self, grad_key)
        grad_wv = weight_grad(normed_self, grad_value)
        grad_normed_self = (
            project_back(grad_query, wq) + project_back(grad_key, wk) + project_back(grad_value, wv)
        )
        norm_value, norm_pull = jax.vjp(norm_rows, inputs, self_norm_scale)
        self_part, grad_gain_self = norm_pull(grad_normed_self)
        grad_inputs.append(grad_after_self + self_part)
        local = (
            grad_gain_self,
            grad_wq,
            grad_wk,
            grad_wv,
            grad_wo,
            grad_table,
            grad_gain_cross,
            grad_cq,
            cross_key_gradient,
            grad_cv,
            grad_co,
            grad_gain_ff,
            gate_weight_gradient,
            grad_w_up,
            grad_w_down,
        )
        summed = (
            lax.psum_scatter(local[0], ("dp", "seq"), scatter_dimension=0, tiled=True),
            lax.psum_scatter(local[1], ("dp", "seq"), scatter_dimension=0, tiled=True),
            lax.psum_scatter(local[2], ("dp", "seq"), scatter_dimension=0, tiled=True),
            lax.psum_scatter(local[3], ("dp", "seq"), scatter_dimension=0, tiled=True),
            lax.psum_scatter(local[4], ("dp", "seq"), scatter_dimension=0, tiled=True),
            lax.psum_scatter(local[5], ("dp", "seq"), scatter_dimension=0, tiled=True),
            lax.psum_scatter(local[6], ("dp", "seq"), scatter_dimension=0, tiled=True),
            lax.psum_scatter(local[7], ("dp", "seq"), scatter_dimension=0, tiled=True),
            lax.psum_scatter(local[8], ("dp", "seq"), scatter_dimension=0, tiled=True),
            lax.psum_scatter(local[9], ("dp", "seq"), scatter_dimension=0, tiled=True),
            lax.psum_scatter(local[10], ("dp", "seq"), scatter_dimension=0, tiled=True),
            lax.psum_scatter(local[11], ("dp", "seq"), scatter_dimension=0, tiled=True),
            lax.psum_scatter(local[12], ("dp", "seq"), scatter_dimension=0, tiled=True),
            lax.psum_scatter(local[13], ("dp", "seq"), scatter_dimension=0, tiled=True),
            lax.psum_scatter(local[14], ("dp", "seq"), scatter_dimension=0, tiled=True),
        )
        grad_shards = tuple((before + after for before, after in zip(grad_shards, summed)))
    return (jnp.stack(outputs), jnp.stack(grad_inputs), jnp.stack(grad_encoders)) + tuple(
        grad_shards
    )


TILE = 256
GROUP = 8
LANES = 128
AHEAD = 2
F32 = jnp.float32
BF16 = jnp.bfloat16


def contract(left, right, left_dim, right_dim):
    return lax.dot_general(
        left, right, (((left_dim,), (right_dim,)), ((), ())), preferred_element_type=F32
    )


def head_mask(head):
    lane = lax.broadcasted_iota(jnp.int32, (1, LANES), 1)
    keep = (lane < HEAD_DIM) if head % 2 == 0 else (lane >= HEAD_DIM)
    return keep.astype(F32).astype(BF16)


def bias_table(line):
    first = jnp.concatenate(
        [line if j == 0 else pltpu.roll(line, j, 1) for j in range(8)], axis=0
    )
    return [first if r == 0 else pltpu.roll(first, 8 * r, 1) for r in range(TILE // 8)]


def line_of(table):
    total = None
    for r in range(TILE // 8):
        part = table[8 * r : 8 * r + 8, :]
        part = part if r == 0 else pltpu.roll(part, TILE - 8 * r, 1)
        total = part if total is None else total + part
    line = total[0:1, :]
    for j in range(1, 8):
        line = line + pltpu.roll(total[j : j + 1, :], TILE - j, 1)
    return line


def positions():
    return (
        lax.broadcasted_iota(jnp.int32, (TILE, TILE), 0),
        lax.broadcasted_iota(jnp.int32, (TILE, TILE), 1),
    )


def pair_lanes(head):
    return slice((head // 2) * LANES, (head // 2 + 1) * LANES)


def head_rows(head):
    return slice(head * HEAD_DIM, (head + 1) * HEAD_DIM)


def tile_places():
    core = lax.axis_index("dp") % 2
    own = [2 * s + (core + s) % 2 for s in range(4)]
    par = [2 * s + (1 - core + s) % 2 for s in range(4)]
    return own + par + [tile // 2 for tile in own]


def place_tiles(causal, meta_ref, own, par):
    moves = []
    count = own.shape[0] // TILE
    places = tile_places() if causal and meta_ref is None else meta_ref
    for ref, base in ((own, 0), (par, count)):
        for s in range(count):
            target = places[base + s] + 1 if causal else base + s
            moves.append((ref, s, target))
    return moves


def rows_at(tile):
    return pl.ds(pl.multiple_of(tile * TILE, TILE), TILE)


def fill_tables(line_ref, tab, adj):
    for h in range(line_ref.shape[0]):
        line = line_ref[h]
        far = line[:, TILE - 1 : TILE]
        for r, rows in enumerate(bias_table(line - far)):
            adj[h, 8 * r : 8 * r + 8, :] = rows
        k_pos, q_pos = positions()
        table = adj[h]
        tab[h] = jnp.where(k_pos <= q_pos, table, NEG)
        adj[h] = jnp.where(k_pos > q_pos, table, 0.0)


BIAS_LANE, EMPTY_LANE = 16, 17


def lane_of():
    return lax.broadcasted_iota(jnp.int32, (1, LANES), 1) % HEAD_DIM


def by_parity(lanes):
    even = (jnp.arange(LANES) < HEAD_DIM)[None, :]
    zero = jnp.zeros_like(lanes)
    return jnp.stack([jnp.where(even, zero, lanes), jnp.where(even, lanes, zero)])


def key_lanes(codes):
    lane = jnp.arange(LANES, dtype=jnp.int32)[None, :] % HEAD_DIM
    documents = (codes[:, None] == lane) & (lane < BIAS_LANE)
    ones = (lane >= BIAS_LANE) & (lane < EMPTY_LANE)
    return by_parity((documents | ones | ((lane == EMPTY_LANE) & (codes[:, None] < 0))).astype(BF16))


def query_lanes(codes):
    lane = jnp.arange(LANES, dtype=jnp.int32)[None, :] % HEAD_DIM
    other = ((codes[:, None] != lane) & (lane < BIAS_LANE)) | (lane == EMPTY_LANE)
    return by_parity(jnp.where(other, NEG, 0.0).astype(BF16))


def with_lanes(head, rows, lanes):
    return rows * head_mask(head) + lanes


def far_lane(head, line_ref):
    lane = lax.broadcasted_iota(jnp.int32, (1, LANES), 1)
    at = BIAS_LANE + (HEAD_DIM if head % 2 == 0 else 0)
    return jnp.where(lane == at, line_ref[head][:, TILE - 1 : TILE], 0.0).astype(BF16)


def query_with_lanes(causal, h, q_ref, qext_ref, line_ref):
    rows = with_lanes(h, q_ref[:, pair_lanes(h)], qext_ref[h % 2])
    return rows + far_lane(h, line_ref) if causal else rows


def visit_pairs(causal, meta_ref, region):
    if not causal:
        region(0, False)
        return
    i = pl.program_id(1)
    if meta_ref is None:
        own = 2 * i + (lax.axis_index("dp") + i) % 2
        pairs = own // 2
    else:
        own, pairs = meta_ref[i], meta_ref[8 + i]
    region(own, True)
    lax.fori_loop(0, pairs, lambda j, c: (region(own - 2 * (j + 1), False), c)[1], 0)


def biased(scores, causal, near, j, h, tab, adj):
    if causal and near:
        return scores + (tab[h] if j else adj[h])
    return scores


def attend_kernel(causal, meta_ref, q_ref, ko, vo, kp, vp, qext_ref, kext_ref, line_ref,
                  o_ref, lse_ref, kb, vt, qx, tab, adj, m_s, l_s, acc):
    @pl.when(pl.program_id(1) == 0)
    def _():
        for ref, s, target in place_tiles(causal, meta_ref, ko, kp):
            for h in range(GROUP):
                kb[h, rows_at(target), :] = with_lanes(
                    h, ref[s * TILE : (s + 1) * TILE, pair_lanes(h)], kext_ref[h % 2, rows_at(target), :]
                )
        for ref, s, target in place_tiles(causal, meta_ref, vo, vp):
            vt[target] = ref[s * TILE : (s + 1) * TILE, :].T
        if causal:
            for h in range(GROUP):
                kb[h, 0:TILE, :] = kext_ref[h % 2, 0:TILE, :]
            vt[0] = jnp.zeros(vt.shape[1:], BF16)
            fill_tables(line_ref, tab, adj)

    for h in range(GROUP):
        qx[h] = query_with_lanes(causal, h, q_ref, qext_ref, line_ref)
    m_s[...] = jnp.full(m_s.shape, NEG, F32)
    l_s[...] = jnp.zeros(l_s.shape, F32)
    acc[...] = jnp.zeros(acc.shape, F32)

    def region(tile, near):
        def scores_of_head(h):
            return [contract(kb[h, rows_at(tile + j), :], qx[h], 1, 1) for j in range(2)]

        ready = [scores_of_head(h) for h in range(AHEAD)]
        for h in range(GROUP):
            if h + AHEAD < GROUP:
                ready.append(scores_of_head(h + AHEAD))
            scores = [biased(ready[h][j], causal, near, j, h, tab, adj) for j in range(2)]
            before = m_s[h : h + 1, :]
            largest = jnp.maximum(
                before, jnp.max(jnp.maximum(scores[0], scores[1]), axis=0, keepdims=True)
            )
            raised = [jnp.exp(piece - largest) for piece in scores]
            scale = jnp.exp(before - largest)
            m_s[h : h + 1, :] = largest
            l_s[h : h + 1, :] = l_s[h : h + 1, :] * scale + jnp.sum(
                raised[0] + raised[1], axis=0, keepdims=True
            )
            rows = head_rows(h)
            mixed = contract(vt[tile, rows, :], raised[0].astype(BF16), 1, 0) + contract(
                vt[tile + 1, rows, :], raised[1].astype(BF16), 1, 0
            )
            acc[rows, :] = acc[rows, :] * scale + mixed

    visit_pairs(causal, meta_ref, region)
    for h in range(GROUP):
        rows = head_rows(h)
        acc[rows, :] = acc[rows, :] / l_s[h : h + 1, :]
        lse_ref[0, h : h + 1, :] = m_s[h : h + 1, :] + jnp.log(l_s[h : h + 1, :])
    o_ref[...] = acc[...].T.astype(BF16)


def attend_back_kernel(causal, meta_ref, q_ref, ko, vo, kp, vp, qext_ref, kext_ref, line_ref,
                       do_ref, o_ref, lse_ref, dq_ref, own_ref, par_ref, gline_ref, gall_ref,
                       kb, vb, kt, qm, dm, qx, d_s, tab, adj, dq_acc, dk_acc, dv_acc, gt, gall):
    i = pl.program_id(1)
    group = q_ref.shape[1] // HEAD_DIM

    @pl.when(i == 0)
    def _():
        for ref, s, target in place_tiles(causal, meta_ref, ko, kp):
            for h in range(group):
                kb[h, rows_at(target), :] = with_lanes(
                    h, ref[s * TILE : (s + 1) * TILE, pair_lanes(h)], kext_ref[h % 2, rows_at(target), :]
                )
        for ref, s, target in place_tiles(causal, meta_ref, vo, vp):
            vb[rows_at(target), :] = ref[s * TILE : (s + 1) * TILE, :]
        for ref, s, target in place_tiles(causal, meta_ref, ko, kp):
            turned = ref[s * TILE : (s + 1) * TILE, :].T
            for h in range(group):
                kt[target, h, 0:HEAD_DIM, :] = turned[head_rows(h), :]
        dk_acc[...] = jnp.zeros(dk_acc.shape, F32)
        dv_acc[...] = jnp.zeros(dv_acc.shape, F32)
        if causal:
            for h in range(group):
                kb[h, 0:TILE, :] = kext_ref[h % 2, 0:TILE, :]
            vb[0:TILE, :] = jnp.zeros((TILE, vb.shape[1]), BF16)
            kt[0] = jnp.zeros(kt.shape[1:], BF16)
            for t in range(kt.shape[0]):
                for h in range(group):
                    kt[t, h, HEAD_DIM:, :] = jnp.ones((kt.shape[2] - HEAD_DIM, TILE), BF16)
            gt[...] = jnp.zeros(gt.shape, F32)
            gall[...] = jnp.zeros(gall.shape, F32)
            fill_tables(line_ref, tab, adj)

    for h in range(group):
        lanes = pair_lanes(h)
        pair, rows = h // 2, slice((h % 2) * TILE, (h % 2 + 1) * TILE)
        qm[pair, rows, :] = q_ref[:, lanes] * head_mask(h)
        dm[pair, rows, :] = do_ref[:, lanes] * head_mask(h)
        qx[h] = query_with_lanes(causal, h, q_ref, qext_ref, line_ref)
    both = jnp.concatenate([head_mask(0)] * 8 + [head_mask(1)] * 8, axis=0)
    for pair in range(group // 2):
        lanes = pair_lanes(2 * pair)
        product = do_ref[:, lanes].astype(F32) * o_ref[:, lanes].astype(F32)
        high = product.astype(BF16)
        low = (product - high.astype(F32)).astype(BF16)
        inner = contract(both, high, 1, 1) + contract(both, low, 1, 1)
        d_s[2 * pair : 2 * pair + 1, :] = inner[0:1, :]
        d_s[2 * pair + 1 : 2 * pair + 2, :] = inner[8:9, :]
    dq_acc[...] = jnp.zeros(dq_acc.shape, F32)

    def region(tile, near):
        def products_of_head(h):
            half = slice((h % 2) * TILE, (h % 2 + 1) * TILE)
            return [
                (
                    contract(kb[h, rows_at(tile + j), :], qx[h], 1, 1),
                    contract(vb[rows_at(tile + j), pair_lanes(h)], dm[h // 2, half, :], 1, 1),
                )
                for j in range(2)
            ]

        ready = [products_of_head(h) for h in range(AHEAD)]
        probs_low, grads_low = {}, {}
        for h in range(group):
            if h + AHEAD < group:
                ready.append(products_of_head(h + AHEAD))
            back = None
            for j in range(2):
                scores, grad_probs = ready[h][j]
                probs = jnp.exp(biased(scores, causal, near, j, h, tab, adj) - lse_ref[0, h : h + 1, :])
                grads = probs * (grad_probs - d_s[h : h + 1, :])
                low = grads.astype(BF16)
                probs_low[h, j], grads_low[h, j] = probs.astype(BF16), low
                if causal and near:
                    rounded = low.astype(F32)
                    if j == 0:
                        k_pos, q_pos = positions()
                        rounded = jnp.where(k_pos > q_pos, rounded, 0.0)
                    gt[h] += rounded
                part = contract(kt[tile + j, h], low, 1, 0)
                back = part if back is None else back + part
            dq_acc[head_rows(h), :] += back[0:HEAD_DIM, :]
            if causal:
                gall[h : h + 1, :] += back[HEAD_DIM : HEAD_DIM + 1, :]
            if h % 2 == 1:
                pair = h // 2
                lanes = pair_lanes(h)
                for j in range(2):
                    dv_acc[rows_at(tile + j), lanes] += contract(
                        jnp.concatenate([probs_low[h - 1, j], probs_low[h, j]], axis=1), dm[pair], 1, 0
                    )
                    dk_acc[rows_at(tile + j), lanes] += contract(
                        jnp.concatenate([grads_low[h - 1, j], grads_low[h, j]], axis=1), qm[pair], 1, 0
                    )

    visit_pairs(causal, meta_ref, region)
    dq_ref[...] = dq_acc[...].T.astype(BF16)

    @pl.when(i == pl.num_programs(1) - 1)
    def _():
        for j, total in enumerate((dk_acc, dv_acc)):
            for ref, s, target in place_tiles(causal, meta_ref, own_ref.at[j], par_ref.at[j]):
                ref[s * TILE : (s + 1) * TILE, :] = total[rows_at(target), :].astype(BF16)
        for h in range(group):
            if causal:
                gline_ref[h] = line_of(gt[h])
                gall_ref[h] = gall[h : h + 1, :]
            else:
                gline_ref[h] = jnp.zeros((1, TILE), F32)
                gall_ref[h] = jnp.zeros((1, TILE), F32)


VMEM_LIMIT = 60 * 1024 * 1024


def attention_specs(own_rows, par_rows, keys, group=GROUP):
    groups = HEADS // group
    lanes = group * HEAD_DIM
    return [
        pl.BlockSpec((TILE, lanes), lambda g, i, meta: (i, g)),
        pl.BlockSpec((own_rows, lanes), lambda g, i, meta: (0, g)),
        pl.BlockSpec((own_rows, lanes), lambda g, i, meta: (0, groups + g)),
        pl.BlockSpec((par_rows, lanes), lambda g, i, meta: (0, g)),
        pl.BlockSpec((par_rows, lanes), lambda g, i, meta: (0, groups + g)),
        pl.BlockSpec((2, TILE, LANES), lambda g, i, meta: (0, i, 0)),
        pl.BlockSpec((2, keys, LANES), lambda g, i, meta: (0, 0, 0)),
        pl.BlockSpec((group, 1, TILE), lambda g, i, meta: (g, 0, 0)),
    ]


def without_meta(spec):
    return pl.BlockSpec(spec.block_shape, lambda g, i: spec.index_map(g, i, None))


def attention_scratch(keys, lanes, table):
    return [
        pltpu.VMEM((GROUP, keys, LANES), BF16),
        pltpu.VMEM((keys // TILE, lanes, TILE), BF16),
        pltpu.VMEM((GROUP, TILE, LANES), BF16),
        pltpu.VMEM(table, F32),
        pltpu.VMEM(table, F32),
        pltpu.VMEM((8, TILE), F32),
        pltpu.VMEM((8, TILE), F32),
        pltpu.VMEM((lanes, TILE), F32),
    ]


def attend_fast(meta, query, kv_own, kv_par, qext, kext, line, causal):
    tokens, width = query.shape
    own_rows, par_rows, keys = kv_own.shape[0], kv_par.shape[0], kext.shape[1]
    groups, lanes = HEADS // GROUP, GROUP * HEAD_DIM
    table = (GROUP, TILE, TILE) if causal else (1, 8, LANES)
    return pl.pallas_call(
        functools.partial(attend_kernel, causal),
        grid_spec=pltpu.PrefetchScalarGridSpec(
            num_scalar_prefetch=1,
            grid=(groups, tokens // TILE),
            in_specs=attention_specs(own_rows, par_rows, keys),
            out_specs=[
                pl.BlockSpec((TILE, lanes), lambda g, i, meta: (i, g)),
                pl.BlockSpec((1, GROUP, TILE), lambda g, i, meta: (g, 0, i)),
            ],
            scratch_shapes=attention_scratch(keys, lanes, table),
        ),
        out_shape=[
            jax.ShapeDtypeStruct((tokens, width), BF16),
            jax.ShapeDtypeStruct((groups, GROUP, tokens), F32),
        ],
        compiler_params=pltpu.CompilerParams(vmem_limit_bytes=VMEM_LIMIT),
        cost_estimate=pl.CostEstimate(
            flops=tokens * keys * width * 4, bytes_accessed=4 * (tokens + keys) * width,
            transcendentals=tokens * keys * HEADS // 2,
        ),
        name="attend_self" if causal else "attend_cross",
    )(meta, query, kv_own, kv_own, kv_par, kv_par, qext, kext, line)


def back_scratch(keys, group, causal):
    lanes = group * HEAD_DIM
    table = (group, TILE, TILE) if causal else (1, 8, LANES)
    return [
        pltpu.VMEM((group, keys, LANES), BF16),
        pltpu.VMEM((keys, lanes), BF16),
        pltpu.VMEM((keys // TILE, group, HEAD_DIM + (16 if causal else 0), TILE), BF16),
        pltpu.VMEM((group // 2, 2 * TILE, LANES), BF16),
        pltpu.VMEM((group // 2, 2 * TILE, LANES), BF16),
        pltpu.VMEM((group, TILE, LANES), BF16),
        pltpu.VMEM((8, TILE), F32),
        pltpu.VMEM(table, F32),
        pltpu.VMEM(table, F32),
        pltpu.VMEM((lanes, TILE), F32),
        pltpu.VMEM((keys, lanes), F32),
        pltpu.VMEM((keys, lanes), F32),
        pltpu.VMEM(table, F32),
        pltpu.VMEM((8, TILE), F32),
    ]


def attend_back_fast(meta, query, kv_own, kv_par, qext, kext, line, grad_mixed, mixed, lse, causal):
    tokens, width = query.shape
    own_rows, par_rows, keys = kv_own.shape[0], kv_par.shape[0], kext.shape[1]
    groups, lanes = HEADS // GROUP, GROUP * HEAD_DIM
    table = (GROUP, TILE, TILE) if causal else (1, 8, LANES)
    block = pl.BlockSpec((TILE, lanes), lambda g, i, meta: (i, g))
    line_spec = pl.BlockSpec((GROUP, 1, TILE), lambda g, i, meta: (g, 0, 0))
    return pl.pallas_call(
        functools.partial(attend_back_kernel, causal),
        grid_spec=pltpu.PrefetchScalarGridSpec(
            num_scalar_prefetch=1,
            grid=(groups, tokens // TILE),
            in_specs=attention_specs(own_rows, par_rows, keys)
            + [block, block, pl.BlockSpec((1, GROUP, TILE), lambda g, i, meta: (g, 0, i))],
            out_specs=[
                block,
                pl.BlockSpec((2, own_rows, lanes), lambda g, i, meta: (0, 0, g)),
                pl.BlockSpec((2, par_rows, lanes), lambda g, i, meta: (0, 0, g)),
                line_spec,
                line_spec,
            ],
            scratch_shapes=back_scratch(keys, GROUP, causal),
        ),
        out_shape=[
            jax.ShapeDtypeStruct((tokens, width), BF16),
            jax.ShapeDtypeStruct((2, own_rows, width), BF16),
            jax.ShapeDtypeStruct((2, par_rows, width), BF16),
            jax.ShapeDtypeStruct((HEADS, 1, TILE), F32),
            jax.ShapeDtypeStruct((HEADS, 1, TILE), F32),
        ],
        compiler_params=pltpu.CompilerParams(vmem_limit_bytes=VMEM_LIMIT),
        cost_estimate=pl.CostEstimate(
            flops=tokens * keys * width * 10, bytes_accessed=10 * (tokens + keys) * width,
            transcendentals=tokens * keys * HEADS // 2,
        ),
        name="attend_self_back" if causal else "attend_cross_back",
    )(meta, query, kv_own, kv_own, kv_par, kv_par, qext, kext, line, grad_mixed, mixed, lse)


AXES = ("dp", "seq")


def exchange(value, dp_bit, seq_bit):
    pairs = [
        (dp * 4 + seq, (dp ^ dp_bit) * 4 + (seq ^ seq_bit)) for dp in range(8) for seq in range(4)
    ]
    return lax.ppermute(value, AXES, pairs)


CORE, Z_LOW, Z_HIGH, X, Y = (1, 0), (2, 0), (4, 0), (0, 1), (0, 2)


def move_pairs(a, b):
    pairs = []
    for z in range(4):
        for core in range(2):
            for s in range(4):
                micro, half_core = (s >> 1) ^ a, (s & 1) ^ b
                pairs.append(((2 * z + core) * 4 + s, (2 * z + half_core) * 4 + 2 * core + micro))
    return pairs


ROUNDS = ((0, 0), (0, 1), (1, 0), (1, 1))


def take(value, index, axis):
    return lax.dynamic_index_in_dim(value, index, axis, keepdims=False)


MESH = pl.DeviceIdType.MESH


class Links:
    def __init__(self):
        dp, seq = lax.axis_index("dp"), lax.axis_index("seq")
        self.seq = seq
        self.z, self.core, self.y, self.x = dp // 2, dp % 2, seq // 2, seq % 2
        self.at_z = [{"dp": ((self.z + k) % 4) * 2 + self.core, "seq": seq} for k in (1, 2, 3)]
        self.at_x = {"dp": dp, "seq": seq + 1 - 2 * self.x}
        self.at_y = {"dp": dp, "seq": seq + 2 - 4 * self.y}
        self.at_core = {"dp": dp + 1 - 2 * self.core, "seq": seq}

    def at_plane(self, core, seq):
        return {"dp": 2 * self.z + core, "seq": seq}

    def greet(self):
        partners = list(self.at_z)
        for flip in (0, 1):
            for k in range(4):
                if flip or k:
                    core = 1 - self.core if flip else self.core
                    partners.append(self.at_plane(core, (self.seq + k) % 4))
        barrier = pltpu.get_barrier_semaphore()
        for partner in partners:
            pl.semaphore_signal(barrier, inc=1, device_id=partner, device_id_type=MESH)
        pl.semaphore_wait(barrier, len(partners))


def remote(source, target, send_sem, recv_sem, device):
    return pltpu.make_async_remote_copy(
        src_ref=source,
        dst_ref=target,
        send_sem=send_sem,
        recv_sem=recv_sem,
        device_id=device,
        device_id_type=MESH,
    )


def move_tokens(links, sources, targets, parts, local_sem, send_sem, recv_sem):
    waits = []
    for r, (a, b) in enumerate(ROUNDS):
        micro = 1 - links.y if a else links.y
        core = 1 - links.x if b else links.x
        chip = 2 * links.core + micro
        stays = (core == links.core) & (chip == links.seq)
        for n, (source, target, part) in enumerate(zip(sources, targets, parts)):
            if part is None:
                piece = source.at[micro]
            else:
                piece = source.at[micro, 0, pl.ds(b * part, part)]
            slot = target.at[links.seq]
            here = pltpu.make_async_copy(piece, slot, local_sem.at[r, n])
            away = remote(piece, slot, send_sem.at[r, n], recv_sem.at[r, n], links.at_plane(core, chip))

            @pl.when(stays)
            def _(here=here):
                here.start()

            @pl.when(jnp.logical_not(stays))
            def _(away=away):
                away.start()

            waits.append((stays, here, away))

    def finish():
        for stays, here, away in waits:
            @pl.when(stays)
            def _(here=here):
                here.wait()

            @pl.when(jnp.logical_not(stays))
            def _(away=away):
                away.wait()

    return finish


class Gather:
    def __init__(self, links, shards, wholes, local_sem, send_sem, recv_sem):
        self.links, self.shards, self.wholes = links, shards, wholes
        self.along_z = [len(shard.shape) == 3 for shard in shards]
        self.local_sem, self.send_sem, self.recv_sem = local_sem, send_sem, recv_sem

    def copy(self, w, slot, source, target, device):
        return remote(source, target, self.send_sem.at[w, slot], self.recv_sem.at[w, slot], device)

    def copies(self, stage, w):
        links, whole = self.links, self.wholes[w]
        z, core, y, x = links.z, links.core, links.y, links.x
        half = whole.shape[-1] // 2
        left, right = pl.ds(0, half), pl.ds(half, half)
        if stage == 0:
            own = whole.at[z, core, y, x]
            return [self.copy(w, k, self.shards[w], own, links.at_z[k]) for k in range(3)]
        if stage == 1:
            one, two = whole.at[:, core, y, x, :, left], whole.at[:, core, y, x, :, right]
            if self.along_z[w]:
                shard = self.shards[w]
                return [
                    self.copy(w, 3, shard.at[:, :, left], one, links.at_x),
                    self.copy(w, 4, shard.at[:, :, right], two, links.at_y),
                ]
            return [self.copy(w, 3, one, one, links.at_x), self.copy(w, 4, two, two, links.at_y)]
        if stage == 2:
            one, two = whole.at[:, core, y, :, :, left], whole.at[:, core, :, x, :, right]
            return [self.copy(w, 5, one, one, links.at_y), self.copy(w, 6, two, two, links.at_x)]
        both = whole.at[:, core]
        return [self.copy(w, 7, both, both, links.at_core)]

    def local(self, w):
        links = self.links
        z = slice(None) if self.along_z[w] else links.z
        own = self.wholes[w].at[z, links.core, links.y, links.x]
        return pltpu.make_async_copy(self.shards[w], own, self.local_sem.at[w])

    def begin(self):
        for w in range(len(self.shards)):
            self.local(w).start()
            for copy in self.copies(1 if self.along_z[w] else 0, w):
                copy.start()

    def advance(self, stage, w):
        if stage == (2 if self.along_z[w] else 1):
            self.local(w).wait()
        for copy in self.copies(stage - 1, w):
            copy.wait_recv()
        for copy in self.copies(stage, w):
            copy.start()

    def steps(self):
        count = len(self.shards)
        order = []
        for t in range(count + 2):
            order += [(stage, t - stage + 1) for stage in (1, 2, 3) if 0 <= t - stage + 1 < count]
        return order

    def end(self):
        for w in range(len(self.shards)):
            for copy in self.copies(3, w):
                copy.wait_recv()
            for stage in range(1 if self.along_z[w] else 0, 4):
                for copy in self.copies(stage, w):
                    copy.wait_send()


def gather_kernel(count, later, parts, *refs):
    tokens = len(parts)
    shards, early, moved = refs[:count], refs[count : count + later], refs[count + later : count + later + tokens]
    refs = refs[count + later + tokens :]
    wholes, lines, settled = refs[:count], refs[count : count + later], refs[count + later : count + later + tokens]
    refs = refs[count + later + tokens :]
    local_sem, send_sem, recv_sem, z_local, z_send, z_recv, move_local, move_send, move_recv = refs
    links = Links()
    links.greet()
    gather = Gather(links, shards, wholes, local_sem, send_sem, recv_sem)
    gather.begin()
    finish = move_tokens(links, moved, settled, parts, move_local, move_send, move_recv)
    waits = []
    for w in range(later):
        own = lines[w].at[links.z]
        here = pltpu.make_async_copy(early[w], own, z_local.at[w])
        here.start()
        waits.append(here)
        for k in range(3):
            away = remote(early[w], own, z_send.at[w, k], z_recv.at[w, k], links.at_z[k])
            away.start()
            waits.append(away)
    for stage, w in gather.steps():
        gather.advance(stage, w)
    gather.end()
    finish()
    for copy in waits:
        copy.wait()


def attend_gather_kernel(count, q_ref, ko, vo, kp, vp, qext_ref, kext_ref, line_ref, *refs):
    sources, (o_ref, lse_ref), refs = refs[:count], refs[count : count + 2], refs[count + 2 :]
    wholes, scratch = refs[:count], refs[count : count + 8]
    shards = refs[count + 8 : 2 * count + 8]
    load_sem, local_sem, send_sem, recv_sem = refs[2 * count + 8 :]
    links = Links()
    gather = Gather(links, shards, wholes, local_sem, send_sem, recv_sem)
    step = pl.program_id(0) * pl.num_programs(1) + pl.program_id(1)
    total = (HEADS * HEAD_DIM // q_ref.shape[1]) * 4
    @pl.when(step == 0)
    def _():
        links.greet()
        loads = [pltpu.make_async_copy(sources[w], shards[w], load_sem.at[w]) for w in range(count)]
        for load in loads:
            load.start()
        for load in loads:
            load.wait()
        gather.begin()

    attend_kernel(True, None, q_ref, ko, vo, kp, vp, qext_ref, kext_ref, line_ref, o_ref, lse_ref, *scratch)
    for n in range(total):
        todo = [item for at, item in GATHER_PLAN if at == n]
        if todo or n == total - 1:
            @pl.when(step == n)
            def _(todo=todo, n=n):
                for stage, w in todo:
                    gather.advance(stage, w)
                if n == total - 1:
                    gather.end()


GATHER_PLAN = (
    (0, (1, 3)), (1, (2, 0)), (1, (1, 4)), (2, (2, 1)), (2, (1, 5)), (3, (2, 2)), (3, (1, 6)), (4, (1, 7)),
    (5, (2, 3)), (5, (3, 0)), (6, (2, 4)), (6, (2, 5)), (7, (3, 1)), (7, (2, 6)), (7, (2, 7)), (7, (3, 2)),
    (7, (3, 3)), (7, (3, 4)), (7, (3, 5)), (7, (3, 6)), (7, (3, 7)),
)


def attend_gather(query, kv_own, kv_par, qext, kext, line, shards):
    tokens, width = query.shape
    own_rows, par_rows, keys = kv_own.shape[0], kv_par.shape[0], kext.shape[1]
    groups, lanes, count = HEADS // GROUP, GROUP * HEAD_DIM, len(shards)
    table = (GROUP, TILE, TILE)
    whole = pl.BlockSpec(memory_space=pl.ANY)
    outs = pl.pallas_call(
        functools.partial(attend_gather_kernel, count),
        grid=(groups, tokens // TILE),
        in_specs=[without_meta(spec) for spec in attention_specs(own_rows, par_rows, keys)] + [whole] * count,
        out_specs=[
            pl.BlockSpec((TILE, lanes), lambda g, i: (i, g)),
            pl.BlockSpec((1, GROUP, TILE), lambda g, i: (g, 0, i)),
        ]
        + [whole] * count,
        scratch_shapes=attention_scratch(keys, lanes, table)
        + [pltpu.VMEM(shard.shape, BF16) for shard in shards]
        + [
            pltpu.SemaphoreType.DMA((count,)),
            pltpu.SemaphoreType.DMA((count,)),
            pltpu.SemaphoreType.DMA((count, 8)),
            pltpu.SemaphoreType.DMA((count, 8)),
        ],
        out_shape=[
            jax.ShapeDtypeStruct((tokens, width), BF16),
            jax.ShapeDtypeStruct((groups, GROUP, tokens), F32),
        ]
        + [jax.ShapeDtypeStruct((4, 2, 2, 2, *shard.shape[-2:]), BF16) for shard in shards],
        compiler_params=pltpu.CompilerParams(
            vmem_limit_bytes=VMEM_LIMIT, collective_id=2, has_side_effects=True
        ),
        cost_estimate=pl.CostEstimate(
            flops=tokens * keys * width * 4, bytes_accessed=4 * (tokens + keys) * width,
            transcendentals=tokens * keys * HEADS // 2,
        ),
        name="attend_gather",
    )(query, kv_own, kv_own, kv_par, kv_par, qext, kext, line, *shards)
    return outs[0], outs[1], [whole.reshape(-1, whole.shape[-1]) for whole in outs[2:]]


def gather_weights(shards, early, moved):
    count, later, tokens = len(shards), len(early), len(moved)
    sent = sum(shard.size for shard in shards) * 2
    parts = [None if value.ndim == 3 else value.shape[2] // 2 for value in moved]
    settled = [
        jax.ShapeDtypeStruct((4, value.shape[1] if part is None else part, value.shape[-1]), BF16)
        for value, part in zip(moved, parts)
    ]
    outs = pl.pallas_call(
        functools.partial(gather_kernel, count, later, parts),
        in_specs=[pl.BlockSpec(memory_space=pltpu.VMEM)] * (count + later)
        + [pl.BlockSpec(memory_space=pl.ANY)] * tokens,
        out_specs=[pl.BlockSpec(memory_space=pl.ANY)] * (count + later + tokens),
        out_shape=[jax.ShapeDtypeStruct((4, 2, 2, 2, *shard.shape), BF16) for shard in shards]
        + [jax.ShapeDtypeStruct((4, *shard.shape), BF16) for shard in early]
        + settled,
        scratch_shapes=[
            pltpu.SemaphoreType.DMA((count,)),
            pltpu.SemaphoreType.DMA((count, 8)),
            pltpu.SemaphoreType.DMA((count, 8)),
            pltpu.SemaphoreType.DMA((later,)),
            pltpu.SemaphoreType.DMA((later, 3)),
            pltpu.SemaphoreType.DMA((later, 3)),
            pltpu.SemaphoreType.DMA((4, tokens)),
            pltpu.SemaphoreType.DMA((4, tokens)),
            pltpu.SemaphoreType.DMA((4, tokens)),
        ],
        compiler_params=pltpu.CompilerParams(
            vmem_limit_bytes=VMEM_LIMIT, collective_id=0, has_side_effects=True
        ),
        cost_estimate=pl.CostEstimate(flops=0, transcendentals=0, bytes_accessed=500 * sent),
        name="gather_weights",
    )(*shards, *early, *moved)
    wholes = [whole.reshape(-1, whole.shape[-1]) for whole in outs[:count]]
    return wholes, outs[count : count + later], outs[count + later :]


def add_low(first, second):
    return (first.astype(F32) + second.astype(F32)).astype(BF16)


def return_tokens_kernel(links, source, target, part, local_sem, send_sem, recv_sem):
    waits, starts = [], []
    mine = 2 * (links.seq % 2) + links.core
    for s in range(4):
        half = (links.core + s) % 2
        slot = target.at[links.seq % 2, pl.ds(pl.multiple_of(half * part, part), part)]
        stays = (links.y == links.core) & (links.seq == s)
        here = pltpu.make_async_copy(source.at[s], slot, local_sem)
        away = remote(source.at[s], slot, send_sem.at[s], recv_sem.at[mine], links.at_plane(links.y, s))

        def start(stays=stays, here=here, away=away):
            @pl.when(stays)
            def _():
                here.start()

            @pl.when(jnp.logical_not(stays))
            def _():
                away.start()

        starts.append(start)
        waits.append((stays, here, away))

    def finish():
        for stays, here, away in waits:
            @pl.when(stays)
            def _(here=here):
                here.wait()

            @pl.when(jnp.logical_not(stays))
            def _(away=away):
                away.wait_send()

        for j in range(4):
            arrived = remote(
                source.at[0], target.at[0, pl.ds(0, part)], send_sem.at[0], recv_sem.at[j],
                links.at_core,
            )

            @pl.when(jnp.logical_not((links.y == links.core) & (mine == j)))
            def _(arrived=arrived):
                arrived.wait_recv()

    return starts, finish


class Scatter:
    def __init__(self, links, grads, sums, scratch):
        count = len(grads)
        self.links, self.grads, self.sums = links, grads, sums
        self.kept, self.got_one, self.got_two, self.got_z, self.own, self.totals = (
            scratch[j * count : (j + 1) * count] for j in range(6)
        )
        self.load_sem, self.store_sem, self.send_sem, self.recv_sem = scratch[6 * count :]

    def copy(self, w, slot, source, target, device):
        return remote(source, target, self.send_sem.at[w, slot], self.recv_sem.at[w, slot], device)

    def copies(self, stage, w):
        links, kept = self.links, self.kept[w]
        z, core, y, x = links.z, links.core, links.y, links.x
        half = kept.shape[-1] // 2
        left, right = pl.ds(0, half), pl.ds(half, half)
        if stage == 0:
            return [self.copy(w, 0, self.grads[w].at[:, 1 - core], kept, links.at_core)]
        if stage == 1:
            got = self.got_one[w]
            return [
                self.copy(w, 1, kept.at[:, :, 1 - x, :, left], got.at[0], links.at_x),
                self.copy(w, 2, kept.at[:, 1 - y, :, :, right], got.at[1], links.at_y),
            ]
        if stage == 2:
            got = self.got_two[w]
            return [
                self.copy(w, 3, kept.at[:, 1 - y, x, :, left], got.at[0], links.at_y),
                self.copy(w, 4, kept.at[:, y, 1 - x, :, right], got.at[1], links.at_x),
            ]
        return [
            self.copy(w, 5 + k, kept.at[(z + k + 1) % 4, y, x], self.got_z[w].at[k], links.at_z[k])
            for k in range(3)
        ]

    def load(self, w):
        return pltpu.make_async_copy(self.grads[w].at[:, self.links.core], self.own[w], self.load_sem.at[w])

    def store(self, w):
        return pltpu.make_async_copy(self.totals[w], self.sums[w], self.store_sem.at[w])

    def begin(self):
        for w in range(len(self.grads)):
            for copy in self.copies(0, w):
                copy.start()
            self.load(w).start()

    def advance(self, stage, w):
        kept, own, one, two = self.kept[w], self.own[w], self.got_one[w], self.got_two[w]
        z, y, x = self.links.z, self.links.y, self.links.x
        half, kind = kept.shape[-1] // 2, kept.dtype

        def add(first, second):
            return (first.astype(F32) + second.astype(F32)).astype(kind)

        def core_step(b, carry):
            zz, yy, xx = b // 4, (b // 2) % 2, b % 2
            kept[zz, yy, xx] = add(kept[zz, yy, xx], own[zz, yy, xx])
            return carry

        def one_step(b, carry):
            zz, other = b // 2, b % 2
            kept[zz, other, x, :, 0:half] = add(kept[zz, other, x, :, 0:half], one[0, zz, other])
            kept[zz, y, other, :, half : 2 * half] = add(
                kept[zz, y, other, :, half : 2 * half], one[1, zz, other]
            )
            return carry

        def two_step(zz, carry):
            kept[zz, y, x, :, 0:half] = add(kept[zz, y, x, :, 0:half], two[0, zz])
            kept[zz, y, x, :, half : 2 * half] = add(kept[zz, y, x, :, half : 2 * half], two[1, zz])
            return carry

        if stage == 1:
            self.load(w).wait()
        for copy in self.copies(stage - 1, w):
            copy.wait_recv()
        if stage < 4:
            lax.fori_loop(0, (16, 8, 4)[stage - 1], (core_step, one_step, two_step)[stage - 1], 0)
            for copy in self.copies(stage, w):
                copy.start()
        else:
            total = kept[z, y, x].astype(F32)
            for k in range(3):
                total = total + self.got_z[w][k].astype(F32)
            self.totals[w][...] = total
            self.store(w).start()

    def steps(self):
        count = len(self.grads)
        order = []
        for t in range(count + 3):
            order += [(stage, t - stage + 1) for stage in (1, 2, 3, 4) if 0 <= t - stage + 1 < count]
        return order

    def end(self):
        for w in range(len(self.grads)):
            self.store(w).wait()
            for stage in range(4):
                for copy in self.copies(stage, w):
                    copy.wait_send()


def scatter_scratch(shapes, types):
    count = len(shapes)

    def buffers(*lead, halved=False):
        return [
            pltpu.VMEM((*lead, rows, width // 2 if halved else width), kind)
            for (rows, width), kind in zip(shapes, types)
        ]

    return (
        buffers(4, 2, 2)
        + buffers(2, 4, 2, halved=True)
        + buffers(2, 4, halved=True)
        + buffers(3)
        + buffers(4, 2, 2)
        + [pltpu.VMEM(shape, F32) for shape in shapes]
        + [
            pltpu.SemaphoreType.DMA((count,)),
            pltpu.SemaphoreType.DMA((count,)),
            pltpu.SemaphoreType.DMA((count, 8)),
            pltpu.SemaphoreType.DMA((count, 8)),
        ]
    )


def rows_by_device(grads):
    return [grad.reshape(4, 2, 2, 2, grad.shape[0] // 32, grad.shape[1]) for grad in grads]


def scatter_kernel(count, part, *refs):
    grads, tokens, sums, returned = refs[:count], refs[count], refs[count + 1 : 2 * count + 1], refs[2 * count + 1]
    scratch, (back_local, back_send, back_recv) = refs[2 * count + 2 : -3], refs[-3:]
    links = Links()
    links.greet()
    scatter = Scatter(links, grads, sums, scratch)
    scatter.begin()
    starts, finish = return_tokens_kernel(links, tokens, returned, part, back_local, back_send, back_recv)
    for start in starts:
        start()
    for stage, w in scatter.steps():
        scatter.advance(stage, w)
    scatter.end()
    finish()


def attend_scatter_kernel(count, *refs):
    inputs, grads, tokens, refs = refs[:11], refs[11 : 11 + count], refs[11 + count], refs[12 + count :]
    outs, sums, returned, refs = refs[:5], refs[5 : 5 + count], refs[5 + count], refs[6 + count :]
    scratch, buffers, (back_local, back_send, back_recv) = refs[:14], refs[14:-3], refs[-3:]
    links = Links()
    scatter = Scatter(links, grads, sums, buffers)
    step = pl.program_id(0) * pl.num_programs(1) + pl.program_id(1)
    total = (HEADS * HEAD_DIM // inputs[0].shape[1]) * 4

    def tokens_back():
        return return_tokens_kernel(
            links, tokens, returned, tokens.shape[1], back_local, back_send, back_recv
        )

    @pl.when(step == 0)
    def _():
        links.greet()
        scatter.begin()
        for start in tokens_back()[0]:
            start()

    attend_back_kernel(True, None, *inputs, *outs, *scratch)
    for n in range(total):
        todo = [item for at, item in SCATTER_PACE if at == n]
        if todo or n == total - 1:
            @pl.when(step == n)
            def _(todo=todo, n=n):
                for stage, w in todo:
                    scatter.advance(stage, w)
                if n == total - 1:
                    scatter.end()
                    tokens_back()[1]()


SCATTER_PACE = (
    (1, (1, 0)), (3, (1, 1)), (4, (2, 0)), (4, (1, 2)), (7, (2, 1)), (7, (1, 3)), (8, (3, 0)), (9, (1, 4)),
    (11, (2, 2)), (12, (3, 1)), (12, (2, 3)), (13, (4, 0)), (13, (2, 4)), (14, (3, 2)), (14, (3, 3)),
    (15, (3, 4)), (15, (4, 1)), (15, (4, 2)), (15, (4, 3)), (15, (4, 4)),
)


def attend_scatter(query, kv_own, kv_par, qext, kext, line, grad_mixed, mixed, lse, grads, back):
    tokens, width = query.shape
    own_rows, par_rows, keys = kv_own.shape[0], kv_par.shape[0], kext.shape[1]
    group, count = GROUP // 2, len(grads)
    groups, lanes = HEADS // group, group * HEAD_DIM
    block = pl.BlockSpec((TILE, lanes), lambda g, i: (i, g))
    line_spec = pl.BlockSpec((group, 1, TILE), lambda g, i: (g, 0, 0))
    whole = pl.BlockSpec(memory_space=pl.ANY)
    shapes = [(grad.shape[0] // 32, grad.shape[1]) for grad in grads]
    outs = pl.pallas_call(
        functools.partial(attend_scatter_kernel, count),
        grid=(groups, tokens // TILE),
        in_specs=[without_meta(spec) for spec in attention_specs(own_rows, par_rows, keys, group)]
        + [block, block, pl.BlockSpec((1, group, TILE), lambda g, i: (g, 0, i))]
        + [whole] * (count + 1),
        out_specs=[
            block,
            pl.BlockSpec((2, own_rows, lanes), lambda g, i: (0, 0, g)),
            pl.BlockSpec((2, par_rows, lanes), lambda g, i: (0, 0, g)),
            line_spec,
            line_spec,
        ]
        + [whole] * (count + 1),
        scratch_shapes=back_scratch(keys, group, True)
        + scatter_scratch(shapes, [grad.dtype for grad in grads])
        + [
            pltpu.SemaphoreType.DMA,
            pltpu.SemaphoreType.DMA((4,)),
            pltpu.SemaphoreType.DMA((4,)),
        ],
        out_shape=[
            jax.ShapeDtypeStruct((tokens, width), BF16),
            jax.ShapeDtypeStruct((2, own_rows, width), BF16),
            jax.ShapeDtypeStruct((2, par_rows, width), BF16),
            jax.ShapeDtypeStruct((HEADS, 1, TILE), F32),
            jax.ShapeDtypeStruct((HEADS, 1, TILE), F32),
        ]
        + [jax.ShapeDtypeStruct(shape, F32) for shape in shapes]
        + [jax.ShapeDtypeStruct((2, 2 * back.shape[1], width), BF16)],
        compiler_params=pltpu.CompilerParams(
            vmem_limit_bytes=67043328, collective_id=3, has_side_effects=True
        ),
        cost_estimate=pl.CostEstimate(
            flops=tokens * keys * width * 10, bytes_accessed=10 * (tokens + keys) * width,
            transcendentals=tokens * keys * HEADS // 2,
        ),
        name="attend_scatter",
    )(query, kv_own, kv_own, kv_par, kv_par, qext, kext, line, grad_mixed, mixed,
      lse.reshape(groups, group, tokens), *rows_by_device(grads), back)
    return outs[:5], outs[5 : 5 + count], outs[5 + count]


def scatter_grads(grads, tokens):
    part = tokens.shape[1]
    count = len(grads)
    shapes = [(grad.shape[0] // 32, grad.shape[1]) for grad in grads]
    types = [grad.dtype for grad in grads]

    return pl.pallas_call(
        functools.partial(scatter_kernel, count, part),
        in_specs=[pl.BlockSpec(memory_space=pl.ANY)] * (count + 1),
        out_specs=[pl.BlockSpec(memory_space=pl.ANY)] * (count + 1),
        out_shape=[jax.ShapeDtypeStruct(shape, F32) for shape in shapes]
        + [jax.ShapeDtypeStruct((2, 2 * part, tokens.shape[2]), BF16)],
        scratch_shapes=scatter_scratch(shapes, types)
        + [
            pltpu.SemaphoreType.DMA,
            pltpu.SemaphoreType.DMA((4,)),
            pltpu.SemaphoreType.DMA((4,)),
        ],
        compiler_params=pltpu.CompilerParams(
            vmem_limit_bytes=67043328, collective_id=1, has_side_effects=True
        ),
        cost_estimate=pl.CostEstimate(
            flops=0, transcendentals=0, bytes_accessed=16 * sum(grad.size for grad in grads)
        ),
        name="scatter_grads",
    )(*rows_by_device(grads), tokens)


def norm_scale(value):
    return lax.rsqrt(jnp.mean(value * value, axis=-1, keepdims=True) + EPS)


def normed(value, gain):
    return (value * norm_scale(value) * gain).astype(BF16)


def norm_back(value, gain, grad):
    scale = norm_scale(value)
    scaled = grad * gain
    inner = jnp.mean(scaled * value, axis=-1, keepdims=True)
    return (
        scale * scaled - (scale * scale * scale) * value * inner,
        jnp.sum(grad * value * scale, axis=0),
    )


def dot(rows, weight):
    return jnp.dot(rows, weight, preferred_element_type=F32)


def dot_back(grads, weight):
    return contract(grads, weight, 1, 1)


def dot_weight(rows, grads):
    return contract(rows, grads, 0, 0).astype(BF16)


def fast_body(
    hidden_in,
    encoder_states,
    segments,
    enc_segments,
    grad_out,
    norm_self,
    q_self,
    k_self,
    v_self,
    o_self,
    rel_bias,
    norm_cross,
    q_cross,
    k_cross,
    v_cross,
    o_cross,
    norm_ff,
    wi_gate,
    wi_up,
    wo_ff,
):
    dp, seq = lax.axis_index("dp"), lax.axis_index("seq")
    core, z_low, z_high, y, x = dp % 2, (dp // 2) % 2, dp // 4, seq // 2, seq % 2
    place = (core, z_low, z_high, y, x)
    rows_dev, width = hidden_in.shape[2], hidden_in.shape[3]
    enc_dev = encoder_states.shape[2]
    part, enc_part = rows_dev // 2, enc_dev // 2
    owned_micro = seq % 2

    def send_tokens(pieces_of):
        return [
            lax.ppermute(pieces_of((seq // 2) ^ a, b), AXES, move_pairs(a, b)) for a, b in ROUNDS
        ]

    def settle(received):
        slots = []
        for s in range(4):
            index = 2 * ((s >> 1) ^ owned_micro) + ((s & 1) ^ core)
            slots.append(lax.select_n(index, *received))
        return jnp.stack(slots)

    def return_tokens(value):
        received = []
        for a, b in ROUNDS:
            index = 2 * (owned_micro ^ a) + (core ^ b)
            back = [(target, source) for source, target in move_pairs(a, b)]
            received.append(lax.ppermute(take(value, index, 0), AXES, back))
        flag = seq // 2
        micro = []
        for m in range(2):
            micro.append(
                jnp.concatenate(
                    [jnp.where((flag ^ m) == 0, received[b], received[2 + b]) for b in range(2)],
                    axis=0,
                )
            )
        return jnp.stack(micro)[:, None]

    codes = jnp.concatenate([segments[:, 0], enc_segments[:, 0]], axis=1).astype(BF16)
    codes = jnp.pad(codes, ((0, 0), (0, width - codes.shape[1])))
    codes = jnp.broadcast_to(codes[:, None], (2, 8, width))

    small = jnp.concatenate([norm_self, norm_cross, norm_ff, rel_bias])
    small_rows = norm_self.shape[0]
    small = jnp.broadcast_to(jnp.pad(small, (0, 2 * LANES - small.shape[0])), (8, 2 * LANES))
    wholes, ff_lines, (inputs_low, encoder, codes) = gather_weights(
        [small, k_self, v_self, q_self], [wi_gate, wi_up, wo_ff], [hidden_in, encoder_states, codes]
    )
    small, wk, wv, wq = wholes
    small = small.reshape(32, 8, 2 * LANES)[:, 0].astype(F32)
    gain_self, gain_cross, gain_ff = (
        small[:, j * small_rows : (j + 1) * small_rows].reshape(-1) for j in range(3)
    )
    table = small[:, 3 * small_rows : 3 * small_rows + rel_bias.shape[0]].reshape(BUCKETS, HEADS)
    ff = wi_gate.shape[1]

    inputs_low = inputs_low.reshape(4 * part, width)
    encoder = encoder.reshape(4 * enc_part, width)
    codes = codes[:, 0].astype(jnp.int32)
    seg_parts = codes[:, :rows_dev].reshape(4, 2, part)
    enc_parts = codes[:, rows_dev : rows_dev + enc_dev].reshape(4, 2, enc_part)

    def of_core(parts, which):
        return jnp.stack([take(parts[s], which ^ (s & 1), 0) for s in range(4)])

    seg_own = of_core(seg_parts, core)
    enc_own, enc_par = of_core(enc_parts, core), of_core(enc_parts, 1 - core)
    quarter = jnp.arange(4, dtype=jnp.int32)
    at_own = 2 * quarter + (core ^ (quarter % 2))
    at_par = 2 * quarter + ((1 - core) ^ (quarter % 2))
    tile_last = seg_parts.reshape(8, part)[:, -1]
    first_tile = jnp.sum((tile_last[None, :] < seg_own[:, :1]).astype(jnp.int32), axis=1)
    pairs = jnp.maximum(at_own - first_tile, 0) // 2
    meta = jnp.concatenate([at_own, at_par, pairs]).astype(jnp.int32)
    seg_keys = jnp.concatenate([jnp.full((part,), -1, jnp.int32), seg_parts.reshape(-1)])
    query_codes, key_codes = query_lanes(seg_own.reshape(-1)), key_lanes(seg_keys)
    cross_codes = key_lanes(jnp.concatenate([enc_own, enc_par]).reshape(-1))
    near = (
        buckets_of(jnp.arange(TILE, dtype=jnp.int32))[:, None] == jnp.arange(BUCKETS)[None, :]
    ).astype(F32)
    line = jnp.dot(near, table, precision=lax.Precision.HIGHEST).T.reshape(HEADS, 1, TILE)

    inputs = inputs_low.astype(F32)
    normed_self = normed(inputs, gain_self)
    kv_own = jnp.concatenate(
        [dot(normed_self, wk).astype(BF16), dot(normed_self, wv).astype(BF16)], axis=1
    )
    kv_par = exchange(kv_own, *CORE)
    query = dot(normed_self, wq).astype(BF16)
    mixed, self_lse, wholes = attend_gather(
        query, kv_own, kv_par, query_codes, key_codes, line,
        [*ff_lines, k_cross, v_cross, o_self, q_cross, o_cross],
    )
    w_gate, w_up, w_down, ck, cv, wo, cq, co = wholes
    cross_kv_own = jnp.concatenate(
        [dot(encoder, ck).astype(BF16), dot(encoder, cv).astype(BF16)], axis=1
    )
    cross_kv_par = exchange(cross_kv_own, *CORE)
    cross_kv_par, late_grad = lax.optimization_barrier((cross_kv_par, grad_out))
    out_parts = send_tokens(lambda micro, b: take(late_grad[:, 0, b * part : (b + 1) * part], micro, 0))
    after_self = inputs + dot(mixed, wo)
    normed_cross = normed(after_self, gain_cross)
    cross_query = dot(normed_cross, cq).astype(BF16)
    cross_mixed, cross_lse = attend_fast(
        meta, cross_query, cross_kv_own, cross_kv_par, query_codes, cross_codes, line, False
    )
    after_cross = after_self + dot(cross_mixed, co)
    normed_ff = normed(after_cross, gain_ff)
    gate, up_values = dot(normed_ff, w_gate), dot(normed_ff, w_up)
    hidden = gelu_mix(gate, up_values).astype(BF16)
    result = (after_cross + dot(hidden, w_down)).astype(BF16)
    block_out = return_tokens(result.reshape(4, part, width))

    out_low = settle(out_parts).reshape(4 * part, width)
    grad_result = out_low.astype(F32)
    grad_w_down = dot_weight(hidden, out_low)
    grad_hidden = dot_back(out_low, w_down)
    mix_value, mix_pull = jax.vjp(gelu_mix, gate, up_values)
    grad_gate, grad_up = (piece.astype(BF16) for piece in mix_pull(grad_hidden))
    grad_w_gate, grad_w_up = dot_weight(normed_ff, grad_gate), dot_weight(normed_ff, grad_up)
    grad_normed_ff = dot_back(grad_gate, w_gate) + dot_back(grad_up, w_up)
    ff_part, grad_gain_ff = norm_back(after_cross, gain_ff, grad_normed_ff)
    grad_after_cross = grad_result + ff_part
    cross_out_low = grad_after_cross.astype(BF16)
    grad_co = dot_weight(cross_mixed, cross_out_low)
    grad_cross_mixed = dot_back(cross_out_low, co).astype(BF16)
    grad_cross_query, cross_own, cross_par, unused, unused = attend_back_fast(
        meta, cross_query, cross_kv_own, cross_kv_par, query_codes, cross_codes, line,
        grad_cross_mixed, cross_mixed, cross_lse, False,
    )
    grad_cross_query, block_out = lax.optimization_barrier((grad_cross_query, block_out))
    cross_got = add_low(cross_own, exchange(cross_par, *CORE))
    grad_ck, grad_cv = dot_weight(encoder, cross_got[0]), dot_weight(encoder, cross_got[1])
    grad_encoder = (dot_back(cross_got[0], ck) + dot_back(cross_got[1], cv)).astype(BF16)
    grad_encoder = grad_encoder.reshape(4, enc_part, width)
    grad_cq = dot_weight(normed_cross, grad_cross_query)
    grad_normed_cross = dot_back(grad_cross_query, cq)
    cross_part, grad_gain_cross = norm_back(after_self, gain_cross, grad_normed_cross)
    grad_after_self = grad_after_cross + cross_part
    self_out_low = grad_after_self.astype(BF16)
    grad_wo = dot_weight(mixed, self_out_low)
    grad_mixed = dot_back(self_out_low, wo).astype(BF16)
    (grad_query, self_own, self_par, grad_line, grad_all), ff_grads, grad_encoder = (
        attend_scatter(
            query, kv_own, kv_par, query_codes, key_codes, line, grad_mixed, mixed, self_lse,
            [grad_w_gate, grad_w_up, grad_w_down, grad_co, grad_cq], grad_encoder,
        )
    )
    grad_w_gate, grad_w_up, grad_w_down, grad_co, grad_cq = ff_grads
    grad_encoder = grad_encoder.astype(F32)[:, None]
    self_got = add_low(self_own, exchange(self_par, *CORE))
    grad_wq = dot_weight(normed_self, grad_query)
    grad_wk, grad_wv = dot_weight(normed_self, self_got[0]), dot_weight(normed_self, self_got[1])
    grad_normed_self = (
        dot_back(grad_query, wq) + dot_back(self_got[0], wk) + dot_back(self_got[1], wv)
    )
    self_part, grad_gain_self = norm_back(inputs, gain_self, grad_normed_self)
    grad_hidden_in = (grad_after_self + self_part).astype(BF16).reshape(4, part, width)

    grad_table = jnp.dot(near.T, grad_line.reshape(HEADS, TILE).T, precision=lax.Precision.HIGHEST)
    grad_far = jnp.sum((grad_all - grad_line).reshape(HEADS, TILE), axis=1)
    grad_table = grad_table.at[BUCKETS - 1].add(grad_far)
    small_grads = [piece.reshape(32, -1) for piece in (grad_gain_self, grad_gain_cross, grad_gain_ff)]
    small_grads = jnp.concatenate(small_grads + [grad_table.reshape(32, -1)], axis=1)
    small_grads = jnp.pad(small_grads, ((0, 0), (0, 2 * LANES - small_grads.shape[1])))
    small_grads = jnp.broadcast_to(small_grads[:, None], (32, 8, 2 * LANES)).reshape(256, 2 * LANES)
    order = [
        grad_ck, grad_cv, grad_wk, grad_wv,
        grad_wo, grad_wq, small_grads,
    ]
    (
        grad_ck, grad_cv, grad_wk, grad_wv,
        grad_wo, grad_wq, small_grads, grad_hidden_in,
    ) = scatter_grads(order, grad_hidden_in)
    small_grads = small_grads[0]
    return (
        block_out,
        grad_hidden_in.astype(F32)[:, None],
        grad_encoder,
        small_grads[:small_rows],
        grad_wq,
        grad_wk,
        grad_wv,
        grad_wo,
        small_grads[3 * small_rows : 3 * small_rows + rel_bias.shape[0]],
        small_grads[small_rows : 2 * small_rows],
        grad_cq,
        grad_ck,
        grad_cv,
        grad_co,
        small_grads[2 * small_rows : 3 * small_rows],
        grad_w_gate,
        grad_w_up,
        grad_w_down,
    )


def fits_fast(mesh):
    return mesh.shape["dp"] == 8 and mesh.shape["seq"] == 4


def solution(mesh):
    return jax.shard_map(
        fast_body if fits_fast(mesh) else general_body,
        mesh=mesh,
        in_specs=(
            P(None, "dp", "seq", None),
            P(None, "dp", "seq", None),
            P(None, "dp", "seq"),
            P(None, "dp", "seq"),
            P(None, "dp", "seq", None),
            P(("dp", "seq")),
            P(("dp", "seq"), None),
            P(("dp", "seq"), None),
            P(("dp", "seq"), None),
            P(("dp", "seq"), None),
            P(("dp", "seq")),
            P(("dp", "seq")),
            P(("dp", "seq"), None),
            P(("dp", "seq"), None),
            P(("dp", "seq"), None),
            P(("dp", "seq"), None),
            P(("dp", "seq")),
            P(("dp", "seq"), None),
            P(("dp", "seq"), None),
            P(("dp", "seq"), None),
        ),
        out_specs=(
            P(None, "dp", "seq", None),
            P(None, "dp", "seq", None),
            P(None, "dp", "seq", None),
            P(("dp", "seq")),
            P(("dp", "seq"), None),
            P(("dp", "seq"), None),
            P(("dp", "seq"), None),
            P(("dp", "seq"), None),
            P(("dp", "seq")),
            P(("dp", "seq")),
            P(("dp", "seq"), None),
            P(("dp", "seq"), None),
            P(("dp", "seq"), None),
            P(("dp", "seq"), None),
            P(("dp", "seq")),
            P(("dp", "seq"), None),
            P(("dp", "seq"), None),
            P(("dp", "seq"), None),
        ),
        check_vma=False,
    )
```

```python
import functools
import math

import jax
import jax.numpy as jnp
from jax import lax
from jax.experimental import pallas as pl
from jax.experimental.pallas import tpu as pltpu
from jax.sharding import PartitionSpec as P

HEADS = 16
HEAD_DIM = 64
BUCKETS = 32
MAX_DIST = 128


EPS = 1e-06
NEG = -1e30


def norm_rows(value, gain):
    return value * lax.rsqrt(jnp.mean(value * value, axis=-1, keepdims=True) + EPS) * gain


def bucket_edges():
    half = BUCKETS // 2
    return [math.ceil(half * (MAX_DIST / half) ** (step / half)) for step in range(1, half)]


def buckets_of(distance):
    half = BUCKETS // 2
    far = half + sum(((distance >= edge).astype(jnp.int32) for edge in bucket_edges()))
    return jnp.where(distance < half, distance, far)


def by_heads(values):
    return values.reshape(values.shape[0], values.shape[1], HEADS, HEAD_DIM)


def join_heads(values):
    return values.reshape(values.shape[0], values.shape[1], HEADS * HEAD_DIM)


def project(rows, weight_matrix):
    return jnp.dot(rows, weight_matrix, preferred_element_type=jnp.float32)


def project_back(grads, weight_matrix):
    return jnp.einsum("stn,kn->stk", grads, weight_matrix, preferred_element_type=jnp.float32)


def weight_grad(rows, grads):
    return jnp.einsum("stk,stn->kn", rows, grads, preferred_element_type=jnp.float32)


def gelu_mix(gate, up_values):
    return jax.nn.gelu(gate, approximate=True) * up_values


def scores_of(q_rows, keys, bias, allowed):
    scores = jnp.einsum("sqhd,skhd->shqk", q_rows, keys, preferred_element_type=jnp.float32) + bias
    return jnp.where(allowed[:, None], scores, NEG)


def attend(q_rows, keys, values, bias, allowed):
    scores = scores_of(q_rows, keys, bias, allowed)
    largest = jnp.max(scores, axis=-1, keepdims=True)
    raised = jnp.exp(scores - largest)
    total = jnp.sum(raised, axis=-1, keepdims=True)
    probs = raised / total
    mixed = jnp.einsum(
        "shqk,skhd->sqhd", probs.astype(jnp.bfloat16), values, preferred_element_type=jnp.float32
    )
    return (join_heads(mixed).astype(jnp.bfloat16), largest + jnp.log(total))


def attend_back(q_rows, keys, values, bias, allowed, log_total, grad_mixed):
    scores = scores_of(q_rows, keys, bias, allowed)
    probs = jnp.exp(scores - log_total)
    grad_probs = jnp.einsum(
        "sqhd,skhd->shqk", grad_mixed, values, preferred_element_type=jnp.float32
    )
    inner = jnp.sum(probs * grad_probs, axis=-1, keepdims=True)
    grad_scores = (probs * (grad_probs - inner)).astype(jnp.bfloat16)
    grad_query = jnp.einsum(
        "shqk,skhd->sqhd", grad_scores, keys, preferred_element_type=jnp.float32
    )
    grad_keys = jnp.einsum(
        "shqk,sqhd->skhd", grad_scores, q_rows, preferred_element_type=jnp.float32
    )
    grad_values = jnp.einsum(
        "shqk,sqhd->skhd",
        probs.astype(jnp.bfloat16),
        grad_mixed,
        preferred_element_type=jnp.float32,
    )
    return (join_heads(grad_query), join_heads(grad_keys), join_heads(grad_values), grad_scores)


def general_body(
    hidden_in,
    encoder_states,
    segments,
    enc_segments,
    grad_out,
    norm_self,
    q_self,
    k_self,
    v_self,
    o_self,
    rel_bias,
    norm_cross,
    q_cross,
    k_cross,
    v_cross,
    o_cross,
    norm_ff,
    wi_gate,
    wi_up,
    wo_ff,
):
    shards = (
        norm_self,
        q_self,
        k_self,
        v_self,
        o_self,
        rel_bias,
        norm_cross,
        q_cross,
        k_cross,
        v_cross,
        o_cross,
        norm_ff,
        wi_gate,
        wi_up,
        wo_ff,
    )
    micro_count = hidden_in.shape[0]
    rows_dev = hidden_in.shape[2]
    seg_whole, enc_seg_whole = (
        lax.all_gather(segments, "seq", axis=2, tiled=True),
        lax.all_gather(enc_segments, "seq", axis=2, tiled=True),
    )
    length = seg_whole.shape[2]
    positions = lax.axis_index("seq") * rows_dev + jnp.arange(rows_dev, dtype=jnp.int32)
    columns = jnp.arange(length, dtype=jnp.int32)
    distance = jnp.maximum(positions[:, None] - columns[None, :], 0)
    bucket_indicator = (
        buckets_of(distance)[None] == jnp.arange(BUCKETS, dtype=jnp.int32)[:, None, None]
    ).astype(jnp.bfloat16)
    causal = columns[None, :] <= positions[:, None]
    grad_shards = tuple((jnp.zeros(piece.shape, jnp.float32) for piece in shards))
    outputs, grad_inputs, grad_encoders = ([], [], [])
    for micro in range(micro_count):
        params = (
            lax.all_gather(shards[0], ("dp", "seq"), axis=0, tiled=True),
            lax.all_gather(shards[1], ("dp", "seq"), axis=0, tiled=True),
            lax.all_gather(shards[2], ("dp", "seq"), axis=0, tiled=True),
            lax.all_gather(shards[3], ("dp", "seq"), axis=0, tiled=True),
            lax.all_gather(shards[4], ("dp", "seq"), axis=0, tiled=True),
            lax.all_gather(shards[5], ("dp", "seq"), axis=0, tiled=True),
            lax.all_gather(shards[6], ("dp", "seq"), axis=0, tiled=True),
            lax.all_gather(shards[7], ("dp", "seq"), axis=0, tiled=True),
            lax.all_gather(shards[8], ("dp", "seq"), axis=0, tiled=True),
            lax.all_gather(shards[9], ("dp", "seq"), axis=0, tiled=True),
            lax.all_gather(shards[10], ("dp", "seq"), axis=0, tiled=True),
            lax.all_gather(shards[11], ("dp", "seq"), axis=0, tiled=True),
            lax.all_gather(shards[12], ("dp", "seq"), axis=0, tiled=True),
            lax.all_gather(shards[13], ("dp", "seq"), axis=0, tiled=True),
            lax.all_gather(shards[14], ("dp", "seq"), axis=0, tiled=True),
        )
        (
            gain_self,
            wq,
            wk,
            wv,
            wo,
            table_flat,
            gain_cross,
            cq,
            ck,
            cv,
            co,
            gain_ff,
            w_gate,
            w_up,
            w_down,
        ) = params
        bias = jnp.einsum(
            "pia,pw->wia",
            bucket_indicator,
            table_flat.reshape(BUCKETS, HEADS),
            preferred_element_type=jnp.float32,
        )
        inputs = hidden_in[micro].astype(jnp.float32)
        encoder = encoder_states[micro]
        seg_own = segments[micro]
        self_allowed = (seg_own[:, :, None] == seg_whole[micro][:, None, :]) & causal[None]
        cross_allowed = seg_own[:, :, None] == enc_seg_whole[micro][:, None, :]
        self_norm_scale = gain_self.astype(jnp.float32)
        cross_gain = gain_cross.astype(jnp.float32)
        ff_gain = gain_ff.astype(jnp.float32)
        normed_self = norm_rows(inputs, self_norm_scale).astype(jnp.bfloat16)
        query = project(normed_self, wq).astype(jnp.bfloat16)
        key_own = project(normed_self, wk).astype(jnp.bfloat16)
        value_own = project(normed_self, wv).astype(jnp.bfloat16)
        cross_key_own = project(encoder, ck).astype(jnp.bfloat16)
        cross_value_own = project(encoder, cv).astype(jnp.bfloat16)
        keys, values, cross_keys, cross_values = (
            lax.all_gather(key_own, "seq", axis=1, tiled=True),
            lax.all_gather(value_own, "seq", axis=1, tiled=True),
            lax.all_gather(cross_key_own, "seq", axis=1, tiled=True),
            lax.all_gather(cross_value_own, "seq", axis=1, tiled=True),
        )
        mixed, self_log_normalizer = attend(
            by_heads(query), by_heads(keys), by_heads(values), bias, self_allowed
        )
        after_self = inputs + project(mixed, wo)
        normed_cross = norm_rows(after_self, cross_gain).astype(jnp.bfloat16)
        cross_query = project(normed_cross, cq).astype(jnp.bfloat16)
        cross_mixed, cross_log = attend(
            by_heads(cross_query), by_heads(cross_keys), by_heads(cross_values), 0.0, cross_allowed
        )
        after_cross = after_self + project(cross_mixed, co)
        normed_ff = norm_rows(after_cross, ff_gain).astype(jnp.bfloat16)
        gate = project(normed_ff, w_gate)
        up_values = project(normed_ff, w_up)
        hidden = gelu_mix(gate, up_values).astype(jnp.bfloat16)
        result = after_cross + project(hidden, w_down)
        outputs.append(result.astype(jnp.bfloat16))
        params = (
            lax.all_gather(shards[0], ("dp", "seq"), axis=0, tiled=True),
            lax.all_gather(shards[1], ("dp", "seq"), axis=0, tiled=True),
            lax.all_gather(shards[2], ("dp", "seq"), axis=0, tiled=True),
            lax.all_gather(shards[3], ("dp", "seq"), axis=0, tiled=True),
            lax.all_gather(shards[4], ("dp", "seq"), axis=0, tiled=True),
            lax.all_gather(shards[5], ("dp", "seq"), axis=0, tiled=True),
            lax.all_gather(shards[6], ("dp", "seq"), axis=0, tiled=True),
            lax.all_gather(shards[7], ("dp", "seq"), axis=0, tiled=True),
            lax.all_gather(shards[8], ("dp", "seq"), axis=0, tiled=True),
            lax.all_gather(shards[9], ("dp", "seq"), axis=0, tiled=True),
            lax.all_gather(shards[10], ("dp", "seq"), axis=0, tiled=True),
            lax.all_gather(shards[11], ("dp", "seq"), axis=0, tiled=True),
            lax.all_gather(shards[12], ("dp", "seq"), axis=0, tiled=True),
            lax.all_gather(shards[13], ("dp", "seq"), axis=0, tiled=True),
            lax.all_gather(shards[14], ("dp", "seq"), axis=0, tiled=True),
        )
        (
            gain_self,
            wq,
            wk,
            wv,
            wo,
            table_flat,
            gain_cross,
            cq,
            ck,
            cv,
            co,
            gain_ff,
            w_gate,
            w_up,
            w_down,
        ) = params
        grad_result = grad_out[micro].astype(jnp.float32)
        out_low = grad_out[micro]
        grad_w_down = weight_grad(hidden, out_low)
        grad_hidden = project_back(out_low, w_down)
        mix_value, mix_pull = jax.vjp(gelu_mix, gate, up_values)
        grad_gate, grad_up = mix_pull(grad_hidden)
        grad_gate = grad_gate.astype(jnp.bfloat16)
        grad_up = grad_up.astype(jnp.bfloat16)
        gate_weight_gradient = weight_grad(normed_ff, grad_gate)
        grad_w_up = weight_grad(normed_ff, grad_up)
        grad_normed_ff = project_back(grad_gate, w_gate) + project_back(grad_up, w_up)
        norm_value, norm_pull = jax.vjp(norm_rows, after_cross, ff_gain)
        ff_part, grad_gain_ff = norm_pull(grad_normed_ff)
        grad_after_cross = grad_result + ff_part
        cross_out_low = grad_after_cross.astype(jnp.bfloat16)
        grad_co = weight_grad(cross_mixed, cross_out_low)
        grad_cross_mixed = project_back(cross_out_low, co).astype(jnp.bfloat16)
        grad_cross_query, cross_key_terms, cross_value_terms, cross_scores = attend_back(
            by_heads(cross_query),
            by_heads(cross_keys),
            by_heads(cross_values),
            0.0,
            cross_allowed,
            cross_log,
            by_heads(grad_cross_mixed),
        )
        grad_cross_key, grad_cross_value = (
            lax.psum_scatter(
                cross_key_terms.astype(jnp.bfloat16), "seq", scatter_dimension=1, tiled=True
            ).astype(jnp.float32),
            lax.psum_scatter(
                cross_value_terms.astype(jnp.bfloat16), "seq", scatter_dimension=1, tiled=True
            ).astype(jnp.float32),
        )
        grad_cross_key = grad_cross_key.astype(jnp.bfloat16)
        grad_cross_value = grad_cross_value.astype(jnp.bfloat16)
        cross_key_gradient = weight_grad(encoder, grad_cross_key)
        grad_cv = weight_grad(encoder, grad_cross_value)
        grad_encoders.append(project_back(grad_cross_key, ck) + project_back(grad_cross_value, cv))
        grad_cross_query = grad_cross_query.astype(jnp.bfloat16)
        grad_cq = weight_grad(normed_cross, grad_cross_query)
        grad_normed_cross = project_back(grad_cross_query, cq)
        norm_value, norm_pull = jax.vjp(norm_rows, after_self, cross_gain)
        cross_part, grad_gain_cross = norm_pull(grad_normed_cross)
        grad_after_self = grad_after_cross + cross_part
        self_out_low = grad_after_self.astype(jnp.bfloat16)
        grad_wo = weight_grad(mixed, self_out_low)
        grad_mixed = project_back(self_out_low, wo).astype(jnp.bfloat16)
        grad_query, key_terms, value_terms, self_attention_logits = attend_back(
            by_heads(query),
            by_heads(keys),
            by_heads(values),
            bias,
            self_allowed,
            self_log_normalizer,
            by_heads(grad_mixed),
        )
        grad_table = jnp.einsum(
            "dcma,uma->uc",
            self_attention_logits,
            bucket_indicator,
            preferred_element_type=jnp.float32,
        ).reshape(-1)
        grad_key, grad_value = (
            lax.psum_scatter(
                key_terms.astype(jnp.bfloat16), "seq", scatter_dimension=1, tiled=True
            ).astype(jnp.float32),
            lax.psum_scatter(
                value_terms.astype(jnp.bfloat16), "seq", scatter_dimension=1, tiled=True
            ).astype(jnp.float32),
        )
        grad_key = grad_key.astype(jnp.bfloat16)
        grad_value = grad_value.astype(jnp.bfloat16)
        grad_query = grad_query.astype(jnp.bfloat16)
        grad_wq = weight_grad(normed_self, grad_query)
        grad_wk = weight_grad(normed_self, grad_key)
        grad_wv = weight_grad(normed_self, grad_value)
        grad_normed_self = (
            project_back(grad_query, wq) + project_back(grad_key, wk) + project_back(grad_value, wv)
        )
        norm_value, norm_pull = jax.vjp(norm_rows, inputs, self_norm_scale)
        self_part, grad_gain_self = norm_pull(grad_normed_self)
        grad_inputs.append(grad_after_self + self_part)
        local = (
            grad_gain_self,
            grad_wq,
            grad_wk,
            grad_wv,
            grad_wo,
            grad_table,
            grad_gain_cross,
            grad_cq,
            cross_key_gradient,
            grad_cv,
            grad_co,
            grad_gain_ff,
            gate_weight_gradient,
            grad_w_up,
            grad_w_down,
        )
        summed = (
            lax.psum_scatter(local[0], ("dp", "seq"), scatter_dimension=0, tiled=True),
            lax.psum_scatter(local[1], ("dp", "seq"), scatter_dimension=0, tiled=True),
            lax.psum_scatter(local[2], ("dp", "seq"), scatter_dimension=0, tiled=True),
            lax.psum_scatter(local[3], ("dp", "seq"), scatter_dimension=0, tiled=True),
            lax.psum_scatter(local[4], ("dp", "seq"), scatter_dimension=0, tiled=True),
            lax.psum_scatter(local[5], ("dp", "seq"), scatter_dimension=0, tiled=True),
            lax.psum_scatter(local[6], ("dp", "seq"), scatter_dimension=0, tiled=True),
            lax.psum_scatter(local[7], ("dp", "seq"), scatter_dimension=0, tiled=True),
            lax.psum_scatter(local[8], ("dp", "seq"), scatter_dimension=0, tiled=True),
            lax.psum_scatter(local[9], ("dp", "seq"), scatter_dimension=0, tiled=True),
            lax.psum_scatter(local[10], ("dp", "seq"), scatter_dimension=0, tiled=True),
            lax.psum_scatter(local[11], ("dp", "seq"), scatter_dimension=0, tiled=True),
            lax.psum_scatter(local[12], ("dp", "seq"), scatter_dimension=0, tiled=True),
            lax.psum_scatter(local[13], ("dp", "seq"), scatter_dimension=0, tiled=True),
            lax.psum_scatter(local[14], ("dp", "seq"), scatter_dimension=0, tiled=True),
        )
        grad_shards = tuple((before + after for before, after in zip(grad_shards, summed)))
    return (jnp.stack(outputs), jnp.stack(grad_inputs), jnp.stack(grad_encoders)) + tuple(
        grad_shards
    )


TILE = 256
GROUP = 8
LANES = 128
AHEAD = 2
F32 = jnp.float32
BF16 = jnp.bfloat16


def contract(left, right, left_dim, right_dim):
    return lax.dot_general(
        left, right, (((left_dim,), (right_dim,)), ((), ())), preferred_element_type=F32
    )


def head_mask(head):
    lane = lax.broadcasted_iota(jnp.int32, (1, LANES), 1)
    keep = (lane < HEAD_DIM) if head % 2 == 0 else (lane >= HEAD_DIM)
    return keep.astype(F32).astype(BF16)


def bias_table(line):
    first = jnp.concatenate(
        [line if j == 0 else pltpu.roll(line, j, 1) for j in range(8)], axis=0
    )
    return [first if r == 0 else pltpu.roll(first, 8 * r, 1) for r in range(TILE // 8)]


def line_of(table):
    total = None
    for r in range(TILE // 8):
        part = table[8 * r : 8 * r + 8, :]
        part = part if r == 0 else pltpu.roll(part, TILE - 8 * r, 1)
        total = part if total is None else total + part
    line = total[0:1, :]
    for j in range(1, 8):
        line = line + pltpu.roll(total[j : j + 1, :], TILE - j, 1)
    return line


def positions():
    return (
        lax.broadcasted_iota(jnp.int32, (TILE, TILE), 0),
        lax.broadcasted_iota(jnp.int32, (TILE, TILE), 1),
    )


def pair_lanes(head):
    return slice((head // 2) * LANES, (head // 2 + 1) * LANES)


def head_rows(head):
    return slice(head * HEAD_DIM, (head + 1) * HEAD_DIM)


def tile_places():
    core = lax.axis_index("dp") % 2
    own = [2 * s + (core + s) % 2 for s in range(4)]
    par = [2 * s + (1 - core + s) % 2 for s in range(4)]
    return own + par + [tile // 2 for tile in own]


def place_tiles(causal, meta_ref, own, par):
    moves = []
    count = own.shape[0] // TILE
    places = tile_places() if causal and meta_ref is None else meta_ref
    for ref, base in ((own, 0), (par, count)):
        for s in range(count):
            target = places[base + s] + 1 if causal else base + s
            moves.append((ref, s, target))
    return moves


def rows_at(tile):
    return pl.ds(pl.multiple_of(tile * TILE, TILE), TILE)


def fill_tables(line_ref, tab, adj):
    for h in range(line_ref.shape[0]):
        line = line_ref[h]
        far = line[:, TILE - 1 : TILE]
        for r, rows in enumerate(bias_table(line - far)):
            adj[h, 8 * r : 8 * r + 8, :] = rows
        k_pos, q_pos = positions()
        table = adj[h]
        tab[h] = jnp.where(k_pos <= q_pos, table, NEG)
        adj[h] = jnp.where(k_pos > q_pos, table, 0.0)


BIAS_LANE, EMPTY_LANE = 16, 17


def lane_of():
    return lax.broadcasted_iota(jnp.int32, (1, LANES), 1) % HEAD_DIM


def by_parity(lanes):
    even = (jnp.arange(LANES) < HEAD_DIM)[None, :]
    zero = jnp.zeros_like(lanes)
    return jnp.stack([jnp.where(even, zero, lanes), jnp.where(even, lanes, zero)])


def key_lanes(codes):
    lane = jnp.arange(LANES, dtype=jnp.int32)[None, :] % HEAD_DIM
    documents = (codes[:, None] == lane) & (lane < BIAS_LANE)
    ones = (lane >= BIAS_LANE) & (lane < EMPTY_LANE)
    return by_parity((documents | ones | ((lane == EMPTY_LANE) & (codes[:, None] < 0))).astype(BF16))


def query_lanes(codes):
    lane = jnp.arange(LANES, dtype=jnp.int32)[None, :] % HEAD_DIM
    other = ((codes[:, None] != lane) & (lane < BIAS_LANE)) | (lane == EMPTY_LANE)
    return by_parity(jnp.where(other, NEG, 0.0).astype(BF16))


def with_lanes(head, rows, lanes):
    return rows * head_mask(head) + lanes


def far_lane(head, line_ref):
    lane = lax.broadcasted_iota(jnp.int32, (1, LANES), 1)
    at = BIAS_LANE + (HEAD_DIM if head % 2 == 0 else 0)
    return jnp.where(lane == at, line_ref[head][:, TILE - 1 : TILE], 0.0).astype(BF16)


def query_with_lanes(causal, h, q_ref, qext_ref, line_ref):
    rows = with_lanes(h, q_ref[:, pair_lanes(h)], qext_ref[h % 2])
    return rows + far_lane(h, line_ref) if causal else rows


def visit_pairs(causal, meta_ref, region):
    if not causal:
        region(0, False)
        return
    i = pl.program_id(1)
    if meta_ref is None:
        own = 2 * i + (lax.axis_index("dp") + i) % 2
        pairs = own // 2
    else:
        own, pairs = meta_ref[i], meta_ref[8 + i]
    region(own, True)
    lax.fori_loop(0, pairs, lambda j, c: (region(own - 2 * (j + 1), False), c)[1], 0)


def biased(scores, causal, near, j, h, tab, adj):
    if causal and near:
        return scores + (tab[h] if j else adj[h])
    return scores


def attend_kernel(causal, meta_ref, q_ref, ko, vo, kp, vp, qext_ref, kext_ref, line_ref,
                  o_ref, lse_ref, kb, vt, qx, tab, adj, m_s, l_s, acc):
    @pl.when(pl.program_id(1) == 0)
    def _():
        for ref, s, target in place_tiles(causal, meta_ref, ko, kp):
            for h in range(GROUP):
                kb[h, rows_at(target), :] = with_lanes(
                    h, ref[s * TILE : (s + 1) * TILE, pair_lanes(h)], kext_ref[h % 2, rows_at(target), :]
                )
        for ref, s, target in place_tiles(causal, meta_ref, vo, vp):
            vt[target] = ref[s * TILE : (s + 1) * TILE, :].T
        if causal:
            for h in range(GROUP):
                kb[h, 0:TILE, :] = kext_ref[h % 2, 0:TILE, :]
            vt[0] = jnp.zeros(vt.shape[1:], BF16)
            fill_tables(line_ref, tab, adj)

    for h in range(GROUP):
        qx[h] = query_with_lanes(causal, h, q_ref, qext_ref, line_ref)
    m_s[...] = jnp.full(m_s.shape, NEG, F32)
    l_s[...] = jnp.zeros(l_s.shape, F32)
    acc[...] = jnp.zeros(acc.shape, F32)

    def region(tile, near):
        def scores_of_head(h):
            return [contract(kb[h, rows_at(tile + j), :], qx[h], 1, 1) for j in range(2)]

        ready = [scores_of_head(h) for h in range(AHEAD)]
        for h in range(GROUP):
            if h + AHEAD < GROUP:
                ready.append(scores_of_head(h + AHEAD))
            scores = [biased(ready[h][j], causal, near, j, h, tab, adj) for j in range(2)]
            before = m_s[h : h + 1, :]
            largest = jnp.maximum(
                before, jnp.max(jnp.maximum(scores[0], scores[1]), axis=0, keepdims=True)
            )
            raised = [jnp.exp(piece - largest) for piece in scores]
            scale = jnp.exp(before - largest)
            m_s[h : h + 1, :] = largest
            l_s[h : h + 1, :] = l_s[h : h + 1, :] * scale + jnp.sum(
                raised[0] + raised[1], axis=0, keepdims=True
            )
            rows = head_rows(h)
            mixed = contract(vt[tile, rows, :], raised[0].astype(BF16), 1, 0) + contract(
                vt[tile + 1, rows, :], raised[1].astype(BF16), 1, 0
            )
            acc[rows, :] = acc[rows, :] * scale + mixed

    visit_pairs(causal, meta_ref, region)
    for h in range(GROUP):
        rows = head_rows(h)
        acc[rows, :] = acc[rows, :] / l_s[h : h + 1, :]
        lse_ref[0, h : h + 1, :] = m_s[h : h + 1, :] + jnp.log(l_s[h : h + 1, :])
    o_ref[...] = acc[...].T.astype(BF16)


def attend_back_kernel(causal, meta_ref, q_ref, ko, vo, kp, vp, qext_ref, kext_ref, line_ref,
                       do_ref, o_ref, lse_ref, dq_ref, own_ref, par_ref, gline_ref, gall_ref,
                       kb, vb, kt, qm, dm, qx, d_s, tab, adj, dq_acc, dk_acc, dv_acc, gt, gall):
    i = pl.program_id(1)
    group = q_ref.shape[1] // HEAD_DIM

    @pl.when(i == 0)
    def _():
        for ref, s, target in place_tiles(causal, meta_ref, ko, kp):
            for h in range(group):
                kb[h, rows_at(target), :] = with_lanes(
                    h, ref[s * TILE : (s + 1) * TILE, pair_lanes(h)], kext_ref[h % 2, rows_at(target), :]
                )
        for ref, s, target in place_tiles(causal, meta_ref, vo, vp):
            vb[rows_at(target), :] = ref[s * TILE : (s + 1) * TILE, :]
        for ref, s, target in place_tiles(causal, meta_ref, ko, kp):
            turned = ref[s * TILE : (s + 1) * TILE, :].T
            for h in range(group):
                kt[target, h, 0:HEAD_DIM, :] = turned[head_rows(h), :]
        dk_acc[...] = jnp.zeros(dk_acc.shape, F32)
        dv_acc[...] = jnp.zeros(dv_acc.shape, F32)
        if causal:
            for h in range(group):
                kb[h, 0:TILE, :] = kext_ref[h % 2, 0:TILE, :]
            vb[0:TILE, :] = jnp.zeros((TILE, vb.shape[1]), BF16)
            kt[0] = jnp.zeros(kt.shape[1:], BF16)
            for t in range(kt.shape[0]):
                for h in range(group):
                    kt[t, h, HEAD_DIM:, :] = jnp.ones((kt.shape[2] - HEAD_DIM, TILE), BF16)
            gt[...] = jnp.zeros(gt.shape, F32)
            gall[...] = jnp.zeros(gall.shape, F32)
            fill_tables(line_ref, tab, adj)

    for h in range(group):
        lanes = pair_lanes(h)
        pair, rows = h // 2, slice((h % 2) * TILE, (h % 2 + 1) * TILE)
        qm[pair, rows, :] = q_ref[:, lanes] * head_mask(h)
        dm[pair, rows, :] = do_ref[:, lanes] * head_mask(h)
        qx[h] = query_with_lanes(causal, h, q_ref, qext_ref, line_ref)
    both = jnp.concatenate([head_mask(0)] * 8 + [head_mask(1)] * 8, axis=0)
    for pair in range(group // 2):
        lanes = pair_lanes(2 * pair)
        product = do_ref[:, lanes].astype(F32) * o_ref[:, lanes].astype(F32)
        high = product.astype(BF16)
        low = (product - high.astype(F32)).astype(BF16)
        inner = contract(both, high, 1, 1) + contract(both, low, 1, 1)
        d_s[2 * pair : 2 * pair + 1, :] = inner[0:1, :]
        d_s[2 * pair + 1 : 2 * pair + 2, :] = inner[8:9, :]
    dq_acc[...] = jnp.zeros(dq_acc.shape, F32)

    def region(tile, near):
        def products_of_head(h):
            half = slice((h % 2) * TILE, (h % 2 + 1) * TILE)
            return [
                (
                    contract(kb[h, rows_at(tile + j), :], qx[h], 1, 1),
                    contract(vb[rows_at(tile + j), pair_lanes(h)], dm[h // 2, half, :], 1, 1),
                )
                for j in range(2)
            ]

        ready = [products_of_head(h) for h in range(AHEAD)]
        probs_low, grads_low = {}, {}
        for h in range(group):
            if h + AHEAD < group:
                ready.append(products_of_head(h + AHEAD))
            back = None
            for j in range(2):
                scores, grad_probs = ready[h][j]
                probs = jnp.exp(biased(scores, causal, near, j, h, tab, adj) - lse_ref[0, h : h + 1, :])
                grads = probs * (grad_probs - d_s[h : h + 1, :])
                low = grads.astype(BF16)
                probs_low[h, j], grads_low[h, j] = probs.astype(BF16), low
                if causal and near:
                    rounded = low.astype(F32)
                    if j == 0:
                        k_pos, q_pos = positions()
                        rounded = jnp.where(k_pos > q_pos, rounded, 0.0)
                    gt[h] += rounded
                part = contract(kt[tile + j, h], low, 1, 0)
                back = part if back is None else back + part
            dq_acc[head_rows(h), :] += back[0:HEAD_DIM, :]
            if causal:
                gall[h : h + 1, :] += back[HEAD_DIM : HEAD_DIM + 1, :]
            if h % 2 == 1:
                pair = h // 2
                lanes = pair_lanes(h)
                for j in range(2):
                    dv_acc[rows_at(tile + j), lanes] += contract(
                        jnp.concatenate([probs_low[h - 1, j], probs_low[h, j]], axis=1), dm[pair], 1, 0
                    )
                    dk_acc[rows_at(tile + j), lanes] += contract(
                        jnp.concatenate([grads_low[h - 1, j], grads_low[h, j]], axis=1), qm[pair], 1, 0
                    )

    visit_pairs(causal, meta_ref, region)
    dq_ref[...] = dq_acc[...].T.astype(BF16)

    @pl.when(i == pl.num_programs(1) - 1)
    def _():
        for j, total in enumerate((dk_acc, dv_acc)):
            for ref, s, target in place_tiles(causal, meta_ref, own_ref.at[j], par_ref.at[j]):
                ref[s * TILE : (s + 1) * TILE, :] = total[rows_at(target), :].astype(BF16)
        for h in range(group):
            if causal:
                gline_ref[h] = line_of(gt[h])
                gall_ref[h] = gall[h : h + 1, :]
            else:
                gline_ref[h] = jnp.zeros((1, TILE), F32)
                gall_ref[h] = jnp.zeros((1, TILE), F32)


VMEM_LIMIT = 60 * 1024 * 1024


def attention_specs(own_rows, par_rows, keys, group=GROUP):
    groups = HEADS // group
    lanes = group * HEAD_DIM
    return [
        pl.BlockSpec((TILE, lanes), lambda g, i, meta: (i, g)),
        pl.BlockSpec((own_rows, lanes), lambda g, i, meta: (0, g)),
        pl.BlockSpec((own_rows, lanes), lambda g, i, meta: (0, groups + g)),
        pl.BlockSpec((par_rows, lanes), lambda g, i, meta: (0, g)),
        pl.BlockSpec((par_rows, lanes), lambda g, i, meta: (0, groups + g)),
        pl.BlockSpec((2, TILE, LANES), lambda g, i, meta: (0, i, 0)),
        pl.BlockSpec((2, keys, LANES), lambda g, i, meta: (0, 0, 0)),
        pl.BlockSpec((group, 1, TILE), lambda g, i, meta: (g, 0, 0)),
    ]


def without_meta(spec):
    return pl.BlockSpec(spec.block_shape, lambda g, i: spec.index_map(g, i, None))


def attention_scratch(keys, lanes, table):
    return [
        pltpu.VMEM((GROUP, keys, LANES), BF16),
        pltpu.VMEM((keys // TILE, lanes, TILE), BF16),
        pltpu.VMEM((GROUP, TILE, LANES), BF16),
        pltpu.VMEM(table, F32),
        pltpu.VMEM(table, F32),
        pltpu.VMEM((8, TILE), F32),
        pltpu.VMEM((8, TILE), F32),
        pltpu.VMEM((lanes, TILE), F32),
    ]


def attend_fast(meta, query, kv_own, kv_par, qext, kext, line, causal):
    tokens, width = query.shape
    own_rows, par_rows, keys = kv_own.shape[0], kv_par.shape[0], kext.shape[1]
    groups, lanes = HEADS // GROUP, GROUP * HEAD_DIM
    table = (GROUP, TILE, TILE) if causal else (1, 8, LANES)
    return pl.pallas_call(
        functools.partial(attend_kernel, causal),
        grid_spec=pltpu.PrefetchScalarGridSpec(
            num_scalar_prefetch=1,
            grid=(groups, tokens // TILE),
            in_specs=attention_specs(own_rows, par_rows, keys),
            out_specs=[
                pl.BlockSpec((TILE, lanes), lambda g, i, meta: (i, g)),
                pl.BlockSpec((1, GROUP, TILE), lambda g, i, meta: (g, 0, i)),
            ],
            scratch_shapes=attention_scratch(keys, lanes, table),
        ),
        out_shape=[
            jax.ShapeDtypeStruct((tokens, width), BF16),
            jax.ShapeDtypeStruct((groups, GROUP, tokens), F32),
        ],
        compiler_params=pltpu.CompilerParams(vmem_limit_bytes=VMEM_LIMIT),
        cost_estimate=pl.CostEstimate(
            flops=tokens * keys * width * 4, bytes_accessed=4 * (tokens + keys) * width,
            transcendentals=tokens * keys * HEADS // 2,
        ),
        name="attend_self" if causal else "attend_cross",
    )(meta, query, kv_own, kv_own, kv_par, kv_par, qext, kext, line)


def back_scratch(keys, group, causal):
    lanes = group * HEAD_DIM
    table = (group, TILE, TILE) if causal else (1, 8, LANES)
    return [
        pltpu.VMEM((group, keys, LANES), BF16),
        pltpu.VMEM((keys, lanes), BF16),
        pltpu.VMEM((keys // TILE, group, HEAD_DIM + (16 if causal else 0), TILE), BF16),
        pltpu.VMEM((group // 2, 2 * TILE, LANES), BF16),
        pltpu.VMEM((group // 2, 2 * TILE, LANES), BF16),
        pltpu.VMEM((group, TILE, LANES), BF16),
        pltpu.VMEM((8, TILE), F32),
        pltpu.VMEM(table, F32),
        pltpu.VMEM(table, F32),
        pltpu.VMEM((lanes, TILE), F32),
        pltpu.VMEM((keys, lanes), F32),
        pltpu.VMEM((keys, lanes), F32),
        pltpu.VMEM(table, F32),
        pltpu.VMEM((8, TILE), F32),
    ]


def attend_back_fast(meta, query, kv_own, kv_par, qext, kext, line, grad_mixed, mixed, lse, causal):
    tokens, width = query.shape
    own_rows, par_rows, keys = kv_own.shape[0], kv_par.shape[0], kext.shape[1]
    groups, lanes = HEADS // GROUP, GROUP * HEAD_DIM
    table = (GROUP, TILE, TILE) if causal else (1, 8, LANES)
    block = pl.BlockSpec((TILE, lanes), lambda g, i, meta: (i, g))
    line_spec = pl.BlockSpec((GROUP, 1, TILE), lambda g, i, meta: (g, 0, 0))
    return pl.pallas_call(
        functools.partial(attend_back_kernel, causal),
        grid_spec=pltpu.PrefetchScalarGridSpec(
            num_scalar_prefetch=1,
            grid=(groups, tokens // TILE),
            in_specs=attention_specs(own_rows, par_rows, keys)
            + [block, block, pl.BlockSpec((1, GROUP, TILE), lambda g, i, meta: (g, 0, i))],
            out_specs=[
                block,
                pl.BlockSpec((2, own_rows, lanes), lambda g, i, meta: (0, 0, g)),
                pl.BlockSpec((2, par_rows, lanes), lambda g, i, meta: (0, 0, g)),
                line_spec,
                line_spec,
            ],
            scratch_shapes=back_scratch(keys, GROUP, causal),
        ),
        out_shape=[
            jax.ShapeDtypeStruct((tokens, width), BF16),
            jax.ShapeDtypeStruct((2, own_rows, width), BF16),
            jax.ShapeDtypeStruct((2, par_rows, width), BF16),
            jax.ShapeDtypeStruct((HEADS, 1, TILE), F32),
            jax.ShapeDtypeStruct((HEADS, 1, TILE), F32),
        ],
        compiler_params=pltpu.CompilerParams(vmem_limit_bytes=VMEM_LIMIT),
        cost_estimate=pl.CostEstimate(
            flops=tokens * keys * width * 10, bytes_accessed=10 * (tokens + keys) * width,
            transcendentals=tokens * keys * HEADS // 2,
        ),
        name="attend_self_back" if causal else "attend_cross_back",
    )(meta, query, kv_own, kv_own, kv_par, kv_par, qext, kext, line, grad_mixed, mixed, lse)


AXES = ("dp", "seq")


def exchange(value, dp_bit, seq_bit):
    pairs = [
        (dp * 4 + seq, (dp ^ dp_bit) * 4 + (seq ^ seq_bit)) for dp in range(8) for seq in range(4)
    ]
    return lax.ppermute(value, AXES, pairs)


CORE, Z_LOW, Z_HIGH, X, Y = (1, 0), (2, 0), (4, 0), (0, 1), (0, 2)


def move_pairs(a, b):
    pairs = []
    for z in range(4):
        for core in range(2):
            for s in range(4):
                micro, half_core = (s >> 1) ^ a, (s & 1) ^ b
                pairs.append(((2 * z + core) * 4 + s, (2 * z + half_core) * 4 + 2 * core + micro))
    return pairs


ROUNDS = ((0, 0), (0, 1), (1, 0), (1, 1))


def take(value, index, axis):
    return lax.dynamic_index_in_dim(value, index, axis, keepdims=False)


MESH = pl.DeviceIdType.MESH


class Links:
    def __init__(self):
        dp, seq = lax.axis_index("dp"), lax.axis_index("seq")
        self.seq = seq
        self.z, self.core, self.y, self.x = dp // 2, dp % 2, seq // 2, seq % 2
        self.at_z = [{"dp": ((self.z + k) % 4) * 2 + self.core, "seq": seq} for k in (1, 2, 3)]
        self.at_x = {"dp": dp, "seq": seq + 1 - 2 * self.x}
        self.at_y = {"dp": dp, "seq": seq + 2 - 4 * self.y}
        self.at_core = {"dp": dp + 1 - 2 * self.core, "seq": seq}

    def at_plane(self, core, seq):
        return {"dp": 2 * self.z + core, "seq": seq}

    def greet(self):
        partners = list(self.at_z)
        for flip in (0, 1):
            for k in range(4):
                if flip or k:
                    core = 1 - self.core if flip else self.core
                    partners.append(self.at_plane(core, (self.seq + k) % 4))
        barrier = pltpu.get_barrier_semaphore()
        for partner in partners:
            pl.semaphore_signal(barrier, inc=1, device_id=partner, device_id_type=MESH)
        pl.semaphore_wait(barrier, len(partners))


def remote(source, target, send_sem, recv_sem, device):
    return pltpu.make_async_remote_copy(
        src_ref=source,
        dst_ref=target,
        send_sem=send_sem,
        recv_sem=recv_sem,
        device_id=device,
        device_id_type=MESH,
    )


def move_tokens(links, sources, targets, parts, local_sem, send_sem, recv_sem):
    waits = []
    for r, (a, b) in enumerate(ROUNDS):
        micro = 1 - links.y if a else links.y
        core = 1 - links.x if b else links.x
        chip = 2 * links.core + micro
        stays = (core == links.core) & (chip == links.seq)
        for n, (source, target, part) in enumerate(zip(sources, targets, parts)):
            if part is None:
                piece = source.at[micro]
            else:
                piece = source.at[micro, 0, pl.ds(b * part, part)]
            slot = target.at[links.seq]
            here = pltpu.make_async_copy(piece, slot, local_sem.at[r, n])
            away = remote(piece, slot, send_sem.at[r, n], recv_sem.at[r, n], links.at_plane(core, chip))

            @pl.when(stays)
            def _(here=here):
                here.start()

            @pl.when(jnp.logical_not(stays))
            def _(away=away):
                away.start()

            waits.append((stays, here, away))

    def finish():
        for stays, here, away in waits:
            @pl.when(stays)
            def _(here=here):
                here.wait()

            @pl.when(jnp.logical_not(stays))
            def _(away=away):
                away.wait()

    return finish


class Gather:
    def __init__(self, links, shards, wholes, local_sem, send_sem, recv_sem, plane_first=()):
        self.links, self.shards, self.wholes = links, shards, wholes
        self.plane_first = plane_first
        self.along_z = [len(shard.shape) == 3 for shard in shards]
        self.local_sem, self.send_sem, self.recv_sem = local_sem, send_sem, recv_sem

    def copy(self, w, slot, source, target, device):
        return remote(source, target, self.send_sem.at[w, slot], self.recv_sem.at[w, slot], device)

    def copies(self, stage, w):
        links, whole = self.links, self.wholes[w]
        z, core, y, x = links.z, links.core, links.y, links.x
        half = whole.shape[-1] // 2
        left, right = pl.ds(0, half), pl.ds(half, half)
        if w in self.plane_first and stage < 3:
            if stage == 0:
                own, shard = whole.at[z, core, y, x], self.shards[w]
                return [
                    self.copy(w, 0, shard.at[:, left], own.at[:, left], links.at_x),
                    self.copy(w, 1, shard.at[:, right], own.at[:, right], links.at_y),
                ]
            if stage == 1:
                one, two = whole.at[z, core, y, :, :, left], whole.at[z, core, :, x, :, right]
                return [self.copy(w, 2, one, one, links.at_y), self.copy(w, 3, two, two, links.at_x)]
            plane = whole.at[z, core]
            return [self.copy(w, 4 + k, plane, plane, links.at_z[k]) for k in range(3)]
        if stage == 0:
            own = whole.at[z, core, y, x]
            return [self.copy(w, k, self.shards[w], own, links.at_z[k]) for k in range(3)]
        if stage == 1:
            one, two = whole.at[:, core, y, x, :, left], whole.at[:, core, y, x, :, right]
            if self.along_z[w]:
                shard = self.shards[w]
                return [
                    self.copy(w, 3, shard.at[:, :, left], one, links.at_x),
                    self.copy(w, 4, shard.at[:, :, right], two, links.at_y),
                ]
            return [self.copy(w, 3, one, one, links.at_x), self.copy(w, 4, two, two, links.at_y)]
        if stage == 2:
            one, two = whole.at[:, core, y, :, :, left], whole.at[:, core, :, x, :, right]
            return [self.copy(w, 5, one, one, links.at_y), self.copy(w, 6, two, two, links.at_x)]
        both = whole.at[:, core]
        return [self.copy(w, 7, both, both, links.at_core)]

    def local(self, w):
        links = self.links
        z = slice(None) if self.along_z[w] else links.z
        own = self.wholes[w].at[z, links.core, links.y, links.x]
        return pltpu.make_async_copy(self.shards[w], own, self.local_sem.at[w])

    def begin(self):
        count = len(self.shards)
        for w in [*self.plane_first, *(w for w in range(count) if w not in self.plane_first)]:
            self.local(w).start()
            for copy in self.copies(1 if self.along_z[w] else 0, w):
                copy.start()

    def advance(self, stage, w):
        if stage == (2 if self.along_z[w] else 1):
            self.local(w).wait()
        for copy in self.copies(stage - 1, w):
            copy.wait_recv()
        for copy in self.copies(stage, w):
            copy.start()

    def steps(self):
        count = len(self.shards)
        order = []
        for t in range(count + 2):
            order += [(stage, t - stage + 1) for stage in (1, 2, 3) if 0 <= t - stage + 1 < count]
        return order

    def end(self):
        for w in range(len(self.shards)):
            for copy in self.copies(3, w):
                copy.wait_recv()
            for stage in range(1 if self.along_z[w] else 0, 4):
                for copy in self.copies(stage, w):
                    copy.wait_send()


def gather_kernel(count, later, parts, *refs):
    tokens = len(parts)
    shards, early, moved = refs[:count], refs[count : count + later], refs[count + later : count + later + tokens]
    refs = refs[count + later + tokens :]
    wholes, lines, settled = refs[:count], refs[count : count + later], refs[count + later : count + later + tokens]
    refs = refs[count + later + tokens :]
    local_sem, send_sem, recv_sem, z_local, z_send, z_recv, move_local, move_send, move_recv = refs
    links = Links()
    links.greet()
    gather = Gather(links, shards, wholes, local_sem, send_sem, recv_sem)
    gather.begin()
    finish = move_tokens(links, moved, settled, parts, move_local, move_send, move_recv)
    waits = []
    for w in range(later):
        own = lines[w].at[links.z]
        here = pltpu.make_async_copy(early[w], own, z_local.at[w])
        here.start()
        waits.append(here)
        for k in range(3):
            away = remote(early[w], own, z_send.at[w, k], z_recv.at[w, k], links.at_z[k])
            away.start()
            waits.append(away)
    for stage, w in gather.steps():
        gather.advance(stage, w)
    gather.end()
    finish()
    for copy in waits:
        copy.wait()


def attend_gather_kernel(count, q_ref, ko, vo, kp, vp, qext_ref, kext_ref, line_ref, *refs):
    sources, (o_ref, lse_ref), refs = refs[:count], refs[count : count + 2], refs[count + 2 :]
    wholes, scratch = refs[:count], refs[count : count + 8]
    shards = refs[count + 8 : 2 * count + 8]
    load_sem, local_sem, send_sem, recv_sem = refs[2 * count + 8 :]
    links = Links()
    gather = Gather(links, shards, wholes, local_sem, send_sem, recv_sem, PLANE_FIRST)
    step = pl.program_id(0) * pl.num_programs(1) + pl.program_id(1)
    total = (HEADS * HEAD_DIM // q_ref.shape[1]) * 4
    @pl.when(step == 0)
    def _():
        links.greet()
        loads = [pltpu.make_async_copy(sources[w], shards[w], load_sem.at[w]) for w in range(count)]
        for load in loads:
            load.start()
        for load in loads:
            load.wait()
        gather.begin()

    attend_kernel(True, None, q_ref, ko, vo, kp, vp, qext_ref, kext_ref, line_ref, o_ref, lse_ref, *scratch)
    for n in range(total):
        todo = [item for at, item in GATHER_PLAN if at == n]
        if todo or n == total - 1:
            @pl.when(step == n)
            def _(todo=todo, n=n):
                for stage, w in todo:
                    gather.advance(stage, w)
                if n == total - 1:
                    gather.end()


PLANE_FIRST = (5, 6, 7)
GATHER_PLAN = (
    (0, (1, 5)), (0, (1, 6)), (0, (1, 7)), (0, (2, 5)), (1, (2, 6)), (1, (2, 7)), (1, (1, 3)), (1, (2, 0)),
    (2, (1, 4)), (3, (2, 1)), (4, (2, 2)), (5, (2, 3)), (5, (3, 0)), (6, (2, 4)), (6, (3, 5)), (7, (3, 1)),
    (7, (3, 6)), (7, (3, 2)), (7, (3, 3)), (7, (3, 4)), (7, (3, 7)),
)


def attend_gather(query, kv_own, kv_par, qext, kext, line, shards):
    tokens, width = query.shape
    own_rows, par_rows, keys = kv_own.shape[0], kv_par.shape[0], kext.shape[1]
    groups, lanes, count = HEADS // GROUP, GROUP * HEAD_DIM, len(shards)
    table = (GROUP, TILE, TILE)
    whole = pl.BlockSpec(memory_space=pl.ANY)
    outs = pl.pallas_call(
        functools.partial(attend_gather_kernel, count),
        grid=(groups, tokens // TILE),
        in_specs=[without_meta(spec) for spec in attention_specs(own_rows, par_rows, keys)] + [whole] * count,
        out_specs=[
            pl.BlockSpec((TILE, lanes), lambda g, i: (i, g)),
            pl.BlockSpec((1, GROUP, TILE), lambda g, i: (g, 0, i)),
        ]
        + [whole] * count,
        scratch_shapes=attention_scratch(keys, lanes, table)
        + [pltpu.VMEM(shard.shape, BF16) for shard in shards]
        + [
            pltpu.SemaphoreType.DMA((count,)),
            pltpu.SemaphoreType.DMA((count,)),
            pltpu.SemaphoreType.DMA((count, 8)),
            pltpu.SemaphoreType.DMA((count, 8)),
        ],
        out_shape=[
            jax.ShapeDtypeStruct((tokens, width), BF16),
            jax.ShapeDtypeStruct((groups, GROUP, tokens), F32),
        ]
        + [jax.ShapeDtypeStruct((4, 2, 2, 2, *shard.shape[-2:]), BF16) for shard in shards],
        compiler_params=pltpu.CompilerParams(
            vmem_limit_bytes=VMEM_LIMIT, collective_id=2, has_side_effects=True
        ),
        cost_estimate=pl.CostEstimate(
            flops=tokens * keys * width * 4, bytes_accessed=4 * (tokens + keys) * width,
            transcendentals=tokens * keys * HEADS // 2,
        ),
        name="attend_gather",
    )(query, kv_own, kv_own, kv_par, kv_par, qext, kext, line, *shards)
    return outs[0], outs[1], [whole.reshape(-1, whole.shape[-1]) for whole in outs[2:]]


def gather_weights(shards, early, moved):
    count, later, tokens = len(shards), len(early), len(moved)
    sent = sum(shard.size for shard in shards) * 2
    parts = [None if value.ndim == 3 else value.shape[2] // 2 for value in moved]
    settled = [
        jax.ShapeDtypeStruct((4, value.shape[1] if part is None else part, value.shape[-1]), BF16)
        for value, part in zip(moved, parts)
    ]
    outs = pl.pallas_call(
        functools.partial(gather_kernel, count, later, parts),
        in_specs=[pl.BlockSpec(memory_space=pltpu.VMEM)] * (count + later)
        + [pl.BlockSpec(memory_space=pl.ANY)] * tokens,
        out_specs=[pl.BlockSpec(memory_space=pl.ANY)] * (count + later + tokens),
        out_shape=[jax.ShapeDtypeStruct((4, 2, 2, 2, *shard.shape), BF16) for shard in shards]
        + [jax.ShapeDtypeStruct((4, *shard.shape), BF16) for shard in early]
        + settled,
        scratch_shapes=[
            pltpu.SemaphoreType.DMA((count,)),
            pltpu.SemaphoreType.DMA((count, 8)),
            pltpu.SemaphoreType.DMA((count, 8)),
            pltpu.SemaphoreType.DMA((later,)),
            pltpu.SemaphoreType.DMA((later, 3)),
            pltpu.SemaphoreType.DMA((later, 3)),
            pltpu.SemaphoreType.DMA((4, tokens)),
            pltpu.SemaphoreType.DMA((4, tokens)),
            pltpu.SemaphoreType.DMA((4, tokens)),
        ],
        compiler_params=pltpu.CompilerParams(
            vmem_limit_bytes=VMEM_LIMIT, collective_id=0, has_side_effects=True
        ),
        cost_estimate=pl.CostEstimate(flops=0, transcendentals=0, bytes_accessed=500 * sent),
        name="gather_weights",
    )(*shards, *early, *moved)
    wholes = [whole.reshape(-1, whole.shape[-1]) for whole in outs[:count]]
    return wholes, outs[count : count + later], outs[count + later :]


def add_low(first, second):
    return (first.astype(F32) + second.astype(F32)).astype(BF16)


def return_tokens_kernel(links, source, target, part, local_sem, send_sem, recv_sem):
    waits, starts = [], []
    mine = 2 * (links.seq % 2) + links.core
    for s in range(4):
        half = (links.core + s) % 2
        slot = target.at[links.seq % 2, pl.ds(pl.multiple_of(half * part, part), part)]
        stays = (links.y == links.core) & (links.seq == s)
        here = pltpu.make_async_copy(source.at[s], slot, local_sem)
        away = remote(source.at[s], slot, send_sem.at[s], recv_sem.at[mine], links.at_plane(links.y, s))

        def start(stays=stays, here=here, away=away):
            @pl.when(stays)
            def _():
                here.start()

            @pl.when(jnp.logical_not(stays))
            def _():
                away.start()

        starts.append(start)
        waits.append((stays, here, away))

    def finish():
        for stays, here, away in waits:
            @pl.when(stays)
            def _(here=here):
                here.wait()

            @pl.when(jnp.logical_not(stays))
            def _(away=away):
                away.wait_send()

        for j in range(4):
            arrived = remote(
                source.at[0], target.at[0, pl.ds(0, part)], send_sem.at[0], recv_sem.at[j],
                links.at_core,
            )

            @pl.when(jnp.logical_not((links.y == links.core) & (mine == j)))
            def _(arrived=arrived):
                arrived.wait_recv()

    return starts, finish


class Scatter:
    def __init__(self, links, grads, sums, scratch):
        count = len(grads)
        self.links, self.grads, self.sums = links, grads, sums
        self.kept, self.got_one, self.got_two, self.got_z, self.own, self.totals = (
            scratch[j * count : (j + 1) * count] for j in range(6)
        )
        self.load_sem, self.store_sem, self.send_sem, self.recv_sem = scratch[6 * count :]

    def copy(self, w, slot, source, target, device):
        return remote(source, target, self.send_sem.at[w, slot], self.recv_sem.at[w, slot], device)

    def copies(self, stage, w):
        links, kept = self.links, self.kept[w]
        z, core, y, x = links.z, links.core, links.y, links.x
        half = kept.shape[-1] // 2
        left, right = pl.ds(0, half), pl.ds(half, half)
        if stage == 0:
            return [self.copy(w, 0, self.grads[w].at[:, 1 - core], kept, links.at_core)]
        if stage == 1:
            got = self.got_one[w]
            return [
                self.copy(w, 1, kept.at[:, :, 1 - x, :, left], got.at[0], links.at_x),
                self.copy(w, 2, kept.at[:, 1 - y, :, :, right], got.at[1], links.at_y),
            ]
        if stage == 2:
            got = self.got_two[w]
            return [
                self.copy(w, 3, kept.at[:, 1 - y, x, :, left], got.at[0], links.at_y),
                self.copy(w, 4, kept.at[:, y, 1 - x, :, right], got.at[1], links.at_x),
            ]
        return [
            self.copy(w, 5 + k, kept.at[(z + k + 1) % 4, y, x], self.got_z[w].at[k], links.at_z[k])
            for k in range(3)
        ]

    def load(self, w):
        return pltpu.make_async_copy(self.grads[w].at[:, self.links.core], self.own[w], self.load_sem.at[w])

    def store(self, w):
        return pltpu.make_async_copy(self.totals[w], self.sums[w], self.store_sem.at[w])

    def begin(self):
        for w in range(len(self.grads)):
            for copy in self.copies(0, w):
                copy.start()
            self.load(w).start()

    def advance(self, stage, w):
        kept, own, one, two = self.kept[w], self.own[w], self.got_one[w], self.got_two[w]
        z, y, x = self.links.z, self.links.y, self.links.x
        half, kind = kept.shape[-1] // 2, kept.dtype

        def add(first, second):
            return (first.astype(F32) + second.astype(F32)).astype(kind)

        def core_step(b, carry):
            zz, yy, xx = b // 4, (b // 2) % 2, b % 2
            kept[zz, yy, xx] = add(kept[zz, yy, xx], own[zz, yy, xx])
            return carry

        def one_step(b, carry):
            zz, other = b // 2, b % 2
            kept[zz, other, x, :, 0:half] = add(kept[zz, other, x, :, 0:half], one[0, zz, other])
            kept[zz, y, other, :, half : 2 * half] = add(
                kept[zz, y, other, :, half : 2 * half], one[1, zz, other]
            )
            return carry

        def two_step(zz, carry):
            kept[zz, y, x, :, 0:half] = add(kept[zz, y, x, :, 0:half], two[0, zz])
            kept[zz, y, x, :, half : 2 * half] = add(kept[zz, y, x, :, half : 2 * half], two[1, zz])
            return carry

        if stage == 1:
            self.load(w).wait()
        for copy in self.copies(stage - 1, w):
            copy.wait_recv()
        if stage < 4:
            lax.fori_loop(0, (16, 8, 4)[stage - 1], (core_step, one_step, two_step)[stage - 1], 0)
            for copy in self.copies(stage, w):
                copy.start()
        else:
            total = kept[z, y, x].astype(F32)
            for k in range(3):
                total = total + self.got_z[w][k].astype(F32)
            self.totals[w][...] = total
            self.store(w).start()

    def steps(self):
        count = len(self.grads)
        order = []
        for t in range(count + 3):
            order += [(stage, t - stage + 1) for stage in (1, 2, 3, 4) if 0 <= t - stage + 1 < count]
        return order

    def end(self):
        for w in range(len(self.grads)):
            self.store(w).wait()
            for stage in range(4):
                for copy in self.copies(stage, w):
                    copy.wait_send()


def scatter_scratch(shapes, types):
    count = len(shapes)

    def buffers(*lead, halved=False):
        return [
            pltpu.VMEM((*lead, rows, width // 2 if halved else width), kind)
            for (rows, width), kind in zip(shapes, types)
        ]

    return (
        buffers(4, 2, 2)
        + buffers(2, 4, 2, halved=True)
        + buffers(2, 4, halved=True)
        + buffers(3)
        + buffers(4, 2, 2)
        + [pltpu.VMEM(shape, F32) for shape in shapes]
        + [
            pltpu.SemaphoreType.DMA((count,)),
            pltpu.SemaphoreType.DMA((count,)),
            pltpu.SemaphoreType.DMA((count, 8)),
            pltpu.SemaphoreType.DMA((count, 8)),
        ]
    )


def rows_by_device(grads):
    return [grad.reshape(4, 2, 2, 2, grad.shape[0] // 32, grad.shape[1]) for grad in grads]


def scatter_kernel(count, part, *refs):
    grads, tokens, sums, returned = refs[:count], refs[count], refs[count + 1 : 2 * count + 1], refs[2 * count + 1]
    scratch, (back_local, back_send, back_recv) = refs[2 * count + 2 : -3], refs[-3:]
    links = Links()
    links.greet()
    scatter = Scatter(links, grads, sums, scratch)
    scatter.begin()
    starts, finish = return_tokens_kernel(links, tokens, returned, part, back_local, back_send, back_recv)
    for start in starts:
        start()
    for stage, w in scatter.steps():
        scatter.advance(stage, w)
    scatter.end()
    finish()


def attend_scatter_kernel(count, *refs):
    inputs, grads, tokens, refs = refs[:11], refs[11 : 11 + count], refs[11 + count], refs[12 + count :]
    outs, sums, returned, refs = refs[:5], refs[5 : 5 + count], refs[5 + count], refs[6 + count :]
    scratch, buffers, (back_local, back_send, back_recv) = refs[:14], refs[14:-3], refs[-3:]
    links = Links()
    scatter = Scatter(links, grads, sums, buffers)
    step = pl.program_id(0) * pl.num_programs(1) + pl.program_id(1)
    total = (HEADS * HEAD_DIM // inputs[0].shape[1]) * 4

    def tokens_back():
        return return_tokens_kernel(
            links, tokens, returned, tokens.shape[1], back_local, back_send, back_recv
        )

    @pl.when(step == 0)
    def _():
        links.greet()
        scatter.begin()
        for start in tokens_back()[0]:
            start()

    attend_back_kernel(True, None, *inputs, *outs, *scratch)
    for n in range(total):
        todo = [item for at, item in SCATTER_PACE if at == n]
        if todo or n == total - 1:
            @pl.when(step == n)
            def _(todo=todo, n=n):
                for stage, w in todo:
                    scatter.advance(stage, w)
                if n == total - 1:
                    scatter.end()
                    tokens_back()[1]()


SCATTER_PACE = (
    (1, (1, 0)), (3, (1, 1)), (4, (2, 0)), (7, (2, 1)), (7, (1, 2)), (8, (3, 0)), (10, (3, 1)), (10, (1, 3)),
    (12, (2, 2)), (12, (1, 4)), (13, (4, 0)), (13, (2, 3)), (14, (3, 2)), (14, (3, 3)), (15, (2, 4)),
    (15, (4, 1)), (15, (3, 4)), (15, (4, 2)), (15, (4, 3)), (15, (4, 4)),
)


def attend_scatter(query, kv_own, kv_par, qext, kext, line, grad_mixed, mixed, lse, grads, back):
    tokens, width = query.shape
    own_rows, par_rows, keys = kv_own.shape[0], kv_par.shape[0], kext.shape[1]
    group, count = GROUP // 2, len(grads)
    groups, lanes = HEADS // group, group * HEAD_DIM
    block = pl.BlockSpec((TILE, lanes), lambda g, i: (i, g))
    line_spec = pl.BlockSpec((group, 1, TILE), lambda g, i: (g, 0, 0))
    whole = pl.BlockSpec(memory_space=pl.ANY)
    shapes = [(grad.shape[0] // 32, grad.shape[1]) for grad in grads]
    outs = pl.pallas_call(
        functools.partial(attend_scatter_kernel, count),
        grid=(groups, tokens // TILE),
        in_specs=[without_meta(spec) for spec in attention_specs(own_rows, par_rows, keys, group)]
        + [block, block, pl.BlockSpec((1, group, TILE), lambda g, i: (g, 0, i))]
        + [whole] * (count + 1),
        out_specs=[
            block,
            pl.BlockSpec((2, own_rows, lanes), lambda g, i: (0, 0, g)),
            pl.BlockSpec((2, par_rows, lanes), lambda g, i: (0, 0, g)),
            line_spec,
            line_spec,
        ]
        + [whole] * (count + 1),
        scratch_shapes=back_scratch(keys, group, True)
        + scatter_scratch(shapes, [grad.dtype for grad in grads])
        + [
            pltpu.SemaphoreType.DMA,
            pltpu.SemaphoreType.DMA((4,)),
            pltpu.SemaphoreType.DMA((4,)),
        ],
        out_shape=[
            jax.ShapeDtypeStruct((tokens, width), BF16),
            jax.ShapeDtypeStruct((2, own_rows, width), BF16),
            jax.ShapeDtypeStruct((2, par_rows, width), BF16),
            jax.ShapeDtypeStruct((HEADS, 1, TILE), F32),
            jax.ShapeDtypeStruct((HEADS, 1, TILE), F32),
        ]
        + [jax.ShapeDtypeStruct(shape, F32) for shape in shapes]
        + [jax.ShapeDtypeStruct((2, 2 * back.shape[1], width), BF16)],
        compiler_params=pltpu.CompilerParams(
            vmem_limit_bytes=67043328, collective_id=3, has_side_effects=True
        ),
        cost_estimate=pl.CostEstimate(
            flops=tokens * keys * width * 10, bytes_accessed=10 * (tokens + keys) * width,
            transcendentals=tokens * keys * HEADS // 2,
        ),
        name="attend_scatter",
    )(query, kv_own, kv_own, kv_par, kv_par, qext, kext, line, grad_mixed, mixed,
      lse.reshape(groups, group, tokens), *rows_by_device(grads), back)
    return outs[:5], outs[5 : 5 + count], outs[5 + count]


def scatter_grads(grads, tokens):
    part = tokens.shape[1]
    count = len(grads)
    shapes = [(grad.shape[0] // 32, grad.shape[1]) for grad in grads]
    types = [grad.dtype for grad in grads]

    return pl.pallas_call(
        functools.partial(scatter_kernel, count, part),
        in_specs=[pl.BlockSpec(memory_space=pl.ANY)] * (count + 1),
        out_specs=[pl.BlockSpec(memory_space=pl.ANY)] * (count + 1),
        out_shape=[jax.ShapeDtypeStruct(shape, F32) for shape in shapes]
        + [jax.ShapeDtypeStruct((2, 2 * part, tokens.shape[2]), BF16)],
        scratch_shapes=scatter_scratch(shapes, types)
        + [
            pltpu.SemaphoreType.DMA,
            pltpu.SemaphoreType.DMA((4,)),
            pltpu.SemaphoreType.DMA((4,)),
        ],
        compiler_params=pltpu.CompilerParams(
            vmem_limit_bytes=67043328, collective_id=1, has_side_effects=True
        ),
        cost_estimate=pl.CostEstimate(
            flops=0, transcendentals=0, bytes_accessed=16 * sum(grad.size for grad in grads)
        ),
        name="scatter_grads",
    )(*rows_by_device(grads), tokens)


def norm_scale(value):
    return lax.rsqrt(jnp.mean(value * value, axis=-1, keepdims=True) + EPS)


def normed(value, gain):
    return (value * norm_scale(value) * gain).astype(BF16)


def norm_back(value, gain, grad):
    scale = norm_scale(value)
    scaled = grad * gain
    inner = jnp.mean(scaled * value, axis=-1, keepdims=True)
    return (
        scale * scaled - (scale * scale * scale) * value * inner,
        jnp.sum(grad * value * scale, axis=0),
    )


def dot(rows, weight):
    return jnp.dot(rows, weight, preferred_element_type=F32)


def dot_back(grads, weight):
    return contract(grads, weight, 1, 1)


def dot_weight(rows, grads):
    return contract(rows, grads, 0, 0).astype(BF16)


def fast_body(
    hidden_in,
    encoder_states,
    segments,
    enc_segments,
    grad_out,
    norm_self,
    q_self,
    k_self,
    v_self,
    o_self,
    rel_bias,
    norm_cross,
    q_cross,
    k_cross,
    v_cross,
    o_cross,
    norm_ff,
    wi_gate,
    wi_up,
    wo_ff,
):
    dp, seq = lax.axis_index("dp"), lax.axis_index("seq")
    core, z_low, z_high, y, x = dp % 2, (dp // 2) % 2, dp // 4, seq // 2, seq % 2
    place = (core, z_low, z_high, y, x)
    rows_dev, width = hidden_in.shape[2], hidden_in.shape[3]
    enc_dev = encoder_states.shape[2]
    part, enc_part = rows_dev // 2, enc_dev // 2
    owned_micro = seq % 2

    def send_tokens(pieces_of):
        return [
            lax.ppermute(pieces_of((seq // 2) ^ a, b), AXES, move_pairs(a, b)) for a, b in ROUNDS
        ]

    def settle(received):
        slots = []
        for s in range(4):
            index = 2 * ((s >> 1) ^ owned_micro) + ((s & 1) ^ core)
            slots.append(lax.select_n(index, *received))
        return jnp.stack(slots)

    def return_tokens(value):
        received = []
        for a, b in ROUNDS:
            index = 2 * (owned_micro ^ a) + (core ^ b)
            back = [(target, source) for source, target in move_pairs(a, b)]
            received.append(lax.ppermute(take(value, index, 0), AXES, back))
        flag = seq // 2
        micro = []
        for m in range(2):
            micro.append(
                jnp.concatenate(
                    [jnp.where((flag ^ m) == 0, received[b], received[2 + b]) for b in range(2)],
                    axis=0,
                )
            )
        return jnp.stack(micro)[:, None]

    codes = jnp.concatenate([segments[:, 0], enc_segments[:, 0]], axis=1).astype(BF16)
    codes = jnp.pad(codes, ((0, 0), (0, width - codes.shape[1])))
    codes = jnp.broadcast_to(codes[:, None], (2, 8, width))

    small = jnp.concatenate([norm_self, norm_cross, norm_ff, rel_bias])
    small_rows = norm_self.shape[0]
    small = jnp.broadcast_to(jnp.pad(small, (0, 2 * LANES - small.shape[0])), (8, 2 * LANES))
    wholes, ff_lines, (inputs_low, encoder, codes) = gather_weights(
        [small, k_self, v_self, q_self], [wi_gate, wi_up, wo_ff], [hidden_in, encoder_states, codes]
    )
    small, wk, wv, wq = wholes
    small = small.reshape(32, 8, 2 * LANES)[:, 0].astype(F32)
    gain_self, gain_cross, gain_ff = (
        small[:, j * small_rows : (j + 1) * small_rows].reshape(-1) for j in range(3)
    )
    table = small[:, 3 * small_rows : 3 * small_rows + rel_bias.shape[0]].reshape(BUCKETS, HEADS)
    ff = wi_gate.shape[1]

    inputs_low = inputs_low.reshape(4 * part, width)
    encoder = encoder.reshape(4 * enc_part, width)
    codes = codes[:, 0].astype(jnp.int32)
    seg_parts = codes[:, :rows_dev].reshape(4, 2, part)
    enc_parts = codes[:, rows_dev : rows_dev + enc_dev].reshape(4, 2, enc_part)

    def of_core(parts, which):
        return jnp.stack([take(parts[s], which ^ (s & 1), 0) for s in range(4)])

    seg_own = of_core(seg_parts, core)
    enc_own, enc_par = of_core(enc_parts, core), of_core(enc_parts, 1 - core)
    quarter = jnp.arange(4, dtype=jnp.int32)
    at_own = 2 * quarter + (core ^ (quarter % 2))
    at_par = 2 * quarter + ((1 - core) ^ (quarter % 2))
    tile_last = seg_parts.reshape(8, part)[:, -1]
    first_tile = jnp.sum((tile_last[None, :] < seg_own[:, :1]).astype(jnp.int32), axis=1)
    pairs = jnp.maximum(at_own - first_tile, 0) // 2
    meta = jnp.concatenate([at_own, at_par, pairs]).astype(jnp.int32)
    seg_keys = jnp.concatenate([jnp.full((part,), -1, jnp.int32), seg_parts.reshape(-1)])
    query_codes, key_codes = query_lanes(seg_own.reshape(-1)), key_lanes(seg_keys)
    cross_codes = key_lanes(jnp.concatenate([enc_own, enc_par]).reshape(-1))
    near = (
        buckets_of(jnp.arange(TILE, dtype=jnp.int32))[:, None] == jnp.arange(BUCKETS)[None, :]
    ).astype(F32)
    line = jnp.dot(near, table, precision=lax.Precision.HIGHEST).T.reshape(HEADS, 1, TILE)

    inputs = inputs_low.astype(F32)
    normed_self = normed(inputs, gain_self)
    kv_own = jnp.concatenate(
        [dot(normed_self, wk).astype(BF16), dot(normed_self, wv).astype(BF16)], axis=1
    )
    kv_par = exchange(kv_own, *CORE)
    query = dot(normed_self, wq).astype(BF16)
    mixed, self_lse, wholes = attend_gather(
        query, kv_own, kv_par, query_codes, key_codes, line,
        [*ff_lines, k_cross, v_cross, o_self, q_cross, o_cross],
    )
    w_gate, w_up, w_down, ck, cv, wo, cq, co = wholes
    cross_kv_own = jnp.concatenate(
        [dot(encoder, ck).astype(BF16), dot(encoder, cv).astype(BF16)], axis=1
    )
    cross_kv_par = exchange(cross_kv_own, *CORE)
    cross_kv_par, late_grad = lax.optimization_barrier((cross_kv_par, grad_out))
    out_parts = send_tokens(lambda micro, b: take(late_grad[:, 0, b * part : (b + 1) * part], micro, 0))
    after_self = inputs + dot(mixed, wo)
    normed_cross = normed(after_self, gain_cross)
    cross_query = dot(normed_cross, cq).astype(BF16)
    cross_mixed, cross_lse = attend_fast(
        meta, cross_query, cross_kv_own, cross_kv_par, query_codes, cross_codes, line, False
    )
    after_cross = after_self + dot(cross_mixed, co)
    normed_ff = normed(after_cross, gain_ff)
    gate, up_values = dot(normed_ff, w_gate), dot(normed_ff, w_up)
    hidden = gelu_mix(gate, up_values).astype(BF16)
    result = (after_cross + dot(hidden, w_down)).astype(BF16)
    block_out = return_tokens(result.reshape(4, part, width))

    out_low = settle(out_parts).reshape(4 * part, width)
    grad_result = out_low.astype(F32)
    grad_w_down = dot_weight(hidden, out_low)
    grad_hidden = dot_back(out_low, w_down)
    mix_value, mix_pull = jax.vjp(gelu_mix, gate, up_values)
    grad_gate, grad_up = (piece.astype(BF16) for piece in mix_pull(grad_hidden))
    grad_w_gate, grad_w_up = dot_weight(normed_ff, grad_gate), dot_weight(normed_ff, grad_up)
    grad_normed_ff = dot_back(grad_gate, w_gate) + dot_back(grad_up, w_up)
    ff_part, grad_gain_ff = norm_back(after_cross, gain_ff, grad_normed_ff)
    grad_after_cross = grad_result + ff_part
    cross_out_low = grad_after_cross.astype(BF16)
    grad_co = dot_weight(cross_mixed, cross_out_low)
    grad_cross_mixed = dot_back(cross_out_low, co).astype(BF16)
    grad_cross_query, cross_own, cross_par, unused, unused = attend_back_fast(
        meta, cross_query, cross_kv_own, cross_kv_par, query_codes, cross_codes, line,
        grad_cross_mixed, cross_mixed, cross_lse, False,
    )
    grad_cross_query, block_out = lax.optimization_barrier((grad_cross_query, block_out))
    cross_got = add_low(cross_own, exchange(cross_par, *CORE))
    grad_ck, grad_cv = dot_weight(encoder, cross_got[0]), dot_weight(encoder, cross_got[1])
    grad_encoder = (dot_back(cross_got[0], ck) + dot_back(cross_got[1], cv)).astype(BF16)
    grad_encoder = grad_encoder.reshape(4, enc_part, width)
    grad_cq = dot_weight(normed_cross, grad_cross_query)
    grad_normed_cross = dot_back(grad_cross_query, cq)
    cross_part, grad_gain_cross = norm_back(after_self, gain_cross, grad_normed_cross)
    grad_after_self = grad_after_cross + cross_part
    self_out_low = grad_after_self.astype(BF16)
    grad_wo = dot_weight(mixed, self_out_low)
    grad_mixed = dot_back(self_out_low, wo).astype(BF16)
    (grad_query, self_own, self_par, grad_line, grad_all), ff_grads, grad_encoder = (
        attend_scatter(
            query, kv_own, kv_par, query_codes, key_codes, line, grad_mixed, mixed, self_lse,
            [grad_w_gate, grad_w_up, grad_w_down, grad_co, grad_cq], grad_encoder,
        )
    )
    grad_w_gate, grad_w_up, grad_w_down, grad_co, grad_cq = ff_grads
    grad_encoder = grad_encoder.astype(F32)[:, None]
    self_got = add_low(self_own, exchange(self_par, *CORE))
    grad_wq = dot_weight(normed_self, grad_query)
    grad_wk, grad_wv = dot_weight(normed_self, self_got[0]), dot_weight(normed_self, self_got[1])
    grad_normed_self = (
        dot_back(grad_query, wq) + dot_back(self_got[0], wk) + dot_back(self_got[1], wv)
    )
    self_part, grad_gain_self = norm_back(inputs, gain_self, grad_normed_self)
    grad_hidden_in = (grad_after_self + self_part).astype(BF16).reshape(4, part, width)

    grad_table = jnp.dot(near.T, grad_line.reshape(HEADS, TILE).T, precision=lax.Precision.HIGHEST)
    grad_far = jnp.sum((grad_all - grad_line).reshape(HEADS, TILE), axis=1)
    grad_table = grad_table.at[BUCKETS - 1].add(grad_far)
    small_grads = [piece.reshape(32, -1) for piece in (grad_gain_self, grad_gain_cross, grad_gain_ff)]
    small_grads = jnp.concatenate(small_grads + [grad_table.reshape(32, -1)], axis=1)
    small_grads = jnp.pad(small_grads, ((0, 0), (0, 2 * LANES - small_grads.shape[1])))
    small_grads = jnp.broadcast_to(small_grads[:, None], (32, 8, 2 * LANES)).reshape(256, 2 * LANES)
    order = [
        grad_ck, grad_cv, grad_wk, grad_wv,
        grad_wo, grad_wq, small_grads,
    ]
    (
        grad_ck, grad_cv, grad_wk, grad_wv,
        grad_wo, grad_wq, small_grads, grad_hidden_in,
    ) = scatter_grads(order, grad_hidden_in)
    small_grads = small_grads[0]
    return (
        block_out,
        grad_hidden_in.astype(F32)[:, None],
        grad_encoder,
        small_grads[:small_rows],
        grad_wq,
        grad_wk,
        grad_wv,
        grad_wo,
        small_grads[3 * small_rows : 3 * small_rows + rel_bias.shape[0]],
        small_grads[small_rows : 2 * small_rows],
        grad_cq,
        grad_ck,
        grad_cv,
        grad_co,
        small_grads[2 * small_rows : 3 * small_rows],
        grad_w_gate,
        grad_w_up,
        grad_w_down,
    )


def fits_fast(mesh):
    return mesh.shape["dp"] == 8 and mesh.shape["seq"] == 4


def solution(mesh):
    return jax.shard_map(
        fast_body if fits_fast(mesh) else general_body,
        mesh=mesh,
        in_specs=(
            P(None, "dp", "seq", None),
            P(None, "dp", "seq", None),
            P(None, "dp", "seq"),
            P(None, "dp", "seq"),
            P(None, "dp", "seq", None),
            P(("dp", "seq")),
            P(("dp", "seq"), None),
            P(("dp", "seq"), None),
            P(("dp", "seq"), None),
            P(("dp", "seq"), None),
            P(("dp", "seq")),
            P(("dp", "seq")),
            P(("dp", "seq"), None),
            P(("dp", "seq"), None),
            P(("dp", "seq"), None),
            P(("dp", "seq"), None),
            P(("dp", "seq")),
            P(("dp", "seq"), None),
            P(("dp", "seq"), None),
            P(("dp", "seq"), None),
        ),
        out_specs=(
            P(None, "dp", "seq", None),
            P(None, "dp", "seq", None),
            P(None, "dp", "seq", None),
            P(("dp", "seq")),
            P(("dp", "seq"), None),
            P(("dp", "seq"), None),
            P(("dp", "seq"), None),
            P(("dp", "seq"), None),
            P(("dp", "seq")),
            P(("dp", "seq")),
            P(("dp", "seq"), None),
            P(("dp", "seq"), None),
            P(("dp", "seq"), None),
            P(("dp", "seq"), None),
            P(("dp", "seq")),
            P(("dp", "seq"), None),
            P(("dp", "seq"), None),
            P(("dp", "seq"), None),
        ),
        check_vma=False,
    )
```

```python
import functools
import math

import jax
import jax.numpy as jnp
from jax import lax
from jax.experimental import pallas as pl
from jax.experimental.pallas import tpu as pltpu
from jax.sharding import PartitionSpec as P

HEADS = 16
HEAD_DIM = 64
BUCKETS = 32
MAX_DIST = 128


EPS = 1e-06
NEG = -1e30


def norm_rows(value, gain):
    return value * lax.rsqrt(jnp.mean(value * value, axis=-1, keepdims=True) + EPS) * gain


def bucket_edges():
    half = BUCKETS // 2
    return [math.ceil(half * (MAX_DIST / half) ** (step / half)) for step in range(1, half)]


def buckets_of(distance):
    half = BUCKETS // 2
    far = half + sum(((distance >= edge).astype(jnp.int32) for edge in bucket_edges()))
    return jnp.where(distance < half, distance, far)


def by_heads(values):
    return values.reshape(values.shape[0], values.shape[1], HEADS, HEAD_DIM)


def join_heads(values):
    return values.reshape(values.shape[0], values.shape[1], HEADS * HEAD_DIM)


def project(rows, weight_matrix):
    return jnp.dot(rows, weight_matrix, preferred_element_type=jnp.float32)


def project_back(grads, weight_matrix):
    return jnp.einsum("stn,kn->stk", grads, weight_matrix, preferred_element_type=jnp.float32)


def weight_grad(rows, grads):
    return jnp.einsum("stk,stn->kn", rows, grads, preferred_element_type=jnp.float32)


def gelu_mix(gate, up_values):
    return jax.nn.gelu(gate, approximate=True) * up_values


def scores_of(q_rows, keys, bias, allowed):
    scores = jnp.einsum("sqhd,skhd->shqk", q_rows, keys, preferred_element_type=jnp.float32) + bias
    return jnp.where(allowed[:, None], scores, NEG)


def attend(q_rows, keys, values, bias, allowed):
    scores = scores_of(q_rows, keys, bias, allowed)
    largest = jnp.max(scores, axis=-1, keepdims=True)
    raised = jnp.exp(scores - largest)
    total = jnp.sum(raised, axis=-1, keepdims=True)
    probs = raised / total
    mixed = jnp.einsum(
        "shqk,skhd->sqhd", probs.astype(jnp.bfloat16), values, preferred_element_type=jnp.float32
    )
    return (join_heads(mixed).astype(jnp.bfloat16), largest + jnp.log(total))


def attend_back(q_rows, keys, values, bias, allowed, log_total, grad_mixed):
    scores = scores_of(q_rows, keys, bias, allowed)
    probs = jnp.exp(scores - log_total)
    grad_probs = jnp.einsum(
        "sqhd,skhd->shqk", grad_mixed, values, preferred_element_type=jnp.float32
    )
    inner = jnp.sum(probs * grad_probs, axis=-1, keepdims=True)
    grad_scores = (probs * (grad_probs - inner)).astype(jnp.bfloat16)
    grad_query = jnp.einsum(
        "shqk,skhd->sqhd", grad_scores, keys, preferred_element_type=jnp.float32
    )
    grad_keys = jnp.einsum(
        "shqk,sqhd->skhd", grad_scores, q_rows, preferred_element_type=jnp.float32
    )
    grad_values = jnp.einsum(
        "shqk,sqhd->skhd",
        probs.astype(jnp.bfloat16),
        grad_mixed,
        preferred_element_type=jnp.float32,
    )
    return (join_heads(grad_query), join_heads(grad_keys), join_heads(grad_values), grad_scores)


def general_body(
    hidden_in,
    encoder_states,
    segments,
    enc_segments,
    grad_out,
    norm_self,
    q_self,
    k_self,
    v_self,
    o_self,
    rel_bias,
    norm_cross,
    q_cross,
    k_cross,
    v_cross,
    o_cross,
    norm_ff,
    wi_gate,
    wi_up,
    wo_ff,
):
    shards = (
        norm_self,
        q_self,
        k_self,
        v_self,
        o_self,
        rel_bias,
        norm_cross,
        q_cross,
        k_cross,
        v_cross,
        o_cross,
        norm_ff,
        wi_gate,
        wi_up,
        wo_ff,
    )
    micro_count = hidden_in.shape[0]
    rows_dev = hidden_in.shape[2]
    seg_whole, enc_seg_whole = (
        lax.all_gather(segments, "seq", axis=2, tiled=True),
        lax.all_gather(enc_segments, "seq", axis=2, tiled=True),
    )
    length = seg_whole.shape[2]
    positions = lax.axis_index("seq") * rows_dev + jnp.arange(rows_dev, dtype=jnp.int32)
    columns = jnp.arange(length, dtype=jnp.int32)
    distance = jnp.maximum(positions[:, None] - columns[None, :], 0)
    bucket_indicator = (
        buckets_of(distance)[None] == jnp.arange(BUCKETS, dtype=jnp.int32)[:, None, None]
    ).astype(jnp.bfloat16)
    causal = columns[None, :] <= positions[:, None]
    grad_shards = tuple((jnp.zeros(piece.shape, jnp.float32) for piece in shards))
    outputs, grad_inputs, grad_encoders = ([], [], [])
    for micro in range(micro_count):
        params = (
            lax.all_gather(shards[0], ("dp", "seq"), axis=0, tiled=True),
            lax.all_gather(shards[1], ("dp", "seq"), axis=0, tiled=True),
            lax.all_gather(shards[2], ("dp", "seq"), axis=0, tiled=True),
            lax.all_gather(shards[3], ("dp", "seq"), axis=0, tiled=True),
            lax.all_gather(shards[4], ("dp", "seq"), axis=0, tiled=True),
            lax.all_gather(shards[5], ("dp", "seq"), axis=0, tiled=True),
            lax.all_gather(shards[6], ("dp", "seq"), axis=0, tiled=True),
            lax.all_gather(shards[7], ("dp", "seq"), axis=0, tiled=True),
            lax.all_gather(shards[8], ("dp", "seq"), axis=0, tiled=True),
            lax.all_gather(shards[9], ("dp", "seq"), axis=0, tiled=True),
            lax.all_gather(shards[10], ("dp", "seq"), axis=0, tiled=True),
            lax.all_gather(shards[11], ("dp", "seq"), axis=0, tiled=True),
            lax.all_gather(shards[12], ("dp", "seq"), axis=0, tiled=True),
            lax.all_gather(shards[13], ("dp", "seq"), axis=0, tiled=True),
            lax.all_gather(shards[14], ("dp", "seq"), axis=0, tiled=True),
        )
        (
            gain_self,
            wq,
            wk,
            wv,
            wo,
            table_flat,
            gain_cross,
            cq,
            ck,
            cv,
            co,
            gain_ff,
            w_gate,
            w_up,
            w_down,
        ) = params
        bias = jnp.einsum(
            "pia,pw->wia",
            bucket_indicator,
            table_flat.reshape(BUCKETS, HEADS),
            preferred_element_type=jnp.float32,
        )
        inputs = hidden_in[micro].astype(jnp.float32)
        encoder = encoder_states[micro]
        seg_own = segments[micro]
        self_allowed = (seg_own[:, :, None] == seg_whole[micro][:, None, :]) & causal[None]
        cross_allowed = seg_own[:, :, None] == enc_seg_whole[micro][:, None, :]
        self_norm_scale = gain_self.astype(jnp.float32)
        cross_gain = gain_cross.astype(jnp.float32)
        ff_gain = gain_ff.astype(jnp.float32)
        normed_self = norm_rows(inputs, self_norm_scale).astype(jnp.bfloat16)
        query = project(normed_self, wq).astype(jnp.bfloat16)
        key_own = project(normed_self, wk).astype(jnp.bfloat16)
        value_own = project(normed_self, wv).astype(jnp.bfloat16)
        cross_key_own = project(encoder, ck).astype(jnp.bfloat16)
        cross_value_own = project(encoder, cv).astype(jnp.bfloat16)
        keys, values, cross_keys, cross_values = (
            lax.all_gather(key_own, "seq", axis=1, tiled=True),
            lax.all_gather(value_own, "seq", axis=1, tiled=True),
            lax.all_gather(cross_key_own, "seq", axis=1, tiled=True),
            lax.all_gather(cross_value_own, "seq", axis=1, tiled=True),
        )
        mixed, self_log_normalizer = attend(
            by_heads(query), by_heads(keys), by_heads(values), bias, self_allowed
        )
        after_self = inputs + project(mixed, wo)
        normed_cross = norm_rows(after_self, cross_gain).astype(jnp.bfloat16)
        cross_query = project(normed_cross, cq).astype(jnp.bfloat16)
        cross_mixed, cross_log = attend(
            by_heads(cross_query), by_heads(cross_keys), by_heads(cross_values), 0.0, cross_allowed
        )
        after_cross = after_self + project(cross_mixed, co)
        normed_ff = norm_rows(after_cross, ff_gain).astype(jnp.bfloat16)
        gate = project(normed_ff, w_gate)
        up_values = project(normed_ff, w_up)
        hidden = gelu_mix(gate, up_values).astype(jnp.bfloat16)
        result = after_cross + project(hidden, w_down)
        outputs.append(result.astype(jnp.bfloat16))
        params = (
            lax.all_gather(shards[0], ("dp", "seq"), axis=0, tiled=True),
            lax.all_gather(shards[1], ("dp", "seq"), axis=0, tiled=True),
            lax.all_gather(shards[2], ("dp", "seq"), axis=0, tiled=True),
            lax.all_gather(shards[3], ("dp", "seq"), axis=0, tiled=True),
            lax.all_gather(shards[4], ("dp", "seq"), axis=0, tiled=True),
            lax.all_gather(shards[5], ("dp", "seq"), axis=0, tiled=True),
            lax.all_gather(shards[6], ("dp", "seq"), axis=0, tiled=True),
            lax.all_gather(shards[7], ("dp", "seq"), axis=0, tiled=True),
            lax.all_gather(shards[8], ("dp", "seq"), axis=0, tiled=True),
            lax.all_gather(shards[9], ("dp", "seq"), axis=0, tiled=True),
            lax.all_gather(shards[10], ("dp", "seq"), axis=0, tiled=True),
            lax.all_gather(shards[11], ("dp", "seq"), axis=0, tiled=True),
            lax.all_gather(shards[12], ("dp", "seq"), axis=0, tiled=True),
            lax.all_gather(shards[13], ("dp", "seq"), axis=0, tiled=True),
            lax.all_gather(shards[14], ("dp", "seq"), axis=0, tiled=True),
        )
        (
            gain_self,
            wq,
            wk,
            wv,
            wo,
            table_flat,
            gain_cross,
            cq,
            ck,
            cv,
            co,
            gain_ff,
            w_gate,
            w_up,
            w_down,
        ) = params
        grad_result = grad_out[micro].astype(jnp.float32)
        out_low = grad_out[micro]
        grad_w_down = weight_grad(hidden, out_low)
        grad_hidden = project_back(out_low, w_down)
        mix_value, mix_pull = jax.vjp(gelu_mix, gate, up_values)
        grad_gate, grad_up = mix_pull(grad_hidden)
        grad_gate = grad_gate.astype(jnp.bfloat16)
        grad_up = grad_up.astype(jnp.bfloat16)
        gate_weight_gradient = weight_grad(normed_ff, grad_gate)
        grad_w_up = weight_grad(normed_ff, grad_up)
        grad_normed_ff = project_back(grad_gate, w_gate) + project_back(grad_up, w_up)
        norm_value, norm_pull = jax.vjp(norm_rows, after_cross, ff_gain)
        ff_part, grad_gain_ff = norm_pull(grad_normed_ff)
        grad_after_cross = grad_result + ff_part
        cross_out_low = grad_after_cross.astype(jnp.bfloat16)
        grad_co = weight_grad(cross_mixed, cross_out_low)
        grad_cross_mixed = project_back(cross_out_low, co).astype(jnp.bfloat16)
        grad_cross_query, cross_key_terms, cross_value_terms, cross_scores = attend_back(
            by_heads(cross_query),
            by_heads(cross_keys),
            by_heads(cross_values),
            0.0,
            cross_allowed,
            cross_log,
            by_heads(grad_cross_mixed),
        )
        grad_cross_key, grad_cross_value = (
            lax.psum_scatter(
                cross_key_terms.astype(jnp.bfloat16), "seq", scatter_dimension=1, tiled=True
            ).astype(jnp.float32),
            lax.psum_scatter(
                cross_value_terms.astype(jnp.bfloat16), "seq", scatter_dimension=1, tiled=True
            ).astype(jnp.float32),
        )
        grad_cross_key = grad_cross_key.astype(jnp.bfloat16)
        grad_cross_value = grad_cross_value.astype(jnp.bfloat16)
        cross_key_gradient = weight_grad(encoder, grad_cross_key)
        grad_cv = weight_grad(encoder, grad_cross_value)
        grad_encoders.append(project_back(grad_cross_key, ck) + project_back(grad_cross_value, cv))
        grad_cross_query = grad_cross_query.astype(jnp.bfloat16)
        grad_cq = weight_grad(normed_cross, grad_cross_query)
        grad_normed_cross = project_back(grad_cross_query, cq)
        norm_value, norm_pull = jax.vjp(norm_rows, after_self, cross_gain)
        cross_part, grad_gain_cross = norm_pull(grad_normed_cross)
        grad_after_self = grad_after_cross + cross_part
        self_out_low = grad_after_self.astype(jnp.bfloat16)
        grad_wo = weight_grad(mixed, self_out_low)
        grad_mixed = project_back(self_out_low, wo).astype(jnp.bfloat16)
        grad_query, key_terms, value_terms, self_attention_logits = attend_back(
            by_heads(query),
            by_heads(keys),
            by_heads(values),
            bias,
            self_allowed,
            self_log_normalizer,
            by_heads(grad_mixed),
        )
        grad_table = jnp.einsum(
            "dcma,uma->uc",
            self_attention_logits,
            bucket_indicator,
            preferred_element_type=jnp.float32,
        ).reshape(-1)
        grad_key, grad_value = (
            lax.psum_scatter(
                key_terms.astype(jnp.bfloat16), "seq", scatter_dimension=1, tiled=True
            ).astype(jnp.float32),
            lax.psum_scatter(
                value_terms.astype(jnp.bfloat16), "seq", scatter_dimension=1, tiled=True
            ).astype(jnp.float32),
        )
        grad_key = grad_key.astype(jnp.bfloat16)
        grad_value = grad_value.astype(jnp.bfloat16)
        grad_query = grad_query.astype(jnp.bfloat16)
        grad_wq = weight_grad(normed_self, grad_query)
        grad_wk = weight_grad(normed_self, grad_key)
        grad_wv = weight_grad(normed_self, grad_value)
        grad_normed_self = (
            project_back(grad_query, wq) + project_back(grad_key, wk) + project_back(grad_value, wv)
        )
        norm_value, norm_pull = jax.vjp(norm_rows, inputs, self_norm_scale)
        self_part, grad_gain_self = norm_pull(grad_normed_self)
        grad_inputs.append(grad_after_self + self_part)
        local = (
            grad_gain_self,
            grad_wq,
            grad_wk,
            grad_wv,
            grad_wo,
            grad_table,
            grad_gain_cross,
            grad_cq,
            cross_key_gradient,
            grad_cv,
            grad_co,
            grad_gain_ff,
            gate_weight_gradient,
            grad_w_up,
            grad_w_down,
        )
        summed = (
            lax.psum_scatter(local[0], ("dp", "seq"), scatter_dimension=0, tiled=True),
            lax.psum_scatter(local[1], ("dp", "seq"), scatter_dimension=0, tiled=True),
            lax.psum_scatter(local[2], ("dp", "seq"), scatter_dimension=0, tiled=True),
            lax.psum_scatter(local[3], ("dp", "seq"), scatter_dimension=0, tiled=True),
            lax.psum_scatter(local[4], ("dp", "seq"), scatter_dimension=0, tiled=True),
            lax.psum_scatter(local[5], ("dp", "seq"), scatter_dimension=0, tiled=True),
            lax.psum_scatter(local[6], ("dp", "seq"), scatter_dimension=0, tiled=True),
            lax.psum_scatter(local[7], ("dp", "seq"), scatter_dimension=0, tiled=True),
            lax.psum_scatter(local[8], ("dp", "seq"), scatter_dimension=0, tiled=True),
            lax.psum_scatter(local[9], ("dp", "seq"), scatter_dimension=0, tiled=True),
            lax.psum_scatter(local[10], ("dp", "seq"), scatter_dimension=0, tiled=True),
            lax.psum_scatter(local[11], ("dp", "seq"), scatter_dimension=0, tiled=True),
            lax.psum_scatter(local[12], ("dp", "seq"), scatter_dimension=0, tiled=True),
            lax.psum_scatter(local[13], ("dp", "seq"), scatter_dimension=0, tiled=True),
            lax.psum_scatter(local[14], ("dp", "seq"), scatter_dimension=0, tiled=True),
        )
        grad_shards = tuple((before + after for before, after in zip(grad_shards, summed)))
    return (jnp.stack(outputs), jnp.stack(grad_inputs), jnp.stack(grad_encoders)) + tuple(
        grad_shards
    )


TILE = 256
GROUP = 8
LANES = 128
AHEAD = 2
F32 = jnp.float32
BF16 = jnp.bfloat16


def contract(left, right, left_dim, right_dim):
    return lax.dot_general(
        left, right, (((left_dim,), (right_dim,)), ((), ())), preferred_element_type=F32
    )


def head_mask(head):
    lane = lax.broadcasted_iota(jnp.int32, (1, LANES), 1)
    keep = (lane < HEAD_DIM) if head % 2 == 0 else (lane >= HEAD_DIM)
    return keep.astype(F32).astype(BF16)


def bias_table(line):
    first = jnp.concatenate(
        [line if j == 0 else pltpu.roll(line, j, 1) for j in range(8)], axis=0
    )
    return [first if r == 0 else pltpu.roll(first, 8 * r, 1) for r in range(TILE // 8)]


def line_of(table):
    total = None
    for r in range(TILE // 8):
        part = table[8 * r : 8 * r + 8, :]
        part = part if r == 0 else pltpu.roll(part, TILE - 8 * r, 1)
        total = part if total is None else total + part
    line = total[0:1, :]
    for j in range(1, 8):
        line = line + pltpu.roll(total[j : j + 1, :], TILE - j, 1)
    return line


def positions():
    return (
        lax.broadcasted_iota(jnp.int32, (TILE, TILE), 0),
        lax.broadcasted_iota(jnp.int32, (TILE, TILE), 1),
    )


def pair_lanes(head):
    return slice((head // 2) * LANES, (head // 2 + 1) * LANES)


def head_rows(head):
    return slice(head * HEAD_DIM, (head + 1) * HEAD_DIM)


def tile_places():
    core = lax.axis_index("dp") % 2
    own = [2 * s + (core + s) % 2 for s in range(4)]
    par = [2 * s + (1 - core + s) % 2 for s in range(4)]
    return own + par + [tile // 2 for tile in own]


def place_tiles(causal, meta_ref, own, par):
    moves = []
    count = own.shape[0] // TILE
    places = tile_places() if causal and meta_ref is None else meta_ref
    for ref, base in ((own, 0), (par, count)):
        for s in range(count):
            target = places[base + s] + 1 if causal else base + s
            moves.append((ref, s, target))
    return moves


def rows_at(tile):
    return pl.ds(pl.multiple_of(tile * TILE, TILE), TILE)


def fill_tables(line_ref, tab, adj):
    for h in range(line_ref.shape[0]):
        line = line_ref[h]
        far = line[:, TILE - 1 : TILE]
        for r, rows in enumerate(bias_table(line - far)):
            adj[h, 8 * r : 8 * r + 8, :] = rows
        k_pos, q_pos = positions()
        table = adj[h]
        tab[h] = jnp.where(k_pos <= q_pos, table, NEG)
        adj[h] = jnp.where(k_pos > q_pos, table, 0.0)


BIAS_LANE, EMPTY_LANE = 16, 17


def lane_of():
    return lax.broadcasted_iota(jnp.int32, (1, LANES), 1) % HEAD_DIM


def by_parity(lanes):
    even = (jnp.arange(LANES) < HEAD_DIM)[None, :]
    zero = jnp.zeros_like(lanes)
    return jnp.stack([jnp.where(even, zero, lanes), jnp.where(even, lanes, zero)])


def key_lanes(codes):
    lane = jnp.arange(LANES, dtype=jnp.int32)[None, :] % HEAD_DIM
    documents = (codes[:, None] == lane) & (lane < BIAS_LANE)
    ones = (lane >= BIAS_LANE) & (lane < EMPTY_LANE)
    return by_parity((documents | ones | ((lane == EMPTY_LANE) & (codes[:, None] < 0))).astype(BF16))


def query_lanes(codes):
    lane = jnp.arange(LANES, dtype=jnp.int32)[None, :] % HEAD_DIM
    other = ((codes[:, None] != lane) & (lane < BIAS_LANE)) | (lane == EMPTY_LANE)
    return by_parity(jnp.where(other, NEG, 0.0).astype(BF16))


def with_lanes(head, rows, lanes):
    return rows * head_mask(head) + lanes


def far_lane(head, line_ref):
    lane = lax.broadcasted_iota(jnp.int32, (1, LANES), 1)
    at = BIAS_LANE + (HEAD_DIM if head % 2 == 0 else 0)
    return jnp.where(lane == at, line_ref[head][:, TILE - 1 : TILE], 0.0).astype(BF16)


def query_with_lanes(causal, h, q_ref, qext_ref, line_ref):
    rows = with_lanes(h, q_ref[:, pair_lanes(h)], qext_ref[h % 2])
    return rows + far_lane(h, line_ref) if causal else rows


def visit_pairs(causal, meta_ref, region):
    if not causal:
        region(0, False)
        return
    i = pl.program_id(1)
    if meta_ref is None:
        own = 2 * i + (lax.axis_index("dp") + i) % 2
        pairs = own // 2
    else:
        own, pairs = meta_ref[i], meta_ref[8 + i]
    region(own, True)
    lax.fori_loop(0, pairs, lambda j, c: (region(own - 2 * (j + 1), False), c)[1], 0)


def biased(scores, causal, near, j, h, tab, adj):
    if causal and near:
        return scores + (tab[h] if j else adj[h])
    return scores


def attend_kernel(causal, meta_ref, q_ref, ko, vo, kp, vp, qext_ref, kext_ref, line_ref,
                  o_ref, lse_ref, kb, vt, qx, tab, adj, m_s, l_s, acc):
    @pl.when(pl.program_id(1) == 0)
    def _():
        for ref, s, target in place_tiles(causal, meta_ref, ko, kp):
            for h in range(GROUP):
                kb[h, rows_at(target), :] = with_lanes(
                    h, ref[s * TILE : (s + 1) * TILE, pair_lanes(h)], kext_ref[h % 2, rows_at(target), :]
                )
        for ref, s, target in place_tiles(causal, meta_ref, vo, vp):
            vt[target] = ref[s * TILE : (s + 1) * TILE, :].T
        if causal:
            for h in range(GROUP):
                kb[h, 0:TILE, :] = kext_ref[h % 2, 0:TILE, :]
            vt[0] = jnp.zeros(vt.shape[1:], BF16)
            fill_tables(line_ref, tab, adj)

    for h in range(GROUP):
        qx[h] = query_with_lanes(causal, h, q_ref, qext_ref, line_ref)
    m_s[...] = jnp.full(m_s.shape, NEG, F32)
    l_s[...] = jnp.zeros(l_s.shape, F32)
    acc[...] = jnp.zeros(acc.shape, F32)

    def region(tile, near):
        def scores_of_head(h):
            return [contract(kb[h, rows_at(tile + j), :], qx[h], 1, 1) for j in range(2)]

        ready = [scores_of_head(h) for h in range(AHEAD)]
        for h in range(GROUP):
            if h + AHEAD < GROUP:
                ready.append(scores_of_head(h + AHEAD))
            scores = [biased(ready[h][j], causal, near, j, h, tab, adj) for j in range(2)]
            before = m_s[h : h + 1, :]
            largest = jnp.maximum(
                before, jnp.max(jnp.maximum(scores[0], scores[1]), axis=0, keepdims=True)
            )
            raised = [jnp.exp(piece - largest) for piece in scores]
            scale = jnp.exp(before - largest)
            m_s[h : h + 1, :] = largest
            l_s[h : h + 1, :] = l_s[h : h + 1, :] * scale + jnp.sum(
                raised[0] + raised[1], axis=0, keepdims=True
            )
            rows = head_rows(h)
            mixed = contract(vt[tile, rows, :], raised[0].astype(BF16), 1, 0) + contract(
                vt[tile + 1, rows, :], raised[1].astype(BF16), 1, 0
            )
            acc[rows, :] = acc[rows, :] * scale + mixed

    visit_pairs(causal, meta_ref, region)
    for h in range(GROUP):
        rows = head_rows(h)
        acc[rows, :] = acc[rows, :] / l_s[h : h + 1, :]
        lse_ref[0, h : h + 1, :] = m_s[h : h + 1, :] + jnp.log(l_s[h : h + 1, :])
    o_ref[...] = acc[...].T.astype(BF16)


def attend_back_kernel(causal, meta_ref, q_ref, ko, vo, kp, vp, qext_ref, kext_ref, line_ref,
                       do_ref, o_ref, lse_ref, dq_ref, own_ref, par_ref, gline_ref, gall_ref,
                       kb, vb, kt, qm, dm, qx, d_s, tab, adj, dq_acc, dk_acc, dv_acc, gt, gall):
    i = pl.program_id(1)
    group = q_ref.shape[1] // HEAD_DIM

    @pl.when(i == 0)
    def _():
        for ref, s, target in place_tiles(causal, meta_ref, ko, kp):
            for h in range(group):
                kb[h, rows_at(target), :] = with_lanes(
                    h, ref[s * TILE : (s + 1) * TILE, pair_lanes(h)], kext_ref[h % 2, rows_at(target), :]
                )
        for ref, s, target in place_tiles(causal, meta_ref, vo, vp):
            vb[rows_at(target), :] = ref[s * TILE : (s + 1) * TILE, :]
        for ref, s, target in place_tiles(causal, meta_ref, ko, kp):
            turned = ref[s * TILE : (s + 1) * TILE, :].T
            for h in range(group):
                kt[target, h, 0:HEAD_DIM, :] = turned[head_rows(h), :]
        dk_acc[...] = jnp.zeros(dk_acc.shape, F32)
        dv_acc[...] = jnp.zeros(dv_acc.shape, F32)
        if causal:
            for h in range(group):
                kb[h, 0:TILE, :] = kext_ref[h % 2, 0:TILE, :]
            vb[0:TILE, :] = jnp.zeros((TILE, vb.shape[1]), BF16)
            kt[0] = jnp.zeros(kt.shape[1:], BF16)
            for t in range(kt.shape[0]):
                for h in range(group):
                    kt[t, h, HEAD_DIM:, :] = jnp.ones((kt.shape[2] - HEAD_DIM, TILE), BF16)
            gt[...] = jnp.zeros(gt.shape, F32)
            gall[...] = jnp.zeros(gall.shape, F32)
            fill_tables(line_ref, tab, adj)

    for h in range(group):
        lanes = pair_lanes(h)
        pair, rows = h // 2, slice((h % 2) * TILE, (h % 2 + 1) * TILE)
        qm[pair, rows, :] = q_ref[:, lanes] * head_mask(h)
        dm[pair, rows, :] = do_ref[:, lanes] * head_mask(h)
        qx[h] = query_with_lanes(causal, h, q_ref, qext_ref, line_ref)
    both = jnp.concatenate([head_mask(0)] * 8 + [head_mask(1)] * 8, axis=0)
    for pair in range(group // 2):
        lanes = pair_lanes(2 * pair)
        product = do_ref[:, lanes].astype(F32) * o_ref[:, lanes].astype(F32)
        high = product.astype(BF16)
        low = (product - high.astype(F32)).astype(BF16)
        inner = contract(both, high, 1, 1) + contract(both, low, 1, 1)
        d_s[2 * pair : 2 * pair + 1, :] = inner[0:1, :]
        d_s[2 * pair + 1 : 2 * pair + 2, :] = inner[8:9, :]
    dq_acc[...] = jnp.zeros(dq_acc.shape, F32)

    def region(tile, near):
        def products_of_head(h):
            half = slice((h % 2) * TILE, (h % 2 + 1) * TILE)
            return [
                (
                    contract(kb[h, rows_at(tile + j), :], qx[h], 1, 1),
                    contract(vb[rows_at(tile + j), pair_lanes(h)], dm[h // 2, half, :], 1, 1),
                )
                for j in range(2)
            ]

        ready = [products_of_head(h) for h in range(AHEAD)]
        probs_low, grads_low = {}, {}
        for h in range(group):
            if h + AHEAD < group:
                ready.append(products_of_head(h + AHEAD))
            back = None
            for j in range(2):
                scores, grad_probs = ready[h][j]
                probs = jnp.exp(biased(scores, causal, near, j, h, tab, adj) - lse_ref[0, h : h + 1, :])
                grads = probs * (grad_probs - d_s[h : h + 1, :])
                low = grads.astype(BF16)
                probs_low[h, j], grads_low[h, j] = probs.astype(BF16), low
                if causal and near:
                    rounded = low.astype(F32)
                    if j == 0:
                        k_pos, q_pos = positions()
                        rounded = jnp.where(k_pos > q_pos, rounded, 0.0)
                    gt[h] += rounded
                part = contract(kt[tile + j, h], low, 1, 0)
                back = part if back is None else back + part
            dq_acc[head_rows(h), :] += back[0:HEAD_DIM, :]
            if causal:
                gall[h : h + 1, :] += back[HEAD_DIM : HEAD_DIM + 1, :]
            if h % 2 == 1:
                pair = h // 2
                lanes = pair_lanes(h)
                for j in range(2):
                    dv_acc[rows_at(tile + j), lanes] += contract(
                        jnp.concatenate([probs_low[h - 1, j], probs_low[h, j]], axis=1), dm[pair], 1, 0
                    )
                    dk_acc[rows_at(tile + j), lanes] += contract(
                        jnp.concatenate([grads_low[h - 1, j], grads_low[h, j]], axis=1), qm[pair], 1, 0
                    )

    visit_pairs(causal, meta_ref, region)
    dq_ref[...] = dq_acc[...].T.astype(BF16)

    @pl.when(i == pl.num_programs(1) - 1)
    def _():
        for j, total in enumerate((dk_acc, dv_acc)):
            for ref, s, target in place_tiles(causal, meta_ref, own_ref.at[j], par_ref.at[j]):
                ref[s * TILE : (s + 1) * TILE, :] = total[rows_at(target), :].astype(BF16)
        for h in range(group):
            if causal:
                gline_ref[h] = line_of(gt[h])
                gall_ref[h] = gall[h : h + 1, :]
            else:
                gline_ref[h] = jnp.zeros((1, TILE), F32)
                gall_ref[h] = jnp.zeros((1, TILE), F32)


VMEM_LIMIT = 60 * 1024 * 1024


def attention_specs(own_rows, par_rows, keys, group=GROUP):
    groups = HEADS // group
    lanes = group * HEAD_DIM
    return [
        pl.BlockSpec((TILE, lanes), lambda g, i, meta: (i, g)),
        pl.BlockSpec((own_rows, lanes), lambda g, i, meta: (0, g)),
        pl.BlockSpec((own_rows, lanes), lambda g, i, meta: (0, groups + g)),
        pl.BlockSpec((par_rows, lanes), lambda g, i, meta: (0, g)),
        pl.BlockSpec((par_rows, lanes), lambda g, i, meta: (0, groups + g)),
        pl.BlockSpec((2, TILE, LANES), lambda g, i, meta: (0, i, 0)),
        pl.BlockSpec((2, keys, LANES), lambda g, i, meta: (0, 0, 0)),
        pl.BlockSpec((group, 1, TILE), lambda g, i, meta: (g, 0, 0)),
    ]


def without_meta(spec):
    return pl.BlockSpec(spec.block_shape, lambda g, i: spec.index_map(g, i, None))


def attention_scratch(keys, lanes, table):
    return [
        pltpu.VMEM((GROUP, keys, LANES), BF16),
        pltpu.VMEM((keys // TILE, lanes, TILE), BF16),
        pltpu.VMEM((GROUP, TILE, LANES), BF16),
        pltpu.VMEM(table, F32),
        pltpu.VMEM(table, F32),
        pltpu.VMEM((8, TILE), F32),
        pltpu.VMEM((8, TILE), F32),
        pltpu.VMEM((lanes, TILE), F32),
    ]


def attend_fast(meta, query, kv_own, kv_par, qext, kext, line, causal):
    tokens, width = query.shape
    own_rows, par_rows, keys = kv_own.shape[0], kv_par.shape[0], kext.shape[1]
    groups, lanes = HEADS // GROUP, GROUP * HEAD_DIM
    table = (GROUP, TILE, TILE) if causal else (1, 8, LANES)
    return pl.pallas_call(
        functools.partial(attend_kernel, causal),
        grid_spec=pltpu.PrefetchScalarGridSpec(
            num_scalar_prefetch=1,
            grid=(groups, tokens // TILE),
            in_specs=attention_specs(own_rows, par_rows, keys),
            out_specs=[
                pl.BlockSpec((TILE, lanes), lambda g, i, meta: (i, g)),
                pl.BlockSpec((1, GROUP, TILE), lambda g, i, meta: (g, 0, i)),
            ],
            scratch_shapes=attention_scratch(keys, lanes, table),
        ),
        out_shape=[
            jax.ShapeDtypeStruct((tokens, width), BF16),
            jax.ShapeDtypeStruct((groups, GROUP, tokens), F32),
        ],
        compiler_params=pltpu.CompilerParams(vmem_limit_bytes=VMEM_LIMIT),
        cost_estimate=pl.CostEstimate(
            flops=tokens * keys * width * 4, bytes_accessed=4 * (tokens + keys) * width,
            transcendentals=tokens * keys * HEADS // 2,
        ),
        name="attend_self" if causal else "attend_cross",
    )(meta, query, kv_own, kv_own, kv_par, kv_par, qext, kext, line)


def back_scratch(keys, group, causal):
    lanes = group * HEAD_DIM
    table = (group, TILE, TILE) if causal else (1, 8, LANES)
    return [
        pltpu.VMEM((group, keys, LANES), BF16),
        pltpu.VMEM((keys, lanes), BF16),
        pltpu.VMEM((keys // TILE, group, HEAD_DIM + (16 if causal else 0), TILE), BF16),
        pltpu.VMEM((group // 2, 2 * TILE, LANES), BF16),
        pltpu.VMEM((group // 2, 2 * TILE, LANES), BF16),
        pltpu.VMEM((group, TILE, LANES), BF16),
        pltpu.VMEM((8, TILE), F32),
        pltpu.VMEM(table, F32),
        pltpu.VMEM(table, F32),
        pltpu.VMEM((lanes, TILE), F32),
        pltpu.VMEM((keys, lanes), F32),
        pltpu.VMEM((keys, lanes), F32),
        pltpu.VMEM(table, F32),
        pltpu.VMEM((8, TILE), F32),
    ]


def attend_back_fast(meta, query, kv_own, kv_par, qext, kext, line, grad_mixed, mixed, lse, causal):
    tokens, width = query.shape
    own_rows, par_rows, keys = kv_own.shape[0], kv_par.shape[0], kext.shape[1]
    groups, lanes = HEADS // GROUP, GROUP * HEAD_DIM
    table = (GROUP, TILE, TILE) if causal else (1, 8, LANES)
    block = pl.BlockSpec((TILE, lanes), lambda g, i, meta: (i, g))
    line_spec = pl.BlockSpec((GROUP, 1, TILE), lambda g, i, meta: (g, 0, 0))
    return pl.pallas_call(
        functools.partial(attend_back_kernel, causal),
        grid_spec=pltpu.PrefetchScalarGridSpec(
            num_scalar_prefetch=1,
            grid=(groups, tokens // TILE),
            in_specs=attention_specs(own_rows, par_rows, keys)
            + [block, block, pl.BlockSpec((1, GROUP, TILE), lambda g, i, meta: (g, 0, i))],
            out_specs=[
                block,
                pl.BlockSpec((2, own_rows, lanes), lambda g, i, meta: (0, 0, g)),
                pl.BlockSpec((2, par_rows, lanes), lambda g, i, meta: (0, 0, g)),
                line_spec,
                line_spec,
            ],
            scratch_shapes=back_scratch(keys, GROUP, causal),
        ),
        out_shape=[
            jax.ShapeDtypeStruct((tokens, width), BF16),
            jax.ShapeDtypeStruct((2, own_rows, width), BF16),
            jax.ShapeDtypeStruct((2, par_rows, width), BF16),
            jax.ShapeDtypeStruct((HEADS, 1, TILE), F32),
            jax.ShapeDtypeStruct((HEADS, 1, TILE), F32),
        ],
        compiler_params=pltpu.CompilerParams(vmem_limit_bytes=VMEM_LIMIT),
        cost_estimate=pl.CostEstimate(
            flops=tokens * keys * width * 10, bytes_accessed=10 * (tokens + keys) * width,
            transcendentals=tokens * keys * HEADS // 2,
        ),
        name="attend_self_back" if causal else "attend_cross_back",
    )(meta, query, kv_own, kv_own, kv_par, kv_par, qext, kext, line, grad_mixed, mixed, lse)


AXES = ("dp", "seq")


def exchange(value, dp_bit, seq_bit):
    pairs = [
        (dp * 4 + seq, (dp ^ dp_bit) * 4 + (seq ^ seq_bit)) for dp in range(8) for seq in range(4)
    ]
    return lax.ppermute(value, AXES, pairs)


CORE, Z_LOW, Z_HIGH, X, Y = (1, 0), (2, 0), (4, 0), (0, 1), (0, 2)


def move_pairs(a, b):
    pairs = []
    for z in range(4):
        for core in range(2):
            for s in range(4):
                micro, half_core = (s >> 1) ^ a, (s & 1) ^ b
                pairs.append(((2 * z + core) * 4 + s, (2 * z + half_core) * 4 + 2 * core + micro))
    return pairs


ROUNDS = ((0, 0), (0, 1), (1, 0), (1, 1))


def take(value, index, axis):
    return lax.dynamic_index_in_dim(value, index, axis, keepdims=False)


MESH = pl.DeviceIdType.MESH


class Links:
    def __init__(self):
        dp, seq = lax.axis_index("dp"), lax.axis_index("seq")
        self.seq = seq
        self.z, self.core, self.y, self.x = dp // 2, dp % 2, seq // 2, seq % 2
        self.at_z = [{"dp": ((self.z + k) % 4) * 2 + self.core, "seq": seq} for k in (1, 2, 3)]
        self.at_x = {"dp": dp, "seq": seq + 1 - 2 * self.x}
        self.at_y = {"dp": dp, "seq": seq + 2 - 4 * self.y}
        self.at_core = {"dp": dp + 1 - 2 * self.core, "seq": seq}

    def at_plane(self, core, seq):
        return {"dp": 2 * self.z + core, "seq": seq}

    def greet(self):
        partners = list(self.at_z)
        for flip in (0, 1):
            for k in range(4):
                if flip or k:
                    core = 1 - self.core if flip else self.core
                    partners.append(self.at_plane(core, (self.seq + k) % 4))
        barrier = pltpu.get_barrier_semaphore()
        for partner in partners:
            pl.semaphore_signal(barrier, inc=1, device_id=partner, device_id_type=MESH)
        pl.semaphore_wait(barrier, len(partners))


def remote(source, target, send_sem, recv_sem, device):
    return pltpu.make_async_remote_copy(
        src_ref=source,
        dst_ref=target,
        send_sem=send_sem,
        recv_sem=recv_sem,
        device_id=device,
        device_id_type=MESH,
    )


def move_tokens(links, sources, targets, parts, local_sem, send_sem, recv_sem):
    waits = []
    for r, (a, b) in enumerate(ROUNDS):
        micro = 1 - links.y if a else links.y
        core = 1 - links.x if b else links.x
        chip = 2 * links.core + micro
        stays = (core == links.core) & (chip == links.seq)
        for n, (source, target, part) in enumerate(zip(sources, targets, parts)):
            if part is None:
                piece = source.at[micro]
            else:
                piece = source.at[micro, 0, pl.ds(b * part, part)]
            slot = target.at[links.seq]
            here = pltpu.make_async_copy(piece, slot, local_sem.at[r, n])
            away = remote(piece, slot, send_sem.at[r, n], recv_sem.at[r, n], links.at_plane(core, chip))

            @pl.when(stays)
            def _(here=here):
                here.start()

            @pl.when(jnp.logical_not(stays))
            def _(away=away):
                away.start()

            waits.append((stays, here, away))

    def finish():
        for stays, here, away in waits:
            @pl.when(stays)
            def _(here=here):
                here.wait()

            @pl.when(jnp.logical_not(stays))
            def _(away=away):
                away.wait()

    return finish


class Gather:
    def __init__(self, links, shards, wholes, local_sem, send_sem, recv_sem, plane_first=()):
        self.links, self.shards, self.wholes = links, shards, wholes
        self.plane_first = plane_first
        self.along_z = [len(shard.shape) == 3 for shard in shards]
        self.local_sem, self.send_sem, self.recv_sem = local_sem, send_sem, recv_sem

    def copy(self, w, slot, source, target, device):
        return remote(source, target, self.send_sem.at[w, slot], self.recv_sem.at[w, slot], device)

    def copies(self, stage, w):
        links, whole = self.links, self.wholes[w]
        z, core, y, x = links.z, links.core, links.y, links.x
        half = whole.shape[-1] // 2
        left, right = pl.ds(0, half), pl.ds(half, half)
        if w in self.plane_first and stage < 3:
            if stage == 0:
                own, shard = whole.at[z, core, y, x], self.shards[w]
                return [
                    self.copy(w, 0, shard.at[:, left], own.at[:, left], links.at_x),
                    self.copy(w, 1, shard.at[:, right], own.at[:, right], links.at_y),
                ]
            if stage == 1:
                one, two = whole.at[z, core, y, :, :, left], whole.at[z, core, :, x, :, right]
                return [self.copy(w, 2, one, one, links.at_y), self.copy(w, 3, two, two, links.at_x)]
            plane = whole.at[z, core]
            return [self.copy(w, 4 + k, plane, plane, links.at_z[k]) for k in range(3)]
        if stage == 0:
            own = whole.at[z, core, y, x]
            return [self.copy(w, k, self.shards[w], own, links.at_z[k]) for k in range(3)]
        if stage == 1:
            one, two = whole.at[:, core, y, x, :, left], whole.at[:, core, y, x, :, right]
            if self.along_z[w]:
                shard = self.shards[w]
                return [
                    self.copy(w, 3, shard.at[:, :, left], one, links.at_x),
                    self.copy(w, 4, shard.at[:, :, right], two, links.at_y),
                ]
            return [self.copy(w, 3, one, one, links.at_x), self.copy(w, 4, two, two, links.at_y)]
        if stage == 2:
            one, two = whole.at[:, core, y, :, :, left], whole.at[:, core, :, x, :, right]
            return [self.copy(w, 5, one, one, links.at_y), self.copy(w, 6, two, two, links.at_x)]
        both = whole.at[:, core]
        return [self.copy(w, 7, both, both, links.at_core)]

    def local(self, w):
        links = self.links
        z = slice(None) if self.along_z[w] else links.z
        own = self.wholes[w].at[z, links.core, links.y, links.x]
        return pltpu.make_async_copy(self.shards[w], own, self.local_sem.at[w])

    def begin(self):
        count = len(self.shards)
        for w in [*self.plane_first, *(w for w in range(count) if w not in self.plane_first)]:
            self.local(w).start()
            for copy in self.copies(1 if self.along_z[w] else 0, w):
                copy.start()

    def advance(self, stage, w):
        if stage == (2 if self.along_z[w] else 1):
            self.local(w).wait()
        for copy in self.copies(stage - 1, w):
            copy.wait_recv()
        for copy in self.copies(stage, w):
            copy.start()

    def steps(self):
        count = len(self.shards)
        order = []
        for t in range(count + 2):
            order += [(stage, t - stage + 1) for stage in (1, 2, 3) if 0 <= t - stage + 1 < count]
        return order

    def end(self):
        for w in range(len(self.shards)):
            for copy in self.copies(3, w):
                copy.wait_recv()
            for stage in range(1 if self.along_z[w] else 0, 4):
                for copy in self.copies(stage, w):
                    copy.wait_send()


def gather_kernel(count, later, parts, *refs):
    tokens = len(parts)
    shards, early, moved = refs[:count], refs[count : count + later], refs[count + later : count + later + tokens]
    refs = refs[count + later + tokens :]
    wholes, lines, settled = refs[:count], refs[count : count + later], refs[count + later : count + later + tokens]
    refs = refs[count + later + tokens :]
    local_sem, send_sem, recv_sem, z_local, z_send, z_recv, move_local, move_send, move_recv = refs
    links = Links()
    links.greet()
    gather = Gather(links, shards, wholes, local_sem, send_sem, recv_sem)
    gather.begin()
    finish = move_tokens(links, moved, settled, parts, move_local, move_send, move_recv)
    waits = []
    for w in range(later):
        own = lines[w].at[links.z]
        here = pltpu.make_async_copy(early[w], own, z_local.at[w])
        here.start()
        waits.append(here)
        for k in range(3):
            away = remote(early[w], own, z_send.at[w, k], z_recv.at[w, k], links.at_z[k])
            away.start()
            waits.append(away)
    for stage, w in gather.steps():
        gather.advance(stage, w)
    gather.end()
    finish()
    for copy in waits:
        copy.wait()


def attend_gather_kernel(count, q_ref, ko, vo, kp, vp, qext_ref, kext_ref, line_ref, *refs):
    sources, (o_ref, lse_ref), refs = refs[:count], refs[count : count + 2], refs[count + 2 :]
    wholes, scratch = refs[:count], refs[count : count + 8]
    shards = refs[count + 8 : 2 * count + 8]
    load_sem, local_sem, send_sem, recv_sem = refs[2 * count + 8 :]
    links = Links()
    gather = Gather(links, shards, wholes, local_sem, send_sem, recv_sem, PLANE_FIRST)
    step = pl.program_id(0) * pl.num_programs(1) + pl.program_id(1)
    total = (HEADS * HEAD_DIM // q_ref.shape[1]) * 4
    @pl.when(step == 0)
    def _():
        links.greet()
        loads = [pltpu.make_async_copy(sources[w], shards[w], load_sem.at[w]) for w in range(count)]
        for load in loads:
            load.start()
        for load in loads:
            load.wait()
        gather.begin()

    attend_kernel(True, None, q_ref, ko, vo, kp, vp, qext_ref, kext_ref, line_ref, o_ref, lse_ref, *scratch)
    for n in range(total):
        todo = [item for at, item in GATHER_PLAN if at == n]
        if todo or n == total - 1:
            @pl.when(step == n)
            def _(todo=todo, n=n):
                for stage, w in todo:
                    gather.advance(stage, w)
                if n == total - 1:
                    gather.end()


PLANE_FIRST = (5, 6, 7)
GATHER_PLAN = (
    (0, (1, 5)), (0, (1, 6)), (0, (1, 7)), (0, (2, 5)), (1, (2, 6)), (1, (2, 7)), (1, (1, 3)), (1, (2, 0)),
    (2, (1, 4)), (3, (2, 1)), (4, (2, 2)), (5, (2, 3)), (5, (3, 0)), (6, (2, 4)), (6, (3, 5)), (7, (3, 1)),
    (7, (3, 6)), (7, (3, 2)), (7, (3, 3)), (7, (3, 4)), (7, (3, 7)),
)


def attend_gather(query, kv_own, kv_par, qext, kext, line, shards):
    tokens, width = query.shape
    own_rows, par_rows, keys = kv_own.shape[0], kv_par.shape[0], kext.shape[1]
    groups, lanes, count = HEADS // GROUP, GROUP * HEAD_DIM, len(shards)
    table = (GROUP, TILE, TILE)
    whole = pl.BlockSpec(memory_space=pl.ANY)
    outs = pl.pallas_call(
        functools.partial(attend_gather_kernel, count),
        grid=(groups, tokens // TILE),
        in_specs=[without_meta(spec) for spec in attention_specs(own_rows, par_rows, keys)] + [whole] * count,
        out_specs=[
            pl.BlockSpec((TILE, lanes), lambda g, i: (i, g)),
            pl.BlockSpec((1, GROUP, TILE), lambda g, i: (g, 0, i)),
        ]
        + [whole] * count,
        scratch_shapes=attention_scratch(keys, lanes, table)
        + [pltpu.VMEM(shard.shape, BF16) for shard in shards]
        + [
            pltpu.SemaphoreType.DMA((count,)),
            pltpu.SemaphoreType.DMA((count,)),
            pltpu.SemaphoreType.DMA((count, 8)),
            pltpu.SemaphoreType.DMA((count, 8)),
        ],
        out_shape=[
            jax.ShapeDtypeStruct((tokens, width), BF16),
            jax.ShapeDtypeStruct((groups, GROUP, tokens), F32),
        ]
        + [jax.ShapeDtypeStruct((4, 2, 2, 2, *shard.shape[-2:]), BF16) for shard in shards],
        compiler_params=pltpu.CompilerParams(
            vmem_limit_bytes=VMEM_LIMIT, collective_id=2, has_side_effects=True
        ),
        cost_estimate=pl.CostEstimate(
            flops=tokens * keys * width * 4, bytes_accessed=4 * (tokens + keys) * width,
            transcendentals=tokens * keys * HEADS // 2,
        ),
        name="attend_gather",
    )(query, kv_own, kv_own, kv_par, kv_par, qext, kext, line, *shards)
    return outs[0], outs[1], [whole.reshape(-1, whole.shape[-1]) for whole in outs[2:]]


def gather_weights(shards, early, moved):
    count, later, tokens = len(shards), len(early), len(moved)
    sent = sum(shard.size for shard in shards) * 2
    parts = [None if value.ndim == 3 else value.shape[2] // 2 for value in moved]
    settled = [
        jax.ShapeDtypeStruct((4, value.shape[1] if part is None else part, value.shape[-1]), BF16)
        for value, part in zip(moved, parts)
    ]
    outs = pl.pallas_call(
        functools.partial(gather_kernel, count, later, parts),
        in_specs=[pl.BlockSpec(memory_space=pltpu.VMEM)] * (count + later)
        + [pl.BlockSpec(memory_space=pl.ANY)] * tokens,
        out_specs=[pl.BlockSpec(memory_space=pl.ANY)] * (count + later + tokens),
        out_shape=[jax.ShapeDtypeStruct((4, 2, 2, 2, *shard.shape), BF16) for shard in shards]
        + [jax.ShapeDtypeStruct((4, *shard.shape), BF16) for shard in early]
        + settled,
        scratch_shapes=[
            pltpu.SemaphoreType.DMA((count,)),
            pltpu.SemaphoreType.DMA((count, 8)),
            pltpu.SemaphoreType.DMA((count, 8)),
            pltpu.SemaphoreType.DMA((later,)),
            pltpu.SemaphoreType.DMA((later, 3)),
            pltpu.SemaphoreType.DMA((later, 3)),
            pltpu.SemaphoreType.DMA((4, tokens)),
            pltpu.SemaphoreType.DMA((4, tokens)),
            pltpu.SemaphoreType.DMA((4, tokens)),
        ],
        compiler_params=pltpu.CompilerParams(
            vmem_limit_bytes=VMEM_LIMIT, collective_id=0, has_side_effects=True
        ),
        cost_estimate=pl.CostEstimate(flops=0, transcendentals=0, bytes_accessed=500 * sent),
        name="gather_weights",
    )(*shards, *early, *moved)
    wholes = [whole.reshape(-1, whole.shape[-1]) for whole in outs[:count]]
    return wholes, outs[count : count + later], outs[count + later :]


def add_low(first, second):
    return (first.astype(F32) + second.astype(F32)).astype(BF16)


def return_tokens_kernel(links, source, target, part, local_sem, send_sem, recv_sem):
    waits, starts = [], []
    mine = 2 * (links.seq % 2) + links.core
    for s in range(4):
        half = (links.core + s) % 2
        slot = target.at[links.seq % 2, pl.ds(pl.multiple_of(half * part, part), part)]
        stays = (links.y == links.core) & (links.seq == s)
        here = pltpu.make_async_copy(source.at[s], slot, local_sem)
        away = remote(source.at[s], slot, send_sem.at[s], recv_sem.at[mine], links.at_plane(links.y, s))

        def start(stays=stays, here=here, away=away):
            @pl.when(stays)
            def _():
                here.start()

            @pl.when(jnp.logical_not(stays))
            def _():
                away.start()

        starts.append(start)
        waits.append((stays, here, away))

    def finish():
        for stays, here, away in waits:
            @pl.when(stays)
            def _(here=here):
                here.wait()

            @pl.when(jnp.logical_not(stays))
            def _(away=away):
                away.wait_send()

        for j in range(4):
            arrived = remote(
                source.at[0], target.at[0, pl.ds(0, part)], send_sem.at[0], recv_sem.at[j],
                links.at_core,
            )

            @pl.when(jnp.logical_not((links.y == links.core) & (mine == j)))
            def _(arrived=arrived):
                arrived.wait_recv()

    return starts, finish


class Scatter:
    def __init__(self, links, grads, sums, scratch):
        count = len(grads)
        self.links, self.grads, self.sums = links, grads, sums
        self.kept, self.got_one, self.got_two, self.got_z, self.own, self.totals = (
            scratch[j * count : (j + 1) * count] for j in range(6)
        )
        self.load_sem, self.store_sem, self.send_sem, self.recv_sem = scratch[6 * count :]

    def copy(self, w, slot, source, target, device):
        return remote(source, target, self.send_sem.at[w, slot], self.recv_sem.at[w, slot], device)

    def copies(self, stage, w):
        links, kept = self.links, self.kept[w]
        z, core, y, x = links.z, links.core, links.y, links.x
        half = kept.shape[-1] // 2
        left, right = pl.ds(0, half), pl.ds(half, half)
        if stage == 0:
            return [self.copy(w, 0, self.grads[w].at[:, 1 - core], kept, links.at_core)]
        if stage == 1:
            got = self.got_one[w]
            return [
                self.copy(w, 1, kept.at[:, :, 1 - x, :, left], got.at[0], links.at_x),
                self.copy(w, 2, kept.at[:, 1 - y, :, :, right], got.at[1], links.at_y),
            ]
        if stage == 2:
            got = self.got_two[w]
            return [
                self.copy(w, 3, kept.at[:, 1 - y, x, :, left], got.at[0], links.at_y),
                self.copy(w, 4, kept.at[:, y, 1 - x, :, right], got.at[1], links.at_x),
            ]
        return [
            self.copy(w, 5 + k, kept.at[(z + k + 1) % 4, y, x], self.got_z[w].at[k], links.at_z[k])
            for k in range(3)
        ]

    def load(self, w):
        return pltpu.make_async_copy(self.grads[w].at[:, self.links.core], self.own[w], self.load_sem.at[w])

    def store(self, w):
        return pltpu.make_async_copy(self.totals[w], self.sums[w], self.store_sem.at[w])

    def begin(self):
        for w in range(len(self.grads)):
            for copy in self.copies(0, w):
                copy.start()
            self.load(w).start()

    def advance(self, stage, w):
        kept, own, one, two = self.kept[w], self.own[w], self.got_one[w], self.got_two[w]
        z, y, x = self.links.z, self.links.y, self.links.x
        half, kind = kept.shape[-1] // 2, kept.dtype

        def add(first, second):
            return (first.astype(F32) + second.astype(F32)).astype(kind)

        def core_step(b, carry):
            zz, yy, xx = b // 4, (b // 2) % 2, b % 2
            kept[zz, yy, xx] = add(kept[zz, yy, xx], own[zz, yy, xx])
            return carry

        def one_step(b, carry):
            zz, other = b // 2, b % 2
            kept[zz, other, x, :, 0:half] = add(kept[zz, other, x, :, 0:half], one[0, zz, other])
            kept[zz, y, other, :, half : 2 * half] = add(
                kept[zz, y, other, :, half : 2 * half], one[1, zz, other]
            )
            return carry

        def two_step(zz, carry):
            kept[zz, y, x, :, 0:half] = add(kept[zz, y, x, :, 0:half], two[0, zz])
            kept[zz, y, x, :, half : 2 * half] = add(kept[zz, y, x, :, half : 2 * half], two[1, zz])
            return carry

        if stage == 1:
            self.load(w).wait()
        for copy in self.copies(stage - 1, w):
            copy.wait_recv()
        if stage < 4:
            lax.fori_loop(0, (16, 8, 4)[stage - 1], (core_step, one_step, two_step)[stage - 1], 0)
            for copy in self.copies(stage, w):
                copy.start()
        else:
            total = kept[z, y, x].astype(F32)
            for k in range(3):
                total = total + self.got_z[w][k].astype(F32)
            self.totals[w][...] = total
            self.store(w).start()

    def steps(self):
        count = len(self.grads)
        order = []
        for t in range(count + 3):
            order += [(stage, t - stage + 1) for stage in (1, 2, 3, 4) if 0 <= t - stage + 1 < count]
        return order

    def end(self):
        for w in range(len(self.grads)):
            self.store(w).wait()
            for stage in range(4):
                for copy in self.copies(stage, w):
                    copy.wait_send()


def scatter_scratch(shapes, types):
    count = len(shapes)

    def buffers(*lead, halved=False):
        return [
            pltpu.VMEM((*lead, rows, width // 2 if halved else width), kind)
            for (rows, width), kind in zip(shapes, types)
        ]

    return (
        buffers(4, 2, 2)
        + buffers(2, 4, 2, halved=True)
        + buffers(2, 4, halved=True)
        + buffers(3)
        + buffers(4, 2, 2)
        + [pltpu.VMEM(shape, F32) for shape in shapes]
        + [
            pltpu.SemaphoreType.DMA((count,)),
            pltpu.SemaphoreType.DMA((count,)),
            pltpu.SemaphoreType.DMA((count, 8)),
            pltpu.SemaphoreType.DMA((count, 8)),
        ]
    )


def rows_by_device(grads):
    return [grad.reshape(4, 2, 2, 2, grad.shape[0] // 32, grad.shape[1]) for grad in grads]


def scatter_kernel(count, part, *refs):
    grads, tokens, sums, returned = refs[:count], refs[count], refs[count + 1 : 2 * count + 1], refs[2 * count + 1]
    scratch, (back_local, back_send, back_recv) = refs[2 * count + 2 : -3], refs[-3:]
    links = Links()
    links.greet()
    scatter = Scatter(links, grads, sums, scratch)
    scatter.begin()
    starts, finish = return_tokens_kernel(links, tokens, returned, part, back_local, back_send, back_recv)
    for stage, w in scatter.steps():
        scatter.advance(stage, w)
        if (stage, w) == (2, count - 1):
            for start in starts:
                start()
    scatter.end()
    finish()


def attend_scatter_kernel(count, *refs):
    inputs, grads, tokens, refs = refs[:11], refs[11 : 11 + count], refs[11 + count], refs[12 + count :]
    outs, sums, returned, refs = refs[:5], refs[5 : 5 + count], refs[5 + count], refs[6 + count :]
    scratch, buffers, (back_local, back_send, back_recv) = refs[:14], refs[14:-3], refs[-3:]
    links = Links()
    scatter = Scatter(links, grads, sums, buffers)
    step = pl.program_id(0) * pl.num_programs(1) + pl.program_id(1)
    total = (HEADS * HEAD_DIM // inputs[0].shape[1]) * 4

    def tokens_back():
        return return_tokens_kernel(
            links, tokens, returned, tokens.shape[1], back_local, back_send, back_recv
        )

    @pl.when(step == 0)
    def _():
        links.greet()
        scatter.begin()
        for start in tokens_back()[0]:
            start()

    attend_back_kernel(True, None, *inputs, *outs, *scratch)
    for n in range(total):
        todo = [item for at, item in SCATTER_PACE if at == n]
        if todo or n == total - 1:
            @pl.when(step == n)
            def _(todo=todo, n=n):
                for stage, w in todo:
                    scatter.advance(stage, w)
                if n == total - 1:
                    scatter.end()
                    tokens_back()[1]()


SCATTER_PACE = (
    (1, (1, 0)), (3, (1, 1)), (4, (2, 0)), (7, (2, 1)), (7, (1, 2)), (8, (3, 0)), (10, (3, 1)), (10, (1, 3)),
    (12, (2, 2)), (12, (1, 4)), (13, (4, 0)), (13, (2, 3)), (14, (3, 2)), (14, (3, 3)), (15, (2, 4)),
    (15, (4, 1)), (15, (3, 4)), (15, (4, 2)), (15, (4, 3)), (15, (4, 4)),
)


def attend_scatter(query, kv_own, kv_par, qext, kext, line, grad_mixed, mixed, lse, grads, back):
    tokens, width = query.shape
    own_rows, par_rows, keys = kv_own.shape[0], kv_par.shape[0], kext.shape[1]
    group, count = GROUP // 2, len(grads)
    groups, lanes = HEADS // group, group * HEAD_DIM
    block = pl.BlockSpec((TILE, lanes), lambda g, i: (i, g))
    line_spec = pl.BlockSpec((group, 1, TILE), lambda g, i: (g, 0, 0))
    whole = pl.BlockSpec(memory_space=pl.ANY)
    shapes = [(grad.shape[0] // 32, grad.shape[1]) for grad in grads]
    outs = pl.pallas_call(
        functools.partial(attend_scatter_kernel, count),
        grid=(groups, tokens // TILE),
        in_specs=[without_meta(spec) for spec in attention_specs(own_rows, par_rows, keys, group)]
        + [block, block, pl.BlockSpec((1, group, TILE), lambda g, i: (g, 0, i))]
        + [whole] * (count + 1),
        out_specs=[
            block,
            pl.BlockSpec((2, own_rows, lanes), lambda g, i: (0, 0, g)),
            pl.BlockSpec((2, par_rows, lanes), lambda g, i: (0, 0, g)),
            line_spec,
            line_spec,
        ]
        + [whole] * (count + 1),
        scratch_shapes=back_scratch(keys, group, True)
        + scatter_scratch(shapes, [grad.dtype for grad in grads])
        + [
            pltpu.SemaphoreType.DMA,
            pltpu.SemaphoreType.DMA((4,)),
            pltpu.SemaphoreType.DMA((4,)),
        ],
        out_shape=[
            jax.ShapeDtypeStruct((tokens, width), BF16),
            jax.ShapeDtypeStruct((2, own_rows, width), BF16),
            jax.ShapeDtypeStruct((2, par_rows, width), BF16),
            jax.ShapeDtypeStruct((HEADS, 1, TILE), F32),
            jax.ShapeDtypeStruct((HEADS, 1, TILE), F32),
        ]
        + [jax.ShapeDtypeStruct(shape, F32) for shape in shapes]
        + [jax.ShapeDtypeStruct((2, 2 * back.shape[1], width), BF16)],
        compiler_params=pltpu.CompilerParams(
            vmem_limit_bytes=67043328, collective_id=3, has_side_effects=True
        ),
        cost_estimate=pl.CostEstimate(
            flops=tokens * keys * width * 10, bytes_accessed=10 * (tokens + keys) * width,
            transcendentals=tokens * keys * HEADS // 2,
        ),
        name="attend_scatter",
    )(query, kv_own, kv_own, kv_par, kv_par, qext, kext, line, grad_mixed, mixed,
      lse.reshape(groups, group, tokens), *rows_by_device(grads), back)
    return outs[:5], outs[5 : 5 + count], outs[5 + count]


def scatter_grads(grads, tokens):
    part = tokens.shape[1]
    count = len(grads)
    shapes = [(grad.shape[0] // 32, grad.shape[1]) for grad in grads]
    types = [grad.dtype for grad in grads]

    return pl.pallas_call(
        functools.partial(scatter_kernel, count, part),
        in_specs=[pl.BlockSpec(memory_space=pl.ANY)] * (count + 1),
        out_specs=[pl.BlockSpec(memory_space=pl.ANY)] * (count + 1),
        out_shape=[jax.ShapeDtypeStruct(shape, F32) for shape in shapes]
        + [jax.ShapeDtypeStruct((2, 2 * part, tokens.shape[2]), BF16)],
        scratch_shapes=scatter_scratch(shapes, types)
        + [
            pltpu.SemaphoreType.DMA,
            pltpu.SemaphoreType.DMA((4,)),
            pltpu.SemaphoreType.DMA((4,)),
        ],
        compiler_params=pltpu.CompilerParams(
            vmem_limit_bytes=67043328, collective_id=1, has_side_effects=True
        ),
        cost_estimate=pl.CostEstimate(
            flops=0, transcendentals=0, bytes_accessed=16 * sum(grad.size for grad in grads)
        ),
        name="scatter_grads",
    )(*rows_by_device(grads), tokens)


def norm_scale(value):
    return lax.rsqrt(jnp.mean(value * value, axis=-1, keepdims=True) + EPS)


def normed(value, gain):
    return (value * norm_scale(value) * gain).astype(BF16)


def norm_back(value, gain, grad):
    scale = norm_scale(value)
    scaled = grad * gain
    inner = jnp.mean(scaled * value, axis=-1, keepdims=True)
    return (
        scale * scaled - (scale * scale * scale) * value * inner,
        jnp.sum(grad * value * scale, axis=0),
    )


def dot(rows, weight):
    return jnp.dot(rows, weight, preferred_element_type=F32)


def dot_back(grads, weight):
    return contract(grads, weight, 1, 1)


def dot_weight(rows, grads):
    return contract(rows, grads, 0, 0).astype(BF16)


def fast_body(
    hidden_in,
    encoder_states,
    segments,
    enc_segments,
    grad_out,
    norm_self,
    q_self,
    k_self,
    v_self,
    o_self,
    rel_bias,
    norm_cross,
    q_cross,
    k_cross,
    v_cross,
    o_cross,
    norm_ff,
    wi_gate,
    wi_up,
    wo_ff,
):
    dp, seq = lax.axis_index("dp"), lax.axis_index("seq")
    core, z_low, z_high, y, x = dp % 2, (dp // 2) % 2, dp // 4, seq // 2, seq % 2
    place = (core, z_low, z_high, y, x)
    rows_dev, width = hidden_in.shape[2], hidden_in.shape[3]
    enc_dev = encoder_states.shape[2]
    part, enc_part = rows_dev // 2, enc_dev // 2
    owned_micro = seq % 2

    def send_tokens(pieces_of):
        return [
            lax.ppermute(pieces_of((seq // 2) ^ a, b), AXES, move_pairs(a, b)) for a, b in ROUNDS
        ]

    def settle(received):
        slots = []
        for s in range(4):
            index = 2 * ((s >> 1) ^ owned_micro) + ((s & 1) ^ core)
            slots.append(lax.select_n(index, *received))
        return jnp.stack(slots)

    def return_tokens(value):
        received = []
        for a, b in ROUNDS:
            index = 2 * (owned_micro ^ a) + (core ^ b)
            back = [(target, source) for source, target in move_pairs(a, b)]
            received.append(lax.ppermute(take(value, index, 0), AXES, back))
        flag = seq // 2
        micro = []
        for m in range(2):
            micro.append(
                jnp.concatenate(
                    [jnp.where((flag ^ m) == 0, received[b], received[2 + b]) for b in range(2)],
                    axis=0,
                )
            )
        return jnp.stack(micro)[:, None]

    codes = jnp.concatenate([segments[:, 0], enc_segments[:, 0]], axis=1).astype(BF16)
    codes = jnp.pad(codes, ((0, 0), (0, width - codes.shape[1])))
    codes = jnp.broadcast_to(codes[:, None], (2, 8, width))

    small = jnp.concatenate([norm_self, norm_cross, norm_ff, rel_bias])
    small_rows = norm_self.shape[0]
    small = jnp.broadcast_to(jnp.pad(small, (0, 2 * LANES - small.shape[0])), (8, 2 * LANES))
    wholes, ff_lines, (inputs_low, encoder, codes) = gather_weights(
        [small, k_self, v_self, q_self], [wi_gate, wi_up, wo_ff], [hidden_in, encoder_states, codes]
    )
    small, wk, wv, wq = wholes
    small = small.reshape(32, 8, 2 * LANES)[:, 0].astype(F32)
    gain_self, gain_cross, gain_ff = (
        small[:, j * small_rows : (j + 1) * small_rows].reshape(-1) for j in range(3)
    )
    table = small[:, 3 * small_rows : 3 * small_rows + rel_bias.shape[0]].reshape(BUCKETS, HEADS)
    ff = wi_gate.shape[1]

    inputs_low = inputs_low.reshape(4 * part, width)
    encoder = encoder.reshape(4 * enc_part, width)
    codes = codes[:, 0].astype(jnp.int32)
    seg_parts = codes[:, :rows_dev].reshape(4, 2, part)
    enc_parts = codes[:, rows_dev : rows_dev + enc_dev].reshape(4, 2, enc_part)

    def of_core(parts, which):
        return jnp.stack([take(parts[s], which ^ (s & 1), 0) for s in range(4)])

    seg_own = of_core(seg_parts, core)
    enc_own, enc_par = of_core(enc_parts, core), of_core(enc_parts, 1 - core)
    quarter = jnp.arange(4, dtype=jnp.int32)
    at_own = 2 * quarter + (core ^ (quarter % 2))
    at_par = 2 * quarter + ((1 - core) ^ (quarter % 2))
    tile_last = seg_parts.reshape(8, part)[:, -1]
    first_tile = jnp.sum((tile_last[None, :] < seg_own[:, :1]).astype(jnp.int32), axis=1)
    pairs = jnp.maximum(at_own - first_tile, 0) // 2
    meta = jnp.concatenate([at_own, at_par, pairs]).astype(jnp.int32)
    seg_keys = jnp.concatenate([jnp.full((part,), -1, jnp.int32), seg_parts.reshape(-1)])
    query_codes, key_codes = query_lanes(seg_own.reshape(-1)), key_lanes(seg_keys)
    cross_codes = key_lanes(jnp.concatenate([enc_own, enc_par]).reshape(-1))
    near = (
        buckets_of(jnp.arange(TILE, dtype=jnp.int32))[:, None] == jnp.arange(BUCKETS)[None, :]
    ).astype(F32)
    line = jnp.dot(near, table, precision=lax.Precision.HIGHEST).T.reshape(HEADS, 1, TILE)

    inputs = inputs_low.astype(F32)
    normed_self = normed(inputs, gain_self)
    kv_own = jnp.concatenate(
        [dot(normed_self, wk).astype(BF16), dot(normed_self, wv).astype(BF16)], axis=1
    )
    kv_par = exchange(kv_own, *CORE)
    query = dot(normed_self, wq).astype(BF16)
    mixed, self_lse, wholes = attend_gather(
        query, kv_own, kv_par, query_codes, key_codes, line,
        [*ff_lines, k_cross, v_cross, o_self, q_cross, o_cross],
    )
    w_gate, w_up, w_down, ck, cv, wo, cq, co = wholes
    cross_kv_own = jnp.concatenate(
        [dot(encoder, ck).astype(BF16), dot(encoder, cv).astype(BF16)], axis=1
    )
    cross_kv_par = exchange(cross_kv_own, *CORE)
    cross_kv_par, late_grad = lax.optimization_barrier((cross_kv_par, grad_out))
    out_parts = send_tokens(lambda micro, b: take(late_grad[:, 0, b * part : (b + 1) * part], micro, 0))
    after_self = inputs + dot(mixed, wo)
    normed_cross = normed(after_self, gain_cross)
    cross_query = dot(normed_cross, cq).astype(BF16)
    cross_mixed, cross_lse = attend_fast(
        meta, cross_query, cross_kv_own, cross_kv_par, query_codes, cross_codes, line, False
    )
    after_cross = after_self + dot(cross_mixed, co)
    normed_ff = normed(after_cross, gain_ff)
    gate, up_values = dot(normed_ff, w_gate), dot(normed_ff, w_up)
    hidden = gelu_mix(gate, up_values).astype(BF16)
    result = (after_cross + dot(hidden, w_down)).astype(BF16)
    block_out = return_tokens(result.reshape(4, part, width))

    out_low = settle(out_parts).reshape(4 * part, width)
    grad_result = out_low.astype(F32)
    grad_w_down = dot_weight(hidden, out_low)
    grad_hidden = dot_back(out_low, w_down)
    mix_value, mix_pull = jax.vjp(gelu_mix, gate, up_values)
    grad_gate, grad_up = (piece.astype(BF16) for piece in mix_pull(grad_hidden))
    grad_w_gate, grad_w_up = dot_weight(normed_ff, grad_gate), dot_weight(normed_ff, grad_up)
    grad_normed_ff = dot_back(grad_gate, w_gate) + dot_back(grad_up, w_up)
    ff_part, grad_gain_ff = norm_back(after_cross, gain_ff, grad_normed_ff)
    grad_after_cross = grad_result + ff_part
    cross_out_low = grad_after_cross.astype(BF16)
    grad_co = dot_weight(cross_mixed, cross_out_low)
    grad_cross_mixed = dot_back(cross_out_low, co).astype(BF16)
    grad_cross_query, cross_own, cross_par, unused, unused = attend_back_fast(
        meta, cross_query, cross_kv_own, cross_kv_par, query_codes, cross_codes, line,
        grad_cross_mixed, cross_mixed, cross_lse, False,
    )
    grad_cross_query, block_out = lax.optimization_barrier((grad_cross_query, block_out))
    cross_got = add_low(cross_own, exchange(cross_par, *CORE))
    grad_ck, grad_cv = dot_weight(encoder, cross_got[0]), dot_weight(encoder, cross_got[1])
    grad_encoder = (dot_back(cross_got[0], ck) + dot_back(cross_got[1], cv)).astype(BF16)
    grad_encoder = grad_encoder.reshape(4, enc_part, width)
    grad_cq = dot_weight(normed_cross, grad_cross_query)
    grad_normed_cross = dot_back(grad_cross_query, cq)
    cross_part, grad_gain_cross = norm_back(after_self, gain_cross, grad_normed_cross)
    grad_after_self = grad_after_cross + cross_part
    self_out_low = grad_after_self.astype(BF16)
    grad_wo = dot_weight(mixed, self_out_low)
    grad_mixed = dot_back(self_out_low, wo).astype(BF16)
    (grad_query, self_own, self_par, grad_line, grad_all), ff_grads, grad_encoder = (
        attend_scatter(
            query, kv_own, kv_par, query_codes, key_codes, line, grad_mixed, mixed, self_lse,
            [grad_w_gate, grad_w_up, grad_w_down, grad_co, grad_cq], grad_encoder,
        )
    )
    grad_w_gate, grad_w_up, grad_w_down, grad_co, grad_cq = ff_grads
    grad_encoder = grad_encoder.astype(F32)[:, None]
    self_got = add_low(self_own, exchange(self_par, *CORE))
    grad_wq = dot_weight(normed_self, grad_query)
    grad_wk, grad_wv = dot_weight(normed_self, self_got[0]), dot_weight(normed_self, self_got[1])
    grad_normed_self = (
        dot_back(grad_query, wq) + dot_back(self_got[0], wk) + dot_back(self_got[1], wv)
    )
    self_part, grad_gain_self = norm_back(inputs, gain_self, grad_normed_self)
    grad_hidden_in = (grad_after_self + self_part).astype(BF16).reshape(4, part, width)

    grad_table = jnp.dot(near.T, grad_line.reshape(HEADS, TILE).T, precision=lax.Precision.HIGHEST)
    grad_far = jnp.sum((grad_all - grad_line).reshape(HEADS, TILE), axis=1)
    grad_table = grad_table.at[BUCKETS - 1].add(grad_far)
    small_grads = [piece.reshape(32, -1) for piece in (grad_gain_self, grad_gain_cross, grad_gain_ff)]
    small_grads = jnp.concatenate(small_grads + [grad_table.reshape(32, -1)], axis=1)
    small_grads = jnp.pad(small_grads, ((0, 0), (0, 2 * LANES - small_grads.shape[1])))
    small_grads = jnp.broadcast_to(small_grads[:, None], (32, 8, 2 * LANES)).reshape(256, 2 * LANES)
    order = [
        grad_ck, grad_cv, grad_wk, grad_wv,
        grad_wo, grad_wq, small_grads,
    ]
    (
        grad_ck, grad_cv, grad_wk, grad_wv,
        grad_wo, grad_wq, small_grads, grad_hidden_in,
    ) = scatter_grads(order, grad_hidden_in)
    small_grads = small_grads[0]
    return (
        block_out,
        grad_hidden_in.astype(F32)[:, None],
        grad_encoder,
        small_grads[:small_rows],
        grad_wq,
        grad_wk,
        grad_wv,
        grad_wo,
        small_grads[3 * small_rows : 3 * small_rows + rel_bias.shape[0]],
        small_grads[small_rows : 2 * small_rows],
        grad_cq,
        grad_ck,
        grad_cv,
        grad_co,
        small_grads[2 * small_rows : 3 * small_rows],
        grad_w_gate,
        grad_w_up,
        grad_w_down,
    )


def fits_fast(mesh):
    return mesh.shape["dp"] == 8 and mesh.shape["seq"] == 4


def solution(mesh):
    return jax.shard_map(
        fast_body if fits_fast(mesh) else general_body,
        mesh=mesh,
        in_specs=(
            P(None, "dp", "seq", None),
            P(None, "dp", "seq", None),
            P(None, "dp", "seq"),
            P(None, "dp", "seq"),
            P(None, "dp", "seq", None),
            P(("dp", "seq")),
            P(("dp", "seq"), None),
            P(("dp", "seq"), None),
            P(("dp", "seq"), None),
            P(("dp", "seq"), None),
            P(("dp", "seq")),
            P(("dp", "seq")),
            P(("dp", "seq"), None),
            P(("dp", "seq"), None),
            P(("dp", "seq"), None),
            P(("dp", "seq"), None),
            P(("dp", "seq")),
            P(("dp", "seq"), None),
            P(("dp", "seq"), None),
            P(("dp", "seq"), None),
        ),
        out_specs=(
            P(None, "dp", "seq", None),
            P(None, "dp", "seq", None),
            P(None, "dp", "seq", None),
            P(("dp", "seq")),
            P(("dp", "seq"), None),
            P(("dp", "seq"), None),
            P(("dp", "seq"), None),
            P(("dp", "seq"), None),
            P(("dp", "seq")),
            P(("dp", "seq")),
            P(("dp", "seq"), None),
            P(("dp", "seq"), None),
            P(("dp", "seq"), None),
            P(("dp", "seq"), None),
            P(("dp", "seq")),
            P(("dp", "seq"), None),
            P(("dp", "seq"), None),
            P(("dp", "seq"), None),
        ),
        check_vma=False,
    )
```
